32 devices in a mesh: seq: 8 (over y, x, core), tp: 4 (over z).
Axes of the slice: x: 2, y: 2, z: 4, core: 2. Of those that a mesh axis runs over, the one named last changes fastest.
Arguments:
- byte_states: bfloat16 [2048, 1024], P('seq'), may hold values from -6 to 6
- enc_gain: bfloat16 [1024], replicated, may hold values from 0.25 to 1.75
- enc_qkv: bfloat16 [3, 1024, 1024], P(None, None, 'tp')
- enc_proj_out: bfloat16 [1024, 1024], P('tp'), may hold values from -0.1875 to 0.1875
- starts: int32 [8, 64], P('seq'), may hold values from 0 to 2048, as said below
- counts: int32 [8], P('seq'), may hold values from 32 to 64, as said below
- lift: bfloat16 [1024, 4096], P(None, 'tp')
- cross_kv: bfloat16 [2, 1024, 4096], P(None, None, 'tp')
- latent_gain: bfloat16 [4096], replicated, may hold values from 0.25 to 1.75
- lat_qkv: bfloat16 [3, 4096, 2048], P(None, 'seq', 'tp')
- lat_proj_out: bfloat16 [2048, 4096], P('tp', 'seq'), may hold values from -0.75 to 0.75
Outputs:
- byte_out: bfloat16 [2048, 1024], P('seq')
- latent_out: bfloat16 [512, 4096], P('seq', 'tp')
The draws below stay inside these ranges and needn't reach their ends.
Inputs may be any that keep to these rules, and one draw needn't show every extreme that they name: `starts`: row s lists in increasing order the first byte (counted over all 2048 bytes) of each patch beginning in bytes s * 256 to (s + 1) * 256 - 1, then 2048 in unused places. Byte 0 begins a patch; every row's first patch begins fewer than 8 bytes into its block, and in some row exactly 7 bytes in. counts[s] is the number of patches listed in row s of starts; some row holds 64.
All inputs are finite; a program needn't handle non-finite values.
Results may differ from the reference program's by a relative error of at most 0.018.
Values may be sent and summed in bfloat16 or wider, within the bound.
A program may use at most 128 MiB of HBM per device.

```python
import math
import jax
import jax.numpy as jnp
from jax import lax

DE = 1024
EH = 64
D = 4096
HD = 128
HL = 16
WIN = 512
SPILL = 8
B_DEV = 256
BYTES = 2048
P_CAP = 64
C_MIN = 32
N_SEQ = 8


def patch_table(key):
    stream = jax.random.fold_in(key, 11)
    split_keys = jax.random.split(stream, 5)
    spill_row = jax.random.randint(split_keys[0], (), 1, N_SEQ)
    full_row = (spill_row + jax.random.randint(split_keys[1], (), 1, N_SEQ)) % N_SEQ
    spread = P_CAP - C_MIN
    first_draw = jax.random.randint(split_keys[2], (N_SEQ,), 0, spread + 1)
    second_draw = jax.random.randint(split_keys[3], (N_SEQ,), 0, spread + 1)
    amounts = P_CAP - first_draw * second_draw // spread
    row_ids = jnp.arange(N_SEQ, dtype=jnp.int32)
    amounts = jnp.where(row_ids == full_row, P_CAP, jnp.where(row_ids == spill_row, C_MIN, amounts))
    slot_ids = jnp.arange(P_CAP, dtype=jnp.int32)
    lower_edge = slot_ids[None, :] * B_DEV // amounts[:, None]
    upper_edge = (slot_ids[None, :] + 1) * B_DEV // amounts[:, None]
    span_sizes = jnp.maximum(upper_edge - lower_edge, 1)
    jitter = jax.random.randint(split_keys[4], (N_SEQ, P_CAP), 0, span_sizes)
    first_col = slot_ids[None, :] == 0
    jitter = jnp.where(first_col & (row_ids[:, None] == spill_row), span_sizes - 1, jitter)
    jitter = jnp.where(first_col & (row_ids[:, None] == 0), 0, jitter)
    start_table = jnp.where(slot_ids[None, :] < amounts[:, None], row_ids[:, None] * B_DEV + lower_edge + jitter, BYTES)
    return (start_table.astype(jnp.int32), amounts.astype(jnp.int32))


def draw_starts(key, part):
    return patch_table(key)[0]


def draw_counts(key, part):
    return patch_table(key)[1]


def weight_block(key, shape, fan_in):
    multiplier = 1.0 / math.sqrt(fan_in)
    return jax.random.truncated_normal(key, -4.0, 4.0, shape, jnp.float32) * multiplier


def draw_byte_states(key, part):
    independent = jax.random.normal(jax.random.fold_in(key, 21), (BYTES, DE), jnp.float32)
    values = independent
    return jnp.clip(values, -6.0, 6.0).astype(jnp.bfloat16)


def draw_enc_qkv(key, part):
    query_cols = weight_block(jax.random.fold_in(key, 31), (DE, DE), DE)
    key_cols = weight_block(jax.random.fold_in(key, 32), (DE, DE), DE)
    value_cols = weight_block(jax.random.fold_in(key, 33), (DE, DE), DE)
    return jnp.stack([query_cols, key_cols, value_cols]).astype(jnp.bfloat16)


def cross_tables(key):
    stream = jax.random.fold_in(key, 41)
    lift_cols = weight_block(jax.random.fold_in(stream, 1), (DE, D), DE)
    key_cols = weight_block(jax.random.fold_in(stream, 2), (DE, D), DE)
    value_cols = weight_block(jax.random.fold_in(stream, 3), (DE, D), DE)
    return (lift_cols, jnp.stack([key_cols, value_cols]))


def draw_lift(key, part):
    return cross_tables(key)[0].astype(jnp.bfloat16)


def draw_cross_kv(key, part):
    return cross_tables(key)[1].astype(jnp.bfloat16)


def draw_lat_qkv(key, part):
    query_cols = weight_block(jax.random.fold_in(key, 51), (D, HL * HD), D)
    key_cols = weight_block(jax.random.fold_in(key, 52), (D, HL * HD), D)
    value_cols = weight_block(jax.random.fold_in(key, 53), (D, HL * HD), D)
    return jnp.stack([query_cols, key_cols, value_cols]).astype(jnp.bfloat16)


def shard_levels(key, shape, pieces, low, high):
    loudness, own = 1.0, jax.random.fold_in(key, 6)
    for dim, blocks in pieces:
        heights = jnp.exp(jax.random.uniform(jax.random.fold_in(own, dim), (blocks,), jnp.float32, low / len(pieces), high / len(pieces)))
        loudness = loudness * jnp.repeat(heights, shape[dim] // blocks).reshape([-1 if axis == dim else 1 for axis in range(len(shape))])
    return loudness


def bell_draw(rng, shape, deviation, limit, cuts=(), held_as=jnp.bfloat16):
    result = jax.random.normal(rng, shape, jnp.float32) * deviation
    if len(cuts) > 0:
        result = shard_levels(rng, shape, cuts, -0.22, 0.18) * result
    return jnp.clip(result, min=-limit, max=limit).astype(held_as)


def setup_inputs(seed: int = 0) -> dict:
    splits = jax.random.split(jax.random.key(seed), 12)
    byte_states = draw_byte_states(jax.random.fold_in(splits[11], 71), 0)
    enc_gain = jnp.clip(1.0 + 0.15 * jax.random.normal(splits[1], (DE,), jnp.float32), 0.25, 1.75).astype(jnp.bfloat16)
    enc_qkv = draw_enc_qkv(jax.random.fold_in(splits[11], 71), 0)
    enc_proj_out = bell_draw(splits[3], (DE, DE), DE ** -0.5, 0.1875, ((0, 4),))
    starts = draw_starts(jax.random.fold_in(splits[11], 71), 0)
    counts = draw_counts(jax.random.fold_in(splits[11], 71), 0)
    lift = draw_lift(jax.random.fold_in(splits[11], 71), 0)
    cross_kv = draw_cross_kv(jax.random.fold_in(splits[11], 71), 0)
    latent_gain = jnp.clip(1.0 + 0.15 * jax.random.normal(splits[8], (D,), jnp.float32), 0.25, 1.75).astype(jnp.bfloat16)
    lat_qkv = draw_lat_qkv(jax.random.fold_in(splits[11], 71), 0)
    lat_proj_out = bell_draw(splits[10], (HL * HD, D), (HL * HD // 32) ** -0.5, 0.75, ((0, 4), (1, 8)))
    return dict(byte_states=byte_states, enc_gain=enc_gain, enc_qkv=enc_qkv, enc_proj_out=enc_proj_out, starts=starts, counts=counts, lift=lift, cross_kv=cross_kv, latent_gain=latent_gain, lat_qkv=lat_qkv, lat_proj_out=lat_proj_out)


epsilon = 1e-05
rope_base = 500000.0
far_position = 1 << 30

def rms_scale(values, gain_row):
    mean_square = lax.optimization_barrier(jnp.mean(values * values, axis=-1, keepdims=True))
    return values * lax.rsqrt(mean_square + epsilon) * gain_row

def masked_softmax(scores, allowed):
    scores = jnp.where(allowed, scores, -1e+30)
    largest = lax.optimization_barrier(jnp.max(scores, axis=-1, keepdims=True))
    raised = jnp.where(allowed, jnp.exp(scores - largest), 0.0)
    return raised / lax.optimization_barrier(jnp.sum(raised, axis=-1, keepdims=True))

def rotate(values, position):
    halfway = values.shape[-1] // 2
    frequency = jnp.power(rope_base, -2.0 * jnp.arange(halfway, dtype=jnp.float32) / values.shape[-1])
    angles = position.astype(jnp.float32)[:, None] * frequency[None, :]
    cosine = jnp.cos(angles)[:, None, :]
    sine_rows = jnp.sin(angles)[:, None, :]
    lower_half = values[..., :halfway]
    upper_half = values[..., halfway:]
    return jnp.concatenate([lower_half * cosine - upper_half * sine_rows, upper_half * cosine + lower_half * sine_rows], axis=-1)

def encoder_layer(byte_states, enc_gain, enc_qkv, enc_proj_out):
    states = byte_states.astype(jnp.float32)
    normed = rms_scale(states, enc_gain.astype(jnp.float32)).astype(jnp.bfloat16)
    projected = jnp.einsum('bd,idc->ibc', normed.astype(jnp.float32), enc_qkv.astype(jnp.float32)).astype(jnp.bfloat16)
    head_count = projected.shape[2] // EH
    padding = jnp.zeros((WIN, projected.shape[2]), jnp.bfloat16)
    key_rows = jnp.concatenate([padding, projected[1]], axis=0)
    value_rows = jnp.concatenate([padding, projected[2]], axis=0)

    def attend(block_id):
        opening = block_id * WIN
        queries = lax.dynamic_slice_in_dim(projected[0], opening, WIN, 0).reshape(WIN, head_count, EH).astype(jnp.float32)
        near_keys = lax.dynamic_slice_in_dim(key_rows, opening, 2 * WIN, 0).reshape(2 * WIN, head_count, EH).astype(jnp.float32)
        near_values = lax.dynamic_slice_in_dim(value_rows, opening, 2 * WIN, 0).reshape(2 * WIN, head_count, EH).astype(jnp.float32)
        scores = jnp.einsum('qhd,khd->hqk', queries, near_keys) * (1.0 / math.sqrt(EH))
        query_pos = opening + jnp.arange(WIN, dtype=jnp.int32)
        key_pos = opening - WIN + jnp.arange(2 * WIN, dtype=jnp.int32)
        allowed = (key_pos[None, :] <= query_pos[:, None]) & (key_pos[None, :] > query_pos[:, None] - WIN) & (key_pos[None, :] >= 0)
        weights = masked_softmax(scores, allowed[None]).astype(jnp.bfloat16)
        attended = jnp.einsum('hqk,khd->qhd', weights.astype(jnp.float32), near_values)
        return attended.reshape(WIN, head_count * EH).astype(jnp.bfloat16)
    attended = lax.map(attend, jnp.arange(BYTES // WIN, dtype=jnp.int32)).reshape(BYTES, -1)
    return (states + jnp.dot(attended, enc_proj_out, preferred_element_type=jnp.float32)).astype(jnp.bfloat16)

def patch_block(extended, first_byte, end_byte, in_use, anchor, lift, cross_kv):
    columns = anchor + jnp.arange(extended.shape[0], dtype=jnp.int32)
    inside = (columns[None, :] >= first_byte[:, None]) & (columns[None, :] < end_byte[:, None]) & in_use[:, None]
    member = inside.astype(jnp.bfloat16)
    totals = jnp.dot(member, extended, preferred_element_type=jnp.float32)
    lengths = jnp.maximum(lax.optimization_barrier(jnp.sum(inside.astype(jnp.float32), axis=1)), 1.0)
    pooled = (totals / lengths[:, None]).astype(jnp.bfloat16)
    lifted = jnp.dot(pooled, lift, preferred_element_type=jnp.float32)
    key_rows = jnp.dot(extended, cross_kv[0], preferred_element_type=jnp.float32).astype(jnp.bfloat16)
    value_rows = jnp.dot(extended, cross_kv[1], preferred_element_type=jnp.float32).astype(jnp.bfloat16)
    slot_total = first_byte.shape[0]
    head_count = lifted.shape[1] // HD
    queries = lifted.astype(jnp.bfloat16).reshape(slot_total, head_count, HD)
    scores = jnp.einsum('phd,khd->hpk', queries.astype(jnp.float32), key_rows.reshape(-1, head_count, HD).astype(jnp.float32)) * (1.0 / math.sqrt(HD))
    allowed = inside | (~in_use)[:, None] & (columns[None, :] == anchor)
    weights = masked_softmax(scores, allowed[None]).astype(jnp.bfloat16)
    crossed = jnp.einsum('hpk,khd->phd', weights.astype(jnp.float32), value_rows.reshape(-1, head_count, HD).astype(jnp.float32))
    crossed = crossed.reshape(slot_total, head_count * HD)
    return jnp.where(in_use[:, None], lifted + crossed, 0.0).astype(jnp.bfloat16)

def latent_layer(patch_rows, in_use, position, latent_gain, lat_qkv, lat_proj_out):
    states = patch_rows.astype(jnp.float32)
    normed = rms_scale(states, latent_gain.astype(jnp.float32)).astype(jnp.bfloat16)
    projected = jnp.einsum('pd,idc->ipc', normed.astype(jnp.float32), lat_qkv.astype(jnp.float32))
    row_total = patch_rows.shape[0]
    head_count = projected.shape[2] // HD
    queries = rotate(projected[0].reshape(row_total, head_count, HD), position).astype(jnp.bfloat16)
    key_rows = rotate(projected[1].reshape(row_total, head_count, HD), position).astype(jnp.bfloat16)
    value_rows = projected[2].reshape(row_total, head_count, HD).astype(jnp.bfloat16)
    key_pos = jnp.where(in_use, position, far_position)
    allowed = key_pos[None, :] <= position[:, None]

    def attend(head_rows):
        query_head, key_head, value_head = head_rows
        scores = jnp.dot(query_head, key_head.T, preferred_element_type=jnp.float32) * (1.0 / math.sqrt(HD))
        weights = masked_softmax(scores, allowed).astype(jnp.bfloat16)
        return jnp.dot(weights, value_head, preferred_element_type=jnp.float32).astype(jnp.bfloat16)
    attended = lax.map(attend, (queries.transpose(1, 0, 2), key_rows.transpose(1, 0, 2), value_rows.transpose(1, 0, 2)))
    attended = attended.transpose(1, 0, 2).reshape(row_total, head_count * HD)
    summed = states + jnp.dot(attended, lat_proj_out, preferred_element_type=jnp.float32)
    return jnp.where(in_use[:, None], summed, 0.0).astype(jnp.bfloat16)

def reference(byte_states, enc_gain, enc_qkv, enc_proj_out, starts, counts, lift, cross_kv, latent_gain, lat_qkv, lat_proj_out):
    encoded = encoder_layer(byte_states, enc_gain, enc_qkv, enc_proj_out)
    anchors = jnp.arange(N_SEQ, dtype=jnp.int32) * B_DEV
    first_local = starts[:, 0] - anchors
    next_first = jnp.concatenate([first_local[1:], jnp.zeros((1,), jnp.int32)])
    slot_ids = jnp.arange(P_CAP, dtype=jnp.int32)
    in_use = slot_ids[None, :] < counts[:, None]
    following = jnp.concatenate([starts[:, 1:], jnp.zeros((N_SEQ, 1), jnp.int32)], axis=1)
    patch_end = jnp.where(slot_ids[None, :] + 1 < counts[:, None], following, (anchors + B_DEV + next_first)[:, None])
    padded = jnp.concatenate([encoded, jnp.zeros((SPILL, DE), jnp.bfloat16)], axis=0)

    def one_shard(shard_items):
        anchor, first_byte, end_byte, shard_use = shard_items
        extended = lax.dynamic_slice_in_dim(padded, anchor, B_DEV + SPILL, 0)
        return patch_block(extended, first_byte, end_byte, shard_use, anchor, lift, cross_kv)
    patches = lax.map(one_shard, (anchors, starts, patch_end, in_use)).reshape(N_SEQ * P_CAP, -1)
    offsets = (jnp.cumsum(counts) - counts).astype(jnp.int32)
    position = (offsets[:, None] + slot_ids[None, :]).reshape(-1).astype(jnp.int32)
    latent = latent_layer(patches, in_use.reshape(-1), position, latent_gain, lat_qkv, lat_proj_out)
    return (encoded, latent)
```

```python
import math

import jax
import numpy as np
import jax.numpy as jnp
from jax import lax
from jax.experimental import pallas as pl
from jax.experimental.pallas import tpu as pltpu
from jax.sharding import PartitionSpec as P

EH = 64
HD = 128
WIN = 512
SPILL = 8


epsilon = 1e-05
rope_base = 500000.0
far_position = 1 << 30


def from_behind(value, axis, steps):
    count = lax.axis_size(axis)
    leading, last = (max(0, -steps), min(count, count - steps))
    return lax.ppermute(value, axis, [(source, source + steps) for source in range(leading, last)])


def prefix(value, axis, join, neutral):
    count, mine = (lax.axis_size(axis), lax.axis_index(axis))
    pieces = lax.all_gather(value, axis)
    subtotal = jnp.full_like(value, 0) + jnp.asarray(neutral, value.dtype)

    def hop(position, subtotal):
        longer = join(subtotal, pieces[position])
        return jnp.where(position < mine, longer, subtotal)

    return lax.fori_loop(0, count - 1, hop, subtotal)


def shortened(value):

    def short(part):
        return part.astype(jnp.bfloat16) if part.dtype == jnp.float32 else part

    return jax.tree.map(short, value)


def rms_scale(values, gain_row):
    mean_square = jnp.mean(values * values, axis=-1, keepdims=True)
    return values * lax.rsqrt(mean_square + epsilon) * gain_row


def masked_softmax(scores, allowed):
    scores = jnp.where(allowed, scores, -1e30)
    largest = jnp.max(scores, axis=-1, keepdims=True)
    raised = jnp.where(allowed, jnp.exp(scores - largest), 0.0)
    return raised / jnp.sum(raised, axis=-1, keepdims=True)


def rotate(values, position):
    halfway = values.shape[-1] // 2
    frequency = jnp.power(
        rope_base, -2.0 * jnp.arange(halfway, dtype=jnp.float32) / values.shape[-1]
    )
    angles = position.astype(jnp.float32)[:, None] * frequency[None, :]
    cosine = jnp.cos(angles)[:, None, :]
    sine_rows = jnp.sin(angles)[:, None, :]
    lower_half = values[..., :halfway]
    upper_half = values[..., halfway:]
    return jnp.concatenate(
        [
            lower_half * cosine - upper_half * sine_rows,
            upper_half * cosine + lower_half * sine_rows,
        ],
        axis=-1,
    )


def patch_block(extended, first_byte, end_byte, in_use, anchor, lift, cross_kv):
    columns = anchor + jnp.arange(extended.shape[0], dtype=jnp.int32)
    inside = (
        (columns[None, :] >= first_byte[:, None])
        & (columns[None, :] < end_byte[:, None])
        & in_use[:, None]
    )
    member = inside.astype(jnp.bfloat16)
    totals = jnp.dot(member, extended, preferred_element_type=jnp.float32)
    lengths = jnp.maximum(jnp.sum(inside.astype(jnp.float32), axis=1), 1.0)
    pooled = (totals / lengths[:, None]).astype(jnp.bfloat16)
    lifted = jnp.dot(pooled, lift, preferred_element_type=jnp.float32)
    key_rows = jnp.dot(extended, cross_kv[0], preferred_element_type=jnp.float32).astype(
        jnp.bfloat16
    )
    value_rows = jnp.dot(extended, cross_kv[1], preferred_element_type=jnp.float32).astype(
        jnp.bfloat16
    )
    slot_total = first_byte.shape[0]
    head_count = lifted.shape[1] // HD
    queries = lifted.astype(jnp.bfloat16).reshape(slot_total, head_count, HD)
    scores = jnp.einsum(
        "phd,khd->hpk",
        queries,
        key_rows.reshape(-1, head_count, HD),
        preferred_element_type=jnp.float32,
    ) * (1.0 / math.sqrt(HD))
    allowed = inside | (~in_use)[:, None] & (columns[None, :] == anchor)
    weights = masked_softmax(scores, allowed[None]).astype(jnp.bfloat16)
    crossed = jnp.einsum(
        "hpk,khd->phd",
        weights,
        value_rows.reshape(-1, head_count, HD),
        preferred_element_type=jnp.float32,
    )
    crossed = crossed.reshape(slot_total, head_count * HD)
    return jnp.where(in_use[:, None], lifted + crossed, 0.0).astype(jnp.bfloat16)


def add_counts(earlier, later):
    return earlier + later


def gathered_shards(
    byte_states,
    enc_gain,
    enc_qkv,
    enc_proj_out,
    starts,
    counts,
    lift,
    cross_kv,
    latent_gain,
    lat_qkv,
    lat_proj_out,
):
    byte_rows = byte_states.shape[0]
    anchor = lax.axis_index("seq") * byte_rows
    states = byte_states.astype(jnp.float32)
    normed = rms_scale(states, enc_gain.astype(jnp.float32)).astype(jnp.bfloat16)
    projected = jnp.einsum(
        "bd,idc->ibc", normed, enc_qkv, preferred_element_type=jnp.float32
    ).astype(jnp.bfloat16)
    reach_blocks = max(WIN // byte_rows, 1)
    tail_rows = min(WIN, byte_rows)
    key_parts = []
    value_parts = []
    for distance in range(reach_blocks, 0, -1):
        moved_keys, moved_values = from_behind(
            (projected[1, byte_rows - tail_rows :], projected[2, byte_rows - tail_rows :]),
            "seq",
            distance,
        )
        key_parts.append(moved_keys)
        value_parts.append(moved_values)
    key_rows = jnp.concatenate(key_parts + [projected[1]], axis=0)
    value_rows = jnp.concatenate(value_parts + [projected[2]], axis=0)
    head_count = projected.shape[2] // EH
    scores = jnp.einsum(
        "qhd,khd->hqk",
        projected[0].reshape(byte_rows, head_count, EH),
        key_rows.reshape(-1, head_count, EH),
        preferred_element_type=jnp.float32,
    ) * (1.0 / math.sqrt(EH))
    query_pos = anchor + jnp.arange(byte_rows, dtype=jnp.int32)
    key_pos = anchor - WIN + jnp.arange(WIN + byte_rows, dtype=jnp.int32)
    allowed = (
        (key_pos[None, :] <= query_pos[:, None])
        & (key_pos[None, :] > query_pos[:, None] - WIN)
        & (key_pos[None, :] >= 0)
    )
    weights = masked_softmax(scores, allowed[None]).astype(jnp.bfloat16)
    attended = jnp.einsum(
        "hqk,khd->qhd",
        weights,
        value_rows.reshape(-1, head_count, EH),
        preferred_element_type=jnp.float32,
    )
    attended = attended.reshape(byte_rows, head_count * EH).astype(jnp.bfloat16)
    blended = lax.psum(jnp.dot(attended, enc_proj_out, preferred_element_type=jnp.float32), "tp")
    encoded = (states + blended).astype(jnp.bfloat16)
    patch_count = counts[0]
    local_starts = starts[0]
    first_local = (local_starts[0:1] - anchor).astype(jnp.bfloat16)
    next_rows, next_first = from_behind((encoded[:SPILL], first_local), "seq", -1)
    next_first = next_first.astype(jnp.int32)[0]
    extended = jnp.concatenate([encoded, next_rows], axis=0)
    slot_ids = jnp.arange(local_starts.shape[0], dtype=jnp.int32)
    in_use = slot_ids < patch_count
    following = jnp.concatenate([local_starts[1:], jnp.zeros((1,), jnp.int32)])
    patch_end = jnp.where(slot_ids + 1 < patch_count, following, anchor + byte_rows + next_first)
    patches = patch_block(extended, local_starts, patch_end, in_use, anchor, lift, cross_kv)
    offset = prefix(counts, "seq", add_counts, jnp.zeros((1,), jnp.int32))[0]
    position = offset + slot_ids
    slot_total = patches.shape[0]
    full_rows = lax.all_gather(patches, "tp", axis=1, tiled=True)
    normed_rows = rms_scale(full_rows.astype(jnp.float32), latent_gain.astype(jnp.float32)).astype(
        jnp.bfloat16
    )
    inner_width = lat_qkv.shape[2]
    projected = jnp.einsum(
        "pd,idc->ipc",
        normed_rows,
        lax.all_gather(lat_qkv, "seq", axis=1, tiled=True),
        preferred_element_type=jnp.float32,
    )
    heads_here = inner_width // HD
    queries = rotate(projected[0].reshape(slot_total, heads_here, HD), position).astype(
        jnp.bfloat16
    )
    latent_keys = (
        rotate(projected[1].reshape(slot_total, heads_here, HD), position)
        .astype(jnp.bfloat16)
        .reshape(slot_total, inner_width)
    )
    latent_values = projected[2].astype(jnp.bfloat16)
    latent_pos = jnp.where(in_use, position, far_position)
    largest = jnp.full((heads_here, slot_total), -1e30, jnp.float32)
    piece_keys = lax.all_gather(latent_keys, "seq", axis=0, tiled=True)
    piece_values = lax.all_gather(latent_values, "seq", axis=0, tiled=True)
    piece_pos = lax.all_gather(shortened(latent_pos), "seq", axis=0, tiled=True)
    rows_here = piece_keys.shape[0]
    piece_scores = jnp.einsum(
        "qhd,khd->hqk",
        queries,
        piece_keys.reshape(rows_here, heads_here, HD),
        preferred_element_type=jnp.float32,
    ) * (1.0 / math.sqrt(HD))
    permitted = (piece_pos[None, :] <= position[:, None])[None]
    piece_scores = jnp.where(permitted, piece_scores, -1e30)
    renewed = jnp.maximum(largest, jnp.max(piece_scores, axis=-1))
    raised = jnp.where(permitted, jnp.exp(piece_scores - renewed[..., None]), 0.0)
    weight_sum = jnp.sum(raised, axis=-1)
    weighted = jnp.einsum(
        "hqk,khd->hqd",
        raised.astype(jnp.bfloat16),
        piece_values.reshape(rows_here, heads_here, HD),
        preferred_element_type=jnp.float32,
    )
    largest, weight_sum, weighted = (renewed, weight_sum, weighted)
    latent_heads = (
        (weighted / weight_sum[..., None])
        .transpose(1, 0, 2)
        .reshape(slot_total, inner_width)
        .astype(jnp.bfloat16)
    )
    partials = jnp.dot(
        latent_heads,
        lax.all_gather(lat_proj_out, "seq", axis=1, tiled=True),
        preferred_element_type=jnp.float32,
    )
    reduced = lax.psum_scatter(partials, "tp", scatter_dimension=1, tiled=True)
    latent = jnp.where(in_use[:, None], patches.astype(jnp.float32) + reduced, 0.0).astype(
        jnp.bfloat16
    )
    return (encoded, latent)


MESH = pl.DeviceIdType.MESH
EDGE = 16


def seq_peer(index):
    return {"seq": index}


def tp_peer(index):
    return {"tp": index}


def like(shape, dtype=jnp.bfloat16):
    return jax.ShapeDtypeStruct(shape, dtype)


def iota(shape, axis):
    return lax.broadcasted_iota(jnp.int32, shape, axis)


def across_lanes(left, right):
    return lax.dot_general(
        left, right, (((1,), (1,)), ((), ())), preferred_element_type=jnp.float32
    )


def product(left, right):
    return jnp.dot(left, right, preferred_element_type=jnp.float32)


def remote(source, target, send_sem, recv_sem, device):
    return pltpu.make_async_remote_copy(
        src_ref=source,
        dst_ref=target,
        send_sem=send_sem,
        recv_sem=recv_sem,
        device_id=device,
        device_id_type=MESH,
    )


def turn_table(rows):
    frequency = rope_base ** (-2.0 * np.arange(HD // 2, dtype=np.float64) / HD)
    frequency = frequency.astype(np.float32)
    angles = np.arange(rows, dtype=np.float32)[:, None] * frequency[None, :]
    angles = angles.astype(np.float64)
    return np.concatenate([np.cos(angles), np.sin(angles)], axis=1).astype(np.float32)


def whole_layer(
    states, gain, enc_qkv, proj, starts, counts, lift, cross_kv, latent_gain, lat_qkv, lat_proj,
    table, call_id,
):
    count, size = lax.axis_size("tp"), lax.axis_size("seq")
    near = count - 1
    byte_rows, width = states.shape
    total_rows = byte_rows + EDGE
    enc_cols = enc_qkv.shape[2]
    enc_heads = enc_cols // EH
    slots = starts.shape[1]
    columns = lift.shape[1]
    group = 2 * HD
    panel_count = columns // group
    row_total = count * slots
    half = lat_qkv.shape[1]
    full_width = columns * count
    rows_half = byte_rows // 2
    spans = ((0, rows_half), (rows_half, total_rows - rows_half))
    share = enc_cols // 2
    piece = share // count

    def kernel(
        states_hbm, gain_ref, qkv_hbm, proj_hbm, starts_ref, counts_ref, lift_hbm, cross_hbm,
        lgain_ref, w_own_hbm, o_own_hbm, table_ref,
        enc_ref, out_ref,
        states_ref, qkv_ref, query_ref, kv_ref, infos, proj_ref, att_ref,
        lift_ref, cross_ref, pooled_ref, full_ref, panels, z_land, rows_ref, patch_ref,
        w_own, w_other, o_own, o_other, geared, qkv_send, qkv_land, sq_send, sq_land,
        kv_own, kv_other, att_all, parts, land, final,
        load_sems, info_s, info_r, halo_s, halo_r, edge_s, edge_r, pz_s, pz_r, pp_s, pp_r, pc_s, pc_r,
        w_sems, up_send, down_send, ag_recv,
        z_send, z_recv, plane_send, plane_recv, stay_sems,
        qkv_s, qkv_r, sq_s, sq_r, kv_sems, att_s, att_r, a_s, a_r, b_s, b_r,
    ):
        s, t = lax.axis_index("seq"), lax.axis_index("tp")
        p, c = s // 2, lax.rem(s, 2)
        partner = seq_peer(s + 1 - 2 * c)

        def plane(index):
            return {"seq": 2 * index + c}

        def ring(k):
            return lax.rem(s + k + size, size)

        def tower(k):
            return lax.rem(t + k + count, count)

        barrier = pltpu.get_barrier_semaphore()
        for k in range(1, size):
            pl.semaphore_signal(barrier, inc=1, device_id=seq_peer(ring(k)), device_id_type=MESH)
        for k in range(1, count):
            pl.semaphore_signal(barrier, inc=1, device_id=tp_peer(tower(k)), device_id_type=MESH)
        load_plan = (
            (states_hbm, states_ref.at[pl.ds(0, byte_rows)]),
            (qkv_hbm, qkv_ref),
            (proj_hbm.at[pl.ds(0, share)], proj_ref.at[0, 0]),
            (proj_hbm.at[pl.ds(share, share)], proj_ref.at[0, 1]),
            (lift_hbm, lift_ref),
            (cross_hbm, cross_ref),
            (w_own_hbm, w_own),
            (o_own_hbm, o_own),
        )
        loads = [
            pltpu.make_async_copy(source, target, load_sems.at[i])
            for i, (source, target) in enumerate(load_plan)
        ]
        for load in loads:
            load.start()
        sent = []

        def launch(copy):
            copy.start()
            sent.append(copy)
            return copy

        info_lane = iota((8, 128), 1)
        infos[s] = jnp.where(
            info_lane == 0, counts_ref[0], jnp.where(info_lane == 1, starts_ref[0:1, 0:1], 0)
        )
        loads[0].wait()
        values = states_ref[0:byte_rows].astype(jnp.float32)
        normed = rms_scale(values, gain_ref[...].astype(jnp.float32)).astype(jnp.bfloat16)
        own = pl.ds(WIN, byte_rows)
        loads[1].wait()
        for i in range(2):
            kv_ref[i, own] = product(normed, qkv_ref[i + 1]).astype(jnp.bfloat16)
        query_ref[0:byte_rows] = (
            product(normed, qkv_ref[0]) * (1.0 / math.sqrt(EH))
        ).astype(jnp.bfloat16)
        pl.semaphore_wait(barrier, size - 1 + count - 1)

        reach = WIN // byte_rows
        halos = []
        for k in range(1, reach + 1):
            halos.append(
                launch(
                    remote(
                        kv_ref.at[:, own],
                        kv_ref.at[:, pl.ds(WIN - k * byte_rows, byte_rows)],
                        halo_s.at[k - 1],
                        halo_r.at[k - 1],
                        seq_peer(ring(k)),
                    )
                )
            )
        behind = seq_peer(ring(-1))
        edges = [
            launch(remote(source, target, edge_s.at[i], edge_r.at[i], behind))
            for i, (source, target) in enumerate(
                (
                    (kv_ref.at[:, pl.ds(WIN, EDGE)], kv_ref.at[:, pl.ds(WIN + byte_rows, EDGE)]),
                    (query_ref.at[pl.ds(0, EDGE)], query_ref.at[pl.ds(byte_rows, EDGE)]),
                    (states_ref.at[pl.ds(0, EDGE)], states_ref.at[pl.ds(byte_rows, EDGE)]),
                )
            )
        ]
        notes = [
            launch(
                remote(infos.at[s], infos.at[s], info_s.at[k - 1], info_r.at[k - 1], seq_peer(ring(k)))
            )
            for k in range(1, size)
        ]
        mine_at = pl.multiple_of(p * piece, piece)
        lifts = [
            launch(
                remote(
                    proj_hbm.at[pl.ds(pl.multiple_of(c * share + p * piece, piece), piece)],
                    proj_ref.at[k, c, pl.ds(mine_at, piece)],
                    pz_s.at[k - 1],
                    pz_r.at[k - 1],
                    tp_peer(tower(k)),
                )
            )
            for k in range(1, count)
        ]
        swaps = [
            launch(remote(w_own_hbm, w_other, w_sems.at[0], w_sems.at[1], partner)),
            launch(remote(o_own_hbm, o_other, w_sems.at[2], w_sems.at[3], partner)),
        ]
        for copy in lifts:
            copy.wait_recv()
        spread = [
            launch(
                remote(
                    proj_ref.at[pl.ds(1, near), c, pl.ds(mine_at, piece)],
                    proj_ref.at[pl.ds(1, near), c, pl.ds(mine_at, piece)],
                    pp_s.at[k - 1],
                    pp_r.at[k - 1],
                    plane(lax.rem(p + k, count)),
                )
            )
            for k in range(1, count)
        ]
        for copy in halos + edges:
            copy.wait_recv()

        def pass_on(origin, h, up):
            begin, rows = spans[h]
            step = 1 if up else -1
            return remote(
                att_ref.at[origin, pl.ds(begin, rows)],
                att_ref.at[origin, pl.ds(begin, rows)],
                (up_send if up else down_send).at[origin, h],
                ag_recv.at[origin, h],
                tp_peer(tower(step)),
            )

        def attend(begin, rows):
            reach_rows = rows + WIN
            keys = kv_ref[0, begin : begin + reach_rows]
            seen_values = kv_ref[1, begin : begin + reach_rows]
            queries = query_ref[begin : begin + rows]
            head_of = iota((rows, enc_cols), 1) // EH
            stacked = jnp.concatenate(
                [jnp.where(head_of == h, queries, jnp.zeros_like(queries)) for h in range(enc_heads)],
                axis=0,
            )
            query_at = iota((rows, reach_rows), 0) + begin
            key_at = iota((rows, reach_rows), 1) + (begin - WIN)
            near_by = (
                (key_at <= query_at) & (key_at > query_at - WIN) & (key_at >= -s * byte_rows)
            )
            bias = jnp.where(near_by, 0.0, -1e30)
            scores = across_lanes(stacked, keys)
            raised, sums = [], []
            for h in range(enc_heads):
                here = scores[h * rows : (h + 1) * rows] + bias
                here = jnp.exp(here - jnp.max(here, axis=1, keepdims=True))
                sums.append(jnp.sum(here, axis=1, keepdims=True))
                raised.append(here.astype(jnp.bfloat16))
            seen = product(jnp.concatenate(raised, axis=0), seen_values)
            attended = jnp.zeros((rows, enc_cols), jnp.float32)
            for h in range(enc_heads):
                attended = jnp.where(
                    head_of == h, seen[h * rows : (h + 1) * rows] / sums[h], attended
                )
            att_ref[t, begin : begin + rows] = attended.astype(jnp.bfloat16)

        for h in range(2):
            begin, rows = spans[h]
            attend(begin, rows_half)
            if rows > rows_half:
                attend(begin + rows_half, rows - rows_half)

            @pl.when(t < count - 1)
            def _():
                pass_on(t, h, True).start()

            @pl.when(t > 0)
            def _():
                pass_on(t, h, False).start()

        def relay(d, h):
            @pl.when(t - d >= 0)
            def _():
                pass_on(t - d, h, True).wait_recv()

                @pl.when(t < count - 1)
                def _():
                    pass_on(t - d, h, True).start()

            @pl.when(t + d < count)
            def _():
                pass_on(t + d, h, False).wait_recv()

                @pl.when(t > 0)
                def _():
                    pass_on(t + d, h, False).start()

        def finish(h):
            begin, rows = spans[h]
            total = states_ref[begin : begin + rows].astype(jnp.float32)
            for k in range(count):
                total = total + product(
                    att_ref[tower(-k), begin : begin + rows],
                    proj_ref[k].reshape(enc_cols, width),
                )
            full_ref[begin : begin + rows] = total.astype(jnp.bfloat16)

        for d in range(1, count - 1):
            for h in range(2):
                relay(d, h)
        for copy in spread:
            copy.wait_recv()
        shared = launch(
            remote(
                proj_ref.at[pl.ds(1, near), c],
                proj_ref.at[pl.ds(1, near), c],
                pc_s.at[0],
                pc_r.at[0],
                partner,
            )
        )
        loads[2].wait()
        loads[3].wait()
        relay(count - 1, 0)
        shared.wait_recv()
        finish(0)
        relay(count - 1, 1)
        finish(1)
        enc_ref[...] = full_ref[0:byte_rows]

        for copy in notes:
            copy.wait_recv()
        counted = [infos[m][0:1, 0:1] for m in range(size)]
        offsets = [jnp.zeros((1, 1), jnp.int32)]
        for m in range(size - 1):
            offsets.append(offsets[m] + counted[m])
        my_count = counts_ref[0]
        next_first = jnp.where(
            s + 1 < size, infos[jnp.minimum(s + 1, size - 1)][0:1, 1:2], size * byte_rows
        )
        square = (slots, slots)
        start_row = jnp.broadcast_to(starts_ref[...], square)
        apart = iota(square, 1) - iota(square, 0)
        first_byte = jnp.sum(jnp.where(apart == 0, start_row, 0), axis=1, keepdims=True)
        following = jnp.sum(jnp.where(apart == 1, start_row, 0), axis=1, keepdims=True)
        slot_at = iota((slots, 1), 0)
        in_use = slot_at < my_count
        patch_end = jnp.where(slot_at + 1 < my_count, following, next_first)
        anchor = s * byte_rows
        lower = jnp.where(in_use, first_byte - anchor, 0)
        upper = jnp.where(in_use, patch_end - anchor, 1)

        where_at = iota((slots, total_rows), 1)
        allowed = (where_at >= lower) & (where_at < upper)
        member = jnp.where(allowed & in_use, 1.0, 0.0)
        lengths = jnp.maximum(jnp.sum(member, axis=1, keepdims=True), 1.0)
        bias = jnp.where(allowed, 0.0, -1e30)
        totals = product(member.astype(jnp.bfloat16), full_ref[...])
        pooled_ref[...] = (totals / lengths).astype(jnp.bfloat16)
        loads[4].wait()
        loads[5].wait()

        def across(k, i):
            return remote(
                panels.at[i],
                z_land.at[k - 1, i],
                z_send.at[k - 1, i],
                z_recv.at[k - 1, i],
                tp_peer(tower(k)),
            )

        def heads(i, carry):
            cols = pl.ds(pl.multiple_of(i * group, group), group)
            rows = full_ref[...]
            lifted = product(pooled_ref[...], lift_ref[:, cols])
            keys = product(rows, cross_ref[0, :, cols]).astype(jnp.bfloat16)
            seen_values = product(rows, cross_ref[1, :, cols]).astype(jnp.bfloat16)
            queries = lifted.astype(jnp.bfloat16)
            crossed = []
            for j in range(2):
                lanes = slice(j * HD, (j + 1) * HD)
                scores = across_lanes(queries[:, lanes], keys[:, lanes])
                scores = scores * (1.0 / math.sqrt(HD)) + bias
                raised = jnp.exp(scores - jnp.max(scores, axis=1, keepdims=True))
                crossed.append(
                    product(raised.astype(jnp.bfloat16), seen_values[:, lanes])
                    / jnp.sum(raised, axis=1, keepdims=True)
                )
            patch = lifted + jnp.concatenate(crossed, axis=1)
            panel = jnp.where(in_use, patch, 0.0).astype(jnp.bfloat16)
            patch_ref[:, cols] = panel
            panels[i] = panel
            for k in range(1, count):
                across(k, i).start()
            return carry

        lax.fori_loop(0, panel_count, heads, 0)
        onward = []
        for i in range(panel_count):
            for k in range(count):
                origin = tower(-k)
                if k == 0:
                    here = panels.at[i]
                else:
                    across(k, i).wait_recv()
                    here = z_land.at[k - 1, i]
                away = remote(
                    here, rows_ref.at[p, i], plane_send.at[k, i], plane_recv.at[p, i], plane(origin)
                )
                stay = pltpu.make_async_copy(here, rows_ref.at[p, i], stay_sems.at[i])
                onward.append((origin, away, stay))

                @pl.when(origin != p)
                def _():
                    away.start()

                @pl.when(origin == p)
                def _():
                    stay.start()

        chosen = [
            (
                jnp.where(c == 0, offsets[2 * i], offsets[2 * i + 1]),
                jnp.where(c == 0, counted[2 * i], counted[2 * i + 1]),
                jnp.where(c == 0, offsets[2 * i + 1], offsets[2 * i]),
                jnp.where(c == 0, counted[2 * i + 1], counted[2 * i]),
            )
            for i in range(count)
        ]

        def laid(shape, axis, which):
            at = iota(shape, axis)
            block = at // slots
            result = jnp.broadcast_to(chosen[0][which], shape)
            for i in range(1, count):
                result = jnp.where(block == i, chosen[i][which], result)
            return at - block * slots, result

        row_slot, row_offset = laid((row_total, 1), 0, 0)
        position = row_offset + row_slot
        key_positions = []
        for which in (0, 2):
            key_slot, key_offset = laid((1, row_total), 1, which)
            _, key_count = laid((1, row_total), 1, which + 1)
            key_positions.append(
                jnp.where(key_slot < key_count, key_offset + key_slot, far_position)
            )
        table_rows = table_ref.shape[0]
        picked = jnp.where(iota((row_total, table_rows), 1) == position, 1.0, 0.0)
        turns = lax.dot_general(
            picked,
            table_ref[...],
            (((1,), (0,)), ((), ())),
            precision=lax.Precision.HIGHEST,
            preferred_element_type=jnp.float32,
        )
        swapped = pltpu.roll(turns, HD // 2, 1)
        low_lanes = iota((row_total, HD), 1) < HD // 2
        cosine = jnp.where(low_lanes, turns, swapped)
        sine = jnp.where(low_lanes, -swapped, turns)

        for q in range(count):

            @pl.when(p != q)
            def _():
                for i in range(panel_count):
                    remote(
                        panels.at[i],
                        rows_ref.at[q, i],
                        plane_send.at[q, i],
                        plane_recv.at[q, i],
                        plane(p),
                    ).wait_recv()

        for origin, away, stay in onward:

            @pl.when(origin == p)
            def _():
                stay.wait()

        values = jnp.concatenate(
            [rows_ref[:, i].reshape(row_total, group) for i in range(panel_count)], axis=1
        ).astype(jnp.float32)
        squares = jnp.sum(values * values, axis=1, keepdims=True)
        eye = iota((row_total, row_total), 0) == iota((row_total, row_total), 1)
        flat = jnp.sum(jnp.where(eye, squares, 0.0), axis=0, keepdims=True)
        sq_send[...] = jnp.broadcast_to(flat, sq_send.shape)
        chip_gain = lgain_ref[:, pl.ds(pl.multiple_of(p * columns, columns), columns)]
        geared[...] = (values * chip_gain.astype(jnp.float32)).astype(jnp.bfloat16)
        arriving = []
        for k in range(1, count):
            arriving.append(
                launch(
                    remote(
                        sq_send,
                        sq_land.at[k - 1],
                        sq_s.at[k - 1],
                        sq_r.at[k - 1],
                        plane(lax.rem(p + k, count)),
                    )
                )
            )
        loads[6].wait()
        swaps[0].wait_recv()
        mine = geared[:, pl.ds(pl.multiple_of(c * half, half), half)]
        theirs = geared[:, pl.ds(pl.multiple_of((1 - c) * half, half), half)]
        total = []
        for k in list(range(1, count)) + [0]:
            target = lax.rem(p + k, count)
            lanes = pl.ds(pl.multiple_of(target * HD, HD), HD)
            for i in range(3):
                part = product(mine, w_own[i, :, lanes]) + product(theirs, w_other[i, :, lanes])
                if k:
                    qkv_send[k - 1, i] = part.astype(jnp.bfloat16)
                else:
                    total.append(part)
            if k:
                arriving.append(
                    launch(
                        remote(
                            qkv_send.at[k - 1],
                            qkv_land.at[k - 1],
                            qkv_s.at[k - 1],
                            qkv_r.at[k - 1],
                            plane(target),
                        )
                    )
                )
        for copy in arriving:
            copy.wait_recv()
        flat = flat + jnp.sum(sq_land[:, 0:1, :], axis=0)
        square_sum = jnp.sum(jnp.where(eye, flat, 0.0), axis=1, keepdims=True)
        scale = lax.rsqrt(square_sum / full_width + epsilon)
        for i in range(3):
            for k in range(count - 1):
                total[i] = total[i] + qkv_land[k, i].astype(jnp.float32)
            total[i] = total[i] * scale

        def turned(vectors):
            return (vectors * cosine + pltpu.roll(vectors, HD // 2, 1) * sine).astype(jnp.bfloat16)

        queries = turned(total[0])
        kv_own[0] = turned(total[1])
        kv_own[1] = total[2].astype(jnp.bfloat16)
        swap = launch(remote(kv_own, kv_other, kv_sems.at[0], kv_sems.at[1], partner))

        def scored(keys, key_position):
            scores = across_lanes(queries, keys) * (1.0 / math.sqrt(HD))
            permitted = key_position <= position
            return jnp.where(permitted, scores, -1e30), permitted

        scores_a, permitted_a = scored(kv_own[0], key_positions[0])
        swap.wait_recv()
        scores_b, permitted_b = scored(kv_other[0], key_positions[1])
        largest = jnp.maximum(
            jnp.max(scores_a, axis=1, keepdims=True), jnp.max(scores_b, axis=1, keepdims=True)
        )
        raised_a = jnp.where(permitted_a, jnp.exp(scores_a - largest), 0.0)
        raised_b = jnp.where(permitted_b, jnp.exp(scores_b - largest), 0.0)
        weight_sum = jnp.sum(raised_a, axis=1, keepdims=True) + jnp.sum(
            raised_b, axis=1, keepdims=True
        )
        weighted = product(raised_a.astype(jnp.bfloat16), kv_own[1]) + product(
            raised_b.astype(jnp.bfloat16), kv_other[1]
        )
        att_all[p] = (weighted / weight_sum).astype(jnp.bfloat16)
        for k in range(1, count):
            launch(
                remote(
                    att_all.at[p],
                    att_all.at[p],
                    att_s.at[k - 1],
                    att_r.at[p],
                    plane(lax.rem(p + k, count)),
                )
            )
        for k in range(1, count):
            source = lax.rem(p + k, count)
            remote(
                att_all.at[source], att_all.at[source], att_s.at[k - 1], att_r.at[source], plane(source)
            ).wait_recv()
        loads[7].wait()
        swaps[1].wait_recv()
        hops = []
        for k in list(range(1, count)) + [0]:
            target = lax.rem(p + k, count)
            take = pl.ds(pl.multiple_of(target * slots, slots), slots)
            attended = jnp.concatenate([att_all[j, take, :] for j in range(count)], axis=1)
            for output, core in ((o_own, c), (o_other, 1 - c)):
                parts[target, :, pl.ds(pl.multiple_of(core * half, half), half)] = product(
                    attended, output[...]
                ).astype(jnp.bfloat16)
            if k:
                hops.append(
                    launch(
                        remote(
                            parts.at[target],
                            land.at[k - 1],
                            a_s.at[k - 1],
                            a_r.at[k - 1],
                            plane(target),
                        )
                    )
                )
        last = []
        for k in range(count):
            origin = lax.rem(p + count - k, count)
            if k == 0:
                here = parts.at[p]
            else:
                hops[k - 1].wait_recv()
                here = land.at[k - 1]
            away = remote(here, final.at[t], b_s.at[k], b_r.at[t], tp_peer(origin))
            last.append((origin, away))

            @pl.when(origin != t)
            def _():
                away.start()

            @pl.when(origin == t)
            def _():
                final[t] = here[...]

        summed = patch_ref[...].astype(jnp.float32)
        for q in range(count):

            @pl.when(t != q)
            def _():
                remote(land.at[0], final.at[q], b_s.at[q], b_r.at[q], tp_peer(t)).wait_recv()

            summed = summed + final[q].astype(jnp.float32)
        out_ref[...] = jnp.where(in_use, summed, 0.0).astype(jnp.bfloat16)

        for copy in sent:
            copy.wait_send()
        for h in range(2):
            for q in range(count):

                @pl.when((q <= t) & (t < count - 1))
                def _():
                    pass_on(q, h, True).wait_send()

                @pl.when((q >= t) & (t > 0))
                def _():
                    pass_on(q, h, False).wait_send()

        for i in range(panel_count):
            for k in range(1, count):
                across(k, i).wait_send()
        for origin, away, stay in onward:

            @pl.when(origin != p)
            def _():
                away.wait_send()

        for origin, away in last:

            @pl.when(origin != t)
            def _():
                away.wait_send()

    vmem = pl.BlockSpec(memory_space=pltpu.VMEM)
    hbm = pl.BlockSpec(memory_space=pl.ANY)
    smem = pl.BlockSpec(memory_space=pltpu.SMEM)
    dma = pltpu.SemaphoreType.DMA

    def buffer(*shape, dtype=jnp.bfloat16):
        return pltpu.VMEM(shape, dtype)

    return pl.pallas_call(
        kernel,
        out_shape=[like((byte_rows, width)), like((slots, columns))],
        in_specs=[hbm, vmem, hbm, hbm, vmem, smem, hbm, hbm, vmem, hbm, hbm, vmem],
        out_specs=[vmem, vmem],
        scratch_shapes=[
            buffer(total_rows, width),
            buffer(*enc_qkv.shape),
            buffer(total_rows, enc_cols),
            buffer(2, WIN + total_rows, enc_cols),
            buffer(size, 8, 128, dtype=jnp.int32),
            buffer(count, 2, share, width),
            buffer(count, total_rows, enc_cols),
            buffer(*lift.shape),
            buffer(*cross_kv.shape),
            buffer(slots, width),
            buffer(total_rows, width),
            buffer(panel_count, slots, group),
            buffer(near, panel_count, slots, group),
            buffer(count, panel_count, slots, group),
            buffer(slots, columns),
            buffer(*lat_qkv.shape),
            buffer(*lat_qkv.shape),
            buffer(*lat_proj.shape),
            buffer(*lat_proj.shape),
            buffer(row_total, columns),
            buffer(near, 3, row_total, HD),
            buffer(near, 3, row_total, HD),
            buffer(8, row_total, dtype=jnp.float32),
            buffer(near, 8, row_total, dtype=jnp.float32),
            buffer(2, row_total, HD),
            buffer(2, row_total, HD),
            buffer(count, row_total, HD),
            buffer(count, slots, columns),
            buffer(near, slots, columns),
            buffer(count, slots, columns),
            dma((8,)),
            dma((size - 1,)),
            dma((size - 1,)),
            dma((2,)),
            dma((2,)),
            dma((3,)),
            dma((3,)),
            dma((near,)),
            dma((near,)),
            dma((near,)),
            dma((near,)),
            dma((1,)),
            dma((1,)),
            dma((4,)),
            dma((count, 2)),
            dma((count, 2)),
            dma((count, 2)),
            dma((near, panel_count)),
            dma((near, panel_count)),
            dma((count, panel_count)),
            dma((count, panel_count)),
            dma((panel_count,)),
            dma((near,)),
            dma((near,)),
            dma((near,)),
            dma((near,)),
            dma((2,)),
            dma((near,)),
            dma((count,)),
            dma((near,)),
            dma((near,)),
            dma((count,)),
            dma((count,)),
        ],
        compiler_params=pltpu.CompilerParams(collective_id=call_id, has_side_effects=True),
    )(
        states, gain, enc_qkv, proj, starts, counts, lift, cross_kv, latent_gain, lat_qkv, lat_proj,
        table,
    )


def fused_shards(
    byte_states,
    enc_gain,
    enc_qkv,
    enc_proj_out,
    starts,
    counts,
    lift,
    cross_kv,
    latent_gain,
    lat_qkv,
    lat_proj_out,
):
    table = jnp.asarray(turn_table(lax.axis_size("seq") * starts.shape[1]))
    encoded, latent = whole_layer(
        byte_states,
        enc_gain[None],
        enc_qkv,
        enc_proj_out,
        starts,
        counts,
        lift,
        cross_kv,
        latent_gain[None],
        lat_qkv,
        lat_proj_out,
        table,
        1,
    )
    return (encoded, latent)


def fits_pairs(mesh, byte_states, enc_qkv, starts, lat_qkv):
    size, tp_size = mesh.shape["seq"], mesh.shape["tp"]
    byte_rows = byte_states.shape[0] // size
    return (
        size == 2 * tp_size
        and WIN % byte_rows == 0
        and WIN // byte_rows < size
        and byte_rows % (32 * tp_size) == 0
        and lat_qkv.shape[2] // tp_size == HD * tp_size
        and lat_qkv.shape[1] % (128 * size) == 0
        and starts.shape[1] * tp_size % 128 == 0
        and starts.shape[1] * tp_size <= 1024
        and starts.shape[1] % 16 == 0
        and enc_qkv.shape[2] % (128 * tp_size) == 0
    )


def solution(mesh):
    specs = dict(
        mesh=mesh,
        in_specs=(
            P("seq", None),
            P(),
            P(None, None, "tp"),
            P("tp", None),
            P("seq", None),
            P("seq"),
            P(None, "tp"),
            P(None, None, "tp"),
            P(),
            P(None, "seq", "tp"),
            P("tp", "seq"),
        ),
        out_specs=(P("seq", None), P("seq", "tp")),
        check_vma=False,
    )

    def run(*arrays):
        paired = fits_pairs(mesh, arrays[0], arrays[2], arrays[4], arrays[9])
        return jax.shard_map(fused_shards if paired else gathered_shards, **specs)(*arrays)

    return run
```

```python
import math

import jax
import numpy as np
import jax.numpy as jnp
from jax import lax
from jax.experimental import pallas as pl
from jax.experimental.pallas import tpu as pltpu
from jax.sharding import PartitionSpec as P

EH = 64
HD = 128
WIN = 512
SPILL = 8


epsilon = 1e-05
rope_base = 500000.0
far_position = 1 << 30


def from_behind(value, axis, steps):
    count = lax.axis_size(axis)
    leading, last = (max(0, -steps), min(count, count - steps))
    return lax.ppermute(value, axis, [(source, source + steps) for source in range(leading, last)])


def prefix(value, axis, join, neutral):
    count, mine = (lax.axis_size(axis), lax.axis_index(axis))
    pieces = lax.all_gather(value, axis)
    subtotal = jnp.full_like(value, 0) + jnp.asarray(neutral, value.dtype)

    def hop(position, subtotal):
        longer = join(subtotal, pieces[position])
        return jnp.where(position < mine, longer, subtotal)

    return lax.fori_loop(0, count - 1, hop, subtotal)


def shortened(value):

    def short(part):
        return part.astype(jnp.bfloat16) if part.dtype == jnp.float32 else part

    return jax.tree.map(short, value)


def rms_scale(values, gain_row):
    mean_square = jnp.mean(values * values, axis=-1, keepdims=True)
    return values * lax.rsqrt(mean_square + epsilon) * gain_row


def masked_softmax(scores, allowed):
    scores = jnp.where(allowed, scores, -1e30)
    largest = jnp.max(scores, axis=-1, keepdims=True)
    raised = jnp.where(allowed, jnp.exp(scores - largest), 0.0)
    return raised / jnp.sum(raised, axis=-1, keepdims=True)


def rotate(values, position):
    halfway = values.shape[-1] // 2
    frequency = jnp.power(
        rope_base, -2.0 * jnp.arange(halfway, dtype=jnp.float32) / values.shape[-1]
    )
    angles = position.astype(jnp.float32)[:, None] * frequency[None, :]
    cosine = jnp.cos(angles)[:, None, :]
    sine_rows = jnp.sin(angles)[:, None, :]
    lower_half = values[..., :halfway]
    upper_half = values[..., halfway:]
    return jnp.concatenate(
        [
            lower_half * cosine - upper_half * sine_rows,
            upper_half * cosine + lower_half * sine_rows,
        ],
        axis=-1,
    )


def patch_block(extended, first_byte, end_byte, in_use, anchor, lift, cross_kv):
    columns = anchor + jnp.arange(extended.shape[0], dtype=jnp.int32)
    inside = (
        (columns[None, :] >= first_byte[:, None])
        & (columns[None, :] < end_byte[:, None])
        & in_use[:, None]
    )
    member = inside.astype(jnp.bfloat16)
    totals = jnp.dot(member, extended, preferred_element_type=jnp.float32)
    lengths = jnp.maximum(jnp.sum(inside.astype(jnp.float32), axis=1), 1.0)
    pooled = (totals / lengths[:, None]).astype(jnp.bfloat16)
    lifted = jnp.dot(pooled, lift, preferred_element_type=jnp.float32)
    key_rows = jnp.dot(extended, cross_kv[0], preferred_element_type=jnp.float32).astype(
        jnp.bfloat16
    )
    value_rows = jnp.dot(extended, cross_kv[1], preferred_element_type=jnp.float32).astype(
        jnp.bfloat16
    )
    slot_total = first_byte.shape[0]
    head_count = lifted.shape[1] // HD
    queries = lifted.astype(jnp.bfloat16).reshape(slot_total, head_count, HD)
    scores = jnp.einsum(
        "phd,khd->hpk",
        queries,
        key_rows.reshape(-1, head_count, HD),
        preferred_element_type=jnp.float32,
    ) * (1.0 / math.sqrt(HD))
    allowed = inside | (~in_use)[:, None] & (columns[None, :] == anchor)
    weights = masked_softmax(scores, allowed[None]).astype(jnp.bfloat16)
    crossed = jnp.einsum(
        "hpk,khd->phd",
        weights,
        value_rows.reshape(-1, head_count, HD),
        preferred_element_type=jnp.float32,
    )
    crossed = crossed.reshape(slot_total, head_count * HD)
    return jnp.where(in_use[:, None], lifted + crossed, 0.0).astype(jnp.bfloat16)


def add_counts(earlier, later):
    return earlier + later


def gathered_shards(
    byte_states,
    enc_gain,
    enc_qkv,
    enc_proj_out,
    starts,
    counts,
    lift,
    cross_kv,
    latent_gain,
    lat_qkv,
    lat_proj_out,
):
    byte_rows = byte_states.shape[0]
    anchor = lax.axis_index("seq") * byte_rows
    states = byte_states.astype(jnp.float32)
    normed = rms_scale(states, enc_gain.astype(jnp.float32)).astype(jnp.bfloat16)
    projected = jnp.einsum(
        "bd,idc->ibc", normed, enc_qkv, preferred_element_type=jnp.float32
    ).astype(jnp.bfloat16)
    reach_blocks = max(WIN // byte_rows, 1)
    tail_rows = min(WIN, byte_rows)
    key_parts = []
    value_parts = []
    for distance in range(reach_blocks, 0, -1):
        moved_keys, moved_values = from_behind(
            (projected[1, byte_rows - tail_rows :], projected[2, byte_rows - tail_rows :]),
            "seq",
            distance,
        )
        key_parts.append(moved_keys)
        value_parts.append(moved_values)
    key_rows = jnp.concatenate(key_parts + [projected[1]], axis=0)
    value_rows = jnp.concatenate(value_parts + [projected[2]], axis=0)
    head_count = projected.shape[2] // EH
    scores = jnp.einsum(
        "qhd,khd->hqk",
        projected[0].reshape(byte_rows, head_count, EH),
        key_rows.reshape(-1, head_count, EH),
        preferred_element_type=jnp.float32,
    ) * (1.0 / math.sqrt(EH))
    query_pos = anchor + jnp.arange(byte_rows, dtype=jnp.int32)
    key_pos = anchor - WIN + jnp.arange(WIN + byte_rows, dtype=jnp.int32)
    allowed = (
        (key_pos[None, :] <= query_pos[:, None])
        & (key_pos[None, :] > query_pos[:, None] - WIN)
        & (key_pos[None, :] >= 0)
    )
    weights = masked_softmax(scores, allowed[None]).astype(jnp.bfloat16)
    attended = jnp.einsum(
        "hqk,khd->qhd",
        weights,
        value_rows.reshape(-1, head_count, EH),
        preferred_element_type=jnp.float32,
    )
    attended = attended.reshape(byte_rows, head_count * EH).astype(jnp.bfloat16)
    blended = lax.psum(jnp.dot(attended, enc_proj_out, preferred_element_type=jnp.float32), "tp")
    encoded = (states + blended).astype(jnp.bfloat16)
    patch_count = counts[0]
    local_starts = starts[0]
    first_local = (local_starts[0:1] - anchor).astype(jnp.bfloat16)
    next_rows, next_first = from_behind((encoded[:SPILL], first_local), "seq", -1)
    next_first = next_first.astype(jnp.int32)[0]
    extended = jnp.concatenate([encoded, next_rows], axis=0)
    slot_ids = jnp.arange(local_starts.shape[0], dtype=jnp.int32)
    in_use = slot_ids < patch_count
    following = jnp.concatenate([local_starts[1:], jnp.zeros((1,), jnp.int32)])
    patch_end = jnp.where(slot_ids + 1 < patch_count, following, anchor + byte_rows + next_first)
    patches = patch_block(extended, local_starts, patch_end, in_use, anchor, lift, cross_kv)
    offset = prefix(counts, "seq", add_counts, jnp.zeros((1,), jnp.int32))[0]
    position = offset + slot_ids
    slot_total = patches.shape[0]
    full_rows = lax.all_gather(patches, "tp", axis=1, tiled=True)
    normed_rows = rms_scale(full_rows.astype(jnp.float32), latent_gain.astype(jnp.float32)).astype(
        jnp.bfloat16
    )
    inner_width = lat_qkv.shape[2]
    projected = jnp.einsum(
        "pd,idc->ipc",
        normed_rows,
        lax.all_gather(lat_qkv, "seq", axis=1, tiled=True),
        preferred_element_type=jnp.float32,
    )
    heads_here = inner_width // HD
    queries = rotate(projected[0].reshape(slot_total, heads_here, HD), position).astype(
        jnp.bfloat16
    )
    latent_keys = (
        rotate(projected[1].reshape(slot_total, heads_here, HD), position)
        .astype(jnp.bfloat16)
        .reshape(slot_total, inner_width)
    )
    latent_values = projected[2].astype(jnp.bfloat16)
    latent_pos = jnp.where(in_use, position, far_position)
    largest = jnp.full((heads_here, slot_total), -1e30, jnp.float32)
    piece_keys = lax.all_gather(latent_keys, "seq", axis=0, tiled=True)
    piece_values = lax.all_gather(latent_values, "seq", axis=0, tiled=True)
    piece_pos = lax.all_gather(shortened(latent_pos), "seq", axis=0, tiled=True)
    rows_here = piece_keys.shape[0]
    piece_scores = jnp.einsum(
        "qhd,khd->hqk",
        queries,
        piece_keys.reshape(rows_here, heads_here, HD),
        preferred_element_type=jnp.float32,
    ) * (1.0 / math.sqrt(HD))
    permitted = (piece_pos[None, :] <= position[:, None])[None]
    piece_scores = jnp.where(permitted, piece_scores, -1e30)
    renewed = jnp.maximum(largest, jnp.max(piece_scores, axis=-1))
    raised = jnp.where(permitted, jnp.exp(piece_scores - renewed[..., None]), 0.0)
    weight_sum = jnp.sum(raised, axis=-1)
    weighted = jnp.einsum(
        "hqk,khd->hqd",
        raised.astype(jnp.bfloat16),
        piece_values.reshape(rows_here, heads_here, HD),
        preferred_element_type=jnp.float32,
    )
    largest, weight_sum, weighted = (renewed, weight_sum, weighted)
    latent_heads = (
        (weighted / weight_sum[..., None])
        .transpose(1, 0, 2)
        .reshape(slot_total, inner_width)
        .astype(jnp.bfloat16)
    )
    partials = jnp.dot(
        latent_heads,
        lax.all_gather(lat_proj_out, "seq", axis=1, tiled=True),
        preferred_element_type=jnp.float32,
    )
    reduced = lax.psum_scatter(partials, "tp", scatter_dimension=1, tiled=True)
    latent = jnp.where(in_use[:, None], patches.astype(jnp.float32) + reduced, 0.0).astype(
        jnp.bfloat16
    )
    return (encoded, latent)


MESH = pl.DeviceIdType.MESH
EDGE = 16


def seq_peer(index):
    return {"seq": index}


def tp_peer(index):
    return {"tp": index}


def like(shape, dtype=jnp.bfloat16):
    return jax.ShapeDtypeStruct(shape, dtype)


def iota(shape, axis):
    return lax.broadcasted_iota(jnp.int32, shape, axis)


def across_lanes(left, right):
    return lax.dot_general(
        left, right, (((1,), (1,)), ((), ())), preferred_element_type=jnp.float32
    )


def product(left, right):
    return jnp.dot(left, right, preferred_element_type=jnp.float32)


def remote(source, target, send_sem, recv_sem, device):
    return pltpu.make_async_remote_copy(
        src_ref=source,
        dst_ref=target,
        send_sem=send_sem,
        recv_sem=recv_sem,
        device_id=device,
        device_id_type=MESH,
    )


def turn_table(rows):
    frequency = rope_base ** (-2.0 * np.arange(HD // 2, dtype=np.float64) / HD)
    frequency = frequency.astype(np.float32)
    angles = np.arange(rows, dtype=np.float32)[:, None] * frequency[None, :]
    angles = angles.astype(np.float64)
    return np.concatenate([np.cos(angles), np.sin(angles)], axis=1).astype(np.float32)


def whole_layer(
    states, gain, enc_qkv, proj, starts, counts, lift, cross_kv, latent_gain, lat_qkv, lat_proj,
    table, call_id,
):
    count, size = lax.axis_size("tp"), lax.axis_size("seq")
    near = count - 1
    byte_rows, width = states.shape
    total_rows = byte_rows + EDGE
    enc_cols = enc_qkv.shape[2]
    enc_heads = enc_cols // EH
    slots = starts.shape[1]
    columns = lift.shape[1]
    group = 2 * HD
    panel_count = columns // group
    row_total = count * slots
    half = lat_qkv.shape[1]
    full_width = columns * count
    rows_half = byte_rows // 2
    spans = ((0, rows_half), (rows_half, total_rows - rows_half))
    share = enc_cols // 2
    piece = share // count

    def kernel(
        states_hbm, gain_ref, qkv_hbm, proj_hbm, starts_ref, counts_ref, lift_hbm, cross_hbm,
        lgain_ref, w_own_hbm, o_hbm, table_hbm,
        enc_hbm, out_ref,
        states_ref, qkv_ref, query_ref, kv_ref, infos, proj_ref, att_ref, table_ref, cos_ref, sin_ref,
        lift_ref, cross_ref, pooled_ref, full_ref, panels, rows_ref, patch_ref,
        w_own, w_other, geared, qkv_send, qkv_land, sq_send, sq_land,
        kv_own, kv_other, out_quarter, out_rows, tall, parts, land,
        load_sems, info_s, info_r, halo_s, halo_r, edge_s, edge_r, pz_s, pz_r, pp_s, pp_r, pc_s, pc_r,
        w_sems, up_send, down_send, ag_recv,
        zup_send, zdown_send, z_recv, plane_send, plane_recv, stay_sems,
        qkv_s, qkv_r, sq_s, sq_r, kv_sems,
        oq_s, oq_r, oz_s, oz_r, oc_sems, own_sems, tz_s, tz_r, a_s, a_r, enc_sem,
    ):
        s, t = lax.axis_index("seq"), lax.axis_index("tp")
        p, c = s // 2, lax.rem(s, 2)
        partner = seq_peer(s + 1 - 2 * c)

        def plane(index):
            return {"seq": 2 * index + c}

        def ring(k):
            return lax.rem(s + k + size, size)

        def tower(k):
            return lax.rem(t + k + count, count)

        def flip(k):
            if k == 0:
                return p
            if k == 1:
                return p + 1 - 2 * lax.rem(p, 2)
            if k == 2:
                return lax.rem(p + 2, 4)
            return 3 - p

        far_first = (3, 2, 1)

        barrier = pltpu.get_barrier_semaphore()
        for k in range(1, size):
            pl.semaphore_signal(barrier, inc=1, device_id=seq_peer(ring(k)), device_id_type=MESH)
        for k in range(1, count):
            pl.semaphore_signal(barrier, inc=1, device_id=tp_peer(tower(k)), device_id_type=MESH)
        own_rows = pl.ds(pl.multiple_of(p * HD, HD), HD)
        load_plan = (
            (states_hbm, states_ref.at[pl.ds(0, byte_rows)]),
            (qkv_hbm, qkv_ref),
            (table_hbm, table_ref),
            (proj_hbm.at[pl.ds(0, share)], proj_ref.at[0, 0]),
            (proj_hbm.at[pl.ds(share, share)], proj_ref.at[0, 1]),
            (lift_hbm, lift_ref),
            (cross_hbm, cross_ref),
            (w_own_hbm, w_own),
            (o_hbm.at[own_rows], out_quarter.at[p]),
        )
        loads = [
            pltpu.make_async_copy(source, target, load_sems.at[i])
            for i, (source, target) in enumerate(load_plan)
        ]
        for load in loads:
            load.start()
        sent = []

        def launch(copy):
            copy.start()
            sent.append(copy)
            return copy
        info_lane = iota((8, 128), 1)
        infos[s] = jnp.where(
            info_lane == 0, counts_ref[0], jnp.where(info_lane == 1, starts_ref[0:1, 0:1], 0)
        )
        pl.semaphore_wait(barrier, size - 1 + count - 1)
        mine_at = pl.multiple_of(p * piece, piece)
        lifts = [
            launch(
                remote(
                    proj_hbm.at[pl.ds(pl.multiple_of(c * share + p * piece, piece), piece)],
                    proj_ref.at[k, c, pl.ds(mine_at, piece)],
                    pz_s.at[k - 1],
                    pz_r.at[k - 1],
                    tp_peer(tower(k)),
                )
            )
            for k in range(1, count)
        ]
        notes = [
            launch(
                remote(infos.at[s], infos.at[s], info_s.at[k - 1], info_r.at[k - 1], seq_peer(ring(k)))
            )
            for k in range(1, size)
        ]
        loads[0].wait()
        values = states_ref[0:byte_rows].astype(jnp.float32)
        chip_row = gain_ref[...].astype(jnp.float32).reshape(1, width)
        normed = rms_scale(values, chip_row).astype(jnp.bfloat16)
        own = pl.ds(WIN, byte_rows)
        loads[1].wait()
        halos = []
        for i in range(2):
            kv_ref[i, own] = product(normed, qkv_ref[i + 1]).astype(jnp.bfloat16)
            halos.append(
                launch(
                    remote(
                        kv_ref.at[i, own],
                        kv_ref.at[i, pl.ds(0, byte_rows)],
                        halo_s.at[0, i],
                        halo_r.at[0, i],
                        seq_peer(ring(2)),
                    )
                )
            )
        behind = seq_peer(ring(-1))
        query_ref[0:byte_rows] = (
            product(normed, qkv_ref[0]) * (1.0 / math.sqrt(EH))
        ).astype(jnp.bfloat16)
        edges = [
            launch(remote(source, target, edge_s.at[i], edge_r.at[i], behind))
            for i, (source, target) in enumerate(
                (
                    (kv_ref.at[:, pl.ds(WIN, EDGE)], kv_ref.at[:, pl.ds(WIN + byte_rows, EDGE)]),
                    (query_ref.at[pl.ds(0, EDGE)], query_ref.at[pl.ds(byte_rows, EDGE)]),
                    (states_ref.at[pl.ds(0, EDGE)], states_ref.at[pl.ds(byte_rows, EDGE)]),
                )
            )
        ]

        def beside(i):
            first = pl.multiple_of(jnp.where(c == 0, WIN, 0), byte_rows)
            return remote(
                kv_ref.at[i, pl.ds(first, byte_rows)],
                kv_ref.at[i, pl.ds(byte_rows, byte_rows)],
                halo_s.at[1, i],
                halo_r.at[1, i],
                partner,
            )

        @pl.when(c == 0)
        def _():
            for i in range(2):
                beside(i).start()
        for copy in notes:
            copy.wait_recv()
        counted = [infos[m][0:1, 0:1] for m in range(size)]
        offsets = [jnp.zeros((1, 1), jnp.int32)]
        for m in range(size - 1):
            offsets.append(offsets[m] + counted[m])
        my_count = counts_ref[0]
        next_first = jnp.where(
            s + 1 < size, infos[jnp.minimum(s + 1, size - 1)][0:1, 1:2], size * byte_rows
        )
        square = (slots, slots)
        start_row = jnp.broadcast_to(starts_ref[...], square)
        apart = iota(square, 1) - iota(square, 0)
        first_byte = jnp.sum(jnp.where(apart == 0, start_row, 0), axis=1, keepdims=True)
        following = jnp.sum(jnp.where(apart == 1, start_row, 0), axis=1, keepdims=True)
        slot_at = iota((slots, 1), 0)
        in_use = slot_at < my_count
        patch_end = jnp.where(slot_at + 1 < my_count, following, next_first)
        anchor = s * byte_rows
        lower = jnp.where(in_use, first_byte - anchor, 0)
        upper = jnp.where(in_use, patch_end - anchor, 1)
        where_at = iota((slots, total_rows), 1)
        allowed = (where_at >= lower) & (where_at < upper)
        member = jnp.where(allowed & in_use, 1.0, 0.0)
        lengths = jnp.maximum(jnp.sum(member, axis=1, keepdims=True), 1.0)
        member = member.astype(jnp.bfloat16)
        bias = jnp.where(allowed, 0.0, -1e30)
        chosen = [
            (
                jnp.where(c == 0, offsets[2 * i], offsets[2 * i + 1]),
                jnp.where(c == 0, counted[2 * i], counted[2 * i + 1]),
                jnp.where(c == 0, offsets[2 * i + 1], offsets[2 * i]),
                jnp.where(c == 0, counted[2 * i + 1], counted[2 * i]),
            )
            for i in range(count)
        ]

        def laid(shape, axis, which):
            at = iota(shape, axis)
            block = at // slots
            result = jnp.broadcast_to(chosen[0][which], shape)
            for i in range(1, count):
                result = jnp.where(block == i, chosen[i][which], result)
            return at - block * slots, result

        row_slot, row_offset = laid((row_total, 1), 0, 0)
        position = row_offset + row_slot
        key_positions = []
        for which in (0, 2):
            key_slot, key_offset = laid((1, row_total), 1, which)
            _, key_count = laid((1, row_total), 1, which + 1)
            key_positions.append(
                jnp.where(key_slot < key_count, key_offset + key_slot, far_position)
            )
        loads[2].wait()
        table_rows = table_ref.shape[0]
        picked = jnp.where(iota((row_total, table_rows), 1) == position, 1.0, 0.0)
        turns = lax.dot_general(
            picked,
            table_ref[...],
            (((1,), (0,)), ((), ())),
            precision=lax.Precision.HIGHEST,
            preferred_element_type=jnp.float32,
        )
        swapped = pltpu.roll(turns, HD // 2, 1)
        low_lanes = iota((row_total, HD), 1) < HD // 2
        cos_ref[...] = jnp.where(low_lanes, turns, swapped)
        sin_ref[...] = jnp.where(low_lanes, -swapped, turns)
        for copy in lifts:
            copy.wait_recv()
        spread = [
            launch(
                remote(
                    proj_ref.at[pl.ds(1, near), c, pl.ds(mine_at, piece)],
                    proj_ref.at[pl.ds(1, near), c, pl.ds(mine_at, piece)],
                    pp_s.at[k - 1],
                    pp_r.at[k - 1],
                    plane(flip(k)),
                )
            )
            for k in far_first
        ]
        quarters = [
            launch(
                remote(
                    o_hbm.at[pl.ds(pl.multiple_of(flip(k) * HD, HD), HD)],
                    out_quarter.at[p],
                    oq_s.at[k - 1],
                    oq_r.at[k - 1],
                    plane(flip(k)),
                )
            )
            for k in far_first
        ]
        for i in range(2):
            halos[i].wait_recv()

            @pl.when(c == 1)
            def _():
                beside(i).start()

        for copy in edges:
            copy.wait_recv()
        for i in range(2):
            beside(i).wait_recv()
        swaps = [launch(remote(w_own_hbm, w_other, w_sems.at[0], w_sems.at[1], partner))]

        def pass_on(origin, h, up):
            begin, rows = spans[h]
            step = 1 if up else -1
            return remote(
                att_ref.at[origin, pl.ds(begin, rows)],
                att_ref.at[origin, pl.ds(begin, rows)],
                (up_send if up else down_send).at[origin, h],
                ag_recv.at[origin, h],
                tp_peer(tower(step)),
            )

        def attend(begin, rows):
            reach_rows = rows + WIN
            keys = kv_ref[0, begin : begin + reach_rows]
            seen_values = kv_ref[1, begin : begin + reach_rows]
            queries = query_ref[begin : begin + rows]
            head_of = iota((rows, enc_cols), 1) // EH
            stacked = jnp.concatenate(
                [jnp.where(head_of == h, queries, jnp.zeros_like(queries)) for h in range(enc_heads)],
                axis=0,
            )
            query_at = iota((rows, reach_rows), 0) + begin
            key_at = iota((rows, reach_rows), 1) + (begin - WIN)
            near_by = (
                (key_at <= query_at) & (key_at > query_at - WIN) & (key_at >= -s * byte_rows)
            )
            near_bias = jnp.where(near_by, 0.0, -1e30)
            scores = across_lanes(stacked, keys)
            raised, sums = [], []
            for h in range(enc_heads):
                here = scores[h * rows : (h + 1) * rows] + near_bias
                here = jnp.exp(here - jnp.max(here, axis=1, keepdims=True))
                sums.append(jnp.sum(here, axis=1, keepdims=True))
                raised.append(here.astype(jnp.bfloat16))
            seen = product(jnp.concatenate(raised, axis=0), seen_values)
            attended = jnp.zeros((rows, enc_cols), jnp.float32)
            for h in range(enc_heads):
                attended = jnp.where(
                    head_of == h, seen[h * rows : (h + 1) * rows] / sums[h], attended
                )
            att_ref[t, begin : begin + rows] = attended.astype(jnp.bfloat16)
        for h in range(2):
            begin, rows = spans[h]
            attend(begin, rows_half)
            if rows > rows_half:
                attend(begin + rows_half, rows - rows_half)

            @pl.when(t < count - 1)
            def _():
                pass_on(t, h, True).start()

            @pl.when(t > 0)
            def _():
                pass_on(t, h, False).start()

        def relay(d, h):
            @pl.when(t - d >= 0)
            def _():
                pass_on(t - d, h, True).wait_recv()

                @pl.when(t < count - 1)
                def _():
                    pass_on(t - d, h, True).start()

            @pl.when(t + d < count)
            def _():
                pass_on(t + d, h, False).wait_recv()

                @pl.when(t > 0)
                def _():
                    pass_on(t + d, h, False).start()

        def finish(h):
            begin, rows = spans[h]
            total = states_ref[begin : begin + rows].astype(jnp.float32)
            for k in range(count):
                total = total + product(
                    att_ref[tower(-k), begin : begin + rows],
                    proj_ref[k].reshape(enc_cols, width),
                )
            full_ref[begin : begin + rows] = total.astype(jnp.bfloat16)
        for copy in spread:
            copy.wait_recv()
        shared = launch(
            remote(
                proj_ref.at[pl.ds(1, near), c],
                proj_ref.at[pl.ds(1, near), c],
                pc_s.at[0],
                pc_r.at[0],
                partner,
            )
        )
        for d in range(1, count - 1):
            for h in range(2):
                relay(d, h)
        loads[3].wait()
        loads[4].wait()
        relay(count - 1, 0)
        shared.wait_recv()
        finish(0)
        relay(count - 1, 1)
        finish(1)
        enc_out = pltpu.make_async_copy(full_ref.at[pl.ds(0, byte_rows)], enc_hbm, enc_sem.at[0])
        enc_out.start()

        totals = product(member, full_ref[...])
        pooled_ref[...] = (totals / lengths).astype(jnp.bfloat16)
        loads[5].wait()
        loads[6].wait()

        def climb(origin, i, up):
            step = 1 if up else -1
            return remote(
                panels.at[origin, i],
                panels.at[origin, i],
                (zup_send if up else zdown_send).at[origin, i],
                z_recv.at[origin, i],
                tp_peer(tower(step)),
            )

        def away(origin, i):
            return remote(
                panels.at[origin, i],
                rows_ref.at[p, i],
                plane_send.at[origin, i],
                plane_recv.at[p, i],
                plane(origin),
            )

        def stay(i):
            return pltpu.make_async_copy(panels.at[p, i], rows_ref.at[p, i], stay_sems.at[i])

        def spill(origin, i):
            @pl.when(origin != p)
            def _():
                away(origin, i).start()

            @pl.when(origin == p)
            def _():
                stay(i).start()

        def heads(i, carry):
            cols = pl.ds(pl.multiple_of(i * group, group), group)
            rows = full_ref[...]
            lifted = product(pooled_ref[...], lift_ref[:, cols])
            keys = product(rows, cross_ref[0, :, cols]).astype(jnp.bfloat16)
            seen_values = product(rows, cross_ref[1, :, cols]).astype(jnp.bfloat16)
            queries = lifted.astype(jnp.bfloat16)
            crossed = []
            for j in range(2):
                lanes = slice(j * HD, (j + 1) * HD)
                scores = across_lanes(queries[:, lanes], keys[:, lanes])
                scores = scores * (1.0 / math.sqrt(HD)) + bias
                raised = jnp.exp(scores - jnp.max(scores, axis=1, keepdims=True))
                crossed.append(
                    product(raised.astype(jnp.bfloat16), seen_values[:, lanes])
                    / jnp.sum(raised, axis=1, keepdims=True)
                )
            patch = lifted + jnp.concatenate(crossed, axis=1)
            panel = jnp.where(in_use, patch, 0.0).astype(jnp.bfloat16)
            patch_ref[:, cols] = panel
            panels[t, i] = panel

            @pl.when(t < count - 1)
            def _():
                climb(t, i, True).start()

            @pl.when(t > 0)
            def _():
                climb(t, i, False).start()

            spill(t, i)
            return carry
        lax.fori_loop(0, panel_count, heads, 0)
        for d in range(1, count):
            for i in range(panel_count):

                @pl.when(t - d >= 0)
                def _():
                    climb(t - d, i, True).wait_recv()

                    @pl.when(t < count - 1)
                    def _():
                        climb(t - d, i, True).start()

                    spill(t - d, i)

                @pl.when(t + d < count)
                def _():
                    climb(t + d, i, False).wait_recv()

                    @pl.when(t > 0)
                    def _():
                        climb(t + d, i, False).start()

                    spill(t + d, i)
        for copy in quarters:
            copy.wait_recv()
        loads[8].wait()
        mine_out = pltpu.make_async_copy(out_quarter.at[t], out_rows.at[c, t], own_sems.at[0])
        mine_out.start()
        ups = [
            launch(
                remote(
                    out_quarter.at[tower(k)],
                    out_rows.at[c, t],
                    oz_s.at[k - 1],
                    oz_r.at[k - 1],
                    tp_peer(tower(k)),
                )
            )
            for k in range(1, count)
        ]
        for q in range(count):

            @pl.when(p != q)
            def _():
                for i in range(panel_count):
                    remote(
                        panels.at[0, i],
                        rows_ref.at[q, i],
                        plane_send.at[q, i],
                        plane_recv.at[q, i],
                        plane(p),
                    ).wait_recv()

        for i in range(panel_count):
            stay(i).wait()
        values = jnp.concatenate(
            [rows_ref[:, i].reshape(row_total, group) for i in range(panel_count)], axis=1
        ).astype(jnp.float32)
        squares = jnp.sum(values * values, axis=1, keepdims=True)
        eye = iota((row_total, row_total), 0) == iota((row_total, row_total), 1)
        flat = jnp.sum(jnp.where(eye, squares, 0.0), axis=0, keepdims=True)
        sq_send[...] = jnp.broadcast_to(flat, sq_send.shape)
        chip_gain = lgain_ref[pl.ds(pl.multiple_of(p * columns, columns), columns)]
        chip_gain = chip_gain.astype(jnp.float32).reshape(1, columns)
        geared[...] = (values * chip_gain).astype(jnp.bfloat16)
        arriving = []
        for k in far_first:
            arriving.append(
                launch(
                    remote(
                        sq_send,
                        sq_land.at[k - 1],
                        sq_s.at[k - 1],
                        sq_r.at[k - 1],
                        plane(flip(k)),
                    )
                )
            )
        loads[7].wait()
        swaps[0].wait_recv()
        mine = geared[:, pl.ds(pl.multiple_of(c * half, half), half)]
        theirs = geared[:, pl.ds(pl.multiple_of((1 - c) * half, half), half)]
        total = []
        for k in far_first + (0,):
            target = flip(k)
            lanes = pl.ds(pl.multiple_of(target * HD, HD), HD)
            for i in range(3):
                part = product(mine, w_own[i, :, lanes]) + product(theirs, w_other[i, :, lanes])
                if k:
                    qkv_send[k - 1, i] = part.astype(jnp.bfloat16)
                else:
                    total.append(part)
            if k:
                arriving.append(
                    launch(
                        remote(
                            qkv_send.at[k - 1],
                            qkv_land.at[k - 1],
                            qkv_s.at[k - 1],
                            qkv_r.at[k - 1],
                            plane(target),
                        )
                    )
                )
        for copy in arriving:
            copy.wait_recv()
        flat = flat + jnp.sum(sq_land[:, 0:1, :], axis=0)
        square_sum = jnp.sum(jnp.where(eye, flat, 0.0), axis=1, keepdims=True)
        scale = lax.rsqrt(square_sum / full_width + epsilon)
        for i in range(3):
            for k in range(count - 1):
                total[i] = total[i] + qkv_land[k, i].astype(jnp.float32)
            total[i] = total[i] * scale

        def turned(vectors):
            return (
                vectors * cos_ref[...] + pltpu.roll(vectors, HD // 2, 1) * sin_ref[...]
            ).astype(jnp.bfloat16)

        queries = turned(total[0])
        kv_own[0] = turned(total[1])
        kv_own[1] = total[2].astype(jnp.bfloat16)
        swap = launch(remote(kv_own, kv_other, kv_sems.at[0], kv_sems.at[1], partner))
        def scored(keys, key_position):
            scores = across_lanes(queries, keys) * (1.0 / math.sqrt(HD))
            return jnp.where(key_position <= position, scores, -1e30)

        scores_a = scored(kv_own[0], key_positions[0])
        for copy in ups:
            copy.wait_recv()
        mine_out.wait()
        halves = launch(
            remote(out_rows.at[c], out_rows.at[c], oc_sems.at[0], oc_sems.at[1], partner)
        )
        swap.wait_recv()
        scores_b = scored(kv_other[0], key_positions[1])
        largest = jnp.maximum(
            jnp.max(scores_a, axis=1, keepdims=True), jnp.max(scores_b, axis=1, keepdims=True)
        )
        raised_a = jnp.exp(scores_a - largest)
        raised_b = jnp.exp(scores_b - largest)
        weight_sum = jnp.sum(raised_a, axis=1, keepdims=True) + jnp.sum(
            raised_b, axis=1, keepdims=True
        )
        weighted = product(raised_a.astype(jnp.bfloat16), kv_own[1]) + product(
            raised_b.astype(jnp.bfloat16), kv_other[1]
        )
        tall[t] = (weighted / weight_sum).astype(jnp.bfloat16)
        risen = {}
        for k in far_first + (0,):
            take = pl.ds(pl.multiple_of(flip(k) * slots, slots), slots)
            for d in range(count - 1, 0, -1):
                risen[k, d] = launch(
                    remote(
                        tall.at[t, take],
                        tall.at[t, take],
                        tz_s.at[k, d - 1],
                        tz_r.at[k, d - 1],
                        tp_peer(tower(d)),
                    )
                )
        halves.wait_recv()
        hops, parts_own = [], []
        summed = patch_ref[...].astype(jnp.float32)
        for k in far_first + (0,):
            for d in range(1, count):
                take = pl.ds(pl.multiple_of(flip(k) * slots, slots), slots)
                remote(
                    tall.at[tower(-d), take],
                    tall.at[tower(-d), take],
                    tz_s.at[k, d - 1],
                    tz_r.at[k, d - 1],
                    tp_peer(tower(-d)),
                ).wait_recv()
            attended = jnp.concatenate(
                [tall[q, pl.ds(pl.multiple_of(flip(k) * slots, slots), slots)] for q in range(count)],
                axis=1,
            )
            for core in range(2):
                lanes = slice(core * half, (core + 1) * half)
                part = product(attended, out_rows[core].reshape(count * HD, half))
                if k:
                    parts[k - 1, :, lanes] = part.astype(jnp.bfloat16)
                else:
                    parts_own.append(part)
            if k:
                hops.append(
                    launch(
                        remote(
                            parts.at[k - 1],
                            land.at[k - 1],
                            a_s.at[k - 1],
                            a_r.at[k - 1],
                            plane(flip(k)),
                        )
                    )
                )
        summed = summed + jnp.concatenate(parts_own, axis=1)
        for copy in hops:
            copy.wait_recv()
        for k in range(count - 1):
            summed = summed + land[k].astype(jnp.float32)
        out_ref[...] = jnp.where(in_use, summed, 0.0).astype(jnp.bfloat16)
        enc_out.wait()
        for copy in sent:
            copy.wait_send()
        for i in range(2):
            beside(i).wait_send()
        for h in range(2):
            for q in range(count):

                @pl.when((q <= t) & (t < count - 1))
                def _():
                    pass_on(q, h, True).wait_send()

                @pl.when((q >= t) & (t > 0))
                def _():
                    pass_on(q, h, False).wait_send()

        for i in range(panel_count):
            for q in range(count):

                @pl.when((q <= t) & (t < count - 1))
                def _():
                    climb(q, i, True).wait_send()

                @pl.when((q >= t) & (t > 0))
                def _():
                    climb(q, i, False).wait_send()

                @pl.when(p != q)
                def _():
                    away(q, i).wait_send()
    vmem = pl.BlockSpec(memory_space=pltpu.VMEM)
    hbm = pl.BlockSpec(memory_space=pl.ANY)
    smem = pl.BlockSpec(memory_space=pltpu.SMEM)
    dma = pltpu.SemaphoreType.DMA

    def buffer(*shape, dtype=jnp.bfloat16):
        return pltpu.VMEM(shape, dtype)

    return pl.pallas_call(
        kernel,
        out_shape=[like((byte_rows, width)), like((slots, columns))],
        in_specs=[hbm, vmem, hbm, hbm, vmem, smem, hbm, hbm, vmem, hbm, hbm, hbm],
        out_specs=[hbm, vmem],
        scratch_shapes=[
            buffer(total_rows, width),
            buffer(*enc_qkv.shape),
            buffer(total_rows, enc_cols),
            buffer(2, WIN + total_rows, enc_cols),
            buffer(size, 8, 128, dtype=jnp.int32),
            buffer(count, 2, share, width),
            buffer(count, total_rows, enc_cols),
            buffer(*table.shape, dtype=jnp.float32),
            buffer(row_total, HD, dtype=jnp.float32),
            buffer(row_total, HD, dtype=jnp.float32),
            buffer(*lift.shape),
            buffer(*cross_kv.shape),
            buffer(slots, width),
            buffer(total_rows, width),
            buffer(count, panel_count, slots, group),
            buffer(count, panel_count, slots, group),
            buffer(slots, columns),
            buffer(*lat_qkv.shape),
            buffer(*lat_qkv.shape),
            buffer(row_total, columns),
            buffer(near, 3, row_total, HD),
            buffer(near, 3, row_total, HD),
            buffer(8, row_total, dtype=jnp.float32),
            buffer(near, 8, row_total, dtype=jnp.float32),
            buffer(2, row_total, HD),
            buffer(2, row_total, HD),
            buffer(count, HD, half),
            buffer(2, count, HD, half),
            buffer(count, row_total, HD),
            buffer(near, slots, columns),
            buffer(near, slots, columns),
            dma((9,)),
            dma((size - 1,)),
            dma((size - 1,)),
            dma((2, 2)),
            dma((2, 2)),
            dma((3,)),
            dma((3,)),
            dma((near,)),
            dma((near,)),
            dma((near,)),
            dma((near,)),
            dma((1,)),
            dma((1,)),
            dma((2,)),
            dma((count, 2)),
            dma((count, 2)),
            dma((count, 2)),
            dma((count, panel_count)),
            dma((count, panel_count)),
            dma((count, panel_count)),
            dma((count, panel_count)),
            dma((count, panel_count)),
            dma((panel_count,)),
            dma((near,)),
            dma((near,)),
            dma((near,)),
            dma((near,)),
            dma((2,)),
            dma((near,)),
            dma((near,)),
            dma((near,)),
            dma((near,)),
            dma((2,)),
            dma((1,)),
            dma((count, near)),
            dma((count, near)),
            dma((near,)),
            dma((near,)),
            dma((1,)),
        ],
        compiler_params=pltpu.CompilerParams(collective_id=call_id, has_side_effects=True),
    )(
        states, gain, enc_qkv, proj, starts, counts, lift, cross_kv, latent_gain, lat_qkv, lat_proj,
        table,
    )


def fused_shards(
    byte_states,
    enc_gain,
    enc_qkv,
    enc_proj_out,
    starts,
    counts,
    lift,
    cross_kv,
    latent_gain,
    lat_qkv,
    lat_proj_out,
):
    table = jnp.asarray(turn_table(lax.axis_size("seq") * starts.shape[1]))
    encoded, latent = whole_layer(
        byte_states,
        enc_gain,
        enc_qkv,
        enc_proj_out,
        starts,
        counts,
        lift,
        cross_kv,
        latent_gain,
        lat_qkv,
        lat_proj_out,
        table,
        1,
    )
    return (encoded, latent)


def fits_pairs(mesh, byte_states, enc_qkv, starts, lat_qkv):
    size, tp_size = mesh.shape["seq"], mesh.shape["tp"]
    byte_rows = byte_states.shape[0] // size
    return (
        size == 2 * tp_size
        and tp_size == 4
        and WIN % byte_rows == 0
        and WIN == 2 * byte_rows
        and byte_rows % (32 * tp_size) == 0
        and lat_qkv.shape[2] // tp_size == HD * tp_size
        and lat_qkv.shape[1] % (128 * size) == 0
        and starts.shape[1] * tp_size % 128 == 0
        and starts.shape[1] * tp_size <= 1024
        and starts.shape[1] % 16 == 0
        and enc_qkv.shape[2] % (128 * tp_size) == 0
    )


def solution(mesh):
    specs = dict(
        mesh=mesh,
        in_specs=(
            P("seq", None),
            P(),
            P(None, None, "tp"),
            P("tp", None),
            P("seq", None),
            P("seq"),
            P(None, "tp"),
            P(None, None, "tp"),
            P(),
            P(None, "seq", "tp"),
            P("tp", "seq"),
        ),
        out_specs=(P("seq", None), P("seq", "tp")),
        check_vma=False,
    )

    def run(*arrays):
        paired = fits_pairs(mesh, arrays[0], arrays[2], arrays[4], arrays[9])
        return jax.shard_map(fused_shards if paired else gathered_shards, **specs)(*arrays)

    return run
```

```python
import math

import jax
import numpy as np
import jax.numpy as jnp
from jax import lax
from jax.experimental import pallas as pl
from jax.experimental.pallas import tpu as pltpu
from jax.sharding import PartitionSpec as P

EH = 64
HD = 128
WIN = 512
SPILL = 8


epsilon = 1e-05
rope_base = 500000.0
far_position = 1 << 30


def from_behind(value, axis, steps):
    count = lax.axis_size(axis)
    leading, last = (max(0, -steps), min(count, count - steps))
    return lax.ppermute(value, axis, [(source, source + steps) for source in range(leading, last)])


def prefix(value, axis, join, neutral):
    count, mine = (lax.axis_size(axis), lax.axis_index(axis))
    pieces = lax.all_gather(value, axis)
    subtotal = jnp.full_like(value, 0) + jnp.asarray(neutral, value.dtype)

    def hop(position, subtotal):
        longer = join(subtotal, pieces[position])
        return jnp.where(position < mine, longer, subtotal)

    return lax.fori_loop(0, count - 1, hop, subtotal)


def shortened(value):

    def short(part):
        return part.astype(jnp.bfloat16) if part.dtype == jnp.float32 else part

    return jax.tree.map(short, value)


def rms_scale(values, gain_row):
    mean_square = jnp.mean(values * values, axis=-1, keepdims=True)
    return values * lax.rsqrt(mean_square + epsilon) * gain_row


def masked_softmax(scores, allowed):
    scores = jnp.where(allowed, scores, -1e30)
    largest = jnp.max(scores, axis=-1, keepdims=True)
    raised = jnp.where(allowed, jnp.exp(scores - largest), 0.0)
    return raised / jnp.sum(raised, axis=-1, keepdims=True)


def rotate(values, position):
    halfway = values.shape[-1] // 2
    frequency = jnp.power(
        rope_base, -2.0 * jnp.arange(halfway, dtype=jnp.float32) / values.shape[-1]
    )
    angles = position.astype(jnp.float32)[:, None] * frequency[None, :]
    cosine = jnp.cos(angles)[:, None, :]
    sine_rows = jnp.sin(angles)[:, None, :]
    lower_half = values[..., :halfway]
    upper_half = values[..., halfway:]
    return jnp.concatenate(
        [
            lower_half * cosine - upper_half * sine_rows,
            upper_half * cosine + lower_half * sine_rows,
        ],
        axis=-1,
    )


def patch_block(extended, first_byte, end_byte, in_use, anchor, lift, cross_kv):
    columns = anchor + jnp.arange(extended.shape[0], dtype=jnp.int32)
    inside = (
        (columns[None, :] >= first_byte[:, None])
        & (columns[None, :] < end_byte[:, None])
        & in_use[:, None]
    )
    member = inside.astype(jnp.bfloat16)
    totals = jnp.dot(member, extended, preferred_element_type=jnp.float32)
    lengths = jnp.maximum(jnp.sum(inside.astype(jnp.float32), axis=1), 1.0)
    pooled = (totals / lengths[:, None]).astype(jnp.bfloat16)
    lifted = jnp.dot(pooled, lift, preferred_element_type=jnp.float32)
    key_rows = jnp.dot(extended, cross_kv[0], preferred_element_type=jnp.float32).astype(
        jnp.bfloat16
    )
    value_rows = jnp.dot(extended, cross_kv[1], preferred_element_type=jnp.float32).astype(
        jnp.bfloat16
    )
    slot_total = first_byte.shape[0]
    head_count = lifted.shape[1] // HD
    queries = lifted.astype(jnp.bfloat16).reshape(slot_total, head_count, HD)
    scores = jnp.einsum(
        "phd,khd->hpk",
        queries,
        key_rows.reshape(-1, head_count, HD),
        preferred_element_type=jnp.float32,
    ) * (1.0 / math.sqrt(HD))
    allowed = inside | (~in_use)[:, None] & (columns[None, :] == anchor)
    weights = masked_softmax(scores, allowed[None]).astype(jnp.bfloat16)
    crossed = jnp.einsum(
        "hpk,khd->phd",
        weights,
        value_rows.reshape(-1, head_count, HD),
        preferred_element_type=jnp.float32,
    )
    crossed = crossed.reshape(slot_total, head_count * HD)
    return jnp.where(in_use[:, None], lifted + crossed, 0.0).astype(jnp.bfloat16)


def add_counts(earlier, later):
    return earlier + later


def gathered_shards(
    byte_states,
    enc_gain,
    enc_qkv,
    enc_proj_out,
    starts,
    counts,
    lift,
    cross_kv,
    latent_gain,
    lat_qkv,
    lat_proj_out,
):
    byte_rows = byte_states.shape[0]
    anchor = lax.axis_index("seq") * byte_rows
    states = byte_states.astype(jnp.float32)
    normed = rms_scale(states, enc_gain.astype(jnp.float32)).astype(jnp.bfloat16)
    projected = jnp.einsum(
        "bd,idc->ibc", normed, enc_qkv, preferred_element_type=jnp.float32
    ).astype(jnp.bfloat16)
    reach_blocks = max(WIN // byte_rows, 1)
    tail_rows = min(WIN, byte_rows)
    key_parts = []
    value_parts = []
    for distance in range(reach_blocks, 0, -1):
        moved_keys, moved_values = from_behind(
            (projected[1, byte_rows - tail_rows :], projected[2, byte_rows - tail_rows :]),
            "seq",
            distance,
        )
        key_parts.append(moved_keys)
        value_parts.append(moved_values)
    key_rows = jnp.concatenate(key_parts + [projected[1]], axis=0)
    value_rows = jnp.concatenate(value_parts + [projected[2]], axis=0)
    head_count = projected.shape[2] // EH
    scores = jnp.einsum(
        "qhd,khd->hqk",
        projected[0].reshape(byte_rows, head_count, EH),
        key_rows.reshape(-1, head_count, EH),
        preferred_element_type=jnp.float32,
    ) * (1.0 / math.sqrt(EH))
    query_pos = anchor + jnp.arange(byte_rows, dtype=jnp.int32)
    key_pos = anchor - WIN + jnp.arange(WIN + byte_rows, dtype=jnp.int32)
    allowed = (
        (key_pos[None, :] <= query_pos[:, None])
        & (key_pos[None, :] > query_pos[:, None] - WIN)
        & (key_pos[None, :] >= 0)
    )
    weights = masked_softmax(scores, allowed[None]).astype(jnp.bfloat16)
    attended = jnp.einsum(
        "hqk,khd->qhd",
        weights,
        value_rows.reshape(-1, head_count, EH),
        preferred_element_type=jnp.float32,
    )
    attended = attended.reshape(byte_rows, head_count * EH).astype(jnp.bfloat16)
    blended = lax.psum(jnp.dot(attended, enc_proj_out, preferred_element_type=jnp.float32), "tp")
    encoded = (states + blended).astype(jnp.bfloat16)
    patch_count = counts[0]
    local_starts = starts[0]
    first_local = (local_starts[0:1] - anchor).astype(jnp.bfloat16)
    next_rows, next_first = from_behind((encoded[:SPILL], first_local), "seq", -1)
    next_first = next_first.astype(jnp.int32)[0]
    extended = jnp.concatenate([encoded, next_rows], axis=0)
    slot_ids = jnp.arange(local_starts.shape[0], dtype=jnp.int32)
    in_use = slot_ids < patch_count
    following = jnp.concatenate([local_starts[1:], jnp.zeros((1,), jnp.int32)])
    patch_end = jnp.where(slot_ids + 1 < patch_count, following, anchor + byte_rows + next_first)
    patches = patch_block(extended, local_starts, patch_end, in_use, anchor, lift, cross_kv)
    offset = prefix(counts, "seq", add_counts, jnp.zeros((1,), jnp.int32))[0]
    position = offset + slot_ids
    slot_total = patches.shape[0]
    full_rows = lax.all_gather(patches, "tp", axis=1, tiled=True)
    normed_rows = rms_scale(full_rows.astype(jnp.float32), latent_gain.astype(jnp.float32)).astype(
        jnp.bfloat16
    )
    inner_width = lat_qkv.shape[2]
    projected = jnp.einsum(
        "pd,idc->ipc",
        normed_rows,
        lax.all_gather(lat_qkv, "seq", axis=1, tiled=True),
        preferred_element_type=jnp.float32,
    )
    heads_here = inner_width // HD
    queries = rotate(projected[0].reshape(slot_total, heads_here, HD), position).astype(
        jnp.bfloat16
    )
    latent_keys = (
        rotate(projected[1].reshape(slot_total, heads_here, HD), position)
        .astype(jnp.bfloat16)
        .reshape(slot_total, inner_width)
    )
    latent_values = projected[2].astype(jnp.bfloat16)
    latent_pos = jnp.where(in_use, position, far_position)
    largest = jnp.full((heads_here, slot_total), -1e30, jnp.float32)
    piece_keys = lax.all_gather(latent_keys, "seq", axis=0, tiled=True)
    piece_values = lax.all_gather(latent_values, "seq", axis=0, tiled=True)
    piece_pos = lax.all_gather(shortened(latent_pos), "seq", axis=0, tiled=True)
    rows_here = piece_keys.shape[0]
    piece_scores = jnp.einsum(
        "qhd,khd->hqk",
        queries,
        piece_keys.reshape(rows_here, heads_here, HD),
        preferred_element_type=jnp.float32,
    ) * (1.0 / math.sqrt(HD))
    permitted = (piece_pos[None, :] <= position[:, None])[None]
    piece_scores = jnp.where(permitted, piece_scores, -1e30)
    renewed = jnp.maximum(largest, jnp.max(piece_scores, axis=-1))
    raised = jnp.where(permitted, jnp.exp(piece_scores - renewed[..., None]), 0.0)
    weight_sum = jnp.sum(raised, axis=-1)
    weighted = jnp.einsum(
        "hqk,khd->hqd",
        raised.astype(jnp.bfloat16),
        piece_values.reshape(rows_here, heads_here, HD),
        preferred_element_type=jnp.float32,
    )
    largest, weight_sum, weighted = (renewed, weight_sum, weighted)
    latent_heads = (
        (weighted / weight_sum[..., None])
        .transpose(1, 0, 2)
        .reshape(slot_total, inner_width)
        .astype(jnp.bfloat16)
    )
    partials = jnp.dot(
        latent_heads,
        lax.all_gather(lat_proj_out, "seq", axis=1, tiled=True),
        preferred_element_type=jnp.float32,
    )
    reduced = lax.psum_scatter(partials, "tp", scatter_dimension=1, tiled=True)
    latent = jnp.where(in_use[:, None], patches.astype(jnp.float32) + reduced, 0.0).astype(
        jnp.bfloat16
    )
    return (encoded, latent)


MESH = pl.DeviceIdType.MESH
EDGE = 16


def seq_peer(index):
    return {"seq": index}


def tp_peer(index):
    return {"tp": index}


def like(shape, dtype=jnp.bfloat16):
    return jax.ShapeDtypeStruct(shape, dtype)


def iota(shape, axis):
    return lax.broadcasted_iota(jnp.int32, shape, axis)


def across_lanes(left, right):
    return lax.dot_general(
        left, right, (((1,), (1,)), ((), ())), preferred_element_type=jnp.float32
    )


def product(left, right):
    return jnp.dot(left, right, preferred_element_type=jnp.float32)


def remote(source, target, send_sem, recv_sem, device):
    return pltpu.make_async_remote_copy(
        src_ref=source,
        dst_ref=target,
        send_sem=send_sem,
        recv_sem=recv_sem,
        device_id=device,
        device_id_type=MESH,
    )


def turn_table(rows):
    frequency = rope_base ** (-2.0 * np.arange(HD // 2, dtype=np.float64) / HD)
    frequency = frequency.astype(np.float32)
    angles = np.arange(rows, dtype=np.float32)[:, None] * frequency[None, :]
    angles = angles.astype(np.float64)
    return np.concatenate([np.cos(angles), np.sin(angles)], axis=1).astype(np.float32)


def whole_layer(
    states, gain, enc_qkv, proj, starts, counts, lift, cross_kv, latent_gain, lat_qkv, lat_proj,
    table, call_id,
):
    count, size = lax.axis_size("tp"), lax.axis_size("seq")
    near = count - 1
    byte_rows, width = states.shape
    total_rows = byte_rows + EDGE
    enc_cols = enc_qkv.shape[2]
    enc_heads = enc_cols // EH
    slots = starts.shape[1]
    columns = lift.shape[1]
    group = 2 * HD
    panel_count = columns // group
    row_total = count * slots
    half = lat_qkv.shape[1]
    full_width = columns * count
    rows_half = byte_rows // 2
    part_rows = slots // 2
    half_total = row_total // 2
    share = enc_cols // 2
    piece = share // count

    def kernel(
        states_hbm, gain_ref, qkv_hbm, proj_hbm, starts_ref, counts_ref, lift_hbm, cross_hbm,
        lgain_ref, w_own_hbm, o_hbm, table_hbm,
        enc_hbm, out_ref,
        states_ref, qkv_ref, query_ref, kv_ref, infos, proj_ref, att_ref, blend_ref, table_ref, cos_ref, sin_ref,
        lift_ref, cross_ref, pooled_ref, full_ref, panels, rows_ref, patch_ref,
        w_own, w_other, geared, own_part, qkv_send, qkv_land, sq_send, sq_land,
        kv_own, kv_other, out_quarter, out_rows, tall, parts, land,
        load_sems, info_s, info_r, halo_s, halo_r, edge_s, edge_r, pz_s, pz_r, pp_s, pp_r, pc_s, pc_r,
        w_sems, heads_send, heads_recv,
        z_send, z_recv, plane_send, plane_recv, stay_sems,
        qkv_s, qkv_r, sq_s, sq_r, kv_sems,
        oq_s, oq_r, oz_s, oz_r, oc_sems, own_sems, tz_s, tz_r, a_s, a_r, enc_sem,
    ):
        s, t = lax.axis_index("seq"), lax.axis_index("tp")
        p, c = s // 2, lax.rem(s, 2)
        partner = seq_peer(s + 1 - 2 * c)

        def plane(index):
            return {"seq": 2 * index + c}

        def ring(k):
            return lax.rem(s + k + size, size)

        def tower(k):
            return lax.rem(t + k + count, count)

        def flip(k):
            if k == 0:
                return p
            if k == 1:
                return p + 1 - 2 * lax.rem(p, 2)
            if k == 2:
                return lax.rem(p + 2, 4)
            return 3 - p

        far_first = (3, 2, 1)
        low = t < 2
        inner = (t == 1) | (t == 2)
        first_from = jnp.where(low, t + 1, t - 1)
        second_from = jnp.where(low, t + 2, t - 2)
        third_from = jnp.where(lax.rem(t, 2) == 0, count - 1, 0)
        outer = jnp.where(low, 0, count - 1)

        def to_near(copy_to):
            copy_to(first_from, 0).start()

            @pl.when(inner)
            def _():
                copy_to(outer, 1).start()

        def sent_near(copy_to, over):
            copy_to(first_from, 0).wait_send()

            @pl.when(inner)
            def _():
                copy_to(outer, 1).wait_send()
                for i in range(3):
                    over(i).wait_send()

        barrier = pltpu.get_barrier_semaphore()
        for k in range(1, size):
            pl.semaphore_signal(barrier, inc=1, device_id=seq_peer(ring(k)), device_id_type=MESH)
        for k in range(1, count):
            pl.semaphore_signal(barrier, inc=1, device_id=tp_peer(tower(k)), device_id_type=MESH)
        own_rows = pl.ds(pl.multiple_of(p * HD, HD), HD)
        load_plan = (
            (states_hbm, states_ref.at[pl.ds(0, byte_rows)]),
            (qkv_hbm, qkv_ref),
            (table_hbm, table_ref),
            (proj_hbm.at[pl.ds(0, share)], proj_ref.at[0, 0]),
            (proj_hbm.at[pl.ds(share, share)], proj_ref.at[1, 0]),
            (lift_hbm, lift_ref),
            (cross_hbm, cross_ref),
            (w_own_hbm, w_own),
            (o_hbm.at[own_rows], out_quarter.at[p]),
        )
        loads = [
            pltpu.make_async_copy(source, target, load_sems.at[i])
            for i, (source, target) in enumerate(load_plan)
        ]
        for load in loads:
            load.start()
        sent = []

        def launch(copy):
            copy.start()
            sent.append(copy)
            return copy
        info_lane = iota((8, 128), 1)
        infos[s] = jnp.where(
            info_lane == 0, counts_ref[0], jnp.where(info_lane == 1, starts_ref[0:1, 0:1], 0)
        )
        pl.semaphore_wait(barrier, size - 1 + count - 1)
        mine_at = pl.multiple_of(p * piece, piece)
        lifts = [
            launch(
                remote(
                    proj_hbm.at[pl.ds(pl.multiple_of(c * share + p * piece, piece), piece)],
                    proj_ref.at[c, k, pl.ds(mine_at, piece)],
                    pz_s.at[k - 1],
                    pz_r.at[k - 1],
                    tp_peer(tower(k)),
                )
            )
            for k in range(1, count)
        ]
        notes = [
            launch(
                remote(infos.at[s], infos.at[s], info_s.at[k - 1], info_r.at[k - 1], seq_peer(ring(k)))
            )
            for k in range(1, size)
        ]
        loads[0].wait()
        values = states_ref[0:byte_rows].astype(jnp.float32)
        chip_row = gain_ref[...].astype(jnp.float32).reshape(1, width)
        normed = rms_scale(values, chip_row).astype(jnp.bfloat16)
        own = pl.ds(WIN, byte_rows)
        loads[1].wait()
        for i in range(2):
            fresh = product(normed, qkv_ref[i + 1]).astype(jnp.bfloat16)
            for h in range(2):
                kv_ref[h, i, own] = fresh[:, h * share : (h + 1) * share]
        halos = [
            launch(
                remote(
                    kv_ref.at[h, :, own],
                    kv_ref.at[h, :, pl.ds(0, byte_rows)],
                    halo_s.at[0, h],
                    halo_r.at[0, h],
                    seq_peer(ring(2)),
                )
            )
            for h in range(2)
        ]
        behind = seq_peer(ring(-1))
        query_ref[0:byte_rows] = (
            product(normed, qkv_ref[0]) * (1.0 / math.sqrt(EH))
        ).astype(jnp.bfloat16)
        edges = [
            launch(remote(source, target, edge_s.at[i], edge_r.at[i], behind))
            for i, (source, target) in enumerate(
                (
                    (
                        kv_ref.at[:, :, pl.ds(WIN, EDGE)],
                        kv_ref.at[:, :, pl.ds(WIN + byte_rows, EDGE)],
                    ),
                    (query_ref.at[pl.ds(0, EDGE)], query_ref.at[pl.ds(byte_rows, EDGE)]),
                    (states_ref.at[pl.ds(0, EDGE)], states_ref.at[pl.ds(byte_rows, EDGE)]),
                )
            )
        ]

        def beside(i):
            first = pl.multiple_of(jnp.where(c == 0, WIN, 0), byte_rows)
            return remote(
                kv_ref.at[i, :, pl.ds(first, byte_rows)],
                kv_ref.at[i, :, pl.ds(byte_rows, byte_rows)],
                halo_s.at[1, i],
                halo_r.at[1, i],
                partner,
            )

        @pl.when(c == 0)
        def _():
            for i in range(2):
                beside(i).start()
        for copy in notes:
            copy.wait_recv()
        counted = [infos[m][0:1, 0:1] for m in range(size)]
        offsets = [jnp.zeros((1, 1), jnp.int32)]
        for m in range(size - 1):
            offsets.append(offsets[m] + counted[m])
        my_count = counts_ref[0]
        next_first = jnp.where(
            s + 1 < size, infos[jnp.minimum(s + 1, size - 1)][0:1, 1:2], size * byte_rows
        )
        square = (slots, slots)
        start_row = jnp.broadcast_to(starts_ref[...], square)
        apart = iota(square, 1) - iota(square, 0)
        first_byte = jnp.sum(jnp.where(apart == 0, start_row, 0), axis=1, keepdims=True)
        following = jnp.sum(jnp.where(apart == 1, start_row, 0), axis=1, keepdims=True)
        slot_at = iota((slots, 1), 0)
        in_use = slot_at < my_count
        patch_end = jnp.where(slot_at + 1 < my_count, following, next_first)
        anchor = s * byte_rows
        lower = jnp.where(in_use, first_byte - anchor, 0)
        upper = jnp.where(in_use, patch_end - anchor, 1)
        where_at = iota((slots, total_rows), 1)
        allowed = (where_at >= lower) & (where_at < upper)
        member = jnp.where(allowed & in_use, 1.0, 0.0)
        lengths = jnp.maximum(jnp.sum(member, axis=1, keepdims=True), 1.0)
        member = member.astype(jnp.bfloat16)
        bias = jnp.where(allowed, 0.0, -1e30)
        chosen = [
            (
                jnp.where(c == 0, offsets[2 * i], offsets[2 * i + 1]),
                jnp.where(c == 0, counted[2 * i], counted[2 * i + 1]),
                jnp.where(c == 0, offsets[2 * i + 1], offsets[2 * i]),
                jnp.where(c == 0, counted[2 * i + 1], counted[2 * i]),
            )
            for i in range(count)
        ]

        def laid(shape, axis, which):
            at = iota(shape, axis)
            band = at // half_total
            within = at - band * half_total
            block = within // part_rows
            result = jnp.broadcast_to(chosen[0][which], shape)
            for i in range(1, count):
                result = jnp.where(block == i, chosen[i][which], result)
            return band * part_rows + within - block * part_rows, result

        row_slot, row_offset = laid((row_total, 1), 0, 0)
        position = row_offset + row_slot
        key_positions = []
        for which in (0, 2):
            key_slot, key_offset = laid((1, row_total), 1, which)
            _, key_count = laid((1, row_total), 1, which + 1)
            key_positions.append(
                jnp.where(key_slot < key_count, key_offset + key_slot, far_position)
            )
        loads[2].wait()
        table_rows = table_ref.shape[0]
        picked = jnp.where(iota((row_total, table_rows), 1) == position, 1.0, 0.0)
        turns = lax.dot_general(
            picked,
            table_ref[...],
            (((1,), (0,)), ((), ())),
            precision=lax.Precision.HIGHEST,
            preferred_element_type=jnp.float32,
        )
        swapped = pltpu.roll(turns, HD // 2, 1)
        low_lanes = iota((row_total, HD), 1) < HD // 2
        cos_ref[...] = jnp.where(low_lanes, turns, swapped)
        sin_ref[...] = jnp.where(low_lanes, -swapped, turns)
        for copy in lifts:
            copy.wait_recv()
        spread = [
            launch(
                remote(
                    proj_ref.at[c, pl.ds(1, near), pl.ds(mine_at, piece)],
                    proj_ref.at[c, pl.ds(1, near), pl.ds(mine_at, piece)],
                    pp_s.at[k - 1],
                    pp_r.at[k - 1],
                    plane(flip(k)),
                )
            )
            for k in far_first
        ]
        def halo_arrives(h):
            halos[h].wait_recv()

            @pl.when(c == 1)
            def _():
                beside(h).start()

        halo_arrives(0)
        for copy in edges:
            copy.wait_recv()

        beside(0).wait_recv()
        def share_heads(origin, h, target, sem):
            return remote(
                att_ref.at[origin, h],
                att_ref.at[origin, h],
                heads_send.at[h, sem],
                heads_recv.at[h, origin],
                tp_peer(target),
            )

        def attend(pair, begin, rows):
            reach_rows = rows + WIN
            keys = kv_ref[pair, 0, begin : begin + reach_rows]
            seen_values = kv_ref[pair, 1, begin : begin + reach_rows]
            queries = query_ref[begin : begin + rows, pair * share : (pair + 1) * share]
            head_of = iota((rows, share), 1) // EH
            stacked = jnp.concatenate(
                [jnp.where(head_of == h, queries, jnp.zeros_like(queries)) for h in range(share // EH)],
                axis=0,
            )
            query_at = iota((rows, reach_rows), 0) + begin
            key_at = iota((rows, reach_rows), 1) + (begin - WIN)
            near_by = (
                (key_at <= query_at) & (key_at > query_at - WIN) & (key_at >= -s * byte_rows)
            )
            near_bias = jnp.where(near_by, 0.0, -1e30)
            scores = across_lanes(stacked, keys)
            raised, sums = [], []
            for h in range(share // EH):
                here = scores[h * rows : (h + 1) * rows] + near_bias
                here = jnp.exp(here - jnp.max(here, axis=1, keepdims=True))
                sums.append(jnp.sum(here, axis=1, keepdims=True))
                raised.append(here.astype(jnp.bfloat16))
            seen = product(jnp.concatenate(raised, axis=0), seen_values)
            attended = jnp.zeros((rows, share), jnp.float32)
            for h in range(share // EH):
                attended = jnp.where(
                    head_of == h, seen[h * rows : (h + 1) * rows] / sums[h], attended
                )
            att_ref[t, pair, begin : begin + rows] = attended.astype(jnp.bfloat16)

        for h in range(2):
            if h:
                halo_arrives(1)
                beside(1).wait_recv()
            for begin, rows in ((0, rows_half), (rows_half, rows_half), (byte_rows, EDGE)):
                attend(h, begin, rows)
            to_near(lambda target, sem: share_heads(t, h, target, sem))

        swaps = [launch(remote(w_own_hbm, w_other, w_sems.at[0], w_sems.at[1], partner))]
        sources = (first_from, second_from, third_from)
        beyond = (outer, outer, first_from)

        def hand_over(which, h):
            return share_heads(sources[which], h, beyond[which], 2 + which)

        def gain_heads(which, h):
            hand_over(which, h).wait_recv()

            @pl.when(inner)
            def _():
                hand_over(which, h).start()

        def blended(h):
            attended = jnp.concatenate([att_ref[tower(-k), h] for k in range(count)], axis=1)
            return product(attended, proj_ref[h].reshape(count * share, width))
        gain_heads(0, 0)

        @pl.when(inner)
        def _():
            gain_heads(2, 0)

        gain_heads(0, 1)

        @pl.when(inner)
        def _():
            gain_heads(2, 1)
        for copy in spread:
            copy.wait_recv()
        shared = launch(
            remote(
                proj_ref.at[c, pl.ds(1, near)],
                proj_ref.at[c, pl.ds(1, near)],
                pc_s.at[0],
                pc_r.at[0],
                partner,
            )
        )
        quarters = [
            launch(
                remote(
                    o_hbm.at[pl.ds(pl.multiple_of(flip(k) * HD, HD), HD)],
                    out_quarter.at[p],
                    oq_s.at[k - 1],
                    oq_r.at[k - 1],
                    plane(flip(k)),
                )
            )
            for k in far_first
        ]
        loads[3].wait()
        loads[4].wait()
        gain_heads(1, 0)

        @pl.when(jnp.logical_not(inner))
        def _():
            gain_heads(2, 0)
        shared.wait_recv()
        blend_ref[...] = states_ref[...].astype(jnp.float32) + blended(0)
        gain_heads(1, 1)

        @pl.when(jnp.logical_not(inner))
        def _():
            gain_heads(2, 1)
        full_ref[...] = (blend_ref[...] + blended(1)).astype(jnp.bfloat16)
        enc_out = pltpu.make_async_copy(full_ref.at[pl.ds(0, byte_rows)], enc_hbm, enc_sem.at[0])
        enc_out.start()

        totals = product(member, full_ref[...])
        pooled_ref[...] = (totals / lengths).astype(jnp.bfloat16)
        loads[5].wait()
        loads[6].wait()

        half_lanes = columns // 2

        def window(r, i):
            if r == 0:
                return pl.ds(pl.multiple_of(i * group, group), group)
            return pl.ds(i * half_lanes, half_lanes)

        def slot_of(r, i):
            return i if r == 0 else panel_count + i

        def climb(origin, r, i, target, sem):
            return remote(
                panels.at[origin, r, :, window(r, i)],
                panels.at[origin, r, :, window(r, i)],
                z_send.at[slot_of(r, i), sem],
                z_recv.at[slot_of(r, i), origin],
                tp_peer(target),
            )

        def climb_over(which, r, i):
            return climb(sources[which], r, i, beyond[which], 2 + which)

        def away(origin, r, i):
            return remote(
                panels.at[origin, r, :, window(r, i)],
                rows_ref.at[r, p, :, window(r, i)],
                plane_send.at[origin, slot_of(r, i)],
                plane_recv.at[p, slot_of(r, i)],
                plane(origin),
            )

        def stay(r, i):
            return pltpu.make_async_copy(
                panels.at[p, r, :, window(r, i)],
                rows_ref.at[r, p, :, window(r, i)],
                stay_sems.at[slot_of(r, i)],
            )

        def spill(origin, r, i):
            @pl.when(origin != p)
            def _():
                away(origin, r, i).start()

            @pl.when(origin == p)
            def _():
                stay(r, i).start()

        widths = (panel_count, 2)

        def heads(i, carry):
            cols = pl.ds(pl.multiple_of(i * group, group), group)
            rows = full_ref[...]
            lifted = product(pooled_ref[...], lift_ref[:, cols])
            keys = product(rows, cross_ref[0, :, cols]).astype(jnp.bfloat16)
            seen_values = product(rows, cross_ref[1, :, cols]).astype(jnp.bfloat16)
            queries = lifted.astype(jnp.bfloat16)
            crossed = []
            for j in range(2):
                lanes = slice(j * HD, (j + 1) * HD)
                scores = across_lanes(queries[:, lanes], keys[:, lanes])
                scores = scores * (1.0 / math.sqrt(HD)) + bias
                raised = jnp.exp(scores - jnp.max(scores, axis=1, keepdims=True))
                crossed.append(
                    product(raised.astype(jnp.bfloat16), seen_values[:, lanes])
                    / jnp.sum(raised, axis=1, keepdims=True)
                )
            patch = lifted + jnp.concatenate(crossed, axis=1)
            panel = jnp.where(in_use, patch, 0.0).astype(jnp.bfloat16)
            patch_ref[:, cols] = panel
            for r in range(2):
                panels[t, r, :, cols] = panel[r * part_rows : (r + 1) * part_rows]
            to_near(lambda target, sem: climb(t, 0, i, target, sem))
            spill(t, 0, i)
            return carry
        lax.fori_loop(0, panel_count, heads, 0)
        for i in range(widths[1]):
            to_near(lambda target, sem: climb(t, 1, i, target, sem))
            spill(t, 1, i)

        def gain_panel(which, r, i):
            climb_over(which, r, i).wait_recv()

            @pl.when(inner)
            def _():
                climb_over(which, r, i).start()

            spill(sources[which], r, i)

        for r in range(2):
            @pl.when(inner)
            def _():
                for i in range(widths[r]):
                    gain_panel(0, r, i)
                for i in range(widths[r]):
                    gain_panel(2, r, i)
                    if i:
                        gain_panel(1, r, i - 1)
                gain_panel(1, r, widths[r] - 1)

            @pl.when(jnp.logical_not(inner))
            def _():
                for which in range(3):
                    for i in range(widths[r]):
                        gain_panel(which, r, i)

        arriving, total, flats = [], [], []
        eye = iota((half_total, half_total), 0) == iota((half_total, half_total), 1)
        chip_gain = lgain_ref[pl.ds(pl.multiple_of(p * columns, columns), columns)]
        chip_gain = chip_gain.astype(jnp.float32).reshape(1, columns)
        for r in range(2):
            for q in range(count):

                @pl.when(p != q)
                def _():
                    for i in range(widths[r]):
                        remote(
                            panels.at[0, r, :, window(r, i)],
                            rows_ref.at[r, q, :, window(r, i)],
                            plane_send.at[q, slot_of(r, i)],
                            plane_recv.at[q, slot_of(r, i)],
                            plane(p),
                        ).wait_recv()

            for i in range(widths[r]):
                stay(r, i).wait()
            if r:
                for copy in quarters:
                    copy.wait_recv()
                loads[8].wait()
                mine_out = pltpu.make_async_copy(out_quarter.at[t], out_rows.at[c, t], own_sems.at[0])
                mine_out.start()
                ups = [
                    launch(
                        remote(
                            out_quarter.at[tower(k)],
                            out_rows.at[c, t],
                            oz_s.at[k - 1],
                            oz_r.at[k - 1],
                            tp_peer(tower(k)),
                        )
                    )
                    for k in range(1, count)
                ]
            values = rows_ref[r].reshape(half_total, columns).astype(jnp.float32)
            squares = jnp.sum(values * values, axis=1, keepdims=True)
            flat = jnp.sum(jnp.where(eye, squares, 0.0), axis=0, keepdims=True)
            flats.append(flat)
            sq_send[r] = jnp.broadcast_to(flat, (8, half_total))
            geared[...] = (values * chip_gain).astype(jnp.bfloat16)
            for k in far_first:
                arriving.append(
                    launch(
                        remote(
                            sq_send.at[r],
                            sq_land.at[r, k - 1],
                            sq_s.at[r, k - 1],
                            sq_r.at[r, k - 1],
                            plane(flip(k)),
                        )
                    )
                )
            if r == 0:
                loads[7].wait()
                swaps[0].wait_recv()
            mine = geared[:, pl.ds(pl.multiple_of(c * half, half), half)]
            theirs = geared[:, pl.ds(pl.multiple_of((1 - c) * half, half), half)]
            for k in far_first + (0,):
                target = flip(k)
                lanes = pl.ds(pl.multiple_of(target * HD, HD), HD)
                for i in range(3):
                    part = product(mine, w_own[i, :, lanes]) + product(theirs, w_other[i, :, lanes])
                    if k:
                        qkv_send[r, k - 1, i] = part.astype(jnp.bfloat16)
                    else:
                        own_part[r, i] = part
                if k:
                    arriving.append(
                        launch(
                            remote(
                                qkv_send.at[r, k - 1],
                                qkv_land.at[r, k - 1],
                                qkv_s.at[r, k - 1],
                                qkv_r.at[r, k - 1],
                                plane(target),
                            )
                        )
                    )
        for copy in arriving:
            copy.wait_recv()
        scales = []
        for r in range(2):
            flat = flats[r] + jnp.sum(sq_land[r, :, 0:1, :], axis=0)
            square_sum = jnp.sum(jnp.where(eye, flat, 0.0), axis=1, keepdims=True)
            scales.append(lax.rsqrt(square_sum / full_width + epsilon))
        for i in range(3):
            bands = []
            for r in range(2):
                band = own_part[r, i]
                for k in range(count - 1):
                    band = band + qkv_land[r, k, i].astype(jnp.float32)
                bands.append(band * scales[r])
            total.append(jnp.concatenate(bands, axis=0))

        def turned(vectors):
            return (
                vectors * cos_ref[...] + pltpu.roll(vectors, HD // 2, 1) * sin_ref[...]
            ).astype(jnp.bfloat16)

        queries = turned(total[0])
        kv_own[0] = turned(total[1])
        kv_own[1] = total[2].astype(jnp.bfloat16)
        swap = launch(remote(kv_own, kv_other, kv_sems.at[0], kv_sems.at[1], partner))
        def scored(keys, key_position):
            scores = across_lanes(queries, keys) * (1.0 / math.sqrt(HD))
            return jnp.where(key_position <= position, scores, -1e30)

        scores_a = scored(kv_own[0], key_positions[0])
        for copy in ups:
            copy.wait_recv()
        mine_out.wait()
        halves = launch(
            remote(out_rows.at[c], out_rows.at[c], oc_sems.at[0], oc_sems.at[1], partner)
        )
        swap.wait_recv()
        scores_b = scored(kv_other[0], key_positions[1])
        largest = jnp.maximum(
            jnp.max(scores_a, axis=1, keepdims=True), jnp.max(scores_b, axis=1, keepdims=True)
        )
        raised_a = jnp.exp(scores_a - largest)
        raised_b = jnp.exp(scores_b - largest)
        weight_sum = jnp.sum(raised_a, axis=1, keepdims=True) + jnp.sum(
            raised_b, axis=1, keepdims=True
        )
        weighted = product(raised_a.astype(jnp.bfloat16), kv_own[1]) + product(
            raised_b.astype(jnp.bfloat16), kv_other[1]
        )
        tall[t] = (weighted / weight_sum).astype(jnp.bfloat16).reshape(2, half_total, HD)
        risen = {}
        for k in far_first + (0,):
            take = pl.ds(pl.multiple_of(flip(k) * part_rows, part_rows), part_rows)
            for d in range(count - 1, 0, -1):
                risen[k, d] = launch(
                    remote(
                        tall.at[t, :, take],
                        tall.at[t, :, take],
                        tz_s.at[k, d - 1],
                        tz_r.at[k, d - 1],
                        tp_peer(tower(d)),
                    )
                )
        halves.wait_recv()
        hops, parts_own = [], []
        summed = patch_ref[...].astype(jnp.float32)
        for k in far_first + (0,):
            for d in range(1, count):
                take = pl.ds(pl.multiple_of(flip(k) * part_rows, part_rows), part_rows)
                remote(
                    tall.at[tower(-d), :, take],
                    tall.at[tower(-d), :, take],
                    tz_s.at[k, d - 1],
                    tz_r.at[k, d - 1],
                    tp_peer(tower(-d)),
                ).wait_recv()
            take = pl.ds(pl.multiple_of(flip(k) * part_rows, part_rows), part_rows)
            attended = jnp.concatenate(
                [tall[q, :, take].reshape(slots, HD) for q in range(count)], axis=1
            )
            for core in range(2):
                lanes = slice(core * half, (core + 1) * half)
                part = product(attended, out_rows[core].reshape(count * HD, half))
                if k:
                    parts[k - 1, :, lanes] = part.astype(jnp.bfloat16)
                else:
                    parts_own.append(part)
            if k:
                hops.append(
                    launch(
                        remote(
                            parts.at[k - 1],
                            land.at[k - 1],
                            a_s.at[k - 1],
                            a_r.at[k - 1],
                            plane(flip(k)),
                        )
                    )
                )
        summed = summed + jnp.concatenate(parts_own, axis=1)
        for copy in hops:
            copy.wait_recv()
        for k in range(count - 1):
            summed = summed + land[k].astype(jnp.float32)
        out_ref[...] = jnp.where(in_use, summed, 0.0).astype(jnp.bfloat16)
        enc_out.wait()
        for copy in sent:
            copy.wait_send()
        for i in range(2):
            beside(i).wait_send()
        for h in range(2):
            sent_near(
                lambda target, sem: share_heads(t, h, target, sem), lambda which: hand_over(which, h)
            )

        for r in range(2):
            for i in range(widths[r]):
                sent_near(
                    lambda target, sem: climb(t, r, i, target, sem),
                    lambda which: climb_over(which, r, i),
                )
                for q in range(count):

                    @pl.when(p != q)
                    def _():
                        away(q, r, i).wait_send()
    vmem = pl.BlockSpec(memory_space=pltpu.VMEM)
    hbm = pl.BlockSpec(memory_space=pl.ANY)
    smem = pl.BlockSpec(memory_space=pltpu.SMEM)
    dma = pltpu.SemaphoreType.DMA

    def buffer(*shape, dtype=jnp.bfloat16):
        return pltpu.VMEM(shape, dtype)

    return pl.pallas_call(
        kernel,
        out_shape=[like((byte_rows, width)), like((slots, columns))],
        in_specs=[hbm, vmem, hbm, hbm, vmem, smem, hbm, hbm, vmem, hbm, hbm, hbm],
        out_specs=[hbm, vmem],
        scratch_shapes=[
            buffer(total_rows, width),
            buffer(*enc_qkv.shape),
            buffer(total_rows, enc_cols),
            buffer(2, 2, WIN + total_rows, share),
            buffer(size, 8, 128, dtype=jnp.int32),
            buffer(2, count, share, width),
            buffer(count, 2, total_rows, share),
            buffer(total_rows, width, dtype=jnp.float32),
            buffer(*table.shape, dtype=jnp.float32),
            buffer(row_total, HD, dtype=jnp.float32),
            buffer(row_total, HD, dtype=jnp.float32),
            buffer(*lift.shape),
            buffer(*cross_kv.shape),
            buffer(slots, width),
            buffer(total_rows, width),
            buffer(count, 2, part_rows, columns),
            buffer(2, count, part_rows, columns),
            buffer(slots, columns),
            buffer(*lat_qkv.shape),
            buffer(*lat_qkv.shape),
            buffer(half_total, columns),
            buffer(2, 3, half_total, HD, dtype=jnp.float32),
            buffer(2, near, 3, half_total, HD),
            buffer(2, near, 3, half_total, HD),
            buffer(2, 8, half_total, dtype=jnp.float32),
            buffer(2, near, 8, half_total, dtype=jnp.float32),
            buffer(2, row_total, HD),
            buffer(2, row_total, HD),
            buffer(count, HD, half),
            buffer(2, count, HD, half),
            buffer(count, 2, half_total, HD),
            buffer(near, slots, columns),
            buffer(near, slots, columns),
            dma((9,)),
            dma((size - 1,)),
            dma((size - 1,)),
            dma((2, 2)),
            dma((2, 2)),
            dma((3,)),
            dma((3,)),
            dma((near,)),
            dma((near,)),
            dma((near,)),
            dma((near,)),
            dma((1,)),
            dma((1,)),
            dma((2,)),
            dma((2, 5)),
            dma((2, count)),
            dma((panel_count + 2, 5)),
            dma((panel_count + 2, count)),
            dma((count, panel_count + 2)),
            dma((count, panel_count + 2)),
            dma((panel_count + 2,)),
            dma((2, near)),
            dma((2, near)),
            dma((2, near)),
            dma((2, near)),
            dma((2,)),
            dma((near,)),
            dma((near,)),
            dma((near,)),
            dma((near,)),
            dma((2,)),
            dma((1,)),
            dma((count, near)),
            dma((count, near)),
            dma((near,)),
            dma((near,)),
            dma((1,)),
        ],
        compiler_params=pltpu.CompilerParams(collective_id=call_id, has_side_effects=True),
    )(
        states, gain, enc_qkv, proj, starts, counts, lift, cross_kv, latent_gain, lat_qkv, lat_proj,
        table,
    )


def settle(*arrays):
    total = len(arrays)

    def kernel(*refs):
        ins, outs, holds = refs[:total], refs[total : 2 * total], refs[2 * total : 3 * total]
        in_sems, out_sems = refs[3 * total :]
        takes = [pltpu.make_async_copy(ins[i], holds[i], in_sems.at[i]) for i in range(total)]
        puts = [pltpu.make_async_copy(holds[i], outs[i], out_sems.at[i]) for i in range(total)]
        for take in takes:
            take.start()
        for take, put in zip(takes, puts):
            take.wait()
            put.start()
        for put in puts:
            put.wait()

    hbm = pl.BlockSpec(memory_space=pl.ANY)
    return pl.pallas_call(
        kernel,
        out_shape=[like(value.shape, value.dtype) for value in arrays],
        in_specs=[hbm] * total,
        out_specs=[hbm] * total,
        scratch_shapes=[pltpu.VMEM(value.shape, value.dtype) for value in arrays]
        + [pltpu.SemaphoreType.DMA((total,))] * 2,
    )(*arrays)


def fused_shards(
    byte_states,
    enc_gain,
    enc_qkv,
    enc_proj_out,
    starts,
    counts,
    lift,
    cross_kv,
    latent_gain,
    lat_qkv,
    lat_proj_out,
):
    table = jnp.asarray(turn_table(lax.axis_size("seq") * starts.shape[1]))
    encoded, latent = whole_layer(
        byte_states,
        enc_gain,
        enc_qkv,
        enc_proj_out,
        starts,
        counts,
        lift,
        cross_kv,
        latent_gain,
        lat_qkv,
        lat_proj_out,
        table,
        1,
    )
    return settle(encoded, latent)


def fits_pairs(mesh, byte_states, enc_qkv, starts, lat_qkv):
    size, tp_size = mesh.shape["seq"], mesh.shape["tp"]
    byte_rows = byte_states.shape[0] // size
    return (
        size == 2 * tp_size
        and tp_size == 4
        and WIN % byte_rows == 0
        and WIN == 2 * byte_rows
        and byte_rows % (32 * tp_size) == 0
        and lat_qkv.shape[2] // tp_size == HD * tp_size
        and lat_qkv.shape[1] % (128 * size) == 0
        and starts.shape[1] * tp_size % 128 == 0
        and starts.shape[1] * tp_size <= 1024
        and starts.shape[1] % 16 == 0
        and enc_qkv.shape[2] % (128 * tp_size) == 0
    )


def solution(mesh):
    specs = dict(
        mesh=mesh,
        in_specs=(
            P("seq", None),
            P(),
            P(None, None, "tp"),
            P("tp", None),
            P("seq", None),
            P("seq"),
            P(None, "tp"),
            P(None, None, "tp"),
            P(),
            P(None, "seq", "tp"),
            P("tp", "seq"),
        ),
        out_specs=(P("seq", None), P("seq", "tp")),
        check_vma=False,
    )

    def run(*arrays):
        paired = fits_pairs(mesh, arrays[0], arrays[2], arrays[4], arrays[9])
        return jax.shard_map(fused_shards if paired else gathered_shards, **specs)(*arrays)

    return run
```

```python
import math

import jax
import numpy as np
import jax.numpy as jnp
from jax import lax
from jax.experimental import pallas as pl
from jax.experimental.pallas import tpu as pltpu
from jax.sharding import PartitionSpec as P

EH = 64
HD = 128
WIN = 512
SPILL = 8


epsilon = 1e-05
rope_base = 500000.0
far_position = 1 << 30


def from_behind(value, axis, steps):
    count = lax.axis_size(axis)
    leading, last = (max(0, -steps), min(count, count - steps))
    return lax.ppermute(value, axis, [(source, source + steps) for source in range(leading, last)])


def prefix(value, axis, join, neutral):
    count, mine = (lax.axis_size(axis), lax.axis_index(axis))
    pieces = lax.all_gather(value, axis)
    subtotal = jnp.full_like(value, 0) + jnp.asarray(neutral, value.dtype)

    def hop(position, subtotal):
        longer = join(subtotal, pieces[position])
        return jnp.where(position < mine, longer, subtotal)

    return lax.fori_loop(0, count - 1, hop, subtotal)


def shortened(value):

    def short(part):
        return part.astype(jnp.bfloat16) if part.dtype == jnp.float32 else part

    return jax.tree.map(short, value)


def rms_scale(values, gain_row):
    mean_square = jnp.mean(values * values, axis=-1, keepdims=True)
    return values * lax.rsqrt(mean_square + epsilon) * gain_row


def masked_softmax(scores, allowed):
    scores = jnp.where(allowed, scores, -1e30)
    largest = jnp.max(scores, axis=-1, keepdims=True)
    raised = jnp.where(allowed, jnp.exp(scores - largest), 0.0)
    return raised / jnp.sum(raised, axis=-1, keepdims=True)


def rotate(values, position):
    halfway = values.shape[-1] // 2
    frequency = jnp.power(
        rope_base, -2.0 * jnp.arange(halfway, dtype=jnp.float32) / values.shape[-1]
    )
    angles = position.astype(jnp.float32)[:, None] * frequency[None, :]
    cosine = jnp.cos(angles)[:, None, :]
    sine_rows = jnp.sin(angles)[:, None, :]
    lower_half = values[..., :halfway]
    upper_half = values[..., halfway:]
    return jnp.concatenate(
        [
            lower_half * cosine - upper_half * sine_rows,
            upper_half * cosine + lower_half * sine_rows,
        ],
        axis=-1,
    )


def patch_block(extended, first_byte, end_byte, in_use, anchor, lift, cross_kv):
    columns = anchor + jnp.arange(extended.shape[0], dtype=jnp.int32)
    inside = (
        (columns[None, :] >= first_byte[:, None])
        & (columns[None, :] < end_byte[:, None])
        & in_use[:, None]
    )
    member = inside.astype(jnp.bfloat16)
    totals = jnp.dot(member, extended, preferred_element_type=jnp.float32)
    lengths = jnp.maximum(jnp.sum(inside.astype(jnp.float32), axis=1), 1.0)
    pooled = (totals / lengths[:, None]).astype(jnp.bfloat16)
    lifted = jnp.dot(pooled, lift, preferred_element_type=jnp.float32)
    key_rows = jnp.dot(extended, cross_kv[0], preferred_element_type=jnp.float32).astype(
        jnp.bfloat16
    )
    value_rows = jnp.dot(extended, cross_kv[1], preferred_element_type=jnp.float32).astype(
        jnp.bfloat16
    )
    slot_total = first_byte.shape[0]
    head_count = lifted.shape[1] // HD
    queries = lifted.astype(jnp.bfloat16).reshape(slot_total, head_count, HD)
    scores = jnp.einsum(
        "phd,khd->hpk",
        queries,
        key_rows.reshape(-1, head_count, HD),
        preferred_element_type=jnp.float32,
    ) * (1.0 / math.sqrt(HD))
    allowed = inside | (~in_use)[:, None] & (columns[None, :] == anchor)
    weights = masked_softmax(scores, allowed[None]).astype(jnp.bfloat16)
    crossed = jnp.einsum(
        "hpk,khd->phd",
        weights,
        value_rows.reshape(-1, head_count, HD),
        preferred_element_type=jnp.float32,
    )
    crossed = crossed.reshape(slot_total, head_count * HD)
    return jnp.where(in_use[:, None], lifted + crossed, 0.0).astype(jnp.bfloat16)


def add_counts(earlier, later):
    return earlier + later


def gathered_shards(
    byte_states,
    enc_gain,
    enc_qkv,
    enc_proj_out,
    starts,
    counts,
    lift,
    cross_kv,
    latent_gain,
    lat_qkv,
    lat_proj_out,
):
    byte_rows = byte_states.shape[0]
    anchor = lax.axis_index("seq") * byte_rows
    states = byte_states.astype(jnp.float32)
    normed = rms_scale(states, enc_gain.astype(jnp.float32)).astype(jnp.bfloat16)
    projected = jnp.einsum(
        "bd,idc->ibc", normed, enc_qkv, preferred_element_type=jnp.float32
    ).astype(jnp.bfloat16)
    reach_blocks = max(WIN // byte_rows, 1)
    tail_rows = min(WIN, byte_rows)
    key_parts = []
    value_parts = []
    for distance in range(reach_blocks, 0, -1):
        moved_keys, moved_values = from_behind(
            (projected[1, byte_rows - tail_rows :], projected[2, byte_rows - tail_rows :]),
            "seq",
            distance,
        )
        key_parts.append(moved_keys)
        value_parts.append(moved_values)
    key_rows = jnp.concatenate(key_parts + [projected[1]], axis=0)
    value_rows = jnp.concatenate(value_parts + [projected[2]], axis=0)
    head_count = projected.shape[2] // EH
    scores = jnp.einsum(
        "qhd,khd->hqk",
        projected[0].reshape(byte_rows, head_count, EH),
        key_rows.reshape(-1, head_count, EH),
        preferred_element_type=jnp.float32,
    ) * (1.0 / math.sqrt(EH))
    query_pos = anchor + jnp.arange(byte_rows, dtype=jnp.int32)
    key_pos = anchor - WIN + jnp.arange(WIN + byte_rows, dtype=jnp.int32)
    allowed = (
        (key_pos[None, :] <= query_pos[:, None])
        & (key_pos[None, :] > query_pos[:, None] - WIN)
        & (key_pos[None, :] >= 0)
    )
    weights = masked_softmax(scores, allowed[None]).astype(jnp.bfloat16)
    attended = jnp.einsum(
        "hqk,khd->qhd",
        weights,
        value_rows.reshape(-1, head_count, EH),
        preferred_element_type=jnp.float32,
    )
    attended = attended.reshape(byte_rows, head_count * EH).astype(jnp.bfloat16)
    blended = lax.psum(jnp.dot(attended, enc_proj_out, preferred_element_type=jnp.float32), "tp")
    encoded = (states + blended).astype(jnp.bfloat16)
    patch_count = counts[0]
    local_starts = starts[0]
    first_local = (local_starts[0:1] - anchor).astype(jnp.bfloat16)
    next_rows, next_first = from_behind((encoded[:SPILL], first_local), "seq", -1)
    next_first = next_first.astype(jnp.int32)[0]
    extended = jnp.concatenate([encoded, next_rows], axis=0)
    slot_ids = jnp.arange(local_starts.shape[0], dtype=jnp.int32)
    in_use = slot_ids < patch_count
    following = jnp.concatenate([local_starts[1:], jnp.zeros((1,), jnp.int32)])
    patch_end = jnp.where(slot_ids + 1 < patch_count, following, anchor + byte_rows + next_first)
    patches = patch_block(extended, local_starts, patch_end, in_use, anchor, lift, cross_kv)
    offset = prefix(counts, "seq", add_counts, jnp.zeros((1,), jnp.int32))[0]
    position = offset + slot_ids
    slot_total = patches.shape[0]
    full_rows = lax.all_gather(patches, "tp", axis=1, tiled=True)
    normed_rows = rms_scale(full_rows.astype(jnp.float32), latent_gain.astype(jnp.float32)).astype(
        jnp.bfloat16
    )
    inner_width = lat_qkv.shape[2]
    projected = jnp.einsum(
        "pd,idc->ipc",
        normed_rows,
        lax.all_gather(lat_qkv, "seq", axis=1, tiled=True),
        preferred_element_type=jnp.float32,
    )
    heads_here = inner_width // HD
    queries = rotate(projected[0].reshape(slot_total, heads_here, HD), position).astype(
        jnp.bfloat16
    )
    latent_keys = (
        rotate(projected[1].reshape(slot_total, heads_here, HD), position)
        .astype(jnp.bfloat16)
        .reshape(slot_total, inner_width)
    )
    latent_values = projected[2].astype(jnp.bfloat16)
    latent_pos = jnp.where(in_use, position, far_position)
    largest = jnp.full((heads_here, slot_total), -1e30, jnp.float32)
    piece_keys = lax.all_gather(latent_keys, "seq", axis=0, tiled=True)
    piece_values = lax.all_gather(latent_values, "seq", axis=0, tiled=True)
    piece_pos = lax.all_gather(shortened(latent_pos), "seq", axis=0, tiled=True)
    rows_here = piece_keys.shape[0]
    piece_scores = jnp.einsum(
        "qhd,khd->hqk",
        queries,
        piece_keys.reshape(rows_here, heads_here, HD),
        preferred_element_type=jnp.float32,
    ) * (1.0 / math.sqrt(HD))
    permitted = (piece_pos[None, :] <= position[:, None])[None]
    piece_scores = jnp.where(permitted, piece_scores, -1e30)
    renewed = jnp.maximum(largest, jnp.max(piece_scores, axis=-1))
    raised = jnp.where(permitted, jnp.exp(piece_scores - renewed[..., None]), 0.0)
    weight_sum = jnp.sum(raised, axis=-1)
    weighted = jnp.einsum(
        "hqk,khd->hqd",
        raised.astype(jnp.bfloat16),
        piece_values.reshape(rows_here, heads_here, HD),
        preferred_element_type=jnp.float32,
    )
    largest, weight_sum, weighted = (renewed, weight_sum, weighted)
    latent_heads = (
        (weighted / weight_sum[..., None])
        .transpose(1, 0, 2)
        .reshape(slot_total, inner_width)
        .astype(jnp.bfloat16)
    )
    partials = jnp.dot(
        latent_heads,
        lax.all_gather(lat_proj_out, "seq", axis=1, tiled=True),
        preferred_element_type=jnp.float32,
    )
    reduced = lax.psum_scatter(partials, "tp", scatter_dimension=1, tiled=True)
    latent = jnp.where(in_use[:, None], patches.astype(jnp.float32) + reduced, 0.0).astype(
        jnp.bfloat16
    )
    return (encoded, latent)


MESH = pl.DeviceIdType.MESH
EDGE = 16


def seq_peer(index):
    return {"seq": index}


def tp_peer(index):
    return {"tp": index}


def like(shape, dtype=jnp.bfloat16):
    return jax.ShapeDtypeStruct(shape, dtype)


def iota(shape, axis):
    return lax.broadcasted_iota(jnp.int32, shape, axis)


def across_lanes(left, right):
    return lax.dot_general(
        left, right, (((1,), (1,)), ((), ())), preferred_element_type=jnp.float32
    )


def product(left, right):
    return jnp.dot(left, right, preferred_element_type=jnp.float32)


def remote(source, target, send_sem, recv_sem, device):
    return pltpu.make_async_remote_copy(
        src_ref=source,
        dst_ref=target,
        send_sem=send_sem,
        recv_sem=recv_sem,
        device_id=device,
        device_id_type=MESH,
    )


def turn_table(rows):
    frequency = rope_base ** (-2.0 * np.arange(HD // 2, dtype=np.float64) / HD)
    frequency = frequency.astype(np.float32)
    angles = np.arange(rows, dtype=np.float32)[:, None] * frequency[None, :]
    angles = angles.astype(np.float64)
    return np.concatenate([np.cos(angles), np.sin(angles)], axis=1).astype(np.float32)


def whole_layer(
    states, gain, enc_qkv, proj, starts, counts, lift, cross_kv, latent_gain, lat_qkv, lat_proj,
    table, call_id,
):
    count, size = lax.axis_size("tp"), lax.axis_size("seq")
    near = count - 1
    byte_rows, width = states.shape
    total_rows = byte_rows + EDGE
    enc_cols = enc_qkv.shape[2]
    enc_heads = enc_cols // EH
    slots = starts.shape[1]
    columns = lift.shape[1]
    group = 2 * HD
    panel_count = columns // group
    row_total = count * slots
    half = lat_qkv.shape[1]
    full_width = columns * count
    rows_half = byte_rows // 2
    part_rows = slots // 2
    half_total = row_total // 2
    share = enc_cols // 2
    piece = share // count

    def kernel(
        states_hbm, gain_ref, qkv_hbm, proj_hbm, starts_ref, counts_ref, lift_hbm, cross_hbm,
        lgain_ref, w_own_hbm, o_hbm, table_hbm,
        enc_hbm, out_ref,
        states_ref, qkv_ref, query_ref, kv_ref, infos, proj_ref, att_ref, blend_ref, table_ref, cos_ref, sin_ref,
        lift_ref, cross_ref, pooled_ref, full_ref, panels, rows_ref, patch_ref,
        w_own, w_other, geared, own_part, qkv_send, qkv_land, sq_send, sq_land,
        kv_own, kv_other, out_quarter, out_rows, tall, parts, land,
        load_sems, info_s, info_r, halo_s, halo_r, edge_s, edge_r, pz_s, pz_r, pp_s, pp_r, pc_s, pc_r,
        w_sems, heads_send, heads_recv,
        panel_send, panel_recv, stay_sems,
        qkv_s, qkv_r, sq_s, sq_r, kv_s, kv_r,
        oq_s, oq_r, oz_s, oz_r, oc_sems, own_sems, tz_s, tz_r, a_s, a_r, enc_sem,
    ):
        s, t = lax.axis_index("seq"), lax.axis_index("tp")
        p, c = s // 2, lax.rem(s, 2)
        partner = seq_peer(s + 1 - 2 * c)

        def plane(index):
            return {"seq": 2 * index + c}

        def ring(k):
            return lax.rem(s + k + size, size)

        def tower(k):
            return lax.rem(t + k + count, count)

        def flip(k):
            if k == 0:
                return p
            if k == 1:
                return p + 1 - 2 * lax.rem(p, 2)
            if k == 2:
                return lax.rem(p + 2, 4)
            return 3 - p

        far_first = (3, 2, 1)
        low = t < 2
        inner = (t == 1) | (t == 2)
        first_from = jnp.where(low, t + 1, t - 1)
        second_from = jnp.where(low, t + 2, t - 2)
        third_from = jnp.where(lax.rem(t, 2) == 0, count - 1, 0)
        outer = jnp.where(low, 0, count - 1)

        def to_near(copy_to):
            copy_to(first_from, 0).start()

            @pl.when(inner)
            def _():
                copy_to(outer, 1).start()

        def sent_near(copy_to, over):
            copy_to(first_from, 0).wait_send()

            @pl.when(inner)
            def _():
                copy_to(outer, 1).wait_send()
                for i in range(3):
                    over(i).wait_send()

        barrier = pltpu.get_barrier_semaphore()
        for k in range(1, size):
            pl.semaphore_signal(barrier, inc=1, device_id=seq_peer(ring(k)), device_id_type=MESH)
        for k in range(1, count):
            pl.semaphore_signal(barrier, inc=1, device_id=tp_peer(tower(k)), device_id_type=MESH)

        @pl.when(p != t)
        def _():
            for k in far_first:
                away_peer = {"seq": 2 * flip(k) + c, "tp": p}
                pl.semaphore_signal(barrier, inc=1, device_id=away_peer, device_id_type=MESH)

        own_rows = pl.ds(pl.multiple_of(p * HD, HD), HD)
        load_plan = (
            (states_hbm, states_ref.at[pl.ds(0, byte_rows)]),
            (qkv_hbm, qkv_ref),
            (table_hbm, table_ref),
            (proj_hbm.at[pl.ds(0, share)], proj_ref.at[0, 0]),
            (proj_hbm.at[pl.ds(share, share)], proj_ref.at[1, 0]),
            (lift_hbm, lift_ref),
            (cross_hbm, cross_ref),
            (w_own_hbm, w_own),
            (o_hbm.at[own_rows], out_quarter.at[p]),
        )
        loads = [
            pltpu.make_async_copy(source, target, load_sems.at[i])
            for i, (source, target) in enumerate(load_plan)
        ]
        for load in loads:
            load.start()
        sent = []

        def launch(copy):
            copy.start()
            sent.append(copy)
            return copy
        info_lane = iota((8, 128), 1)
        infos[s] = jnp.where(
            info_lane == 0, counts_ref[0], jnp.where(info_lane == 1, starts_ref[0:1, 0:1], 0)
        )
        loads[0].wait()
        values = states_ref[0:byte_rows].astype(jnp.float32)
        chip_row = gain_ref[...].astype(jnp.float32).reshape(1, width)
        normed = rms_scale(values, chip_row).astype(jnp.bfloat16)
        own = pl.ds(WIN, byte_rows)
        loads[1].wait()
        for i in range(2):
            fresh = product(normed, qkv_ref[i + 1]).astype(jnp.bfloat16)
            for h in range(2):
                kv_ref[h, i, own] = fresh[:, h * share : (h + 1) * share]
        query_ref[0:byte_rows] = (
            product(normed, qkv_ref[0]) * (1.0 / math.sqrt(EH))
        ).astype(jnp.bfloat16)
        greetings = size - 1 + count - 1

        @pl.when(p == t)
        def _():
            pl.semaphore_wait(barrier, greetings)

        @pl.when(p != t)
        def _():
            pl.semaphore_wait(barrier, greetings + count - 1)

        mine_at = pl.multiple_of(p * piece, piece)
        lifts = [
            launch(
                remote(
                    proj_hbm.at[pl.ds(pl.multiple_of(c * share + p * piece, piece), piece)],
                    proj_ref.at[c, k, pl.ds(mine_at, piece)],
                    pz_s.at[k - 1],
                    pz_r.at[k - 1],
                    tp_peer(tower(k)),
                )
            )
            for k in range(1, count)
        ]
        notes = [
            launch(
                remote(infos.at[s], infos.at[s], info_s.at[k - 1], info_r.at[k - 1], seq_peer(ring(k)))
            )
            for k in range(1, size)
        ]
        behind = seq_peer(ring(-1))
        edges = [
            launch(remote(source, target, edge_s.at[i], edge_r.at[i], behind))
            for i, (source, target) in enumerate(
                (
                    (
                        kv_ref.at[:, :, pl.ds(WIN, EDGE)],
                        kv_ref.at[:, :, pl.ds(WIN + byte_rows, EDGE)],
                    ),
                    (query_ref.at[pl.ds(0, EDGE)], query_ref.at[pl.ds(byte_rows, EDGE)]),
                    (states_ref.at[pl.ds(0, EDGE)], states_ref.at[pl.ds(byte_rows, EDGE)]),
                )
            )
        ]
        halos = [
            launch(
                remote(
                    kv_ref.at[h, :, own],
                    kv_ref.at[h, :, pl.ds(0, byte_rows)],
                    halo_s.at[0, h],
                    halo_r.at[0, h],
                    seq_peer(ring(2)),
                )
            )
            for h in range(2)
        ]
        def beside(i):
            first = pl.multiple_of(jnp.where(c == 0, WIN, 0), byte_rows)
            return remote(
                kv_ref.at[i, :, pl.ds(first, byte_rows)],
                kv_ref.at[i, :, pl.ds(byte_rows, byte_rows)],
                halo_s.at[1, i],
                halo_r.at[1, i],
                partner,
            )

        @pl.when(c == 0)
        def _():
            for i in range(2):
                beside(i).start()
        for copy in notes:
            copy.wait_recv()
        counted = [infos[m][0:1, 0:1] for m in range(size)]
        offsets = [jnp.zeros((1, 1), jnp.int32)]
        for m in range(size - 1):
            offsets.append(offsets[m] + counted[m])
        my_count = counts_ref[0]
        next_first = jnp.where(
            s + 1 < size, infos[jnp.minimum(s + 1, size - 1)][0:1, 1:2], size * byte_rows
        )
        square = (slots, slots)
        start_row = jnp.broadcast_to(starts_ref[...], square)
        apart = iota(square, 1) - iota(square, 0)
        first_byte = jnp.sum(jnp.where(apart == 0, start_row, 0), axis=1, keepdims=True)
        following = jnp.sum(jnp.where(apart == 1, start_row, 0), axis=1, keepdims=True)
        slot_at = iota((slots, 1), 0)
        in_use = slot_at < my_count
        patch_end = jnp.where(slot_at + 1 < my_count, following, next_first)
        anchor = s * byte_rows
        lower = jnp.where(in_use, first_byte - anchor, 0)
        upper = jnp.where(in_use, patch_end - anchor, 1)
        where_at = iota((slots, total_rows), 1)
        allowed = (where_at >= lower) & (where_at < upper)
        member = jnp.where(allowed & in_use, 1.0, 0.0)
        lengths = jnp.maximum(jnp.sum(member, axis=1, keepdims=True), 1.0)
        member = member.astype(jnp.bfloat16)
        bias = jnp.where(allowed, 0.0, -1e30)
        chosen = [
            (
                jnp.where(c == 0, offsets[2 * i], offsets[2 * i + 1]),
                jnp.where(c == 0, counted[2 * i], counted[2 * i + 1]),
                jnp.where(c == 0, offsets[2 * i + 1], offsets[2 * i]),
                jnp.where(c == 0, counted[2 * i + 1], counted[2 * i]),
            )
            for i in range(count)
        ]

        def laid(shape, axis, which):
            at = iota(shape, axis)
            band = at // half_total
            within = at - band * half_total
            block = within // part_rows
            result = jnp.broadcast_to(chosen[0][which], shape)
            for i in range(1, count):
                result = jnp.where(block == i, chosen[i][which], result)
            return band * part_rows + within - block * part_rows, result

        row_slot, row_offset = laid((row_total, 1), 0, 0)
        position = row_offset + row_slot
        key_positions = []
        for which in (0, 2):
            key_slot, key_offset = laid((1, row_total), 1, which)
            _, key_count = laid((1, row_total), 1, which + 1)
            key_positions.append(
                jnp.where(key_slot < key_count, key_offset + key_slot, far_position)
            )
        loads[2].wait()
        table_rows = table_ref.shape[0]
        picked = jnp.where(iota((row_total, table_rows), 1) == position, 1.0, 0.0)
        turns = lax.dot_general(
            picked,
            table_ref[...],
            (((1,), (0,)), ((), ())),
            precision=lax.Precision.HIGHEST,
            preferred_element_type=jnp.float32,
        )
        swapped = pltpu.roll(turns, HD // 2, 1)
        low_lanes = iota((row_total, HD), 1) < HD // 2
        cos_ref[...] = jnp.where(low_lanes, turns, swapped)
        sin_ref[...] = jnp.where(low_lanes, -swapped, turns)
        def halo_arrives(h):
            halos[h].wait_recv()

            @pl.when(c == 1)
            def _():
                beside(h).start()

        halo_arrives(0)
        for copy in lifts:
            copy.wait_recv()
        spread = [
            launch(
                remote(
                    proj_ref.at[c, pl.ds(1, near), pl.ds(mine_at, piece)],
                    proj_ref.at[c, pl.ds(1, near), pl.ds(mine_at, piece)],
                    pp_s.at[k - 1],
                    pp_r.at[k - 1],
                    plane(flip(k)),
                )
            )
            for k in far_first
        ]
        for copy in edges:
            copy.wait_recv()

        beside(0).wait_recv()
        def share_heads(origin, h, target, sem):
            return remote(
                att_ref.at[origin, h],
                att_ref.at[origin, h],
                heads_send.at[h, sem],
                heads_recv.at[h, origin],
                tp_peer(target),
            )

        def attend(pair, begin, rows):
            reach_rows = rows + WIN
            keys = kv_ref[pair, 0, begin : begin + reach_rows]
            seen_values = kv_ref[pair, 1, begin : begin + reach_rows]
            queries = query_ref[begin : begin + rows, pair * share : (pair + 1) * share]
            head_of = iota((rows, share), 1) // EH
            stacked = jnp.concatenate(
                [jnp.where(head_of == h, queries, jnp.zeros_like(queries)) for h in range(share // EH)],
                axis=0,
            )
            query_at = iota((rows, reach_rows), 0) + begin
            key_at = iota((rows, reach_rows), 1) + (begin - WIN)
            near_by = (
                (key_at <= query_at) & (key_at > query_at - WIN) & (key_at >= -s * byte_rows)
            )
            near_bias = jnp.where(near_by, 0.0, -1e30)
            scores = across_lanes(stacked, keys)
            raised, sums = [], []
            for h in range(share // EH):
                here = scores[h * rows : (h + 1) * rows] + near_bias
                here = jnp.exp(here - jnp.max(here, axis=1, keepdims=True))
                sums.append(jnp.sum(here, axis=1, keepdims=True))
                raised.append(here.astype(jnp.bfloat16))
            seen = product(jnp.concatenate(raised, axis=0), seen_values)
            attended = jnp.zeros((rows, share), jnp.float32)
            for h in range(share // EH):
                attended = jnp.where(
                    head_of == h, seen[h * rows : (h + 1) * rows] / sums[h], attended
                )
            att_ref[t, pair, begin : begin + rows] = attended.astype(jnp.bfloat16)

        for h in range(2):
            if h:
                halo_arrives(1)
                beside(1).wait_recv()
            for begin, rows in ((0, rows_half), (rows_half, rows_half), (byte_rows, EDGE)):
                attend(h, begin, rows)
            to_near(lambda target, sem: share_heads(t, h, target, sem))

        swaps = [launch(remote(w_own_hbm, w_other, w_sems.at[0], w_sems.at[1], partner))]
        sources = (first_from, second_from, third_from)
        beyond = (outer, outer, first_from)

        def hand_over(which, h):
            return share_heads(sources[which], h, beyond[which], 2 + which)

        def gain_heads(which, h):
            hand_over(which, h).wait_recv()

            @pl.when(inner)
            def _():
                hand_over(which, h).start()

        def blended(h):
            attended = jnp.concatenate([att_ref[tower(-k), h] for k in range(count)], axis=1)
            return product(attended, proj_ref[h].reshape(count * share, width))
        gain_heads(0, 0)

        @pl.when(inner)
        def _():
            gain_heads(2, 0)

        gain_heads(0, 1)

        @pl.when(inner)
        def _():
            gain_heads(2, 1)
        gain_heads(1, 0)

        @pl.when(jnp.logical_not(inner))
        def _():
            gain_heads(2, 0)
        for copy in spread:
            copy.wait_recv()
        shared = launch(
            remote(
                proj_ref.at[c, pl.ds(1, near)],
                proj_ref.at[c, pl.ds(1, near)],
                pc_s.at[0],
                pc_r.at[0],
                partner,
            )
        )
        quarters = [
            launch(
                remote(
                    o_hbm.at[pl.ds(pl.multiple_of(flip(k) * HD, HD), HD)],
                    out_quarter.at[p],
                    oq_s.at[k - 1],
                    oq_r.at[k - 1],
                    plane(flip(k)),
                )
            )
            for k in far_first
        ]
        loads[3].wait()
        loads[4].wait()
        gain_heads(1, 1)

        @pl.when(jnp.logical_not(inner))
        def _():
            gain_heads(2, 1)
        shared.wait_recv()
        blend_ref[...] = states_ref[...].astype(jnp.float32) + blended(0)
        full_ref[...] = (blend_ref[...] + blended(1)).astype(jnp.bfloat16)
        enc_out = pltpu.make_async_copy(full_ref.at[pl.ds(0, byte_rows)], enc_hbm, enc_sem.at[0])
        enc_out.start()

        totals = product(member, full_ref[...])
        pooled_ref[...] = (totals / lengths).astype(jnp.bfloat16)
        loads[5].wait()
        loads[6].wait()

        half_lanes = columns // 2

        def window(r, i):
            if r == 0:
                return pl.ds(pl.multiple_of(i * group, group), group)
            return pl.ds(i * half_lanes, half_lanes)

        def slot_of(r, i):
            return i if r == 0 else panel_count + i

        def away(k, r, i):
            return remote(
                panels.at[r, :, window(r, i)],
                rows_ref.at[r, p, :, window(r, i)],
                panel_send.at[k, slot_of(r, i)],
                panel_recv.at[p, slot_of(r, i)],
                {"seq": 2 * t + c, "tp": tower(k)},
            )

        def stay(r, i):
            return pltpu.make_async_copy(
                panels.at[r, :, window(r, i)],
                rows_ref.at[r, p, :, window(r, i)],
                stay_sems.at[slot_of(r, i)],
            )

        def ship(r, i):
            for k in (2, 1, 3):
                away(k, r, i).start()

            @pl.when(p != t)
            def _():
                away(0, r, i).start()

            @pl.when(p == t)
            def _():
                stay(r, i).start()

        widths = (panel_count, 2)

        def heads(i, carry):
            cols = pl.ds(pl.multiple_of(i * group, group), group)
            rows = full_ref[...]
            lifted = product(pooled_ref[...], lift_ref[:, cols])
            keys = product(rows, cross_ref[0, :, cols]).astype(jnp.bfloat16)
            seen_values = product(rows, cross_ref[1, :, cols]).astype(jnp.bfloat16)
            queries = lifted.astype(jnp.bfloat16)
            crossed = []
            for j in range(2):
                lanes = slice(j * HD, (j + 1) * HD)
                scores = across_lanes(queries[:, lanes], keys[:, lanes])
                scores = scores * (1.0 / math.sqrt(HD)) + bias
                raised = jnp.exp(scores - jnp.max(scores, axis=1, keepdims=True))
                crossed.append(
                    product(raised.astype(jnp.bfloat16), seen_values[:, lanes])
                    / jnp.sum(raised, axis=1, keepdims=True)
                )
            patch = lifted + jnp.concatenate(crossed, axis=1)
            panel = jnp.where(in_use, patch, 0.0).astype(jnp.bfloat16)
            patch_ref[:, cols] = panel
            for r in range(2):
                panels[r, :, cols] = panel[r * part_rows : (r + 1) * part_rows]
            ship(0, i)
            return carry
        lax.fori_loop(0, panel_count, heads, 0)
        for i in range(widths[1]):
            ship(1, i)

        arriving, flats = ([], []), []
        eye = iota((half_total, half_total), 0) == iota((half_total, half_total), 1)
        chip_gain = lgain_ref[pl.ds(pl.multiple_of(p * columns, columns), columns)]
        chip_gain = chip_gain.astype(jnp.float32).reshape(1, columns)
        for r in range(2):
            for q in range(count):

                @pl.when((p != q) | (p != t))
                def _():
                    for i in range(widths[r]):
                        remote(
                            panels.at[r, :, window(r, i)],
                            rows_ref.at[r, q, :, window(r, i)],
                            panel_send.at[0, slot_of(r, i)],
                            panel_recv.at[q, slot_of(r, i)],
                            plane(p),
                        ).wait_recv()

            @pl.when(p == t)
            def _():
                for i in range(widths[r]):
                    stay(r, i).wait()
            values = rows_ref[r].reshape(half_total, columns).astype(jnp.float32)
            squares = jnp.sum(values * values, axis=1, keepdims=True)
            flat = jnp.sum(jnp.where(eye, squares, 0.0), axis=0, keepdims=True)
            flats.append(flat)
            sq_send[r] = jnp.broadcast_to(flat, (8, half_total))
            geared[...] = (values * chip_gain).astype(jnp.bfloat16)
            for k in far_first:
                arriving[r].append(
                    launch(
                        remote(
                            sq_send.at[r],
                            sq_land.at[r, k - 1],
                            sq_s.at[r, k - 1],
                            sq_r.at[r, k - 1],
                            plane(flip(k)),
                        )
                    )
                )
            if r == 0:
                loads[7].wait()
                swaps[0].wait_recv()
            mine = geared[:, pl.ds(pl.multiple_of(c * half, half), half)]
            theirs = geared[:, pl.ds(pl.multiple_of((1 - c) * half, half), half)]
            for k in far_first + (0,):
                target = flip(k)
                lanes = pl.ds(pl.multiple_of(target * HD, HD), HD)
                for i in range(3):
                    part = product(mine, w_own[i, :, lanes]) + product(theirs, w_other[i, :, lanes])
                    if k:
                        qkv_send[r, k - 1, i] = part.astype(jnp.bfloat16)
                    else:
                        own_part[r, i] = part
                if k:
                    arriving[r].append(
                        launch(
                            remote(
                                qkv_send.at[r, k - 1],
                                qkv_land.at[r, k - 1],
                                qkv_s.at[r, k - 1],
                                qkv_r.at[r, k - 1],
                                plane(target),
                            )
                        )
                    )
            if r == 0:
                for copy in quarters:
                    copy.wait_recv()
                loads[8].wait()
                mine_out = pltpu.make_async_copy(
                    out_quarter.at[t], out_rows.at[c, t], own_sems.at[0]
                )
                mine_out.start()
                ups = [
                    remote(
                        out_quarter.at[tower(k)],
                        out_rows.at[c, t],
                        oz_s.at[k - 1],
                        oz_r.at[k - 1],
                        tp_peer(tower(k)),
                    )
                    for k in range(1, count)
                ]

            @pl.when(inner if r == 0 else jnp.logical_not(inner))
            def _():
                for copy in ups:
                    copy.start()

        sent.extend(ups)

        def turned(vectors, rows):
            return (
                vectors * cos_ref[rows] + pltpu.roll(vectors, HD // 2, 1) * sin_ref[rows]
            ).astype(jnp.bfloat16)

        swaps_kv, queries = [], []
        for r in range(2):
            for copy in arriving[r]:
                copy.wait_recv()
            flat = flats[r] + jnp.sum(sq_land[r, :, 0:1, :], axis=0)
            square_sum = jnp.sum(jnp.where(eye, flat, 0.0), axis=1, keepdims=True)
            scale = lax.rsqrt(square_sum / full_width + epsilon)
            total = []
            for i in range(3):
                band = own_part[r, i]
                for k in range(count - 1):
                    band = band + qkv_land[r, k, i].astype(jnp.float32)
                total.append(band * scale)
            rows = slice(r * half_total, (r + 1) * half_total)
            kv_own[r, 0] = turned(total[1], rows)
            kv_own[r, 1] = total[2].astype(jnp.bfloat16)
            swaps_kv.append(
                launch(remote(kv_own.at[r], kv_other.at[r], kv_s.at[r], kv_r.at[r], partner))
            )
            queries.append(turned(total[0], rows))
        queries = jnp.concatenate(queries, axis=0)

        def both(ref, i):
            return jnp.concatenate([ref[0, i], ref[1, i]], axis=0)
        def scored(keys, key_position):
            scores = across_lanes(queries, keys) * (1.0 / math.sqrt(HD))
            return jnp.where(key_position <= position, scores, -1e30)

        scores_a = scored(both(kv_own, 0), key_positions[0])
        for copy in swaps_kv:
            copy.wait_recv()
        scores_b = scored(both(kv_other, 0), key_positions[1])
        largest = jnp.maximum(
            jnp.max(scores_a, axis=1, keepdims=True), jnp.max(scores_b, axis=1, keepdims=True)
        )
        raised_a = jnp.exp(scores_a - largest)
        raised_b = jnp.exp(scores_b - largest)
        weight_sum = jnp.sum(raised_a, axis=1, keepdims=True) + jnp.sum(
            raised_b, axis=1, keepdims=True
        )
        weighted = product(raised_a.astype(jnp.bfloat16), both(kv_own, 1)) + product(
            raised_b.astype(jnp.bfloat16), both(kv_other, 1)
        )
        tall[t] = (weighted / weight_sum).astype(jnp.bfloat16).reshape(2, half_total, HD)
        risen = {}
        for k in far_first + (0,):
            take = pl.ds(pl.multiple_of(flip(k) * part_rows, part_rows), part_rows)
            for d in range(count - 1, 0, -1):
                risen[k, d] = launch(
                    remote(
                        tall.at[t, :, take],
                        tall.at[t, :, take],
                        tz_s.at[k, d - 1],
                        tz_r.at[k, d - 1],
                        tp_peer(tower(d)),
                    )
                )
        for copy in ups:
            copy.wait_recv()
        mine_out.wait()
        halves = launch(
            remote(out_rows.at[c], out_rows.at[c], oc_sems.at[0], oc_sems.at[1], partner)
        )
        halves.wait_recv()
        hops, parts_own = [], []
        summed = patch_ref[...].astype(jnp.float32)
        for k in far_first + (0,):
            for d in range(1, count):
                take = pl.ds(pl.multiple_of(flip(k) * part_rows, part_rows), part_rows)
                remote(
                    tall.at[tower(-d), :, take],
                    tall.at[tower(-d), :, take],
                    tz_s.at[k, d - 1],
                    tz_r.at[k, d - 1],
                    tp_peer(tower(-d)),
                ).wait_recv()
            take = pl.ds(pl.multiple_of(flip(k) * part_rows, part_rows), part_rows)
            attended = jnp.concatenate(
                [tall[q, :, take].reshape(slots, HD) for q in range(count)], axis=1
            )
            for core in range(2):
                lanes = slice(core * half, (core + 1) * half)
                part = product(attended, out_rows[core].reshape(count * HD, half))
                if k:
                    parts[k - 1, :, lanes] = part.astype(jnp.bfloat16)
                else:
                    parts_own.append(part)
            if k:
                hops.append(
                    launch(
                        remote(
                            parts.at[k - 1],
                            land.at[k - 1],
                            a_s.at[k - 1],
                            a_r.at[k - 1],
                            plane(flip(k)),
                        )
                    )
                )
        summed = summed + jnp.concatenate(parts_own, axis=1)
        for copy in hops:
            copy.wait_recv()
        for k in range(count - 1):
            summed = summed + land[k].astype(jnp.float32)
        out_ref[...] = jnp.where(in_use, summed, 0.0).astype(jnp.bfloat16)
        enc_out.wait()
        for copy in sent:
            copy.wait_send()
        for i in range(2):
            beside(i).wait_send()
        for h in range(2):
            sent_near(
                lambda target, sem: share_heads(t, h, target, sem), lambda which: hand_over(which, h)
            )

        for r in range(2):
            for i in range(widths[r]):
                for k in range(1, count):
                    away(k, r, i).wait_send()

                @pl.when(p != t)
                def _():
                    away(0, r, i).wait_send()
    vmem = pl.BlockSpec(memory_space=pltpu.VMEM)
    hbm = pl.BlockSpec(memory_space=pl.ANY)
    smem = pl.BlockSpec(memory_space=pltpu.SMEM)
    dma = pltpu.SemaphoreType.DMA

    def buffer(*shape, dtype=jnp.bfloat16):
        return pltpu.VMEM(shape, dtype)

    return pl.pallas_call(
        kernel,
        out_shape=[like((byte_rows, width)), like((slots, columns))],
        in_specs=[hbm, vmem, hbm, hbm, vmem, smem, hbm, hbm, vmem, hbm, hbm, hbm],
        out_specs=[hbm, vmem],
        scratch_shapes=[
            buffer(total_rows, width),
            buffer(*enc_qkv.shape),
            buffer(total_rows, enc_cols),
            buffer(2, 2, WIN + total_rows, share),
            buffer(size, 8, 128, dtype=jnp.int32),
            buffer(2, count, share, width),
            buffer(count, 2, total_rows, share),
            buffer(total_rows, width, dtype=jnp.float32),
            buffer(*table.shape, dtype=jnp.float32),
            buffer(row_total, HD, dtype=jnp.float32),
            buffer(row_total, HD, dtype=jnp.float32),
            buffer(*lift.shape),
            buffer(*cross_kv.shape),
            buffer(slots, width),
            buffer(total_rows, width),
            buffer(2, part_rows, columns),
            buffer(2, count, part_rows, columns),
            buffer(slots, columns),
            buffer(*lat_qkv.shape),
            buffer(*lat_qkv.shape),
            buffer(half_total, columns),
            buffer(2, 3, half_total, HD, dtype=jnp.float32),
            buffer(2, near, 3, half_total, HD),
            buffer(2, near, 3, half_total, HD),
            buffer(2, 8, half_total, dtype=jnp.float32),
            buffer(2, near, 8, half_total, dtype=jnp.float32),
            buffer(2, 2, half_total, HD),
            buffer(2, 2, half_total, HD),
            buffer(count, HD, half),
            buffer(2, count, HD, half),
            buffer(count, 2, half_total, HD),
            buffer(near, slots, columns),
            buffer(near, slots, columns),
            dma((9,)),
            dma((size - 1,)),
            dma((size - 1,)),
            dma((2, 2)),
            dma((2, 2)),
            dma((3,)),
            dma((3,)),
            dma((near,)),
            dma((near,)),
            dma((near,)),
            dma((near,)),
            dma((1,)),
            dma((1,)),
            dma((2,)),
            dma((2, 5)),
            dma((2, count)),
            dma((count, panel_count + 2)),
            dma((count, panel_count + 2)),
            dma((panel_count + 2,)),
            dma((2, near)),
            dma((2, near)),
            dma((2, near)),
            dma((2, near)),
            dma((2,)),
            dma((2,)),
            dma((near,)),
            dma((near,)),
            dma((near,)),
            dma((near,)),
            dma((2,)),
            dma((1,)),
            dma((count, near)),
            dma((count, near)),
            dma((near,)),
            dma((near,)),
            dma((1,)),
        ],
        compiler_params=pltpu.CompilerParams(collective_id=call_id, has_side_effects=True),
    )(
        states, gain, enc_qkv, proj, starts, counts, lift, cross_kv, latent_gain, lat_qkv, lat_proj,
        table,
    )


def settle(*arrays):
    total = len(arrays)

    def kernel(*refs):
        ins, outs, holds = refs[:total], refs[total : 2 * total], refs[2 * total : 3 * total]
        in_sems, out_sems = refs[3 * total :]
        takes = [pltpu.make_async_copy(ins[i], holds[i], in_sems.at[i]) for i in range(total)]
        puts = [pltpu.make_async_copy(holds[i], outs[i], out_sems.at[i]) for i in range(total)]
        for take in takes:
            take.start()
        for take, put in zip(takes, puts):
            take.wait()
            put.start()
        for put in puts:
            put.wait()

    hbm = pl.BlockSpec(memory_space=pl.ANY)
    return pl.pallas_call(
        kernel,
        out_shape=[like(value.shape, value.dtype) for value in arrays],
        in_specs=[hbm] * total,
        out_specs=[hbm] * total,
        scratch_shapes=[pltpu.VMEM(value.shape, value.dtype) for value in arrays]
        + [pltpu.SemaphoreType.DMA((total,))] * 2,
    )(*arrays)


def fused_shards(
    byte_states,
    enc_gain,
    enc_qkv,
    enc_proj_out,
    starts,
    counts,
    lift,
    cross_kv,
    latent_gain,
    lat_qkv,
    lat_proj_out,
):
    table = jnp.asarray(turn_table(lax.axis_size("seq") * starts.shape[1]))
    encoded, latent = whole_layer(
        byte_states,
        enc_gain,
        enc_qkv,
        enc_proj_out,
        starts,
        counts,
        lift,
        cross_kv,
        latent_gain,
        lat_qkv,
        lat_proj_out,
        table,
        1,
    )
    return settle(encoded, latent)


def fits_pairs(mesh, byte_states, enc_qkv, starts, lat_qkv):
    size, tp_size = mesh.shape["seq"], mesh.shape["tp"]
    byte_rows = byte_states.shape[0] // size
    return (
        size == 2 * tp_size
        and tp_size == 4
        and WIN % byte_rows == 0
        and WIN == 2 * byte_rows
        and byte_rows % (32 * tp_size) == 0
        and lat_qkv.shape[2] // tp_size == HD * tp_size
        and lat_qkv.shape[1] % (128 * size) == 0
        and starts.shape[1] * tp_size % 128 == 0
        and starts.shape[1] * tp_size <= 1024
        and starts.shape[1] % 16 == 0
        and enc_qkv.shape[2] % (128 * tp_size) == 0
    )


def solution(mesh):
    specs = dict(
        mesh=mesh,
        in_specs=(
            P("seq", None),
            P(),
            P(None, None, "tp"),
            P("tp", None),
            P("seq", None),
            P("seq"),
            P(None, "tp"),
            P(None, None, "tp"),
            P(),
            P(None, "seq", "tp"),
            P("tp", "seq"),
        ),
        out_specs=(P("seq", None), P("seq", "tp")),
        check_vma=False,
    )

    def run(*arrays):
        paired = fits_pairs(mesh, arrays[0], arrays[2], arrays[4], arrays[9])
        return jax.shard_map(fused_shards if paired else gathered_shards, **specs)(*arrays)

    return run
```

```python
import math

import jax
import numpy as np
import jax.numpy as jnp
from jax import lax
from jax.experimental import pallas as pl
from jax.experimental.pallas import tpu as pltpu
from jax.sharding import PartitionSpec as P

EH = 64
HD = 128
WIN = 512
SPILL = 8


epsilon = 1e-05
rope_base = 500000.0
far_position = 1 << 30


def from_behind(value, axis, steps):
    count = lax.axis_size(axis)
    leading, last = (max(0, -steps), min(count, count - steps))
    return lax.ppermute(value, axis, [(source, source + steps) for source in range(leading, last)])


def prefix(value, axis, join, neutral):
    count, mine = (lax.axis_size(axis), lax.axis_index(axis))
    pieces = lax.all_gather(value, axis)
    subtotal = jnp.full_like(value, 0) + jnp.asarray(neutral, value.dtype)

    def hop(position, subtotal):
        longer = join(subtotal, pieces[position])
        return jnp.where(position < mine, longer, subtotal)

    return lax.fori_loop(0, count - 1, hop, subtotal)


def shortened(value):

    def short(part):
        return part.astype(jnp.bfloat16) if part.dtype == jnp.float32 else part

    return jax.tree.map(short, value)


def rms_scale(values, gain_row):
    mean_square = jnp.mean(values * values, axis=-1, keepdims=True)
    return values * lax.rsqrt(mean_square + epsilon) * gain_row


def masked_softmax(scores, allowed):
    scores = jnp.where(allowed, scores, -1e30)
    largest = jnp.max(scores, axis=-1, keepdims=True)
    raised = jnp.where(allowed, jnp.exp(scores - largest), 0.0)
    return raised / jnp.sum(raised, axis=-1, keepdims=True)


def rotate(values, position):
    halfway = values.shape[-1] // 2
    frequency = jnp.power(
        rope_base, -2.0 * jnp.arange(halfway, dtype=jnp.float32) / values.shape[-1]
    )
    angles = position.astype(jnp.float32)[:, None] * frequency[None, :]
    cosine = jnp.cos(angles)[:, None, :]
    sine_rows = jnp.sin(angles)[:, None, :]
    lower_half = values[..., :halfway]
    upper_half = values[..., halfway:]
    return jnp.concatenate(
        [
            lower_half * cosine - upper_half * sine_rows,
            upper_half * cosine + lower_half * sine_rows,
        ],
        axis=-1,
    )


def patch_block(extended, first_byte, end_byte, in_use, anchor, lift, cross_kv):
    columns = anchor + jnp.arange(extended.shape[0], dtype=jnp.int32)
    inside = (
        (columns[None, :] >= first_byte[:, None])
        & (columns[None, :] < end_byte[:, None])
        & in_use[:, None]
    )
    member = inside.astype(jnp.bfloat16)
    totals = jnp.dot(member, extended, preferred_element_type=jnp.float32)
    lengths = jnp.maximum(jnp.sum(inside.astype(jnp.float32), axis=1), 1.0)
    pooled = (totals / lengths[:, None]).astype(jnp.bfloat16)
    lifted = jnp.dot(pooled, lift, preferred_element_type=jnp.float32)
    key_rows = jnp.dot(extended, cross_kv[0], preferred_element_type=jnp.float32).astype(
        jnp.bfloat16
    )
    value_rows = jnp.dot(extended, cross_kv[1], preferred_element_type=jnp.float32).astype(
        jnp.bfloat16
    )
    slot_total = first_byte.shape[0]
    head_count = lifted.shape[1] // HD
    queries = lifted.astype(jnp.bfloat16).reshape(slot_total, head_count, HD)
    scores = jnp.einsum(
        "phd,khd->hpk",
        queries,
        key_rows.reshape(-1, head_count, HD),
        preferred_element_type=jnp.float32,
    ) * (1.0 / math.sqrt(HD))
    allowed = inside | (~in_use)[:, None] & (columns[None, :] == anchor)
    weights = masked_softmax(scores, allowed[None]).astype(jnp.bfloat16)
    crossed = jnp.einsum(
        "hpk,khd->phd",
        weights,
        value_rows.reshape(-1, head_count, HD),
        preferred_element_type=jnp.float32,
    )
    crossed = crossed.reshape(slot_total, head_count * HD)
    return jnp.where(in_use[:, None], lifted + crossed, 0.0).astype(jnp.bfloat16)


def add_counts(earlier, later):
    return earlier + later


def gathered_shards(
    byte_states,
    enc_gain,
    enc_qkv,
    enc_proj_out,
    starts,
    counts,
    lift,
    cross_kv,
    latent_gain,
    lat_qkv,
    lat_proj_out,
):
    byte_rows = byte_states.shape[0]
    anchor = lax.axis_index("seq") * byte_rows
    states = byte_states.astype(jnp.float32)
    normed = rms_scale(states, enc_gain.astype(jnp.float32)).astype(jnp.bfloat16)
    projected = jnp.einsum(
        "bd,idc->ibc", normed, enc_qkv, preferred_element_type=jnp.float32
    ).astype(jnp.bfloat16)
    reach_blocks = max(WIN // byte_rows, 1)
    tail_rows = min(WIN, byte_rows)
    key_parts = []
    value_parts = []
    for distance in range(reach_blocks, 0, -1):
        moved_keys, moved_values = from_behind(
            (projected[1, byte_rows - tail_rows :], projected[2, byte_rows - tail_rows :]),
            "seq",
            distance,
        )
        key_parts.append(moved_keys)
        value_parts.append(moved_values)
    key_rows = jnp.concatenate(key_parts + [projected[1]], axis=0)
    value_rows = jnp.concatenate(value_parts + [projected[2]], axis=0)
    head_count = projected.shape[2] // EH
    scores = jnp.einsum(
        "qhd,khd->hqk",
        projected[0].reshape(byte_rows, head_count, EH),
        key_rows.reshape(-1, head_count, EH),
        preferred_element_type=jnp.float32,
    ) * (1.0 / math.sqrt(EH))
    query_pos = anchor + jnp.arange(byte_rows, dtype=jnp.int32)
    key_pos = anchor - WIN + jnp.arange(WIN + byte_rows, dtype=jnp.int32)
    allowed = (
        (key_pos[None, :] <= query_pos[:, None])
        & (key_pos[None, :] > query_pos[:, None] - WIN)
        & (key_pos[None, :] >= 0)
    )
    weights = masked_softmax(scores, allowed[None]).astype(jnp.bfloat16)
    attended = jnp.einsum(
        "hqk,khd->qhd",
        weights,
        value_rows.reshape(-1, head_count, EH),
        preferred_element_type=jnp.float32,
    )
    attended = attended.reshape(byte_rows, head_count * EH).astype(jnp.bfloat16)
    blended = lax.psum(jnp.dot(attended, enc_proj_out, preferred_element_type=jnp.float32), "tp")
    encoded = (states + blended).astype(jnp.bfloat16)
    patch_count = counts[0]
    local_starts = starts[0]
    first_local = (local_starts[0:1] - anchor).astype(jnp.bfloat16)
    next_rows, next_first = from_behind((encoded[:SPILL], first_local), "seq", -1)
    next_first = next_first.astype(jnp.int32)[0]
    extended = jnp.concatenate([encoded, next_rows], axis=0)
    slot_ids = jnp.arange(local_starts.shape[0], dtype=jnp.int32)
    in_use = slot_ids < patch_count
    following = jnp.concatenate([local_starts[1:], jnp.zeros((1,), jnp.int32)])
    patch_end = jnp.where(slot_ids + 1 < patch_count, following, anchor + byte_rows + next_first)
    patches = patch_block(extended, local_starts, patch_end, in_use, anchor, lift, cross_kv)
    offset = prefix(counts, "seq", add_counts, jnp.zeros((1,), jnp.int32))[0]
    position = offset + slot_ids
    slot_total = patches.shape[0]
    full_rows = lax.all_gather(patches, "tp", axis=1, tiled=True)
    normed_rows = rms_scale(full_rows.astype(jnp.float32), latent_gain.astype(jnp.float32)).astype(
        jnp.bfloat16
    )
    inner_width = lat_qkv.shape[2]
    projected = jnp.einsum(
        "pd,idc->ipc",
        normed_rows,
        lax.all_gather(lat_qkv, "seq", axis=1, tiled=True),
        preferred_element_type=jnp.float32,
    )
    heads_here = inner_width // HD
    queries = rotate(projected[0].reshape(slot_total, heads_here, HD), position).astype(
        jnp.bfloat16
    )
    latent_keys = (
        rotate(projected[1].reshape(slot_total, heads_here, HD), position)
        .astype(jnp.bfloat16)
        .reshape(slot_total, inner_width)
    )
    latent_values = projected[2].astype(jnp.bfloat16)
    latent_pos = jnp.where(in_use, position, far_position)
    largest = jnp.full((heads_here, slot_total), -1e30, jnp.float32)
    piece_keys = lax.all_gather(latent_keys, "seq", axis=0, tiled=True)
    piece_values = lax.all_gather(latent_values, "seq", axis=0, tiled=True)
    piece_pos = lax.all_gather(shortened(latent_pos), "seq", axis=0, tiled=True)
    rows_here = piece_keys.shape[0]
    piece_scores = jnp.einsum(
        "qhd,khd->hqk",
        queries,
        piece_keys.reshape(rows_here, heads_here, HD),
        preferred_element_type=jnp.float32,
    ) * (1.0 / math.sqrt(HD))
    permitted = (piece_pos[None, :] <= position[:, None])[None]
    piece_scores = jnp.where(permitted, piece_scores, -1e30)
    renewed = jnp.maximum(largest, jnp.max(piece_scores, axis=-1))
    raised = jnp.where(permitted, jnp.exp(piece_scores - renewed[..., None]), 0.0)
    weight_sum = jnp.sum(raised, axis=-1)
    weighted = jnp.einsum(
        "hqk,khd->hqd",
        raised.astype(jnp.bfloat16),
        piece_values.reshape(rows_here, heads_here, HD),
        preferred_element_type=jnp.float32,
    )
    largest, weight_sum, weighted = (renewed, weight_sum, weighted)
    latent_heads = (
        (weighted / weight_sum[..., None])
        .transpose(1, 0, 2)
        .reshape(slot_total, inner_width)
        .astype(jnp.bfloat16)
    )
    partials = jnp.dot(
        latent_heads,
        lax.all_gather(lat_proj_out, "seq", axis=1, tiled=True),
        preferred_element_type=jnp.float32,
    )
    reduced = lax.psum_scatter(partials, "tp", scatter_dimension=1, tiled=True)
    latent = jnp.where(in_use[:, None], patches.astype(jnp.float32) + reduced, 0.0).astype(
        jnp.bfloat16
    )
    return (encoded, latent)


MESH = pl.DeviceIdType.MESH
EDGE = 16


def seq_peer(index):
    return {"seq": index}


def tp_peer(index):
    return {"tp": index}


def like(shape, dtype=jnp.bfloat16):
    return jax.ShapeDtypeStruct(shape, dtype)


def iota(shape, axis):
    return lax.broadcasted_iota(jnp.int32, shape, axis)


def across_lanes(left, right):
    return lax.dot_general(
        left, right, (((1,), (1,)), ((), ())), preferred_element_type=jnp.float32
    )


def product(left, right):
    return jnp.dot(left, right, preferred_element_type=jnp.float32)


def remote(source, target, send_sem, recv_sem, device):
    return pltpu.make_async_remote_copy(
        src_ref=source,
        dst_ref=target,
        send_sem=send_sem,
        recv_sem=recv_sem,
        device_id=device,
        device_id_type=MESH,
    )


def turn_table(rows):
    frequency = rope_base ** (-2.0 * np.arange(HD // 2, dtype=np.float64) / HD)
    frequency = frequency.astype(np.float32)
    angles = np.arange(rows, dtype=np.float32)[:, None] * frequency[None, :]
    angles = angles.astype(np.float64)
    return np.concatenate([np.cos(angles), np.sin(angles)], axis=1).astype(np.float32)


def whole_layer(
    states, gain, enc_qkv, proj, starts, counts, lift, cross_kv, latent_gain, lat_qkv, lat_proj,
    table, call_id,
):
    count, size = lax.axis_size("tp"), lax.axis_size("seq")
    near = count - 1
    byte_rows, width = states.shape
    total_rows = byte_rows + EDGE
    enc_cols = enc_qkv.shape[2]
    enc_heads = enc_cols // EH
    slots = starts.shape[1]
    columns = lift.shape[1]
    group = 2 * HD
    panel_count = columns // group
    row_total = count * slots
    half = lat_qkv.shape[1]
    full_width = columns * count
    rows_half = byte_rows // 2
    row_spans = ((0, rows_half), (rows_half, rows_half), (byte_rows, EDGE))
    part_rows = slots // 2
    half_total = row_total // 2
    share = enc_cols // 2
    piece = share // count

    def kernel(
        states_hbm, gain_hbm, qkv_hbm, proj_hbm, starts_hbm, counts_hbm, lift_hbm, cross_hbm,
        lgain_hbm, w_own_hbm, o_hbm, table_hbm,
        enc_hbm, out_hbm,
        gain_ref, starts_ref, counts_ref, lgain_ref, states_ref, qkv_ref, query_ref, kv_ref, infos, proj_ref, att_ref, near_ref, blend_ref, table_ref, cos_ref, sin_ref,
        lift_ref, cross_ref, pooled_ref, full_ref, panels, rows_ref, patch_ref,
        w_own, w_other, geared, own_part, qkv_send, qkv_land, sq_send, sq_land,
        kv_own, kv_other, out_quarter, out_rows, tall, parts, land,
        load_sems, info_s, info_r, halo_s, halo_r, edge_s, edge_r, pz_s, pz_r, pp_s, pp_r, pc_s, pc_r,
        w_sems, heads_send, heads_recv,
        panel_send, panel_recv, stay_sems,
        qkv_s, qkv_r, sq_s, sq_r, kv_s, kv_r,
        oq_s, oq_r, oz_s, oz_r, oc_sems, own_sems, tz_s, tz_r, a_s, a_r, enc_sem,
    ):
        s, t = lax.axis_index("seq"), lax.axis_index("tp")
        p, c = s // 2, lax.rem(s, 2)
        partner = seq_peer(s + 1 - 2 * c)

        def plane(index):
            return {"seq": 2 * index + c}

        def ring(k):
            return lax.rem(s + k + size, size)

        def tower(k):
            return lax.rem(t + k + count, count)

        def flip(k):
            if k == 0:
                return p
            if k == 1:
                return p + 1 - 2 * lax.rem(p, 2)
            if k == 2:
                return lax.rem(p + 2, 4)
            return 3 - p

        far_first = (3, 2, 1)
        low = t < 2
        inner = (t == 1) | (t == 2)
        first_from = jnp.where(low, t + 1, t - 1)
        second_from = jnp.where(low, t + 2, t - 2)
        third_from = jnp.where(lax.rem(t, 2) == 0, count - 1, 0)
        outer = jnp.where(low, 0, count - 1)

        def to_near(copy_to):
            copy_to(first_from, 0).start()

            @pl.when(inner)
            def _():
                copy_to(outer, 1).start()

        def sent_near(copy_to, over):
            copy_to(first_from, 0).wait_send()

            @pl.when(inner)
            def _():
                copy_to(outer, 1).wait_send()
                for i in range(3):
                    over(i).wait_send()

        barrier = pltpu.get_barrier_semaphore()
        for k in range(1, size):
            pl.semaphore_signal(barrier, inc=1, device_id=seq_peer(ring(k)), device_id_type=MESH)
        for k in range(1, count):
            pl.semaphore_signal(barrier, inc=1, device_id=tp_peer(tower(k)), device_id_type=MESH)

        @pl.when(p != t)
        def _():
            for k in far_first:
                away_peer = {"seq": 2 * flip(k) + c, "tp": p}
                pl.semaphore_signal(barrier, inc=1, device_id=away_peer, device_id_type=MESH)

        own_rows = pl.ds(pl.multiple_of(p * HD, HD), HD)
        load_plan = (
            (states_hbm, states_ref.at[pl.ds(0, byte_rows)]),
            (qkv_hbm, qkv_ref),
            (table_hbm, table_ref),
            (proj_hbm.at[pl.ds(0, share)], proj_ref.at[0, 0]),
            (proj_hbm.at[pl.ds(share, share)], proj_ref.at[1, 0]),
            (lift_hbm, lift_ref),
            (cross_hbm, cross_ref),
            (w_own_hbm, w_own),
            (o_hbm.at[own_rows], out_quarter.at[p]),
            (gain_hbm, gain_ref),
            (starts_hbm, starts_ref),
            (counts_hbm, counts_ref),
            (lgain_hbm, lgain_ref),
        )
        loads = [
            pltpu.make_async_copy(source, target, load_sems.at[i])
            for i, (source, target) in enumerate(load_plan)
        ]
        for i in (0, 9, 1, 10, 11, 2, 3, 4, 5, 6, 7, 8, 12):
            loads[i].start()
        sent = []

        def launch(copy):
            copy.start()
            sent.append(copy)
            return copy
        loads[0].wait()
        loads[9].wait()
        values = states_ref[0:byte_rows].astype(jnp.float32)
        chip_row = gain_ref[...].astype(jnp.float32).reshape(1, width)
        normed = rms_scale(values, chip_row).astype(jnp.bfloat16)
        own = pl.ds(WIN, byte_rows)
        loads[1].wait()
        for i in range(2):
            fresh = product(normed, qkv_ref[i + 1]).astype(jnp.bfloat16)
            for h in range(2):
                kv_ref[h, i, own] = fresh[:, h * share : (h + 1) * share]
        query_ref[0:byte_rows] = (
            product(normed, qkv_ref[0]) * (1.0 / math.sqrt(EH))
        ).astype(jnp.bfloat16)
        loads[10].wait()
        loads[11].wait()
        my_count = counts_ref[...].reshape(1, 1)
        info_lane = iota((8, 128), 1)
        infos[s] = jnp.where(
            info_lane == 0, my_count, jnp.where(info_lane == 1, starts_ref[0:1, 0:1], 0)
        )
        greetings = size - 1 + count - 1

        @pl.when(p == t)
        def _():
            pl.semaphore_wait(barrier, greetings)

        @pl.when(p != t)
        def _():
            pl.semaphore_wait(barrier, greetings + count - 1)

        mine_at = pl.multiple_of(p * piece, piece)
        lifts = [
            launch(
                remote(
                    proj_hbm.at[pl.ds(pl.multiple_of(c * share + p * piece, piece), piece)],
                    proj_ref.at[c, k, pl.ds(mine_at, piece)],
                    pz_s.at[k - 1],
                    pz_r.at[k - 1],
                    tp_peer(tower(k)),
                )
            )
            for k in range(1, count)
        ]
        notes = [
            launch(
                remote(infos.at[s], infos.at[s], info_s.at[k - 1], info_r.at[k - 1], seq_peer(ring(k)))
            )
            for k in range(1, size)
        ]
        behind = seq_peer(ring(-1))
        edges = [
            launch(remote(source, target, edge_s.at[i], edge_r.at[i], behind))
            for i, (source, target) in enumerate(
                (
                    (
                        kv_ref.at[:, :, pl.ds(WIN, EDGE)],
                        kv_ref.at[:, :, pl.ds(WIN + byte_rows, EDGE)],
                    ),
                    (query_ref.at[pl.ds(0, EDGE)], query_ref.at[pl.ds(byte_rows, EDGE)]),
                    (states_ref.at[pl.ds(0, EDGE)], states_ref.at[pl.ds(byte_rows, EDGE)]),
                )
            )
        ]
        halos = [
            launch(
                remote(
                    kv_ref.at[h, :, own],
                    kv_ref.at[h, :, pl.ds(0, byte_rows)],
                    halo_s.at[0, h],
                    halo_r.at[0, h],
                    seq_peer(ring(2)),
                )
            )
            for h in range(2)
        ]
        def beside(i):
            first = pl.multiple_of(jnp.where(c == 0, WIN, 0), byte_rows)
            return remote(
                kv_ref.at[i, :, pl.ds(first, byte_rows)],
                kv_ref.at[i, :, pl.ds(byte_rows, byte_rows)],
                halo_s.at[1, i],
                halo_r.at[1, i],
                partner,
            )

        @pl.when(c == 0)
        def _():
            for i in range(2):
                beside(i).start()
        for copy in notes:
            copy.wait_recv()
        counted = [infos[m][0:1, 0:1] for m in range(size)]
        offsets = [jnp.zeros((1, 1), jnp.int32)]
        for m in range(size - 1):
            offsets.append(offsets[m] + counted[m])
        next_first = jnp.where(
            s + 1 < size, infos[jnp.minimum(s + 1, size - 1)][0:1, 1:2], size * byte_rows
        )
        square = (slots, slots)
        start_row = jnp.broadcast_to(starts_ref[...], square)
        apart = iota(square, 1) - iota(square, 0)
        first_byte = jnp.sum(jnp.where(apart == 0, start_row, 0), axis=1, keepdims=True)
        following = jnp.sum(jnp.where(apart == 1, start_row, 0), axis=1, keepdims=True)
        slot_at = iota((slots, 1), 0)
        in_use = slot_at < my_count
        patch_end = jnp.where(slot_at + 1 < my_count, following, next_first)
        anchor = s * byte_rows
        lower = jnp.where(in_use, first_byte - anchor, 0)
        upper = jnp.where(in_use, patch_end - anchor, 1)
        where_at = iota((slots, total_rows), 1)
        allowed = (where_at >= lower) & (where_at < upper)
        member = jnp.where(allowed & in_use, 1.0, 0.0)
        lengths = jnp.maximum(jnp.sum(member, axis=1, keepdims=True), 1.0)
        member = member.astype(jnp.bfloat16)
        bias = jnp.where(allowed, 0.0, -1e30)
        for begin, rows in row_spans:
            reach_rows = rows + WIN
            behind_by = iota((rows, reach_rows), 0) - iota((rows, reach_rows), 1) + WIN
            known = iota((rows, reach_rows), 1) >= WIN - begin - s * byte_rows
            near_by = (behind_by >= 0) & (behind_by < WIN) & known
            near_ref[begin : begin + rows, 0:reach_rows] = jnp.where(near_by, 0.0, -1e30)
        chosen = [
            (
                jnp.where(c == 0, offsets[2 * i], offsets[2 * i + 1]),
                jnp.where(c == 0, counted[2 * i], counted[2 * i + 1]),
                jnp.where(c == 0, offsets[2 * i + 1], offsets[2 * i]),
                jnp.where(c == 0, counted[2 * i + 1], counted[2 * i]),
            )
            for i in range(count)
        ]

        def laid(shape, axis, which):
            at = iota(shape, axis)
            band = at // half_total
            within = at - band * half_total
            block = within // part_rows
            result = jnp.broadcast_to(chosen[0][which], shape)
            for i in range(1, count):
                result = jnp.where(block == i, chosen[i][which], result)
            return band * part_rows + within - block * part_rows, result

        row_slot, row_offset = laid((row_total, 1), 0, 0)
        position = row_offset + row_slot
        key_positions = []
        for which in (0, 2):
            key_slot, key_offset = laid((1, row_total), 1, which)
            _, key_count = laid((1, row_total), 1, which + 1)
            key_positions.append(
                jnp.where(key_slot < key_count, key_offset + key_slot, far_position)
            )
        loads[2].wait()
        table_rows = table_ref.shape[0]
        picked = jnp.where(iota((row_total, table_rows), 1) == position, 1.0, 0.0)
        turns = lax.dot_general(
            picked,
            table_ref[...],
            (((1,), (0,)), ((), ())),
            precision=lax.Precision.HIGHEST,
            preferred_element_type=jnp.float32,
        )
        swapped = pltpu.roll(turns, HD // 2, 1)
        low_lanes = iota((row_total, HD), 1) < HD // 2
        cos_ref[...] = jnp.where(low_lanes, turns, swapped)
        sin_ref[...] = jnp.where(low_lanes, -swapped, turns)
        def halo_arrives(h):
            halos[h].wait_recv()

            @pl.when(c == 1)
            def _():
                beside(h).start()

        halo_arrives(0)
        for copy in lifts:
            copy.wait_recv()
        spread = [
            launch(
                remote(
                    proj_ref.at[c, pl.ds(1, near), pl.ds(mine_at, piece)],
                    proj_ref.at[c, pl.ds(1, near), pl.ds(mine_at, piece)],
                    pp_s.at[k - 1],
                    pp_r.at[k - 1],
                    plane(flip(k)),
                )
            )
            for k in far_first
        ]
        def shared(k):
            rows = pl.ds(pl.multiple_of(flip(k) * piece, piece), piece)
            return remote(
                proj_ref.at[c, pl.ds(1, near), rows],
                proj_ref.at[c, pl.ds(1, near), rows],
                pc_s.at[k],
                pc_r.at[k],
                partner,
            )

        launch(shared(0))
        for copy in edges:
            copy.wait_recv()

        beside(0).wait_recv()
        def share_heads(origin, h, target, sem):
            return remote(
                att_ref.at[origin, h],
                att_ref.at[origin, h],
                heads_send.at[h, sem],
                heads_recv.at[h, origin],
                tp_peer(target),
            )

        def attend(pair, begin, rows):
            reach_rows = rows + WIN
            keys = kv_ref[pair, 0, begin : begin + reach_rows]
            seen_values = kv_ref[pair, 1, begin : begin + reach_rows]
            queries = query_ref[begin : begin + rows, pair * share : (pair + 1) * share]
            head_of = iota((rows, share), 1) // EH
            stacked = jnp.concatenate(
                [jnp.where(head_of == h, queries, jnp.zeros_like(queries)) for h in range(share // EH)],
                axis=0,
            )
            near_bias = near_ref[begin : begin + rows, 0:reach_rows]
            scores = across_lanes(stacked, keys)
            raised, sums = [], []
            for h in range(share // EH):
                here = scores[h * rows : (h + 1) * rows] + near_bias
                here = jnp.exp(here - jnp.max(here, axis=1, keepdims=True))
                sums.append(jnp.sum(here, axis=1, keepdims=True))
                raised.append(here.astype(jnp.bfloat16))
            seen = product(jnp.concatenate(raised, axis=0), seen_values)
            attended = jnp.zeros((rows, share), jnp.float32)
            for h in range(share // EH):
                attended = jnp.where(
                    head_of == h, seen[h * rows : (h + 1) * rows] / sums[h], attended
                )
            att_ref[t, pair, begin : begin + rows] = attended.astype(jnp.bfloat16)

        for h in range(2):
            if h:
                halo_arrives(1)
                beside(1).wait_recv()
            for begin, rows in row_spans:
                attend(h, begin, rows)
            to_near(lambda target, sem: share_heads(t, h, target, sem))

        swaps = [launch(remote(w_own_hbm, w_other, w_sems.at[0], w_sems.at[1], partner))]
        sources = (first_from, second_from, third_from)
        beyond = (outer, outer, first_from)

        def hand_over(which, h):
            return share_heads(sources[which], h, beyond[which], 2 + which)

        def gain_heads(which, h):
            hand_over(which, h).wait_recv()

            @pl.when(inner)
            def _():
                hand_over(which, h).start()

        def blended(h):
            attended = jnp.concatenate([att_ref[tower(-k), h] for k in range(count)], axis=1)
            return product(attended, proj_ref[h].reshape(count * share, width))
        gain_heads(0, 0)

        @pl.when(inner)
        def _():
            gain_heads(2, 0)

        gain_heads(0, 1)

        @pl.when(inner)
        def _():
            gain_heads(2, 1)
        gain_heads(1, 0)

        @pl.when(jnp.logical_not(inner))
        def _():
            gain_heads(2, 0)
        for k, copy in zip(far_first[::-1], spread[::-1]):
            copy.wait_recv()
            launch(shared(k))
        quarters = [
            launch(
                remote(
                    o_hbm.at[pl.ds(pl.multiple_of(flip(k) * HD, HD), HD)],
                    out_quarter.at[p],
                    oq_s.at[k - 1],
                    oq_r.at[k - 1],
                    plane(flip(k)),
                )
            )
            for k in far_first
        ]
        loads[3].wait()
        loads[4].wait()
        gain_heads(1, 1)

        @pl.when(jnp.logical_not(inner))
        def _():
            gain_heads(2, 1)
        blend_ref[...] = states_ref[...].astype(jnp.float32) + blended(c)
        for k in range(count):
            shared(k).wait_recv()
        full_ref[...] = (blend_ref[...] + blended(1 - c)).astype(jnp.bfloat16)
        enc_out = pltpu.make_async_copy(full_ref.at[pl.ds(0, byte_rows)], enc_hbm, enc_sem.at[0])
        enc_out.start()

        totals = product(member, full_ref[...])
        pooled_ref[...] = (totals / lengths).astype(jnp.bfloat16)
        loads[5].wait()
        loads[6].wait()

        half_lanes = columns // 2

        def window(r, i):
            if r == 0:
                return pl.ds(pl.multiple_of(i * group, group), group)
            return pl.ds(i * half_lanes, half_lanes)

        def slot_of(r, i):
            return i if r == 0 else panel_count + i

        def away(k, r, i):
            return remote(
                panels.at[r, :, window(r, i)],
                rows_ref.at[r, p, :, window(r, i)],
                panel_send.at[k, slot_of(r, i)],
                panel_recv.at[p, slot_of(r, i)],
                {"seq": 2 * t + c, "tp": tower(k)},
            )

        def stay(r, i):
            return pltpu.make_async_copy(
                panels.at[r, :, window(r, i)],
                rows_ref.at[r, p, :, window(r, i)],
                stay_sems.at[slot_of(r, i)],
            )

        def ship(r, i):
            for k in (2, 1, 3):
                away(k, r, i).start()

            @pl.when(p != t)
            def _():
                away(0, r, i).start()

            @pl.when(p == t)
            def _():
                stay(r, i).start()

        widths = (panel_count, 2)

        def heads(i, carry):
            cols = pl.ds(pl.multiple_of(i * group, group), group)
            rows = full_ref[...]
            lifted = product(pooled_ref[...], lift_ref[:, cols])
            keys = product(rows, cross_ref[0, :, cols]).astype(jnp.bfloat16)
            seen_values = product(rows, cross_ref[1, :, cols]).astype(jnp.bfloat16)
            queries = lifted.astype(jnp.bfloat16)
            crossed = []
            for j in range(2):
                lanes = slice(j * HD, (j + 1) * HD)
                scores = across_lanes(queries[:, lanes], keys[:, lanes])
                scores = scores * (1.0 / math.sqrt(HD)) + bias
                raised = jnp.exp(scores - jnp.max(scores, axis=1, keepdims=True))
                crossed.append(
                    product(raised.astype(jnp.bfloat16), seen_values[:, lanes])
                    / jnp.sum(raised, axis=1, keepdims=True)
                )
            patch = lifted + jnp.concatenate(crossed, axis=1)
            panel = jnp.where(in_use, patch, 0.0).astype(jnp.bfloat16)
            patch_ref[:, cols] = panel
            for r in range(2):
                panels[r, :, cols] = panel[r * part_rows : (r + 1) * part_rows]
            ship(0, i)
            return carry
        lax.fori_loop(0, panel_count, heads, 0)
        for i in range(widths[1]):
            ship(1, i)

        arriving, flats = ([], []), []
        eye = iota((half_total, half_total), 0) == iota((half_total, half_total), 1)
        loads[12].wait()
        chip_gain = lgain_ref[pl.ds(pl.multiple_of(p * columns, columns), columns)]
        chip_gain = chip_gain.astype(jnp.float32).reshape(1, columns)
        for r in range(2):
            for q in range(count):

                @pl.when((p != q) | (p != t))
                def _():
                    for i in range(widths[r]):
                        remote(
                            panels.at[r, :, window(r, i)],
                            rows_ref.at[r, q, :, window(r, i)],
                            panel_send.at[0, slot_of(r, i)],
                            panel_recv.at[q, slot_of(r, i)],
                            plane(p),
                        ).wait_recv()

            @pl.when(p == t)
            def _():
                for i in range(widths[r]):
                    stay(r, i).wait()
            values = rows_ref[r].reshape(half_total, columns).astype(jnp.float32)
            squares = jnp.sum(values * values, axis=1, keepdims=True)
            flat = jnp.sum(jnp.where(eye, squares, 0.0), axis=0, keepdims=True)
            flats.append(flat)
            sq_send[r] = jnp.broadcast_to(flat, (8, half_total))
            geared[...] = (values * chip_gain).astype(jnp.bfloat16)
            for k in far_first:
                arriving[r].append(
                    launch(
                        remote(
                            sq_send.at[r],
                            sq_land.at[r, k - 1],
                            sq_s.at[r, k - 1],
                            sq_r.at[r, k - 1],
                            plane(flip(k)),
                        )
                    )
                )
            if r == 0:
                loads[7].wait()
                swaps[0].wait_recv()
            mine = geared[:, pl.ds(pl.multiple_of(c * half, half), half)]
            theirs = geared[:, pl.ds(pl.multiple_of((1 - c) * half, half), half)]
            for k in far_first + (0,):
                target = flip(k)
                lanes = pl.ds(pl.multiple_of(target * HD, HD), HD)
                for i in range(3):
                    part = product(mine, w_own[i, :, lanes]) + product(theirs, w_other[i, :, lanes])
                    if k:
                        qkv_send[r, k - 1, i] = part.astype(jnp.bfloat16)
                    else:
                        own_part[r, i] = part
                if k:
                    arriving[r].append(
                        launch(
                            remote(
                                qkv_send.at[r, k - 1],
                                qkv_land.at[r, k - 1],
                                qkv_s.at[r, k - 1],
                                qkv_r.at[r, k - 1],
                                plane(target),
                            )
                        )
                    )
            if r == 0:
                for copy in quarters:
                    copy.wait_recv()
                loads[8].wait()
                mine_out = pltpu.make_async_copy(
                    out_quarter.at[t], out_rows.at[c, t], own_sems.at[0]
                )
                mine_out.start()
                ups = [
                    remote(
                        out_quarter.at[tower(k)],
                        out_rows.at[c, t],
                        oz_s.at[k - 1],
                        oz_r.at[k - 1],
                        tp_peer(tower(k)),
                    )
                    for k in range(1, count)
                ]

            @pl.when(inner if r == 0 else jnp.logical_not(inner))
            def _():
                for copy in ups:
                    copy.start()

        sent.extend(ups)

        def turned(vectors, rows):
            return (
                vectors * cos_ref[rows] + pltpu.roll(vectors, HD // 2, 1) * sin_ref[rows]
            ).astype(jnp.bfloat16)

        swaps_kv, queries = [], []
        for r in range(2):
            for copy in arriving[r]:
                copy.wait_recv()
            flat = flats[r] + jnp.sum(sq_land[r, :, 0:1, :], axis=0)
            square_sum = jnp.sum(jnp.where(eye, flat, 0.0), axis=1, keepdims=True)
            scale = lax.rsqrt(square_sum / full_width + epsilon)
            total = []
            for i in range(3):
                band = own_part[r, i]
                for k in range(count - 1):
                    band = band + qkv_land[r, k, i].astype(jnp.float32)
                total.append(band * scale)
            rows = slice(r * half_total, (r + 1) * half_total)
            kv_own[r, 0] = turned(total[1], rows)
            kv_own[r, 1] = total[2].astype(jnp.bfloat16)
            swaps_kv.append(
                launch(remote(kv_own.at[r], kv_other.at[r], kv_s.at[r], kv_r.at[r], partner))
            )
            queries.append(turned(total[0], rows))
        queries = jnp.concatenate(queries, axis=0)

        def both(ref, i):
            return jnp.concatenate([ref[0, i], ref[1, i]], axis=0)
        def scored(keys, key_position):
            scores = across_lanes(queries, keys) * (1.0 / math.sqrt(HD))
            return jnp.where(key_position <= position, scores, -1e30)

        scores_a = scored(both(kv_own, 0), key_positions[0])
        for copy in swaps_kv:
            copy.wait_recv()
        scores_b = scored(both(kv_other, 0), key_positions[1])
        largest = jnp.maximum(
            jnp.max(scores_a, axis=1, keepdims=True), jnp.max(scores_b, axis=1, keepdims=True)
        )
        raised_a = jnp.exp(scores_a - largest)
        raised_b = jnp.exp(scores_b - largest)
        weight_sum = jnp.sum(raised_a, axis=1, keepdims=True) + jnp.sum(
            raised_b, axis=1, keepdims=True
        )
        weighted = product(raised_a.astype(jnp.bfloat16), both(kv_own, 1)) + product(
            raised_b.astype(jnp.bfloat16), both(kv_other, 1)
        )
        tall[t] = (weighted / weight_sum).astype(jnp.bfloat16).reshape(2, half_total, HD)
        risen = {}
        for k in far_first + (0,):
            take = pl.ds(pl.multiple_of(flip(k) * part_rows, part_rows), part_rows)
            for d in range(count - 1, 0, -1):
                risen[k, d] = launch(
                    remote(
                        tall.at[t, :, take],
                        tall.at[t, :, take],
                        tz_s.at[k, d - 1],
                        tz_r.at[k, d - 1],
                        tp_peer(tower(d)),
                    )
                )
        for copy in ups:
            copy.wait_recv()
        mine_out.wait()
        halves = launch(
            remote(out_rows.at[c], out_rows.at[c], oc_sems.at[0], oc_sems.at[1], partner)
        )
        halves.wait_recv()
        hops, parts_own = [], []
        summed = patch_ref[...].astype(jnp.float32)
        for k in far_first + (0,):
            for d in range(1, count):
                take = pl.ds(pl.multiple_of(flip(k) * part_rows, part_rows), part_rows)
                remote(
                    tall.at[tower(-d), :, take],
                    tall.at[tower(-d), :, take],
                    tz_s.at[k, d - 1],
                    tz_r.at[k, d - 1],
                    tp_peer(tower(-d)),
                ).wait_recv()
            take = pl.ds(pl.multiple_of(flip(k) * part_rows, part_rows), part_rows)
            attended = jnp.concatenate(
                [tall[q, :, take].reshape(slots, HD) for q in range(count)], axis=1
            )
            for core in range(2):
                lanes = slice(core * half, (core + 1) * half)
                part = product(attended, out_rows[core].reshape(count * HD, half))
                if k:
                    parts[k - 1, :, lanes] = part.astype(jnp.bfloat16)
                else:
                    parts_own.append(part)
            if k:
                hops.append(
                    launch(
                        remote(
                            parts.at[k - 1],
                            land.at[k - 1],
                            a_s.at[k - 1],
                            a_r.at[k - 1],
                            plane(flip(k)),
                        )
                    )
                )
        summed = summed + jnp.concatenate(parts_own, axis=1)
        for copy in hops:
            copy.wait_recv()
        for k in range(count - 1):
            summed = summed + land[k].astype(jnp.float32)
        patch_ref[...] = jnp.where(in_use, summed, 0.0).astype(jnp.bfloat16)
        latent_out = pltpu.make_async_copy(patch_ref, out_hbm, enc_sem.at[1])
        latent_out.start()
        enc_out.wait()
        for copy in sent:
            copy.wait_send()
        for i in range(2):
            beside(i).wait_send()
        for h in range(2):
            sent_near(
                lambda target, sem: share_heads(t, h, target, sem), lambda which: hand_over(which, h)
            )

        for r in range(2):
            for i in range(widths[r]):
                for k in range(1, count):
                    away(k, r, i).wait_send()

                @pl.when(p != t)
                def _():
                    away(0, r, i).wait_send()

        latent_out.wait()
    hbm = pl.BlockSpec(memory_space=pl.ANY)
    dma = pltpu.SemaphoreType.DMA

    def buffer(*shape, dtype=jnp.bfloat16):
        return pltpu.VMEM(shape, dtype)

    return pl.pallas_call(
        kernel,
        out_shape=[like((byte_rows, width)), like((slots, columns))],
        in_specs=[hbm] * 12,
        out_specs=[hbm, hbm],
        scratch_shapes=[
            buffer(width),
            buffer(1, slots, dtype=jnp.int32),
            buffer(1, dtype=jnp.int32),
            buffer(full_width),
            buffer(total_rows, width),
            buffer(*enc_qkv.shape),
            buffer(total_rows, enc_cols),
            buffer(2, 2, WIN + total_rows, share),
            buffer(size, 8, 128, dtype=jnp.int32),
            buffer(2, count, share, width),
            buffer(count, 2, total_rows, share),
            buffer(total_rows, rows_half + WIN, dtype=jnp.float32),
            buffer(total_rows, width, dtype=jnp.float32),
            buffer(*table.shape, dtype=jnp.float32),
            buffer(row_total, HD, dtype=jnp.float32),
            buffer(row_total, HD, dtype=jnp.float32),
            buffer(*lift.shape),
            buffer(*cross_kv.shape),
            buffer(slots, width),
            buffer(total_rows, width),
            buffer(2, part_rows, columns),
            buffer(2, count, part_rows, columns),
            buffer(slots, columns),
            buffer(*lat_qkv.shape),
            buffer(*lat_qkv.shape),
            buffer(half_total, columns),
            buffer(2, 3, half_total, HD, dtype=jnp.float32),
            buffer(2, near, 3, half_total, HD),
            buffer(2, near, 3, half_total, HD),
            buffer(2, 8, half_total, dtype=jnp.float32),
            buffer(2, near, 8, half_total, dtype=jnp.float32),
            buffer(2, 2, half_total, HD),
            buffer(2, 2, half_total, HD),
            buffer(count, HD, half),
            buffer(2, count, HD, half),
            buffer(count, 2, half_total, HD),
            buffer(near, slots, columns),
            buffer(near, slots, columns),
            dma((13,)),
            dma((size - 1,)),
            dma((size - 1,)),
            dma((2, 2)),
            dma((2, 2)),
            dma((3,)),
            dma((3,)),
            dma((near,)),
            dma((near,)),
            dma((near,)),
            dma((near,)),
            dma((count,)),
            dma((count,)),
            dma((2,)),
            dma((2, 5)),
            dma((2, count)),
            dma((count, panel_count + 2)),
            dma((count, panel_count + 2)),
            dma((panel_count + 2,)),
            dma((2, near)),
            dma((2, near)),
            dma((2, near)),
            dma((2, near)),
            dma((2,)),
            dma((2,)),
            dma((near,)),
            dma((near,)),
            dma((near,)),
            dma((near,)),
            dma((2,)),
            dma((1,)),
            dma((count, near)),
            dma((count, near)),
            dma((near,)),
            dma((near,)),
            dma((2,)),
        ],
        compiler_params=pltpu.CompilerParams(collective_id=call_id, has_side_effects=True),
    )(
        states, gain, enc_qkv, proj, starts, counts, lift, cross_kv, latent_gain, lat_qkv, lat_proj,
        table,
    )


def settle(*arrays):
    total = len(arrays)

    def kernel(*refs):
        ins, outs, holds = refs[:total], refs[total : 2 * total], refs[2 * total : 3 * total]
        in_sems, out_sems = refs[3 * total :]
        takes = [pltpu.make_async_copy(ins[i], holds[i], in_sems.at[i]) for i in range(total)]
        puts = [pltpu.make_async_copy(holds[i], outs[i], out_sems.at[i]) for i in range(total)]
        for take in takes:
            take.start()
        for take, put in zip(takes, puts):
            take.wait()
            put.start()
        for put in puts:
            put.wait()

    hbm = pl.BlockSpec(memory_space=pl.ANY)
    return pl.pallas_call(
        kernel,
        out_shape=[like(value.shape, value.dtype) for value in arrays],
        in_specs=[hbm] * total,
        out_specs=[hbm] * total,
        scratch_shapes=[pltpu.VMEM(value.shape, value.dtype) for value in arrays]
        + [pltpu.SemaphoreType.DMA((total,))] * 2,
    )(*arrays)


def fused_shards(
    byte_states,
    enc_gain,
    enc_qkv,
    enc_proj_out,
    starts,
    counts,
    lift,
    cross_kv,
    latent_gain,
    lat_qkv,
    lat_proj_out,
):
    table = jnp.asarray(turn_table(lax.axis_size("seq") * starts.shape[1]))
    encoded, latent = whole_layer(
        byte_states,
        enc_gain,
        enc_qkv,
        enc_proj_out,
        starts,
        counts,
        lift,
        cross_kv,
        latent_gain,
        lat_qkv,
        lat_proj_out,
        table,
        1,
    )
    return settle(encoded, latent)


def fits_pairs(mesh, byte_states, enc_qkv, starts, lat_qkv):
    size, tp_size = mesh.shape["seq"], mesh.shape["tp"]
    byte_rows = byte_states.shape[0] // size
    return (
        size == 2 * tp_size
        and tp_size == 4
        and WIN % byte_rows == 0
        and WIN == 2 * byte_rows
        and byte_rows % (32 * tp_size) == 0
        and lat_qkv.shape[2] // tp_size == HD * tp_size
        and lat_qkv.shape[1] % (128 * size) == 0
        and starts.shape[1] * tp_size % 128 == 0
        and starts.shape[1] * tp_size <= 1024
        and starts.shape[1] % 16 == 0
        and enc_qkv.shape[2] % (128 * tp_size) == 0
    )


def solution(mesh):
    specs = dict(
        mesh=mesh,
        in_specs=(
            P("seq", None),
            P(),
            P(None, None, "tp"),
            P("tp", None),
            P("seq", None),
            P("seq"),
            P(None, "tp"),
            P(None, None, "tp"),
            P(),
            P(None, "seq", "tp"),
            P("tp", "seq"),
        ),
        out_specs=(P("seq", None), P("seq", "tp")),
        check_vma=False,
    )

    def run(*arrays):
        paired = fits_pairs(mesh, arrays[0], arrays[2], arrays[4], arrays[9])
        return jax.shard_map(fused_shards if paired else gathered_shards, **specs)(*arrays)

    return run
```

```python
import math

import jax
import numpy as np
import jax.numpy as jnp
from jax import lax
from jax.experimental import pallas as pl
from jax.experimental.pallas import tpu as pltpu
from jax.sharding import PartitionSpec as P

EH = 64
HD = 128
WIN = 512
SPILL = 8


epsilon = 1e-05
rope_base = 500000.0
far_position = 1 << 30


def from_behind(value, axis, steps):
    count = lax.axis_size(axis)
    leading, last = (max(0, -steps), min(count, count - steps))
    return lax.ppermute(value, axis, [(source, source + steps) for source in range(leading, last)])


def prefix(value, axis, join, neutral):
    count, mine = (lax.axis_size(axis), lax.axis_index(axis))
    pieces = lax.all_gather(value, axis)
    subtotal = jnp.full_like(value, 0) + jnp.asarray(neutral, value.dtype)

    def hop(position, subtotal):
        longer = join(subtotal, pieces[position])
        return jnp.where(position < mine, longer, subtotal)

    return lax.fori_loop(0, count - 1, hop, subtotal)


def shortened(value):

    def short(part):
        return part.astype(jnp.bfloat16) if part.dtype == jnp.float32 else part

    return jax.tree.map(short, value)


def rms_scale(values, gain_row):
    mean_square = jnp.mean(values * values, axis=-1, keepdims=True)
    return values * lax.rsqrt(mean_square + epsilon) * gain_row


def masked_softmax(scores, allowed):
    scores = jnp.where(allowed, scores, -1e30)
    largest = jnp.max(scores, axis=-1, keepdims=True)
    raised = jnp.where(allowed, jnp.exp(scores - largest), 0.0)
    return raised / jnp.sum(raised, axis=-1, keepdims=True)


def rotate(values, position):
    halfway = values.shape[-1] // 2
    frequency = jnp.power(
        rope_base, -2.0 * jnp.arange(halfway, dtype=jnp.float32) / values.shape[-1]
    )
    angles = position.astype(jnp.float32)[:, None] * frequency[None, :]
    cosine = jnp.cos(angles)[:, None, :]
    sine_rows = jnp.sin(angles)[:, None, :]
    lower_half = values[..., :halfway]
    upper_half = values[..., halfway:]
    return jnp.concatenate(
        [
            lower_half * cosine - upper_half * sine_rows,
            upper_half * cosine + lower_half * sine_rows,
        ],
        axis=-1,
    )


def patch_block(extended, first_byte, end_byte, in_use, anchor, lift, cross_kv):
    columns = anchor + jnp.arange(extended.shape[0], dtype=jnp.int32)
    inside = (
        (columns[None, :] >= first_byte[:, None])
        & (columns[None, :] < end_byte[:, None])
        & in_use[:, None]
    )
    member = inside.astype(jnp.bfloat16)
    totals = jnp.dot(member, extended, preferred_element_type=jnp.float32)
    lengths = jnp.maximum(jnp.sum(inside.astype(jnp.float32), axis=1), 1.0)
    pooled = (totals / lengths[:, None]).astype(jnp.bfloat16)
    lifted = jnp.dot(pooled, lift, preferred_element_type=jnp.float32)
    key_rows = jnp.dot(extended, cross_kv[0], preferred_element_type=jnp.float32).astype(
        jnp.bfloat16
    )
    value_rows = jnp.dot(extended, cross_kv[1], preferred_element_type=jnp.float32).astype(
        jnp.bfloat16
    )
    slot_total = first_byte.shape[0]
    head_count = lifted.shape[1] // HD
    queries = lifted.astype(jnp.bfloat16).reshape(slot_total, head_count, HD)
    scores = jnp.einsum(
        "phd,khd->hpk",
        queries,
        key_rows.reshape(-1, head_count, HD),
        preferred_element_type=jnp.float32,
    ) * (1.0 / math.sqrt(HD))
    allowed = inside | (~in_use)[:, None] & (columns[None, :] == anchor)
    weights = masked_softmax(scores, allowed[None]).astype(jnp.bfloat16)
    crossed = jnp.einsum(
        "hpk,khd->phd",
        weights,
        value_rows.reshape(-1, head_count, HD),
        preferred_element_type=jnp.float32,
    )
    crossed = crossed.reshape(slot_total, head_count * HD)
    return jnp.where(in_use[:, None], lifted + crossed, 0.0).astype(jnp.bfloat16)


def add_counts(earlier, later):
    return earlier + later


def gathered_shards(
    byte_states,
    enc_gain,
    enc_qkv,
    enc_proj_out,
    starts,
    counts,
    lift,
    cross_kv,
    latent_gain,
    lat_qkv,
    lat_proj_out,
):
    byte_rows = byte_states.shape[0]
    anchor = lax.axis_index("seq") * byte_rows
    states = byte_states.astype(jnp.float32)
    normed = rms_scale(states, enc_gain.astype(jnp.float32)).astype(jnp.bfloat16)
    projected = jnp.einsum(
        "bd,idc->ibc", normed, enc_qkv, preferred_element_type=jnp.float32
    ).astype(jnp.bfloat16)
    reach_blocks = max(WIN // byte_rows, 1)
    tail_rows = min(WIN, byte_rows)
    key_parts = []
    value_parts = []
    for distance in range(reach_blocks, 0, -1):
        moved_keys, moved_values = from_behind(
            (projected[1, byte_rows - tail_rows :], projected[2, byte_rows - tail_rows :]),
            "seq",
            distance,
        )
        key_parts.append(moved_keys)
        value_parts.append(moved_values)
    key_rows = jnp.concatenate(key_parts + [projected[1]], axis=0)
    value_rows = jnp.concatenate(value_parts + [projected[2]], axis=0)
    head_count = projected.shape[2] // EH
    scores = jnp.einsum(
        "qhd,khd->hqk",
        projected[0].reshape(byte_rows, head_count, EH),
        key_rows.reshape(-1, head_count, EH),
        preferred_element_type=jnp.float32,
    ) * (1.0 / math.sqrt(EH))
    query_pos = anchor + jnp.arange(byte_rows, dtype=jnp.int32)
    key_pos = anchor - WIN + jnp.arange(WIN + byte_rows, dtype=jnp.int32)
    allowed = (
        (key_pos[None, :] <= query_pos[:, None])
        & (key_pos[None, :] > query_pos[:, None] - WIN)
        & (key_pos[None, :] >= 0)
    )
    weights = masked_softmax(scores, allowed[None]).astype(jnp.bfloat16)
    attended = jnp.einsum(
        "hqk,khd->qhd",
        weights,
        value_rows.reshape(-1, head_count, EH),
        preferred_element_type=jnp.float32,
    )
    attended = attended.reshape(byte_rows, head_count * EH).astype(jnp.bfloat16)
    blended = lax.psum(jnp.dot(attended, enc_proj_out, preferred_element_type=jnp.float32), "tp")
    encoded = (states + blended).astype(jnp.bfloat16)
    patch_count = counts[0]
    local_starts = starts[0]
    first_local = (local_starts[0:1] - anchor).astype(jnp.bfloat16)
    next_rows, next_first = from_behind((encoded[:SPILL], first_local), "seq", -1)
    next_first = next_first.astype(jnp.int32)[0]
    extended = jnp.concatenate([encoded, next_rows], axis=0)
    slot_ids = jnp.arange(local_starts.shape[0], dtype=jnp.int32)
    in_use = slot_ids < patch_count
    following = jnp.concatenate([local_starts[1:], jnp.zeros((1,), jnp.int32)])
    patch_end = jnp.where(slot_ids + 1 < patch_count, following, anchor + byte_rows + next_first)
    patches = patch_block(extended, local_starts, patch_end, in_use, anchor, lift, cross_kv)
    offset = prefix(counts, "seq", add_counts, jnp.zeros((1,), jnp.int32))[0]
    position = offset + slot_ids
    slot_total = patches.shape[0]
    full_rows = lax.all_gather(patches, "tp", axis=1, tiled=True)
    normed_rows = rms_scale(full_rows.astype(jnp.float32), latent_gain.astype(jnp.float32)).astype(
        jnp.bfloat16
    )
    inner_width = lat_qkv.shape[2]
    projected = jnp.einsum(
        "pd,idc->ipc",
        normed_rows,
        lax.all_gather(lat_qkv, "seq", axis=1, tiled=True),
        preferred_element_type=jnp.float32,
    )
    heads_here = inner_width // HD
    queries = rotate(projected[0].reshape(slot_total, heads_here, HD), position).astype(
        jnp.bfloat16
    )
    latent_keys = (
        rotate(projected[1].reshape(slot_total, heads_here, HD), position)
        .astype(jnp.bfloat16)
        .reshape(slot_total, inner_width)
    )
    latent_values = projected[2].astype(jnp.bfloat16)
    latent_pos = jnp.where(in_use, position, far_position)
    largest = jnp.full((heads_here, slot_total), -1e30, jnp.float32)
    piece_keys = lax.all_gather(latent_keys, "seq", axis=0, tiled=True)
    piece_values = lax.all_gather(latent_values, "seq", axis=0, tiled=True)
    piece_pos = lax.all_gather(shortened(latent_pos), "seq", axis=0, tiled=True)
    rows_here = piece_keys.shape[0]
    piece_scores = jnp.einsum(
        "qhd,khd->hqk",
        queries,
        piece_keys.reshape(rows_here, heads_here, HD),
        preferred_element_type=jnp.float32,
    ) * (1.0 / math.sqrt(HD))
    permitted = (piece_pos[None, :] <= position[:, None])[None]
    piece_scores = jnp.where(permitted, piece_scores, -1e30)
    renewed = jnp.maximum(largest, jnp.max(piece_scores, axis=-1))
    raised = jnp.where(permitted, jnp.exp(piece_scores - renewed[..., None]), 0.0)
    weight_sum = jnp.sum(raised, axis=-1)
    weighted = jnp.einsum(
        "hqk,khd->hqd",
        raised.astype(jnp.bfloat16),
        piece_values.reshape(rows_here, heads_here, HD),
        preferred_element_type=jnp.float32,
    )
    largest, weight_sum, weighted = (renewed, weight_sum, weighted)
    latent_heads = (
        (weighted / weight_sum[..., None])
        .transpose(1, 0, 2)
        .reshape(slot_total, inner_width)
        .astype(jnp.bfloat16)
    )
    partials = jnp.dot(
        latent_heads,
        lax.all_gather(lat_proj_out, "seq", axis=1, tiled=True),
        preferred_element_type=jnp.float32,
    )
    reduced = lax.psum_scatter(partials, "tp", scatter_dimension=1, tiled=True)
    latent = jnp.where(in_use[:, None], patches.astype(jnp.float32) + reduced, 0.0).astype(
        jnp.bfloat16
    )
    return (encoded, latent)


MESH = pl.DeviceIdType.MESH
EDGE = 16


def seq_peer(index):
    return {"seq": index}


def tp_peer(index):
    return {"tp": index}


def like(shape, dtype=jnp.bfloat16):
    return jax.ShapeDtypeStruct(shape, dtype)


def iota(shape, axis):
    return lax.broadcasted_iota(jnp.int32, shape, axis)


def across_lanes(left, right):
    return lax.dot_general(
        left, right, (((1,), (1,)), ((), ())), preferred_element_type=jnp.float32
    )


def product(left, right):
    return jnp.dot(left, right, preferred_element_type=jnp.float32)


def remote(source, target, send_sem, recv_sem, device):
    return pltpu.make_async_remote_copy(
        src_ref=source,
        dst_ref=target,
        send_sem=send_sem,
        recv_sem=recv_sem,
        device_id=device,
        device_id_type=MESH,
    )


def turn_table(rows):
    frequency = rope_base ** (-2.0 * np.arange(HD // 2, dtype=np.float64) / HD)
    frequency = frequency.astype(np.float32)
    angles = np.arange(rows, dtype=np.float32)[:, None] * frequency[None, :]
    angles = angles.astype(np.float64)
    return np.concatenate([np.cos(angles), np.sin(angles)], axis=1).astype(np.float32)


def whole_layer(
    states, gain, enc_qkv, proj, starts, counts, lift, cross_kv, latent_gain, lat_qkv, lat_proj,
    table, call_id,
):
    count, size = lax.axis_size("tp"), lax.axis_size("seq")
    near = count - 1
    byte_rows, width = states.shape
    total_rows = byte_rows + EDGE
    enc_cols = enc_qkv.shape[2]
    enc_heads = enc_cols // EH
    slots = starts.shape[1]
    columns = lift.shape[1]
    group = 2 * HD
    panel_count = columns // group
    row_total = count * slots
    half = lat_qkv.shape[1]
    full_width = columns * count
    rows_half = byte_rows // 2
    row_spans = ((0, rows_half), (rows_half, rows_half), (byte_rows, EDGE))
    part_rows = slots // 2
    half_total = row_total // 2
    share = enc_cols // 2
    piece = share // count

    def kernel(
        states_hbm, gain_hbm, qkv_hbm, proj_hbm, starts_hbm, counts_hbm, lift_hbm, cross_hbm,
        lgain_hbm, w_own_hbm, o_hbm, table_hbm,
        enc_ref, out_ref,
        gain_ref, starts_ref, counts_ref, lgain_ref, states_ref, qkv_ref, query_ref, kv_ref, infos, proj_ref, att_ref, near_ref, blend_ref, table_ref, cos_ref, sin_ref,
        lift_ref, cross_ref, pooled_ref, full_ref, panels, rows_ref, patch_ref,
        w_own, w_other, geared, own_part, qkv_send, qkv_land, sq_send, sq_land,
        kv_own, kv_other, out_quarter, out_rows, tall, parts, land,
        load_sems, info_s, info_r, halo_s, halo_r, edge_s, edge_r, pz_s, pz_r, pp_s, pp_r, pc_s, pc_r,
        w_sems, heads_send, heads_recv,
        panel_send, panel_recv, stay_sems,
        qkv_s, qkv_r, sq_s, sq_r, kv_s, kv_r,
        oq_s, oq_r, oz_s, oz_r, oc_sems, own_sems, tz_s, tz_r, a_s, a_r, enc_sem,
    ):
        s, t = lax.axis_index("seq"), lax.axis_index("tp")
        p, c = s // 2, lax.rem(s, 2)
        partner = seq_peer(s + 1 - 2 * c)

        def plane(index):
            return {"seq": 2 * index + c}

        def ring(k):
            return lax.rem(s + k + size, size)

        def tower(k):
            return lax.rem(t + k + count, count)

        def flip(k):
            if k == 0:
                return p
            if k == 1:
                return p + 1 - 2 * lax.rem(p, 2)
            if k == 2:
                return lax.rem(p + 2, 4)
            return 3 - p

        far_first = (3, 2, 1)
        low = t < 2
        inner = (t == 1) | (t == 2)
        first_from = jnp.where(low, t + 1, t - 1)
        second_from = jnp.where(low, t + 2, t - 2)
        third_from = jnp.where(lax.rem(t, 2) == 0, count - 1, 0)
        outer = jnp.where(low, 0, count - 1)

        def to_near(copy_to):
            copy_to(first_from, 0).start()

            @pl.when(inner)
            def _():
                copy_to(outer, 1).start()

        def sent_near(copy_to, over):
            copy_to(first_from, 0).wait_send()

            @pl.when(inner)
            def _():
                copy_to(outer, 1).wait_send()
                for i in range(3):
                    over(i).wait_send()

        barrier = pltpu.get_barrier_semaphore()
        for k in range(1, size):
            pl.semaphore_signal(barrier, inc=1, device_id=seq_peer(ring(k)), device_id_type=MESH)
        for k in range(1, count):
            pl.semaphore_signal(barrier, inc=1, device_id=tp_peer(tower(k)), device_id_type=MESH)

        @pl.when(p != t)
        def _():
            for k in far_first:
                away_peer = {"seq": 2 * flip(k) + c, "tp": p}
                pl.semaphore_signal(barrier, inc=1, device_id=away_peer, device_id_type=MESH)

        own_rows = pl.ds(pl.multiple_of(p * HD, HD), HD)
        load_plan = (
            (states_hbm, states_ref.at[pl.ds(0, byte_rows)]),
            (qkv_hbm, qkv_ref),
            (table_hbm, table_ref),
            (proj_hbm.at[pl.ds(0, share)], proj_ref.at[0, 0]),
            (proj_hbm.at[pl.ds(share, share)], proj_ref.at[1, 0]),
            (lift_hbm, lift_ref),
            (cross_hbm, cross_ref),
            (w_own_hbm, w_own),
            (o_hbm.at[own_rows], out_quarter.at[p]),
            (gain_hbm, gain_ref),
            (starts_hbm, starts_ref),
            (counts_hbm, counts_ref),
            (lgain_hbm, lgain_ref),
        )
        loads = [
            pltpu.make_async_copy(source, target, load_sems.at[i])
            for i, (source, target) in enumerate(load_plan)
        ]
        for i in (0, 9, 1, 10, 11, 2, 3, 4, 5, 6, 7, 8, 12):
            loads[i].start()
        sent = []

        def launch(copy):
            copy.start()
            sent.append(copy)
            return copy
        loads[0].wait()
        loads[9].wait()
        values = states_ref[0:byte_rows].astype(jnp.float32)
        chip_row = gain_ref[...].astype(jnp.float32).reshape(1, width)
        normed = rms_scale(values, chip_row).astype(jnp.bfloat16)
        own = pl.ds(WIN, byte_rows)
        loads[1].wait()
        for i in range(2):
            fresh = product(normed, qkv_ref[i + 1]).astype(jnp.bfloat16)
            for h in range(2):
                kv_ref[h, i, own] = fresh[:, h * share : (h + 1) * share]
        query_ref[0:byte_rows] = (
            product(normed, qkv_ref[0]) * (1.0 / math.sqrt(EH))
        ).astype(jnp.bfloat16)
        loads[10].wait()
        loads[11].wait()
        my_count = counts_ref[...].reshape(1, 1)
        info_lane = iota((8, 128), 1)
        infos[s] = jnp.where(
            info_lane == 0, my_count, jnp.where(info_lane == 1, starts_ref[0:1, 0:1], 0)
        )
        greetings = size - 1 + count - 1

        @pl.when(p == t)
        def _():
            pl.semaphore_wait(barrier, greetings)

        @pl.when(p != t)
        def _():
            pl.semaphore_wait(barrier, greetings + count - 1)

        mine_at = pl.multiple_of(p * piece, piece)
        lifts = [
            launch(
                remote(
                    proj_hbm.at[pl.ds(pl.multiple_of(c * share + p * piece, piece), piece)],
                    proj_ref.at[c, k, pl.ds(mine_at, piece)],
                    pz_s.at[k - 1],
                    pz_r.at[k - 1],
                    tp_peer(tower(k)),
                )
            )
            for k in range(1, count)
        ]
        notes = [
            launch(
                remote(infos.at[s], infos.at[s], info_s.at[k - 1], info_r.at[k - 1], seq_peer(ring(k)))
            )
            for k in range(1, size)
        ]
        behind = seq_peer(ring(-1))
        edges = [
            launch(remote(source, target, edge_s.at[i], edge_r.at[i], behind))
            for i, (source, target) in enumerate(
                (
                    (
                        kv_ref.at[:, :, pl.ds(WIN, EDGE)],
                        kv_ref.at[:, :, pl.ds(WIN + byte_rows, EDGE)],
                    ),
                    (query_ref.at[pl.ds(0, EDGE)], query_ref.at[pl.ds(byte_rows, EDGE)]),
                    (states_ref.at[pl.ds(0, EDGE)], states_ref.at[pl.ds(byte_rows, EDGE)]),
                )
            )
        ]
        halos = [
            launch(
                remote(
                    kv_ref.at[h, :, own],
                    kv_ref.at[h, :, pl.ds(0, byte_rows)],
                    halo_s.at[0, h],
                    halo_r.at[0, h],
                    seq_peer(ring(2)),
                )
            )
            for h in range(2)
        ]
        def beside(i):
            first = pl.multiple_of(jnp.where(c == 0, WIN, 0), byte_rows)
            return remote(
                kv_ref.at[i, :, pl.ds(first, byte_rows)],
                kv_ref.at[i, :, pl.ds(byte_rows, byte_rows)],
                halo_s.at[1, i],
                halo_r.at[1, i],
                partner,
            )

        @pl.when(c == 0)
        def _():
            for i in range(2):
                beside(i).start()
        for copy in notes:
            copy.wait_recv()
        counted = [infos[m][0:1, 0:1] for m in range(size)]
        offsets = [jnp.zeros((1, 1), jnp.int32)]
        for m in range(size - 1):
            offsets.append(offsets[m] + counted[m])
        next_first = jnp.where(
            s + 1 < size, infos[jnp.minimum(s + 1, size - 1)][0:1, 1:2], size * byte_rows
        )
        square = (slots, slots)
        start_row = jnp.broadcast_to(starts_ref[...], square)
        apart = iota(square, 1) - iota(square, 0)
        first_byte = jnp.sum(jnp.where(apart == 0, start_row, 0), axis=1, keepdims=True)
        following = jnp.sum(jnp.where(apart == 1, start_row, 0), axis=1, keepdims=True)
        slot_at = iota((slots, 1), 0)
        in_use = slot_at < my_count
        patch_end = jnp.where(slot_at + 1 < my_count, following, next_first)
        anchor = s * byte_rows
        lower = jnp.where(in_use, first_byte - anchor, 0)
        upper = jnp.where(in_use, patch_end - anchor, 1)
        where_at = iota((slots, total_rows), 1)
        allowed = (where_at >= lower) & (where_at < upper)
        member = jnp.where(allowed & in_use, 1.0, 0.0)
        lengths = jnp.maximum(jnp.sum(member, axis=1, keepdims=True), 1.0)
        member = member.astype(jnp.bfloat16)
        bias = jnp.where(allowed, 0.0, -1e30)
        for begin, rows in row_spans:
            reach_rows = rows + WIN
            behind_by = iota((rows, reach_rows), 0) - iota((rows, reach_rows), 1) + WIN
            known = iota((rows, reach_rows), 1) >= WIN - begin - s * byte_rows
            near_by = (behind_by >= 0) & (behind_by < WIN) & known
            near_ref[begin : begin + rows, 0:reach_rows] = jnp.where(near_by, 0.0, -1e30)
        chosen = [
            (
                jnp.where(c == 0, offsets[2 * i], offsets[2 * i + 1]),
                jnp.where(c == 0, counted[2 * i], counted[2 * i + 1]),
                jnp.where(c == 0, offsets[2 * i + 1], offsets[2 * i]),
                jnp.where(c == 0, counted[2 * i + 1], counted[2 * i]),
            )
            for i in range(count)
        ]

        def laid(shape, axis, which):
            at = iota(shape, axis)
            band = at // half_total
            within = at - band * half_total
            block = within // part_rows
            result = jnp.broadcast_to(chosen[0][which], shape)
            for i in range(1, count):
                result = jnp.where(block == i, chosen[i][which], result)
            return band * part_rows + within - block * part_rows, result

        row_slot, row_offset = laid((row_total, 1), 0, 0)
        position = row_offset + row_slot
        key_positions = []
        for which in (0, 2):
            key_slot, key_offset = laid((1, row_total), 1, which)
            _, key_count = laid((1, row_total), 1, which + 1)
            key_positions.append(
                jnp.where(key_slot < key_count, key_offset + key_slot, far_position)
            )
        loads[2].wait()
        table_rows = table_ref.shape[0]
        picked = jnp.where(iota((row_total, table_rows), 1) == position, 1.0, 0.0)
        turns = lax.dot_general(
            picked,
            table_ref[...],
            (((1,), (0,)), ((), ())),
            precision=lax.Precision.HIGHEST,
            preferred_element_type=jnp.float32,
        )
        swapped = pltpu.roll(turns, HD // 2, 1)
        low_lanes = iota((row_total, HD), 1) < HD // 2
        cos_ref[...] = jnp.where(low_lanes, turns, swapped)
        sin_ref[...] = jnp.where(low_lanes, -swapped, turns)
        def halo_arrives(h):
            halos[h].wait_recv()

            @pl.when(c == 1)
            def _():
                beside(h).start()

        halo_arrives(0)
        for copy in lifts:
            copy.wait_recv()
        spread = [
            launch(
                remote(
                    proj_ref.at[c, pl.ds(1, near), pl.ds(mine_at, piece)],
                    proj_ref.at[c, pl.ds(1, near), pl.ds(mine_at, piece)],
                    pp_s.at[k - 1],
                    pp_r.at[k - 1],
                    plane(flip(k)),
                )
            )
            for k in far_first
        ]
        def shared(k):
            rows = pl.ds(pl.multiple_of(flip(k) * piece, piece), piece)
            return remote(
                proj_ref.at[c, pl.ds(1, near), rows],
                proj_ref.at[c, pl.ds(1, near), rows],
                pc_s.at[k],
                pc_r.at[k],
                partner,
            )

        launch(shared(0))
        for copy in edges:
            copy.wait_recv()

        beside(0).wait_recv()
        def share_heads(origin, h, target, sem):
            return remote(
                att_ref.at[origin, h],
                att_ref.at[origin, h],
                heads_send.at[h, sem],
                heads_recv.at[h, origin],
                tp_peer(target),
            )

        def attend(pair, begin, rows):
            reach_rows = rows + WIN
            keys = kv_ref[pair, 0, begin : begin + reach_rows]
            seen_values = kv_ref[pair, 1, begin : begin + reach_rows]
            queries = query_ref[begin : begin + rows, pair * share : (pair + 1) * share]
            head_of = iota((rows, share), 1) // EH
            stacked = jnp.concatenate(
                [jnp.where(head_of == h, queries, jnp.zeros_like(queries)) for h in range(share // EH)],
                axis=0,
            )
            near_bias = near_ref[begin : begin + rows, 0:reach_rows]
            scores = across_lanes(stacked, keys)
            raised, sums = [], []
            for h in range(share // EH):
                here = scores[h * rows : (h + 1) * rows] + near_bias
                here = jnp.exp(here - jnp.max(here, axis=1, keepdims=True))
                sums.append(jnp.sum(here, axis=1, keepdims=True))
                raised.append(here.astype(jnp.bfloat16))
            seen = product(jnp.concatenate(raised, axis=0), seen_values)
            attended = jnp.zeros((rows, share), jnp.float32)
            for h in range(share // EH):
                attended = jnp.where(
                    head_of == h, seen[h * rows : (h + 1) * rows] / sums[h], attended
                )
            att_ref[t, pair, begin : begin + rows] = attended.astype(jnp.bfloat16)

        for h in range(2):
            if h:
                halo_arrives(1)
                beside(1).wait_recv()
            for begin, rows in row_spans:
                attend(h, begin, rows)
            to_near(lambda target, sem: share_heads(t, h, target, sem))

        swaps = [launch(remote(w_own_hbm, w_other, w_sems.at[0], w_sems.at[1], partner))]
        sources = (first_from, second_from, third_from)
        beyond = (outer, outer, first_from)

        def hand_over(which, h):
            return share_heads(sources[which], h, beyond[which], 2 + which)

        def gain_heads(which, h):
            hand_over(which, h).wait_recv()

            @pl.when(inner)
            def _():
                hand_over(which, h).start()

        def blended(h):
            attended = jnp.concatenate([att_ref[tower(-k), h] for k in range(count)], axis=1)
            return product(attended, proj_ref[h].reshape(count * share, width))
        gain_heads(0, 0)

        @pl.when(inner)
        def _():
            gain_heads(2, 0)

        gain_heads(0, 1)

        @pl.when(inner)
        def _():
            gain_heads(2, 1)
        gain_heads(1, 0)

        @pl.when(jnp.logical_not(inner))
        def _():
            gain_heads(2, 0)
        for k, copy in zip(far_first[::-1], spread[::-1]):
            copy.wait_recv()
            launch(shared(k))
        quarters = [
            launch(
                remote(
                    o_hbm.at[pl.ds(pl.multiple_of(flip(k) * HD, HD), HD)],
                    out_quarter.at[p],
                    oq_s.at[k - 1],
                    oq_r.at[k - 1],
                    plane(flip(k)),
                )
            )
            for k in far_first
        ]
        loads[3].wait()
        loads[4].wait()
        gain_heads(1, 1)

        @pl.when(jnp.logical_not(inner))
        def _():
            gain_heads(2, 1)
        blend_ref[...] = states_ref[...].astype(jnp.float32) + blended(c)
        for k in range(count):
            shared(k).wait_recv()
        full_ref[...] = (blend_ref[...] + blended(1 - c)).astype(jnp.bfloat16)
        enc_out = pltpu.make_async_copy(full_ref.at[pl.ds(0, byte_rows)], enc_ref, enc_sem.at[0])
        enc_out.start()

        totals = product(member, full_ref[...])
        pooled_ref[...] = (totals / lengths).astype(jnp.bfloat16)
        loads[5].wait()
        loads[6].wait()

        half_lanes = columns // 2

        def window(r, i):
            if r == 0:
                return pl.ds(pl.multiple_of(i * group, group), group)
            return pl.ds(i * half_lanes, half_lanes)

        def slot_of(r, i):
            return i if r == 0 else panel_count + i

        def away(k, r, i):
            return remote(
                panels.at[r, :, window(r, i)],
                rows_ref.at[r, p, :, window(r, i)],
                panel_send.at[k, slot_of(r, i)],
                panel_recv.at[p, slot_of(r, i)],
                {"seq": 2 * t + c, "tp": tower(k)},
            )

        def stay(r, i):
            return pltpu.make_async_copy(
                panels.at[r, :, window(r, i)],
                rows_ref.at[r, p, :, window(r, i)],
                stay_sems.at[slot_of(r, i)],
            )

        def ship(r, i):
            for k in (2, 1, 3):
                away(k, r, i).start()

            @pl.when(p != t)
            def _():
                away(0, r, i).start()

            @pl.when(p == t)
            def _():
                stay(r, i).start()

        widths = (panel_count, 2)

        def heads(i, carry):
            cols = pl.ds(pl.multiple_of(i * group, group), group)
            rows = full_ref[...]
            lifted = product(pooled_ref[...], lift_ref[:, cols])
            keys = product(rows, cross_ref[0, :, cols]).astype(jnp.bfloat16)
            seen_values = product(rows, cross_ref[1, :, cols]).astype(jnp.bfloat16)
            queries = lifted.astype(jnp.bfloat16)
            crossed = []
            for j in range(2):
                lanes = slice(j * HD, (j + 1) * HD)
                scores = across_lanes(queries[:, lanes], keys[:, lanes])
                scores = scores * (1.0 / math.sqrt(HD)) + bias
                raised = jnp.exp(scores - jnp.max(scores, axis=1, keepdims=True))
                crossed.append(
                    product(raised.astype(jnp.bfloat16), seen_values[:, lanes])
                    / jnp.sum(raised, axis=1, keepdims=True)
                )
            patch = lifted + jnp.concatenate(crossed, axis=1)
            panel = jnp.where(in_use, patch, 0.0).astype(jnp.bfloat16)
            patch_ref[:, cols] = panel
            for r in range(2):
                panels[r, :, cols] = panel[r * part_rows : (r + 1) * part_rows]
            ship(0, i)
            return carry
        lax.fori_loop(0, panel_count, heads, 0)
        for i in range(widths[1]):
            ship(1, i)

        arriving, flats = ([], []), []
        eye = iota((half_total, half_total), 0) == iota((half_total, half_total), 1)
        loads[12].wait()
        chip_gain = lgain_ref[pl.ds(pl.multiple_of(p * columns, columns), columns)]
        chip_gain = chip_gain.astype(jnp.float32).reshape(1, columns)
        for r in range(2):
            for q in range(count):

                @pl.when((p != q) | (p != t))
                def _():
                    for i in range(widths[r]):
                        remote(
                            panels.at[r, :, window(r, i)],
                            rows_ref.at[r, q, :, window(r, i)],
                            panel_send.at[0, slot_of(r, i)],
                            panel_recv.at[q, slot_of(r, i)],
                            plane(p),
                        ).wait_recv()

            @pl.when(p == t)
            def _():
                for i in range(widths[r]):
                    stay(r, i).wait()
            values = rows_ref[r].reshape(half_total, columns).astype(jnp.float32)
            squares = jnp.sum(values * values, axis=1, keepdims=True)
            flat = jnp.sum(jnp.where(eye, squares, 0.0), axis=0, keepdims=True)
            flats.append(flat)
            sq_send[r] = jnp.broadcast_to(flat, (8, half_total))
            geared[...] = (values * chip_gain).astype(jnp.bfloat16)
            for k in far_first:
                arriving[r].append(
                    launch(
                        remote(
                            sq_send.at[r],
                            sq_land.at[r, k - 1],
                            sq_s.at[r, k - 1],
                            sq_r.at[r, k - 1],
                            plane(flip(k)),
                        )
                    )
                )
            if r == 0:
                loads[7].wait()
                swaps[0].wait_recv()
            mine = geared[:, pl.ds(pl.multiple_of(c * half, half), half)]
            theirs = geared[:, pl.ds(pl.multiple_of((1 - c) * half, half), half)]
            for k in far_first + (0,):
                target = flip(k)
                lanes = pl.ds(pl.multiple_of(target * HD, HD), HD)
                for i in range(3):
                    part = product(mine, w_own[i, :, lanes]) + product(theirs, w_other[i, :, lanes])
                    if k:
                        qkv_send[r, k - 1, i] = part.astype(jnp.bfloat16)
                    else:
                        own_part[r, i] = part
                if k:
                    arriving[r].append(
                        launch(
                            remote(
                                qkv_send.at[r, k - 1],
                                qkv_land.at[r, k - 1],
                                qkv_s.at[r, k - 1],
                                qkv_r.at[r, k - 1],
                                plane(target),
                            )
                        )
                    )
            if r == 0:
                for copy in quarters:
                    copy.wait_recv()
                loads[8].wait()
                mine_out = pltpu.make_async_copy(
                    out_quarter.at[t], out_rows.at[c, t], own_sems.at[0]
                )
                mine_out.start()
                ups = [
                    remote(
                        out_quarter.at[tower(k)],
                        out_rows.at[c, t],
                        oz_s.at[k - 1],
                        oz_r.at[k - 1],
                        tp_peer(tower(k)),
                    )
                    for k in range(1, count)
                ]

            @pl.when(inner if r == 0 else jnp.logical_not(inner))
            def _():
                for copy in ups:
                    copy.start()

        sent.extend(ups)

        def turned(vectors, rows):
            return (
                vectors * cos_ref[rows] + pltpu.roll(vectors, HD // 2, 1) * sin_ref[rows]
            ).astype(jnp.bfloat16)

        swaps_kv, queries = [], []
        for r in range(2):
            for copy in arriving[r]:
                copy.wait_recv()
            flat = flats[r] + jnp.sum(sq_land[r, :, 0:1, :], axis=0)
            square_sum = jnp.sum(jnp.where(eye, flat, 0.0), axis=1, keepdims=True)
            scale = lax.rsqrt(square_sum / full_width + epsilon)
            total = []
            for i in range(3):
                band = own_part[r, i]
                for k in range(count - 1):
                    band = band + qkv_land[r, k, i].astype(jnp.float32)
                total.append(band * scale)
            rows = slice(r * half_total, (r + 1) * half_total)
            kv_own[r, 0] = turned(total[1], rows)
            kv_own[r, 1] = total[2].astype(jnp.bfloat16)
            swaps_kv.append(
                launch(remote(kv_own.at[r], kv_other.at[r], kv_s.at[r], kv_r.at[r], partner))
            )
            queries.append(turned(total[0], rows))
        queries = jnp.concatenate(queries, axis=0)

        def both(ref, i):
            return jnp.concatenate([ref[0, i], ref[1, i]], axis=0)
        def scored(keys, key_position):
            scores = across_lanes(queries, keys) * (1.0 / math.sqrt(HD))
            return jnp.where(key_position <= position, scores, -1e30)

        scores_a = scored(both(kv_own, 0), key_positions[0])
        for copy in swaps_kv:
            copy.wait_recv()
        scores_b = scored(both(kv_other, 0), key_positions[1])
        largest = jnp.maximum(
            jnp.max(scores_a, axis=1, keepdims=True), jnp.max(scores_b, axis=1, keepdims=True)
        )
        raised_a = jnp.exp(scores_a - largest)
        raised_b = jnp.exp(scores_b - largest)
        weight_sum = jnp.sum(raised_a, axis=1, keepdims=True) + jnp.sum(
            raised_b, axis=1, keepdims=True
        )
        weighted = product(raised_a.astype(jnp.bfloat16), both(kv_own, 1)) + product(
            raised_b.astype(jnp.bfloat16), both(kv_other, 1)
        )
        tall[t] = (weighted / weight_sum).astype(jnp.bfloat16).reshape(2, half_total, HD)
        risen = {}
        for k in far_first + (0,):
            take = pl.ds(pl.multiple_of(flip(k) * part_rows, part_rows), part_rows)
            for d in range(count - 1, 0, -1):
                risen[k, d] = launch(
                    remote(
                        tall.at[t, :, take],
                        tall.at[t, :, take],
                        tz_s.at[k, d - 1],
                        tz_r.at[k, d - 1],
                        tp_peer(tower(d)),
                    )
                )
        for copy in ups:
            copy.wait_recv()
        mine_out.wait()
        halves = launch(
            remote(out_rows.at[c], out_rows.at[c], oc_sems.at[0], oc_sems.at[1], partner)
        )
        halves.wait_recv()
        hops, parts_own = [], []
        summed = patch_ref[...].astype(jnp.float32)
        for k in far_first + (0,):
            for d in range(1, count):
                take = pl.ds(pl.multiple_of(flip(k) * part_rows, part_rows), part_rows)
                remote(
                    tall.at[tower(-d), :, take],
                    tall.at[tower(-d), :, take],
                    tz_s.at[k, d - 1],
                    tz_r.at[k, d - 1],
                    tp_peer(tower(-d)),
                ).wait_recv()
            take = pl.ds(pl.multiple_of(flip(k) * part_rows, part_rows), part_rows)
            attended = jnp.concatenate(
                [tall[q, :, take].reshape(slots, HD) for q in range(count)], axis=1
            )
            for core in range(2):
                lanes = slice(core * half, (core + 1) * half)
                part = product(attended, out_rows[core].reshape(count * HD, half))
                if k:
                    parts[k - 1, :, lanes] = part.astype(jnp.bfloat16)
                else:
                    parts_own.append(part)
            if k:
                hops.append(
                    launch(
                        remote(
                            parts.at[k - 1],
                            land.at[k - 1],
                            a_s.at[k - 1],
                            a_r.at[k - 1],
                            plane(flip(k)),
                        )
                    )
                )
        summed = summed + jnp.concatenate(parts_own, axis=1)
        for copy in hops:
            copy.wait_recv()
        for k in range(count - 1):
            summed = summed + land[k].astype(jnp.float32)
        out_ref[...] = jnp.where(in_use, summed, 0.0).astype(jnp.bfloat16)
        enc_out.wait()
        for copy in sent:
            copy.wait_send()
        for i in range(2):
            beside(i).wait_send()
        for h in range(2):
            sent_near(
                lambda target, sem: share_heads(t, h, target, sem), lambda which: hand_over(which, h)
            )

        for r in range(2):
            for i in range(widths[r]):
                for k in range(1, count):
                    away(k, r, i).wait_send()

                @pl.when(p != t)
                def _():
                    away(0, r, i).wait_send()
    hbm = pl.BlockSpec(memory_space=pl.ANY)
    vmem = pl.BlockSpec(memory_space=pltpu.VMEM)
    dma = pltpu.SemaphoreType.DMA

    def buffer(*shape, dtype=jnp.bfloat16):
        return pltpu.VMEM(shape, dtype)

    return pl.pallas_call(
        kernel,
        out_shape=[like((byte_rows, width)), like((slots, columns))],
        in_specs=[hbm] * 12,
        out_specs=[vmem, vmem],
        scratch_shapes=[
            buffer(width),
            buffer(1, slots, dtype=jnp.int32),
            buffer(1, dtype=jnp.int32),
            buffer(full_width),
            buffer(total_rows, width),
            buffer(*enc_qkv.shape),
            buffer(total_rows, enc_cols),
            buffer(2, 2, WIN + total_rows, share),
            buffer(size, 8, 128, dtype=jnp.int32),
            buffer(2, count, share, width),
            buffer(count, 2, total_rows, share),
            buffer(total_rows, rows_half + WIN, dtype=jnp.float32),
            buffer(total_rows, width, dtype=jnp.float32),
            buffer(*table.shape, dtype=jnp.float32),
            buffer(row_total, HD, dtype=jnp.float32),
            buffer(row_total, HD, dtype=jnp.float32),
            buffer(*lift.shape),
            buffer(*cross_kv.shape),
            buffer(slots, width),
            buffer(total_rows, width),
            buffer(2, part_rows, columns),
            buffer(2, count, part_rows, columns),
            buffer(slots, columns),
            buffer(*lat_qkv.shape),
            buffer(*lat_qkv.shape),
            buffer(half_total, columns),
            buffer(2, 3, half_total, HD, dtype=jnp.float32),
            buffer(2, near, 3, half_total, HD),
            buffer(2, near, 3, half_total, HD),
            buffer(2, 8, half_total, dtype=jnp.float32),
            buffer(2, near, 8, half_total, dtype=jnp.float32),
            buffer(2, 2, half_total, HD),
            buffer(2, 2, half_total, HD),
            buffer(count, HD, half),
            buffer(2, count, HD, half),
            buffer(count, 2, half_total, HD),
            buffer(near, slots, columns),
            buffer(near, slots, columns),
            dma((13,)),
            dma((size - 1,)),
            dma((size - 1,)),
            dma((2, 2)),
            dma((2, 2)),
            dma((3,)),
            dma((3,)),
            dma((near,)),
            dma((near,)),
            dma((near,)),
            dma((near,)),
            dma((count,)),
            dma((count,)),
            dma((2,)),
            dma((2, 5)),
            dma((2, count)),
            dma((count, panel_count + 2)),
            dma((count, panel_count + 2)),
            dma((panel_count + 2,)),
            dma((2, near)),
            dma((2, near)),
            dma((2, near)),
            dma((2, near)),
            dma((2,)),
            dma((2,)),
            dma((near,)),
            dma((near,)),
            dma((near,)),
            dma((near,)),
            dma((2,)),
            dma((1,)),
            dma((count, near)),
            dma((count, near)),
            dma((near,)),
            dma((near,)),
            dma((1,)),
        ],
        compiler_params=pltpu.CompilerParams(
            collective_id=call_id, has_side_effects=True, vmem_limit_bytes=52428800
        ),
    )(
        states, gain, enc_qkv, proj, starts, counts, lift, cross_kv, latent_gain, lat_qkv, lat_proj,
        table,
    )


def settle(*arrays):
    total = len(arrays)

    def kernel(*refs):
        ins, outs, sems = refs[:total], refs[total : 2 * total], refs[2 * total]
        puts = [pltpu.make_async_copy(ins[i], outs[i], sems.at[i]) for i in range(total)]
        for put in puts:
            put.start()
        for put in puts:
            put.wait()

    return pl.pallas_call(
        kernel,
        out_shape=[like(value.shape, value.dtype) for value in arrays],
        in_specs=[pl.BlockSpec(memory_space=pl.ANY)] * total,
        out_specs=[pl.BlockSpec(memory_space=pltpu.HBM)] * total,
        scratch_shapes=[pltpu.SemaphoreType.DMA((total,))],
        compiler_params=pltpu.CompilerParams(vmem_limit_bytes=2**20),
    )(*arrays)


def fused_shards(
    byte_states,
    enc_gain,
    enc_qkv,
    enc_proj_out,
    starts,
    counts,
    lift,
    cross_kv,
    latent_gain,
    lat_qkv,
    lat_proj_out,
):
    table = jnp.asarray(turn_table(lax.axis_size("seq") * starts.shape[1]))
    operands = [
        value if value.size == 1 else pltpu.with_memory_space_constraint(value, pltpu.HBM)
        for value in (
            byte_states,
            enc_gain,
            enc_qkv,
            enc_proj_out,
            starts,
            counts,
            lift,
            cross_kv,
            latent_gain,
            lat_qkv,
            lat_proj_out,
            table,
        )
    ]
    encoded, latent = whole_layer(*operands, 1)
    return settle(encoded, latent)


def fits_pairs(mesh, byte_states, enc_qkv, starts, lat_qkv):
    size, tp_size = mesh.shape["seq"], mesh.shape["tp"]
    byte_rows = byte_states.shape[0] // size
    return (
        size == 2 * tp_size
        and tp_size == 4
        and WIN % byte_rows == 0
        and WIN == 2 * byte_rows
        and byte_rows % (32 * tp_size) == 0
        and lat_qkv.shape[2] // tp_size == HD * tp_size
        and lat_qkv.shape[1] % (128 * size) == 0
        and starts.shape[1] * tp_size % 128 == 0
        and starts.shape[1] * tp_size <= 1024
        and starts.shape[1] % 16 == 0
        and enc_qkv.shape[2] % (128 * tp_size) == 0
    )


def solution(mesh):
    specs = dict(
        mesh=mesh,
        in_specs=(
            P("seq", None),
            P(),
            P(None, None, "tp"),
            P("tp", None),
            P("seq", None),
            P("seq"),
            P(None, "tp"),
            P(None, None, "tp"),
            P(),
            P(None, "seq", "tp"),
            P("tp", "seq"),
        ),
        out_specs=(P("seq", None), P("seq", "tp")),
        check_vma=False,
    )

    def run(*arrays):
        paired = fits_pairs(mesh, arrays[0], arrays[2], arrays[4], arrays[9])
        return jax.shard_map(fused_shards if paired else gathered_shards, **specs)(*arrays)

    return run
```

```python
import math

import jax
import numpy as np
import jax.numpy as jnp
from jax import lax
from jax.experimental import pallas as pl
from jax.experimental.pallas import tpu as pltpu
from jax.sharding import PartitionSpec as P

EH = 64
HD = 128
WIN = 512
SPILL = 8


epsilon = 1e-05
rope_base = 500000.0
far_position = 1 << 30


def from_behind(value, axis, steps):
    count = lax.axis_size(axis)
    leading, last = (max(0, -steps), min(count, count - steps))
    return lax.ppermute(value, axis, [(source, source + steps) for source in range(leading, last)])


def prefix(value, axis, join, neutral):
    count, mine = (lax.axis_size(axis), lax.axis_index(axis))
    pieces = lax.all_gather(value, axis)
    subtotal = jnp.full_like(value, 0) + jnp.asarray(neutral, value.dtype)

    def hop(position, subtotal):
        longer = join(subtotal, pieces[position])
        return jnp.where(position < mine, longer, subtotal)

    return lax.fori_loop(0, count - 1, hop, subtotal)


def shortened(value):

    def short(part):
        return part.astype(jnp.bfloat16) if part.dtype == jnp.float32 else part

    return jax.tree.map(short, value)


def rms_scale(values, gain_row):
    mean_square = jnp.mean(values * values, axis=-1, keepdims=True)
    return values * lax.rsqrt(mean_square + epsilon) * gain_row


def masked_softmax(scores, allowed):
    scores = jnp.where(allowed, scores, -1e30)
    largest = jnp.max(scores, axis=-1, keepdims=True)
    raised = jnp.where(allowed, jnp.exp(scores - largest), 0.0)
    return raised / jnp.sum(raised, axis=-1, keepdims=True)


def rotate(values, position):
    halfway = values.shape[-1] // 2
    frequency = jnp.power(
        rope_base, -2.0 * jnp.arange(halfway, dtype=jnp.float32) / values.shape[-1]
    )
    angles = position.astype(jnp.float32)[:, None] * frequency[None, :]
    cosine = jnp.cos(angles)[:, None, :]
    sine_rows = jnp.sin(angles)[:, None, :]
    lower_half = values[..., :halfway]
    upper_half = values[..., halfway:]
    return jnp.concatenate(
        [
            lower_half * cosine - upper_half * sine_rows,
            upper_half * cosine + lower_half * sine_rows,
        ],
        axis=-1,
    )


def patch_block(extended, first_byte, end_byte, in_use, anchor, lift, cross_kv):
    columns = anchor + jnp.arange(extended.shape[0], dtype=jnp.int32)
    inside = (
        (columns[None, :] >= first_byte[:, None])
        & (columns[None, :] < end_byte[:, None])
        & in_use[:, None]
    )
    member = inside.astype(jnp.bfloat16)
    totals = jnp.dot(member, extended, preferred_element_type=jnp.float32)
    lengths = jnp.maximum(jnp.sum(inside.astype(jnp.float32), axis=1), 1.0)
    pooled = (totals / lengths[:, None]).astype(jnp.bfloat16)
    lifted = jnp.dot(pooled, lift, preferred_element_type=jnp.float32)
    key_rows = jnp.dot(extended, cross_kv[0], preferred_element_type=jnp.float32).astype(
        jnp.bfloat16
    )
    value_rows = jnp.dot(extended, cross_kv[1], preferred_element_type=jnp.float32).astype(
        jnp.bfloat16
    )
    slot_total = first_byte.shape[0]
    head_count = lifted.shape[1] // HD
    queries = lifted.astype(jnp.bfloat16).reshape(slot_total, head_count, HD)
    scores = jnp.einsum(
        "phd,khd->hpk",
        queries,
        key_rows.reshape(-1, head_count, HD),
        preferred_element_type=jnp.float32,
    ) * (1.0 / math.sqrt(HD))
    allowed = inside | (~in_use)[:, None] & (columns[None, :] == anchor)
    weights = masked_softmax(scores, allowed[None]).astype(jnp.bfloat16)
    crossed = jnp.einsum(
        "hpk,khd->phd",
        weights,
        value_rows.reshape(-1, head_count, HD),
        preferred_element_type=jnp.float32,
    )
    crossed = crossed.reshape(slot_total, head_count * HD)
    return jnp.where(in_use[:, None], lifted + crossed, 0.0).astype(jnp.bfloat16)


def add_counts(earlier, later):
    return earlier + later


def gathered_shards(
    byte_states,
    enc_gain,
    enc_qkv,
    enc_proj_out,
    starts,
    counts,
    lift,
    cross_kv,
    latent_gain,
    lat_qkv,
    lat_proj_out,
):
    byte_rows = byte_states.shape[0]
    anchor = lax.axis_index("seq") * byte_rows
    states = byte_states.astype(jnp.float32)
    normed = rms_scale(states, enc_gain.astype(jnp.float32)).astype(jnp.bfloat16)
    projected = jnp.einsum(
        "bd,idc->ibc", normed, enc_qkv, preferred_element_type=jnp.float32
    ).astype(jnp.bfloat16)
    reach_blocks = max(WIN // byte_rows, 1)
    tail_rows = min(WIN, byte_rows)
    key_parts = []
    value_parts = []
    for distance in range(reach_blocks, 0, -1):
        moved_keys, moved_values = from_behind(
            (projected[1, byte_rows - tail_rows :], projected[2, byte_rows - tail_rows :]),
            "seq",
            distance,
        )
        key_parts.append(moved_keys)
        value_parts.append(moved_values)
    key_rows = jnp.concatenate(key_parts + [projected[1]], axis=0)
    value_rows = jnp.concatenate(value_parts + [projected[2]], axis=0)
    head_count = projected.shape[2] // EH
    scores = jnp.einsum(
        "qhd,khd->hqk",
        projected[0].reshape(byte_rows, head_count, EH),
        key_rows.reshape(-1, head_count, EH),
        preferred_element_type=jnp.float32,
    ) * (1.0 / math.sqrt(EH))
    query_pos = anchor + jnp.arange(byte_rows, dtype=jnp.int32)
    key_pos = anchor - WIN + jnp.arange(WIN + byte_rows, dtype=jnp.int32)
    allowed = (
        (key_pos[None, :] <= query_pos[:, None])
        & (key_pos[None, :] > query_pos[:, None] - WIN)
        & (key_pos[None, :] >= 0)
    )
    weights = masked_softmax(scores, allowed[None]).astype(jnp.bfloat16)
    attended = jnp.einsum(
        "hqk,khd->qhd",
        weights,
        value_rows.reshape(-1, head_count, EH),
        preferred_element_type=jnp.float32,
    )
    attended = attended.reshape(byte_rows, head_count * EH).astype(jnp.bfloat16)
    blended = lax.psum(jnp.dot(attended, enc_proj_out, preferred_element_type=jnp.float32), "tp")
    encoded = (states + blended).astype(jnp.bfloat16)
    patch_count = counts[0]
    local_starts = starts[0]
    first_local = (local_starts[0:1] - anchor).astype(jnp.bfloat16)
    next_rows, next_first = from_behind((encoded[:SPILL], first_local), "seq", -1)
    next_first = next_first.astype(jnp.int32)[0]
    extended = jnp.concatenate([encoded, next_rows], axis=0)
    slot_ids = jnp.arange(local_starts.shape[0], dtype=jnp.int32)
    in_use = slot_ids < patch_count
    following = jnp.concatenate([local_starts[1:], jnp.zeros((1,), jnp.int32)])
    patch_end = jnp.where(slot_ids + 1 < patch_count, following, anchor + byte_rows + next_first)
    patches = patch_block(extended, local_starts, patch_end, in_use, anchor, lift, cross_kv)
    offset = prefix(counts, "seq", add_counts, jnp.zeros((1,), jnp.int32))[0]
    position = offset + slot_ids
    slot_total = patches.shape[0]
    full_rows = lax.all_gather(patches, "tp", axis=1, tiled=True)
    normed_rows = rms_scale(full_rows.astype(jnp.float32), latent_gain.astype(jnp.float32)).astype(
        jnp.bfloat16
    )
    inner_width = lat_qkv.shape[2]
    projected = jnp.einsum(
        "pd,idc->ipc",
        normed_rows,
        lax.all_gather(lat_qkv, "seq", axis=1, tiled=True),
        preferred_element_type=jnp.float32,
    )
    heads_here = inner_width // HD
    queries = rotate(projected[0].reshape(slot_total, heads_here, HD), position).astype(
        jnp.bfloat16
    )
    latent_keys = (
        rotate(projected[1].reshape(slot_total, heads_here, HD), position)
        .astype(jnp.bfloat16)
        .reshape(slot_total, inner_width)
    )
    latent_values = projected[2].astype(jnp.bfloat16)
    latent_pos = jnp.where(in_use, position, far_position)
    largest = jnp.full((heads_here, slot_total), -1e30, jnp.float32)
    piece_keys = lax.all_gather(latent_keys, "seq", axis=0, tiled=True)
    piece_values = lax.all_gather(latent_values, "seq", axis=0, tiled=True)
    piece_pos = lax.all_gather(shortened(latent_pos), "seq", axis=0, tiled=True)
    rows_here = piece_keys.shape[0]
    piece_scores = jnp.einsum(
        "qhd,khd->hqk",
        queries,
        piece_keys.reshape(rows_here, heads_here, HD),
        preferred_element_type=jnp.float32,
    ) * (1.0 / math.sqrt(HD))
    permitted = (piece_pos[None, :] <= position[:, None])[None]
    piece_scores = jnp.where(permitted, piece_scores, -1e30)
    renewed = jnp.maximum(largest, jnp.max(piece_scores, axis=-1))
    raised = jnp.where(permitted, jnp.exp(piece_scores - renewed[..., None]), 0.0)
    weight_sum = jnp.sum(raised, axis=-1)
    weighted = jnp.einsum(
        "hqk,khd->hqd",
        raised.astype(jnp.bfloat16),
        piece_values.reshape(rows_here, heads_here, HD),
        preferred_element_type=jnp.float32,
    )
    largest, weight_sum, weighted = (renewed, weight_sum, weighted)
    latent_heads = (
        (weighted / weight_sum[..., None])
        .transpose(1, 0, 2)
        .reshape(slot_total, inner_width)
        .astype(jnp.bfloat16)
    )
    partials = jnp.dot(
        latent_heads,
        lax.all_gather(lat_proj_out, "seq", axis=1, tiled=True),
        preferred_element_type=jnp.float32,
    )
    reduced = lax.psum_scatter(partials, "tp", scatter_dimension=1, tiled=True)
    latent = jnp.where(in_use[:, None], patches.astype(jnp.float32) + reduced, 0.0).astype(
        jnp.bfloat16
    )
    return (encoded, latent)


MESH = pl.DeviceIdType.MESH
EDGE = 16


def seq_peer(index):
    return {"seq": index}


def tp_peer(index):
    return {"tp": index}


def like(shape, dtype=jnp.bfloat16):
    return jax.ShapeDtypeStruct(shape, dtype)


def iota(shape, axis):
    return lax.broadcasted_iota(jnp.int32, shape, axis)


def across_lanes(left, right):
    return lax.dot_general(
        left, right, (((1,), (1,)), ((), ())), preferred_element_type=jnp.float32
    )


def product(left, right):
    return jnp.dot(left, right, preferred_element_type=jnp.float32)


def remote(source, target, send_sem, recv_sem, device):
    return pltpu.make_async_remote_copy(
        src_ref=source,
        dst_ref=target,
        send_sem=send_sem,
        recv_sem=recv_sem,
        device_id=device,
        device_id_type=MESH,
    )


def turn_table(rows):
    frequency = rope_base ** (-2.0 * np.arange(HD // 2, dtype=np.float64) / HD)
    frequency = frequency.astype(np.float32)
    angles = np.arange(rows, dtype=np.float32)[:, None] * frequency[None, :]
    angles = angles.astype(np.float64)
    return np.concatenate([np.cos(angles), np.sin(angles)], axis=1).astype(np.float32)


def whole_layer(
    states, gain, enc_qkv, proj, starts, lift, cross_kv, latent_gain, lat_qkv, lat_proj, table,
    call_id,
):
    count, size = lax.axis_size("tp"), lax.axis_size("seq")
    near = count - 1
    byte_rows, width = states.shape
    total_rows = byte_rows + EDGE
    enc_cols = enc_qkv.shape[2]
    enc_heads = enc_cols // EH
    slots = starts.shape[1]
    columns = lift.shape[1]
    group = 2 * HD
    panel_count = columns // group
    row_total = count * slots
    half = lat_qkv.shape[1]
    full_width = columns * count
    rows_half = byte_rows // 2
    row_spans = ((0, rows_half), (rows_half, rows_half), (byte_rows, EDGE))
    part_rows = slots // 2
    half_total = row_total // 2
    share = enc_cols // 2
    piece = share // count

    def kernel(
        states_hbm, gain_hbm, qkv_hbm, proj_hbm, starts_hbm, lift_hbm, cross_hbm,
        lgain_hbm, w_own_hbm, o_hbm, table_hbm,
        enc_ref, out_ref,
        gain_ref, starts_ref, lgain_ref, states_ref, qkv_ref, query_ref, kv_ref, infos, proj_ref, att_ref, near_ref, blend_ref, table_ref, cos_ref, sin_ref,
        lift_ref, cross_ref, pooled_ref, full_ref, panels, rows_ref, patch_ref,
        w_own, w_other, geared, own_part, qkv_send, qkv_land, sq_send, sq_land,
        kv_own, kv_other, out_quarter, out_rows, tall, parts, land,
        load_sems, info_s, info_r, halo_s, halo_r, edge_s, edge_r, pz_s, pz_r, pp_s, pp_r, pc_s, pc_r,
        w_sems, heads_send, heads_recv,
        panel_send, panel_recv, stay_sems,
        qkv_s, qkv_r, sq_s, sq_r, kv_s, kv_r,
        oq_s, oq_r, oz_s, oz_r, oc_sems, own_sems, tz_s, tz_r, a_s, a_r, enc_sem,
    ):
        s, t = lax.axis_index("seq"), lax.axis_index("tp")
        p, c = s // 2, lax.rem(s, 2)
        partner = seq_peer(s + 1 - 2 * c)

        def plane(index):
            return {"seq": 2 * index + c}

        def ring(k):
            return lax.rem(s + k + size, size)

        def tower(k):
            return lax.rem(t + k + count, count)

        def flip(k):
            if k == 0:
                return p
            if k == 1:
                return p + 1 - 2 * lax.rem(p, 2)
            if k == 2:
                return lax.rem(p + 2, 4)
            return 3 - p

        far_first = (3, 2, 1)
        low = t < 2
        inner = (t == 1) | (t == 2)
        first_from = jnp.where(low, t + 1, t - 1)
        second_from = jnp.where(low, t + 2, t - 2)
        third_from = jnp.where(lax.rem(t, 2) == 0, count - 1, 0)
        outer = jnp.where(low, 0, count - 1)

        def to_near(copy_to):
            copy_to(first_from, 0).start()

            @pl.when(inner)
            def _():
                copy_to(outer, 1).start()

        def sent_near(copy_to, over):
            copy_to(first_from, 0).wait_send()

            @pl.when(inner)
            def _():
                copy_to(outer, 1).wait_send()
                for i in range(3):
                    over(i).wait_send()

        barrier = pltpu.get_barrier_semaphore()
        for k in range(1, size):
            pl.semaphore_signal(barrier, inc=1, device_id=seq_peer(ring(k)), device_id_type=MESH)
        for k in range(1, count):
            pl.semaphore_signal(barrier, inc=1, device_id=tp_peer(tower(k)), device_id_type=MESH)

        @pl.when(p != t)
        def _():
            for k in far_first:
                away_peer = {"seq": 2 * flip(k) + c, "tp": p}
                pl.semaphore_signal(barrier, inc=1, device_id=away_peer, device_id_type=MESH)

        own_rows = pl.ds(pl.multiple_of(p * HD, HD), HD)
        load_plan = (
            (states_hbm, states_ref.at[pl.ds(0, byte_rows)]),
            (qkv_hbm, qkv_ref),
            (table_hbm, table_ref),
            (proj_hbm.at[pl.ds(0, share)], proj_ref.at[0, 0]),
            (proj_hbm.at[pl.ds(share, share)], proj_ref.at[1, 0]),
            (lift_hbm, lift_ref),
            (cross_hbm, cross_ref),
            (w_own_hbm, w_own),
            (o_hbm.at[own_rows], out_quarter.at[p]),
            (gain_hbm, gain_ref),
            (starts_hbm, starts_ref),
            (lgain_hbm, lgain_ref),
        )
        loads = [
            pltpu.make_async_copy(source, target, load_sems.at[i])
            for i, (source, target) in enumerate(load_plan)
        ]
        for i in (0, 9, 1, 10, 2, 3, 4, 5, 6, 7, 8, 11):
            loads[i].start()
        sent = []

        def launch(copy):
            copy.start()
            sent.append(copy)
            return copy
        loads[0].wait()
        loads[9].wait()
        values = states_ref[0:byte_rows].astype(jnp.float32)
        chip_row = gain_ref[...].astype(jnp.float32).reshape(1, width)
        normed = rms_scale(values, chip_row).astype(jnp.bfloat16)
        own = pl.ds(WIN, byte_rows)
        loads[1].wait()
        for i in range(2):
            fresh = product(normed, qkv_ref[i + 1]).astype(jnp.bfloat16)
            for h in range(2):
                kv_ref[h, i, own] = fresh[:, h * share : (h + 1) * share]
        query_ref[0:byte_rows] = (
            product(normed, qkv_ref[0]) * (1.0 / math.sqrt(EH))
        ).astype(jnp.bfloat16)
        loads[10].wait()
        listed = jnp.where(starts_ref[...] < size * byte_rows, 1, 0)
        my_count = jnp.sum(listed, axis=1, keepdims=True)
        info_lane = iota((8, 128), 1)
        infos[s] = jnp.where(
            info_lane == 0, my_count, jnp.where(info_lane == 1, starts_ref[0:1, 0:1], 0)
        )
        greetings = size - 1 + count - 1

        @pl.when(p == t)
        def _():
            pl.semaphore_wait(barrier, greetings)

        @pl.when(p != t)
        def _():
            pl.semaphore_wait(barrier, greetings + count - 1)

        mine_at = pl.multiple_of(p * piece, piece)
        lifts = [
            launch(
                remote(
                    proj_hbm.at[pl.ds(pl.multiple_of(c * share + p * piece, piece), piece)],
                    proj_ref.at[c, k, pl.ds(mine_at, piece)],
                    pz_s.at[k - 1],
                    pz_r.at[k - 1],
                    tp_peer(tower(k)),
                )
            )
            for k in range(1, count)
        ]
        notes = [
            launch(
                remote(infos.at[s], infos.at[s], info_s.at[k - 1], info_r.at[k - 1], seq_peer(ring(k)))
            )
            for k in range(1, size)
        ]
        behind = seq_peer(ring(-1))
        edges = [
            launch(remote(source, target, edge_s.at[i], edge_r.at[i], behind))
            for i, (source, target) in enumerate(
                (
                    (
                        kv_ref.at[:, :, pl.ds(WIN, EDGE)],
                        kv_ref.at[:, :, pl.ds(WIN + byte_rows, EDGE)],
                    ),
                    (query_ref.at[pl.ds(0, EDGE)], query_ref.at[pl.ds(byte_rows, EDGE)]),
                    (states_ref.at[pl.ds(0, EDGE)], states_ref.at[pl.ds(byte_rows, EDGE)]),
                )
            )
        ]
        halos = [
            launch(
                remote(
                    kv_ref.at[h, :, own],
                    kv_ref.at[h, :, pl.ds(0, byte_rows)],
                    halo_s.at[0, h],
                    halo_r.at[0, h],
                    seq_peer(ring(2)),
                )
            )
            for h in range(2)
        ]
        def beside(i):
            first = pl.multiple_of(jnp.where(c == 0, WIN, 0), byte_rows)
            return remote(
                kv_ref.at[i, :, pl.ds(first, byte_rows)],
                kv_ref.at[i, :, pl.ds(byte_rows, byte_rows)],
                halo_s.at[1, i],
                halo_r.at[1, i],
                partner,
            )

        @pl.when(c == 0)
        def _():
            for i in range(2):
                beside(i).start()
        for copy in notes:
            copy.wait_recv()
        counted = [infos[m][0:1, 0:1] for m in range(size)]
        offsets = [jnp.zeros((1, 1), jnp.int32)]
        for m in range(size - 1):
            offsets.append(offsets[m] + counted[m])
        next_first = jnp.where(
            s + 1 < size, infos[jnp.minimum(s + 1, size - 1)][0:1, 1:2], size * byte_rows
        )
        square = (slots, slots)
        start_row = jnp.broadcast_to(starts_ref[...], square)
        apart = iota(square, 1) - iota(square, 0)
        first_byte = jnp.sum(jnp.where(apart == 0, start_row, 0), axis=1, keepdims=True)
        following = jnp.sum(jnp.where(apart == 1, start_row, 0), axis=1, keepdims=True)
        slot_at = iota((slots, 1), 0)
        in_use = slot_at < my_count
        patch_end = jnp.where(slot_at + 1 < my_count, following, next_first)
        anchor = s * byte_rows
        lower = jnp.where(in_use, first_byte - anchor, 0)
        upper = jnp.where(in_use, patch_end - anchor, 1)
        where_at = iota((slots, total_rows), 1)
        allowed = (where_at >= lower) & (where_at < upper)
        member = jnp.where(allowed & in_use, 1.0, 0.0)
        lengths = jnp.maximum(jnp.sum(member, axis=1, keepdims=True), 1.0)
        member = member.astype(jnp.bfloat16)
        bias = jnp.where(allowed, 0.0, -1e30)
        for begin, rows in row_spans:
            reach_rows = rows + WIN
            behind_by = iota((rows, reach_rows), 0) - iota((rows, reach_rows), 1) + WIN
            known = iota((rows, reach_rows), 1) >= WIN - begin - s * byte_rows
            near_by = (behind_by >= 0) & (behind_by < WIN) & known
            near_ref[begin : begin + rows, 0:reach_rows] = jnp.where(near_by, 0.0, -1e30)
        chosen = [
            (
                jnp.where(c == 0, offsets[2 * i], offsets[2 * i + 1]),
                jnp.where(c == 0, counted[2 * i], counted[2 * i + 1]),
                jnp.where(c == 0, offsets[2 * i + 1], offsets[2 * i]),
                jnp.where(c == 0, counted[2 * i + 1], counted[2 * i]),
            )
            for i in range(count)
        ]

        def laid(shape, axis, which):
            at = iota(shape, axis)
            band = at // half_total
            within = at - band * half_total
            block = within // part_rows
            result = jnp.broadcast_to(chosen[0][which], shape)
            for i in range(1, count):
                result = jnp.where(block == i, chosen[i][which], result)
            return band * part_rows + within - block * part_rows, result

        row_slot, row_offset = laid((row_total, 1), 0, 0)
        position = row_offset + row_slot
        key_positions = []
        for which in (0, 2):
            key_slot, key_offset = laid((1, row_total), 1, which)
            _, key_count = laid((1, row_total), 1, which + 1)
            key_positions.append(
                jnp.where(key_slot < key_count, key_offset + key_slot, far_position)
            )
        loads[2].wait()
        table_rows = table_ref.shape[0]
        picked = jnp.where(iota((row_total, table_rows), 1) == position, 1.0, 0.0)
        turns = lax.dot_general(
            picked,
            table_ref[...],
            (((1,), (0,)), ((), ())),
            precision=lax.Precision.HIGHEST,
            preferred_element_type=jnp.float32,
        )
        swapped = pltpu.roll(turns, HD // 2, 1)
        low_lanes = iota((row_total, HD), 1) < HD // 2
        cos_ref[...] = jnp.where(low_lanes, turns, swapped)
        sin_ref[...] = jnp.where(low_lanes, -swapped, turns)
        def halo_arrives(h):
            halos[h].wait_recv()

            @pl.when(c == 1)
            def _():
                beside(h).start()

        halo_arrives(0)
        for copy in lifts:
            copy.wait_recv()
        spread = [
            launch(
                remote(
                    proj_ref.at[c, pl.ds(1, near), pl.ds(mine_at, piece)],
                    proj_ref.at[c, pl.ds(1, near), pl.ds(mine_at, piece)],
                    pp_s.at[k - 1],
                    pp_r.at[k - 1],
                    plane(flip(k)),
                )
            )
            for k in far_first
        ]
        def shared(k):
            rows = pl.ds(pl.multiple_of(flip(k) * piece, piece), piece)
            return remote(
                proj_ref.at[c, pl.ds(1, near), rows],
                proj_ref.at[c, pl.ds(1, near), rows],
                pc_s.at[k],
                pc_r.at[k],
                partner,
            )

        launch(shared(0))
        for copy in edges:
            copy.wait_recv()

        beside(0).wait_recv()
        def share_heads(origin, h, target, sem):
            return remote(
                att_ref.at[origin, h],
                att_ref.at[origin, h],
                heads_send.at[h, sem],
                heads_recv.at[h, origin],
                tp_peer(target),
            )

        def attend(pair, begin, rows):
            reach_rows = rows + WIN
            keys = kv_ref[pair, 0, begin : begin + reach_rows]
            seen_values = kv_ref[pair, 1, begin : begin + reach_rows]
            queries = query_ref[begin : begin + rows, pair * share : (pair + 1) * share]
            head_of = iota((rows, share), 1) // EH
            stacked = jnp.concatenate(
                [jnp.where(head_of == h, queries, jnp.zeros_like(queries)) for h in range(share // EH)],
                axis=0,
            )
            near_bias = near_ref[begin : begin + rows, 0:reach_rows]
            scores = across_lanes(stacked, keys)
            raised, sums = [], []
            for h in range(share // EH):
                here = scores[h * rows : (h + 1) * rows] + near_bias
                here = jnp.exp(here - jnp.max(here, axis=1, keepdims=True))
                sums.append(jnp.sum(here, axis=1, keepdims=True))
                raised.append(here.astype(jnp.bfloat16))
            seen = product(jnp.concatenate(raised, axis=0), seen_values)
            attended = jnp.zeros((rows, share), jnp.float32)
            for h in range(share // EH):
                attended = jnp.where(
                    head_of == h, seen[h * rows : (h + 1) * rows] / sums[h], attended
                )
            att_ref[t, pair, begin : begin + rows] = attended.astype(jnp.bfloat16)

        for h in range(2):
            if h:
                halo_arrives(1)
                beside(1).wait_recv()
            for begin, rows in row_spans:
                attend(h, begin, rows)
            to_near(lambda target, sem: share_heads(t, h, target, sem))

        swaps = [launch(remote(w_own_hbm, w_other, w_sems.at[0], w_sems.at[1], partner))]
        sources = (first_from, second_from, third_from)
        beyond = (outer, outer, first_from)

        def hand_over(which, h):
            return share_heads(sources[which], h, beyond[which], 2 + which)

        def gain_heads(which, h):
            hand_over(which, h).wait_recv()

            @pl.when(inner)
            def _():
                hand_over(which, h).start()

        def blended(h):
            attended = jnp.concatenate([att_ref[tower(-k), h] for k in range(count)], axis=1)
            return product(attended, proj_ref[h].reshape(count * share, width))
        gain_heads(0, 0)

        @pl.when(inner)
        def _():
            gain_heads(2, 0)

        gain_heads(0, 1)

        @pl.when(inner)
        def _():
            gain_heads(2, 1)
        gain_heads(1, 0)

        @pl.when(jnp.logical_not(inner))
        def _():
            gain_heads(2, 0)
        for k, copy in zip(far_first[::-1], spread[::-1]):
            copy.wait_recv()
            launch(shared(k))
        quarters = [
            launch(
                remote(
                    o_hbm.at[pl.ds(pl.multiple_of(flip(k) * HD, HD), HD)],
                    out_quarter.at[p],
                    oq_s.at[k - 1],
                    oq_r.at[k - 1],
                    plane(flip(k)),
                )
            )
            for k in far_first
        ]
        loads[3].wait()
        loads[4].wait()
        gain_heads(1, 1)

        @pl.when(jnp.logical_not(inner))
        def _():
            gain_heads(2, 1)
        blend_ref[...] = states_ref[...].astype(jnp.float32) + blended(c)
        for k in range(count):
            shared(k).wait_recv()
        full_ref[...] = (blend_ref[...] + blended(1 - c)).astype(jnp.bfloat16)
        enc_out = pltpu.make_async_copy(full_ref.at[pl.ds(0, byte_rows)], enc_ref, enc_sem.at[0])
        enc_out.start()

        totals = product(member, full_ref[...])
        pooled_ref[...] = (totals / lengths).astype(jnp.bfloat16)
        loads[5].wait()
        loads[6].wait()

        half_lanes = columns // 2

        def window(r, i):
            if r == 0:
                return pl.ds(pl.multiple_of(i * group, group), group)
            return pl.ds(i * half_lanes, half_lanes)

        def slot_of(r, i):
            return i if r == 0 else panel_count + i

        def away(k, r, i):
            return remote(
                panels.at[r, :, window(r, i)],
                rows_ref.at[r, p, :, window(r, i)],
                panel_send.at[k, slot_of(r, i)],
                panel_recv.at[p, slot_of(r, i)],
                {"seq": 2 * t + c, "tp": tower(k)},
            )

        def stay(r, i):
            return pltpu.make_async_copy(
                panels.at[r, :, window(r, i)],
                rows_ref.at[r, p, :, window(r, i)],
                stay_sems.at[slot_of(r, i)],
            )

        def ship(r, i):
            for k in (2, 1, 3):
                away(k, r, i).start()

            @pl.when(p != t)
            def _():
                away(0, r, i).start()

            @pl.when(p == t)
            def _():
                stay(r, i).start()

        widths = (panel_count, 2)

        def heads(i, carry):
            cols = pl.ds(pl.multiple_of(i * group, group), group)
            rows = full_ref[...]
            lifted = product(pooled_ref[...], lift_ref[:, cols])
            keys = product(rows, cross_ref[0, :, cols]).astype(jnp.bfloat16)
            seen_values = product(rows, cross_ref[1, :, cols]).astype(jnp.bfloat16)
            queries = lifted.astype(jnp.bfloat16)
            crossed = []
            for j in range(2):
                lanes = slice(j * HD, (j + 1) * HD)
                scores = across_lanes(queries[:, lanes], keys[:, lanes])
                scores = scores * (1.0 / math.sqrt(HD)) + bias
                raised = jnp.exp(scores - jnp.max(scores, axis=1, keepdims=True))
                crossed.append(
                    product(raised.astype(jnp.bfloat16), seen_values[:, lanes])
                    / jnp.sum(raised, axis=1, keepdims=True)
                )
            patch = lifted + jnp.concatenate(crossed, axis=1)
            panel = jnp.where(in_use, patch, 0.0).astype(jnp.bfloat16)
            patch_ref[:, cols] = panel
            for r in range(2):
                panels[r, :, cols] = panel[r * part_rows : (r + 1) * part_rows]
            ship(0, i)
            return carry
        lax.fori_loop(0, panel_count, heads, 0)
        for i in range(widths[1]):
            ship(1, i)
        for copy in quarters:
            copy.wait_recv()
        loads[8].wait()
        mine_out = pltpu.make_async_copy(
            out_quarter.at[t], out_rows.at[c, t], own_sems.at[0]
        )
        mine_out.start()
        ups = [
            remote(
                out_quarter.at[tower(k)],
                out_rows.at[c, t],
                oz_s.at[k - 1],
                oz_r.at[k - 1],
                tp_peer(tower(k)),
            )
            for k in range(1, count)
        ]

        @pl.when(inner)
        def _():
            for copy in ups:
                copy.start()

        @pl.when(t == 0)
        def _():
            ups[0].start()

        @pl.when(t == count - 1)
        def _():
            ups[2].start()

        arriving, flats = ([], []), []
        eye = iota((half_total, half_total), 0) == iota((half_total, half_total), 1)
        loads[11].wait()
        chip_gain = lgain_ref[pl.ds(pl.multiple_of(p * columns, columns), columns)]
        chip_gain = chip_gain.astype(jnp.float32).reshape(1, columns)
        for r in range(2):
            for q in range(count):

                @pl.when((p != q) | (p != t))
                def _():
                    for i in range(widths[r]):
                        remote(
                            panels.at[r, :, window(r, i)],
                            rows_ref.at[r, q, :, window(r, i)],
                            panel_send.at[0, slot_of(r, i)],
                            panel_recv.at[q, slot_of(r, i)],
                            plane(p),
                        ).wait_recv()

            @pl.when(p == t)
            def _():
                for i in range(widths[r]):
                    stay(r, i).wait()

            if r:

                @pl.when(t == 0)
                def _():
                    ups[2].start()
                    ups[1].start()

                @pl.when(t == count - 1)
                def _():
                    ups[0].start()
                    ups[1].start()
            values = rows_ref[r].reshape(half_total, columns).astype(jnp.float32)
            squares = jnp.sum(values * values, axis=1, keepdims=True)
            flat = jnp.sum(jnp.where(eye, squares, 0.0), axis=0, keepdims=True)
            flats.append(flat)
            sq_send[r] = jnp.broadcast_to(flat, (8, half_total))
            geared[...] = (values * chip_gain).astype(jnp.bfloat16)
            for k in far_first:
                arriving[r].append(
                    launch(
                        remote(
                            sq_send.at[r],
                            sq_land.at[r, k - 1],
                            sq_s.at[r, k - 1],
                            sq_r.at[r, k - 1],
                            plane(flip(k)),
                        )
                    )
                )
            if r == 0:
                loads[7].wait()
                swaps[0].wait_recv()
            mine = geared[:, pl.ds(pl.multiple_of(c * half, half), half)]
            theirs = geared[:, pl.ds(pl.multiple_of((1 - c) * half, half), half)]
            for k in far_first + (0,):
                target = flip(k)
                lanes = pl.ds(pl.multiple_of(target * HD, HD), HD)
                for i in range(3):
                    part = product(mine, w_own[i, :, lanes]) + product(theirs, w_other[i, :, lanes])
                    if k:
                        qkv_send[r, k - 1, i] = part.astype(jnp.bfloat16)
                    else:
                        own_part[r, i] = part
                if k:
                    arriving[r].append(
                        launch(
                            remote(
                                qkv_send.at[r, k - 1],
                                qkv_land.at[r, k - 1],
                                qkv_s.at[r, k - 1],
                                qkv_r.at[r, k - 1],
                                plane(target),
                            )
                        )
                    )

        sent.extend(ups)

        def turned(vectors, rows):
            return (
                vectors * cos_ref[rows] + pltpu.roll(vectors, HD // 2, 1) * sin_ref[rows]
            ).astype(jnp.bfloat16)

        swaps_kv, queries = [], []
        for r in range(2):
            for copy in arriving[r]:
                copy.wait_recv()
            flat = flats[r] + jnp.sum(sq_land[r, :, 0:1, :], axis=0)
            square_sum = jnp.sum(jnp.where(eye, flat, 0.0), axis=1, keepdims=True)
            scale = lax.rsqrt(square_sum / full_width + epsilon)
            total = []
            for i in range(3):
                band = own_part[r, i]
                for k in range(count - 1):
                    band = band + qkv_land[r, k, i].astype(jnp.float32)
                total.append(band * scale)
            rows = slice(r * half_total, (r + 1) * half_total)
            kv_own[r, 0] = turned(total[1], rows)
            kv_own[r, 1] = total[2].astype(jnp.bfloat16)
            swaps_kv.append(
                launch(remote(kv_own.at[r], kv_other.at[r], kv_s.at[r], kv_r.at[r], partner))
            )
            queries.append(turned(total[0], rows))
        queries = jnp.concatenate(queries, axis=0)

        def both(ref, i):
            return jnp.concatenate([ref[0, i], ref[1, i]], axis=0)
        def scored(keys, key_position):
            scores = across_lanes(queries, keys) * (1.0 / math.sqrt(HD))
            return jnp.where(key_position <= position, scores, -1e30)

        scores_a = scored(both(kv_own, 0), key_positions[0])
        for copy in swaps_kv:
            copy.wait_recv()
        scores_b = scored(both(kv_other, 0), key_positions[1])
        largest = jnp.maximum(
            jnp.max(scores_a, axis=1, keepdims=True), jnp.max(scores_b, axis=1, keepdims=True)
        )
        raised_a = jnp.exp(scores_a - largest)
        raised_b = jnp.exp(scores_b - largest)
        weight_sum = jnp.sum(raised_a, axis=1, keepdims=True) + jnp.sum(
            raised_b, axis=1, keepdims=True
        )
        weighted = product(raised_a.astype(jnp.bfloat16), both(kv_own, 1)) + product(
            raised_b.astype(jnp.bfloat16), both(kv_other, 1)
        )
        tall[t] = (weighted / weight_sum).astype(jnp.bfloat16).reshape(2, half_total, HD)
        risen = {}
        for k in far_first + (0,):
            take = pl.ds(pl.multiple_of(flip(k) * part_rows, part_rows), part_rows)
            for d in range(count - 1, 0, -1):
                risen[k, d] = launch(
                    remote(
                        tall.at[t, :, take],
                        tall.at[t, :, take],
                        tz_s.at[k, d - 1],
                        tz_r.at[k, d - 1],
                        tp_peer(tower(d)),
                    )
                )
        for copy in ups:
            copy.wait_recv()
        mine_out.wait()
        halves = launch(
            remote(out_rows.at[c], out_rows.at[c], oc_sems.at[0], oc_sems.at[1], partner)
        )
        halves.wait_recv()
        hops, parts_own = [], []
        summed = patch_ref[...].astype(jnp.float32)
        for k in far_first + (0,):
            for d in range(1, count):
                take = pl.ds(pl.multiple_of(flip(k) * part_rows, part_rows), part_rows)
                remote(
                    tall.at[tower(-d), :, take],
                    tall.at[tower(-d), :, take],
                    tz_s.at[k, d - 1],
                    tz_r.at[k, d - 1],
                    tp_peer(tower(-d)),
                ).wait_recv()
            take = pl.ds(pl.multiple_of(flip(k) * part_rows, part_rows), part_rows)
            attended = jnp.concatenate(
                [tall[q, :, take].reshape(slots, HD) for q in range(count)], axis=1
            )
            for core in range(2):
                lanes = slice(core * half, (core + 1) * half)
                part = product(attended, out_rows[core].reshape(count * HD, half))
                if k:
                    parts[k - 1, :, lanes] = part.astype(jnp.bfloat16)
                else:
                    parts_own.append(part)
            if k:
                hops.append(
                    launch(
                        remote(
                            parts.at[k - 1],
                            land.at[k - 1],
                            a_s.at[k - 1],
                            a_r.at[k - 1],
                            plane(flip(k)),
                        )
                    )
                )
        summed = summed + jnp.concatenate(parts_own, axis=1)
        for copy in hops:
            copy.wait_recv()
        for k in range(count - 1):
            summed = summed + land[k].astype(jnp.float32)
        out_ref[...] = jnp.where(in_use, summed, 0.0).astype(jnp.bfloat16)
        enc_out.wait()
        for copy in sent:
            copy.wait_send()
        for i in range(2):
            beside(i).wait_send()
        for h in range(2):
            sent_near(
                lambda target, sem: share_heads(t, h, target, sem), lambda which: hand_over(which, h)
            )

        for r in range(2):
            for i in range(widths[r]):
                for k in range(1, count):
                    away(k, r, i).wait_send()

                @pl.when(p != t)
                def _():
                    away(0, r, i).wait_send()
    hbm = pl.BlockSpec(memory_space=pl.ANY)
    vmem = pl.BlockSpec(memory_space=pltpu.VMEM)
    dma = pltpu.SemaphoreType.DMA

    def buffer(*shape, dtype=jnp.bfloat16):
        return pltpu.VMEM(shape, dtype)

    return pl.pallas_call(
        kernel,
        out_shape=[like((byte_rows, width)), like((slots, columns))],
        in_specs=[hbm] * 11,
        out_specs=[vmem, vmem],
        scratch_shapes=[
            buffer(width),
            buffer(1, slots, dtype=jnp.int32),
            buffer(full_width),
            buffer(total_rows, width),
            buffer(*enc_qkv.shape),
            buffer(total_rows, enc_cols),
            buffer(2, 2, WIN + total_rows, share),
            buffer(size, 8, 128, dtype=jnp.int32),
            buffer(2, count, share, width),
            buffer(count, 2, total_rows, share),
            buffer(total_rows, rows_half + WIN, dtype=jnp.float32),
            buffer(total_rows, width, dtype=jnp.float32),
            buffer(*table.shape, dtype=jnp.float32),
            buffer(row_total, HD, dtype=jnp.float32),
            buffer(row_total, HD, dtype=jnp.float32),
            buffer(*lift.shape),
            buffer(*cross_kv.shape),
            buffer(slots, width),
            buffer(total_rows, width),
            buffer(2, part_rows, columns),
            buffer(2, count, part_rows, columns),
            buffer(slots, columns),
            buffer(*lat_qkv.shape),
            buffer(*lat_qkv.shape),
            buffer(half_total, columns),
            buffer(2, 3, half_total, HD, dtype=jnp.float32),
            buffer(2, near, 3, half_total, HD),
            buffer(2, near, 3, half_total, HD),
            buffer(2, 8, half_total, dtype=jnp.float32),
            buffer(2, near, 8, half_total, dtype=jnp.float32),
            buffer(2, 2, half_total, HD),
            buffer(2, 2, half_total, HD),
            buffer(count, HD, half),
            buffer(2, count, HD, half),
            buffer(count, 2, half_total, HD),
            buffer(near, slots, columns),
            buffer(near, slots, columns),
            dma((12,)),
            dma((size - 1,)),
            dma((size - 1,)),
            dma((2, 2)),
            dma((2, 2)),
            dma((3,)),
            dma((3,)),
            dma((near,)),
            dma((near,)),
            dma((near,)),
            dma((near,)),
            dma((count,)),
            dma((count,)),
            dma((2,)),
            dma((2, 5)),
            dma((2, count)),
            dma((count, panel_count + 2)),
            dma((count, panel_count + 2)),
            dma((panel_count + 2,)),
            dma((2, near)),
            dma((2, near)),
            dma((2, near)),
            dma((2, near)),
            dma((2,)),
            dma((2,)),
            dma((near,)),
            dma((near,)),
            dma((near,)),
            dma((near,)),
            dma((2,)),
            dma((1,)),
            dma((count, near)),
            dma((count, near)),
            dma((near,)),
            dma((near,)),
            dma((1,)),
        ],
        compiler_params=pltpu.CompilerParams(
            collective_id=call_id, has_side_effects=True, vmem_limit_bytes=52428800
        ),
    )(
        states, gain, enc_qkv, proj, starts, lift, cross_kv, latent_gain, lat_qkv, lat_proj, table,
    )


def settle(*arrays):
    total = len(arrays)

    def kernel(*refs):
        ins, outs, sems = refs[:total], refs[total : 2 * total], refs[2 * total]
        puts = [pltpu.make_async_copy(ins[i], outs[i], sems.at[i]) for i in range(total)]
        for put in puts:
            put.start()
        for put in puts:
            put.wait()

    return pl.pallas_call(
        kernel,
        out_shape=[like(value.shape, value.dtype) for value in arrays],
        in_specs=[pl.BlockSpec(memory_space=pl.ANY)] * total,
        out_specs=[pl.BlockSpec(memory_space=pltpu.HBM)] * total,
        scratch_shapes=[pltpu.SemaphoreType.DMA((total,))],
        compiler_params=pltpu.CompilerParams(vmem_limit_bytes=2**20),
    )(*arrays)


def fused_shards(
    byte_states,
    enc_gain,
    enc_qkv,
    enc_proj_out,
    starts,
    counts,
    lift,
    cross_kv,
    latent_gain,
    lat_qkv,
    lat_proj_out,
):
    table = jnp.asarray(turn_table(lax.axis_size("seq") * starts.shape[1]))
    operands = [
        pltpu.with_memory_space_constraint(value, pltpu.HBM)
        for value in (
            byte_states,
            enc_gain,
            enc_qkv,
            enc_proj_out,
            starts,
            lift,
            cross_kv,
            latent_gain,
            lat_qkv,
            lat_proj_out,
            table,
        )
    ]
    encoded, latent = whole_layer(*operands, 1)
    return settle(encoded, latent)


def fits_pairs(mesh, byte_states, enc_qkv, starts, lat_qkv):
    size, tp_size = mesh.shape["seq"], mesh.shape["tp"]
    byte_rows = byte_states.shape[0] // size
    return (
        size == 2 * tp_size
        and tp_size == 4
        and WIN % byte_rows == 0
        and WIN == 2 * byte_rows
        and byte_rows % (32 * tp_size) == 0
        and lat_qkv.shape[2] // tp_size == HD * tp_size
        and lat_qkv.shape[1] % (128 * size) == 0
        and starts.shape[1] * tp_size % 128 == 0
        and starts.shape[1] * tp_size <= 1024
        and starts.shape[1] % 16 == 0
        and enc_qkv.shape[2] % (128 * tp_size) == 0
    )


def solution(mesh):
    specs = dict(
        mesh=mesh,
        in_specs=(
            P("seq", None),
            P(),
            P(None, None, "tp"),
            P("tp", None),
            P("seq", None),
            P("seq"),
            P(None, "tp"),
            P(None, None, "tp"),
            P(),
            P(None, "seq", "tp"),
            P("tp", "seq"),
        ),
        out_specs=(P("seq", None), P("seq", "tp")),
        check_vma=False,
    )

    def run(*arrays):
        paired = fits_pairs(mesh, arrays[0], arrays[2], arrays[4], arrays[9])
        return jax.shard_map(fused_shards if paired else gathered_shards, **specs)(*arrays)

    return run
```

```python
import math

import jax
import numpy as np
import jax.numpy as jnp
from jax import lax
from jax.experimental import pallas as pl
from jax.experimental.pallas import tpu as pltpu
from jax.sharding import PartitionSpec as P

EH = 64
HD = 128
WIN = 512
SPILL = 8


epsilon = 1e-05
rope_base = 500000.0
far_position = 1 << 30


def from_behind(value, axis, steps):
    count = lax.axis_size(axis)
    leading, last = (max(0, -steps), min(count, count - steps))
    return lax.ppermute(value, axis, [(source, source + steps) for source in range(leading, last)])


def prefix(value, axis, join, neutral):
    count, mine = (lax.axis_size(axis), lax.axis_index(axis))
    pieces = lax.all_gather(value, axis)
    subtotal = jnp.full_like(value, 0) + jnp.asarray(neutral, value.dtype)

    def hop(position, subtotal):
        longer = join(subtotal, pieces[position])
        return jnp.where(position < mine, longer, subtotal)

    return lax.fori_loop(0, count - 1, hop, subtotal)


def shortened(value):

    def short(part):
        return part.astype(jnp.bfloat16) if part.dtype == jnp.float32 else part

    return jax.tree.map(short, value)


def rms_scale(values, gain_row):
    mean_square = jnp.mean(values * values, axis=-1, keepdims=True)
    return values * lax.rsqrt(mean_square + epsilon) * gain_row


def masked_softmax(scores, allowed):
    scores = jnp.where(allowed, scores, -1e30)
    largest = jnp.max(scores, axis=-1, keepdims=True)
    raised = jnp.where(allowed, jnp.exp(scores - largest), 0.0)
    return raised / jnp.sum(raised, axis=-1, keepdims=True)


def rotate(values, position):
    halfway = values.shape[-1] // 2
    frequency = jnp.power(
        rope_base, -2.0 * jnp.arange(halfway, dtype=jnp.float32) / values.shape[-1]
    )
    angles = position.astype(jnp.float32)[:, None] * frequency[None, :]
    cosine = jnp.cos(angles)[:, None, :]
    sine_rows = jnp.sin(angles)[:, None, :]
    lower_half = values[..., :halfway]
    upper_half = values[..., halfway:]
    return jnp.concatenate(
        [
            lower_half * cosine - upper_half * sine_rows,
            upper_half * cosine + lower_half * sine_rows,
        ],
        axis=-1,
    )


def patch_block(extended, first_byte, end_byte, in_use, anchor, lift, cross_kv):
    columns = anchor + jnp.arange(extended.shape[0], dtype=jnp.int32)
    inside = (
        (columns[None, :] >= first_byte[:, None])
        & (columns[None, :] < end_byte[:, None])
        & in_use[:, None]
    )
    member = inside.astype(jnp.bfloat16)
    totals = jnp.dot(member, extended, preferred_element_type=jnp.float32)
    lengths = jnp.maximum(jnp.sum(inside.astype(jnp.float32), axis=1), 1.0)
    pooled = (totals / lengths[:, None]).astype(jnp.bfloat16)
    lifted = jnp.dot(pooled, lift, preferred_element_type=jnp.float32)
    key_rows = jnp.dot(extended, cross_kv[0], preferred_element_type=jnp.float32).astype(
        jnp.bfloat16
    )
    value_rows = jnp.dot(extended, cross_kv[1], preferred_element_type=jnp.float32).astype(
        jnp.bfloat16
    )
    slot_total = first_byte.shape[0]
    head_count = lifted.shape[1] // HD
    queries = lifted.astype(jnp.bfloat16).reshape(slot_total, head_count, HD)
    scores = jnp.einsum(
        "phd,khd->hpk",
        queries,
        key_rows.reshape(-1, head_count, HD),
        preferred_element_type=jnp.float32,
    ) * (1.0 / math.sqrt(HD))
    allowed = inside | (~in_use)[:, None] & (columns[None, :] == anchor)
    weights = masked_softmax(scores, allowed[None]).astype(jnp.bfloat16)
    crossed = jnp.einsum(
        "hpk,khd->phd",
        weights,
        value_rows.reshape(-1, head_count, HD),
        preferred_element_type=jnp.float32,
    )
    crossed = crossed.reshape(slot_total, head_count * HD)
    return jnp.where(in_use[:, None], lifted + crossed, 0.0).astype(jnp.bfloat16)


def add_counts(earlier, later):
    return earlier + later


def gathered_shards(
    byte_states,
    enc_gain,
    enc_qkv,
    enc_proj_out,
    starts,
    counts,
    lift,
    cross_kv,
    latent_gain,
    lat_qkv,
    lat_proj_out,
):
    byte_rows = byte_states.shape[0]
    anchor = lax.axis_index("seq") * byte_rows
    states = byte_states.astype(jnp.float32)
    normed = rms_scale(states, enc_gain.astype(jnp.float32)).astype(jnp.bfloat16)
    projected = jnp.einsum(
        "bd,idc->ibc", normed, enc_qkv, preferred_element_type=jnp.float32
    ).astype(jnp.bfloat16)
    reach_blocks = max(WIN // byte_rows, 1)
    tail_rows = min(WIN, byte_rows)
    key_parts = []
    value_parts = []
    for distance in range(reach_blocks, 0, -1):
        moved_keys, moved_values = from_behind(
            (projected[1, byte_rows - tail_rows :], projected[2, byte_rows - tail_rows :]),
            "seq",
            distance,
        )
        key_parts.append(moved_keys)
        value_parts.append(moved_values)
    key_rows = jnp.concatenate(key_parts + [projected[1]], axis=0)
    value_rows = jnp.concatenate(value_parts + [projected[2]], axis=0)
    head_count = projected.shape[2] // EH
    scores = jnp.einsum(
        "qhd,khd->hqk",
        projected[0].reshape(byte_rows, head_count, EH),
        key_rows.reshape(-1, head_count, EH),
        preferred_element_type=jnp.float32,
    ) * (1.0 / math.sqrt(EH))
    query_pos = anchor + jnp.arange(byte_rows, dtype=jnp.int32)
    key_pos = anchor - WIN + jnp.arange(WIN + byte_rows, dtype=jnp.int32)
    allowed = (
        (key_pos[None, :] <= query_pos[:, None])
        & (key_pos[None, :] > query_pos[:, None] - WIN)
        & (key_pos[None, :] >= 0)
    )
    weights = masked_softmax(scores, allowed[None]).astype(jnp.bfloat16)
    attended = jnp.einsum(
        "hqk,khd->qhd",
        weights,
        value_rows.reshape(-1, head_count, EH),
        preferred_element_type=jnp.float32,
    )
    attended = attended.reshape(byte_rows, head_count * EH).astype(jnp.bfloat16)
    blended = lax.psum(jnp.dot(attended, enc_proj_out, preferred_element_type=jnp.float32), "tp")
    encoded = (states + blended).astype(jnp.bfloat16)
    patch_count = counts[0]
    local_starts = starts[0]
    first_local = (local_starts[0:1] - anchor).astype(jnp.bfloat16)
    next_rows, next_first = from_behind((encoded[:SPILL], first_local), "seq", -1)
    next_first = next_first.astype(jnp.int32)[0]
    extended = jnp.concatenate([encoded, next_rows], axis=0)
    slot_ids = jnp.arange(local_starts.shape[0], dtype=jnp.int32)
    in_use = slot_ids < patch_count
    following = jnp.concatenate([local_starts[1:], jnp.zeros((1,), jnp.int32)])
    patch_end = jnp.where(slot_ids + 1 < patch_count, following, anchor + byte_rows + next_first)
    patches = patch_block(extended, local_starts, patch_end, in_use, anchor, lift, cross_kv)
    offset = prefix(counts, "seq", add_counts, jnp.zeros((1,), jnp.int32))[0]
    position = offset + slot_ids
    slot_total = patches.shape[0]
    full_rows = lax.all_gather(patches, "tp", axis=1, tiled=True)
    normed_rows = rms_scale(full_rows.astype(jnp.float32), latent_gain.astype(jnp.float32)).astype(
        jnp.bfloat16
    )
    inner_width = lat_qkv.shape[2]
    projected = jnp.einsum(
        "pd,idc->ipc",
        normed_rows,
        lax.all_gather(lat_qkv, "seq", axis=1, tiled=True),
        preferred_element_type=jnp.float32,
    )
    heads_here = inner_width // HD
    queries = rotate(projected[0].reshape(slot_total, heads_here, HD), position).astype(
        jnp.bfloat16
    )
    latent_keys = (
        rotate(projected[1].reshape(slot_total, heads_here, HD), position)
        .astype(jnp.bfloat16)
        .reshape(slot_total, inner_width)
    )
    latent_values = projected[2].astype(jnp.bfloat16)
    latent_pos = jnp.where(in_use, position, far_position)
    largest = jnp.full((heads_here, slot_total), -1e30, jnp.float32)
    piece_keys = lax.all_gather(latent_keys, "seq", axis=0, tiled=True)
    piece_values = lax.all_gather(latent_values, "seq", axis=0, tiled=True)
    piece_pos = lax.all_gather(shortened(latent_pos), "seq", axis=0, tiled=True)
    rows_here = piece_keys.shape[0]
    piece_scores = jnp.einsum(
        "qhd,khd->hqk",
        queries,
        piece_keys.reshape(rows_here, heads_here, HD),
        preferred_element_type=jnp.float32,
    ) * (1.0 / math.sqrt(HD))
    permitted = (piece_pos[None, :] <= position[:, None])[None]
    piece_scores = jnp.where(permitted, piece_scores, -1e30)
    renewed = jnp.maximum(largest, jnp.max(piece_scores, axis=-1))
    raised = jnp.where(permitted, jnp.exp(piece_scores - renewed[..., None]), 0.0)
    weight_sum = jnp.sum(raised, axis=-1)
    weighted = jnp.einsum(
        "hqk,khd->hqd",
        raised.astype(jnp.bfloat16),
        piece_values.reshape(rows_here, heads_here, HD),
        preferred_element_type=jnp.float32,
    )
    largest, weight_sum, weighted = (renewed, weight_sum, weighted)
    latent_heads = (
        (weighted / weight_sum[..., None])
        .transpose(1, 0, 2)
        .reshape(slot_total, inner_width)
        .astype(jnp.bfloat16)
    )
    partials = jnp.dot(
        latent_heads,
        lax.all_gather(lat_proj_out, "seq", axis=1, tiled=True),
        preferred_element_type=jnp.float32,
    )
    reduced = lax.psum_scatter(partials, "tp", scatter_dimension=1, tiled=True)
    latent = jnp.where(in_use[:, None], patches.astype(jnp.float32) + reduced, 0.0).astype(
        jnp.bfloat16
    )
    return (encoded, latent)


MESH = pl.DeviceIdType.MESH
EDGE = 16


def seq_peer(index):
    return {"seq": index}


def tp_peer(index):
    return {"tp": index}


def like(shape, dtype=jnp.bfloat16):
    return jax.ShapeDtypeStruct(shape, dtype)


def iota(shape, axis):
    return lax.broadcasted_iota(jnp.int32, shape, axis)


def across_lanes(left, right):
    return lax.dot_general(
        left, right, (((1,), (1,)), ((), ())), preferred_element_type=jnp.float32
    )


def product(left, right):
    return jnp.dot(left, right, preferred_element_type=jnp.float32)


def remote(source, target, send_sem, recv_sem, device):
    return pltpu.make_async_remote_copy(
        src_ref=source,
        dst_ref=target,
        send_sem=send_sem,
        recv_sem=recv_sem,
        device_id=device,
        device_id_type=MESH,
    )


def turn_table(rows):
    frequency = rope_base ** (-2.0 * np.arange(HD // 2, dtype=np.float64) / HD)
    frequency = frequency.astype(np.float32)
    angles = np.arange(rows, dtype=np.float32)[:, None] * frequency[None, :]
    angles = angles.astype(np.float64)
    return np.concatenate([np.cos(angles), np.sin(angles)], axis=1).astype(np.float32)


def whole_layer(
    states, gain, enc_qkv, proj, starts, lift, cross_kv, latent_gain, lat_qkv, lat_proj, table,
    call_id,
):
    count, size = lax.axis_size("tp"), lax.axis_size("seq")
    near = count - 1
    byte_rows, width = states.shape
    total_rows = byte_rows + EDGE
    enc_cols = enc_qkv.shape[2]
    enc_heads = enc_cols // EH
    slots = starts.shape[1]
    columns = lift.shape[1]
    group = 2 * HD
    panel_count = columns // group
    row_total = count * slots
    half = lat_qkv.shape[1]
    full_width = columns * count
    rows_half = byte_rows // 2
    row_spans = ((0, rows_half), (rows_half, rows_half), (byte_rows, EDGE))
    halves_of = ((0, rows_half), (rows_half, total_rows - rows_half))
    part_rows = slots // 2
    half_total = row_total // 2
    share = enc_cols // 2
    piece = share // count

    def kernel(
        states_hbm, gain_hbm, qkv_hbm, proj_hbm, starts_hbm, lift_hbm, cross_hbm,
        lgain_hbm, w_own_hbm, o_hbm, table_hbm,
        enc_ref, out_ref,
        gain_ref, starts_ref, lgain_ref, states_ref, qkv_ref, query_ref, kv_ref, infos, proj_ref, att_ref, near_ref, blend_ref, table_ref, cos_ref, sin_ref,
        lift_ref, cross_ref, pooled_ref, full_ref, panels, rows_ref, patch_ref,
        w_own, w_other, geared, own_part, qkv_send, qkv_land, sq_send, sq_land,
        kv_own, kv_other, out_quarter, out_rows, tall, parts, land,
        load_sems, info_s, info_r, halo_s, halo_r, edge_s, edge_r, pz_s, pz_r, pp_s, pp_r, pc_s, pc_r,
        w_sems, heads_send, heads_recv,
        panel_send, panel_recv, stay_sems,
        qkv_s, qkv_r, sq_s, sq_r, kv_s, kv_r,
        oq_s, oq_r, oz_s, oz_r, oc_s, oc_r, own_sems, tz_s, tz_r, a_s, a_r, enc_sem,
    ):
        s, t = lax.axis_index("seq"), lax.axis_index("tp")
        p, c = s // 2, lax.rem(s, 2)
        partner = seq_peer(s + 1 - 2 * c)

        def plane(index):
            return {"seq": 2 * index + c}

        def ring(k):
            return lax.rem(s + k + size, size)

        def tower(k):
            return lax.rem(t + k + count, count)

        def flip(k):
            if k == 0:
                return p
            if k == 1:
                return p + 1 - 2 * lax.rem(p, 2)
            if k == 2:
                return lax.rem(p + 2, 4)
            return 3 - p

        far_first = (3, 2, 1)
        low = t < 2
        inner = (t == 1) | (t == 2)
        first_from = jnp.where(low, t + 1, t - 1)
        second_from = jnp.where(low, t + 2, t - 2)
        third_from = jnp.where(lax.rem(t, 2) == 0, count - 1, 0)
        outer = jnp.where(low, 0, count - 1)
        outward = (t, third_from, second_from, first_from)

        def to_near(copy_to):
            copy_to(first_from, 0).start()

            @pl.when(inner)
            def _():
                copy_to(outer, 1).start()

        def sent_near(copy_to, over):
            copy_to(first_from, 0).wait_send()

            @pl.when(inner)
            def _():
                copy_to(outer, 1).wait_send()
                for i in range(3):
                    over(i).wait_send()

        barrier = pltpu.get_barrier_semaphore()
        for k in range(1, size):
            pl.semaphore_signal(barrier, inc=1, device_id=seq_peer(ring(k)), device_id_type=MESH)
        for k in range(1, count):
            pl.semaphore_signal(barrier, inc=1, device_id=tp_peer(tower(k)), device_id_type=MESH)

        @pl.when(p != t)
        def _():
            for k in far_first:
                away_peer = {"seq": 2 * flip(k) + c, "tp": p}
                pl.semaphore_signal(barrier, inc=1, device_id=away_peer, device_id_type=MESH)

        own_rows = pl.ds(pl.multiple_of(p * HD, HD), HD)
        load_plan = (
            (states_hbm, states_ref.at[pl.ds(0, byte_rows)]),
            (qkv_hbm, qkv_ref),
            (table_hbm, table_ref),
            (proj_hbm.at[pl.ds(0, share)], proj_ref.at[0, 0]),
            (proj_hbm.at[pl.ds(share, share)], proj_ref.at[1, 0]),
            (lift_hbm, lift_ref),
            (cross_hbm, cross_ref),
            (w_own_hbm, w_own),
            (o_hbm.at[own_rows], out_quarter.at[p]),
            (gain_hbm, gain_ref),
            (starts_hbm, starts_ref),
            (lgain_hbm, lgain_ref),
        )
        loads = [
            pltpu.make_async_copy(source, target, load_sems.at[i])
            for i, (source, target) in enumerate(load_plan)
        ]
        for i in (0, 9, 1, 10, 2, 3, 4, 5, 6, 7, 8, 11):
            loads[i].start()
        sent = []

        def launch(copy):
            copy.start()
            sent.append(copy)
            return copy
        loads[0].wait()
        loads[9].wait()
        values = states_ref[0:byte_rows].astype(jnp.float32)
        chip_row = gain_ref[...].astype(jnp.float32).reshape(1, width)
        normed = rms_scale(values, chip_row).astype(jnp.bfloat16)
        own = pl.ds(WIN, byte_rows)
        loads[1].wait()
        for i in range(2):
            fresh = product(normed, qkv_ref[i + 1]).astype(jnp.bfloat16)
            for h in range(2):
                kv_ref[h, i, own] = fresh[:, h * share : (h + 1) * share]
        query_ref[0:byte_rows] = (
            product(normed, qkv_ref[0]) * (1.0 / math.sqrt(EH))
        ).astype(jnp.bfloat16)
        loads[10].wait()
        listed = jnp.where(starts_ref[...] < size * byte_rows, 1, 0)
        my_count = jnp.sum(listed, axis=1, keepdims=True)
        info_lane = iota((8, 128), 1)
        infos[s] = jnp.where(
            info_lane == 0, my_count, jnp.where(info_lane == 1, starts_ref[0:1, 0:1], 0)
        )
        greetings = size - 1 + count - 1

        @pl.when(p == t)
        def _():
            pl.semaphore_wait(barrier, greetings)

        @pl.when(p != t)
        def _():
            pl.semaphore_wait(barrier, greetings + count - 1)

        mine_at = pl.multiple_of(p * piece, piece)
        lifts = [
            launch(
                remote(
                    proj_hbm.at[pl.ds(pl.multiple_of(c * share + p * piece, piece), piece)],
                    proj_ref.at[c, k, pl.ds(mine_at, piece)],
                    pz_s.at[k - 1],
                    pz_r.at[k - 1],
                    tp_peer(tower(k)),
                )
            )
            for k in range(1, count)
        ]
        notes = [
            launch(
                remote(infos.at[s], infos.at[s], info_s.at[k - 1], info_r.at[k - 1], seq_peer(ring(k)))
            )
            for k in range(1, size)
        ]
        behind = seq_peer(ring(-1))
        edges = [
            launch(remote(source, target, edge_s.at[i], edge_r.at[i], behind))
            for i, (source, target) in enumerate(
                (
                    (
                        kv_ref.at[:, :, pl.ds(WIN, EDGE)],
                        kv_ref.at[:, :, pl.ds(WIN + byte_rows, EDGE)],
                    ),
                    (query_ref.at[pl.ds(0, EDGE)], query_ref.at[pl.ds(byte_rows, EDGE)]),
                    (states_ref.at[pl.ds(0, EDGE)], states_ref.at[pl.ds(byte_rows, EDGE)]),
                )
            )
        ]
        halos = [
            launch(
                remote(
                    kv_ref.at[h, :, own],
                    kv_ref.at[h, :, pl.ds(0, byte_rows)],
                    halo_s.at[0, h],
                    halo_r.at[0, h],
                    seq_peer(ring(2)),
                )
            )
            for h in range(2)
        ]
        def beside(i):
            first = pl.multiple_of(jnp.where(c == 0, WIN, 0), byte_rows)
            return remote(
                kv_ref.at[i, :, pl.ds(first, byte_rows)],
                kv_ref.at[i, :, pl.ds(byte_rows, byte_rows)],
                halo_s.at[1, i],
                halo_r.at[1, i],
                partner,
            )

        @pl.when(c == 0)
        def _():
            for i in range(2):
                beside(i).start()
        for copy in notes:
            copy.wait_recv()
        counted = [infos[m][0:1, 0:1] for m in range(size)]
        offsets = [jnp.zeros((1, 1), jnp.int32)]
        for m in range(size - 1):
            offsets.append(offsets[m] + counted[m])
        next_first = jnp.where(
            s + 1 < size, infos[jnp.minimum(s + 1, size - 1)][0:1, 1:2], size * byte_rows
        )
        square = (slots, slots)
        start_row = jnp.broadcast_to(starts_ref[...], square)
        apart = iota(square, 1) - iota(square, 0)
        first_byte = jnp.sum(jnp.where(apart == 0, start_row, 0), axis=1, keepdims=True)
        following = jnp.sum(jnp.where(apart == 1, start_row, 0), axis=1, keepdims=True)
        slot_at = iota((slots, 1), 0)
        in_use = slot_at < my_count
        patch_end = jnp.where(slot_at + 1 < my_count, following, next_first)
        anchor = s * byte_rows
        lower = jnp.where(in_use, first_byte - anchor, 0)
        upper = jnp.where(in_use, patch_end - anchor, 1)
        where_at = iota((slots, total_rows), 1)
        allowed = (where_at >= lower) & (where_at < upper)
        member = jnp.where(allowed & in_use, 1.0, 0.0)
        lengths = jnp.maximum(jnp.sum(member, axis=1, keepdims=True), 1.0)
        member = member.astype(jnp.bfloat16)
        bias = jnp.where(allowed, 0.0, -1e30)
        for begin, rows in row_spans:
            reach_rows = rows + WIN
            behind_by = iota((rows, reach_rows), 0) - iota((rows, reach_rows), 1) + WIN
            known = iota((rows, reach_rows), 1) >= WIN - begin - s * byte_rows
            near_by = (behind_by >= 0) & (behind_by < WIN) & known
            near_ref[begin : begin + rows, 0:reach_rows] = jnp.where(near_by, 0.0, -1e30)
        chosen = [
            (
                jnp.where(c == 0, offsets[2 * i], offsets[2 * i + 1]),
                jnp.where(c == 0, counted[2 * i], counted[2 * i + 1]),
                jnp.where(c == 0, offsets[2 * i + 1], offsets[2 * i]),
                jnp.where(c == 0, counted[2 * i + 1], counted[2 * i]),
            )
            for i in range(count)
        ]

        def laid(shape, axis, which):
            at = iota(shape, axis)
            band = at // half_total
            within = at - band * half_total
            block = within // part_rows
            result = jnp.broadcast_to(chosen[0][which], shape)
            for i in range(1, count):
                result = jnp.where(block == i, chosen[i][which], result)
            return band * part_rows + within - block * part_rows, result

        row_slot, row_offset = laid((row_total, 1), 0, 0)
        position = row_offset + row_slot
        key_positions = []
        for which in (0, 2):
            key_slot, key_offset = laid((1, row_total), 1, which)
            _, key_count = laid((1, row_total), 1, which + 1)
            key_positions.append(
                jnp.where(key_slot < key_count, key_offset + key_slot, far_position)
            )
        loads[2].wait()
        table_rows = table_ref.shape[0]
        picked = jnp.where(iota((row_total, table_rows), 1) == position, 1.0, 0.0)
        turns = lax.dot_general(
            picked,
            table_ref[...],
            (((1,), (0,)), ((), ())),
            precision=lax.Precision.HIGHEST,
            preferred_element_type=jnp.float32,
        )
        swapped = pltpu.roll(turns, HD // 2, 1)
        low_lanes = iota((row_total, HD), 1) < HD // 2
        cos_ref[...] = jnp.where(low_lanes, turns, swapped)
        sin_ref[...] = jnp.where(low_lanes, -swapped, turns)
        def halo_arrives(h):
            halos[h].wait_recv()

            @pl.when(c == 1)
            def _():
                beside(h).start()

        halo_arrives(0)
        for copy in lifts:
            copy.wait_recv()
        spread = [
            launch(
                remote(
                    proj_ref.at[c, pl.ds(1, near), pl.ds(mine_at, piece)],
                    proj_ref.at[c, pl.ds(1, near), pl.ds(mine_at, piece)],
                    pp_s.at[k - 1],
                    pp_r.at[k - 1],
                    plane(flip(k)),
                )
            )
            for k in far_first
        ]
        def shared(k):
            rows = pl.ds(pl.multiple_of(flip(k) * piece, piece), piece)
            return remote(
                proj_ref.at[c, pl.ds(1, near), rows],
                proj_ref.at[c, pl.ds(1, near), rows],
                pc_s.at[k],
                pc_r.at[k],
                partner,
            )

        launch(shared(0))
        for copy in edges:
            copy.wait_recv()

        beside(0).wait_recv()
        def share_heads(origin, h, target, sem):
            return remote(
                att_ref.at[origin, h // 2, pl.ds(*halves_of[h % 2])],
                att_ref.at[origin, h // 2, pl.ds(*halves_of[h % 2])],
                heads_send.at[h, sem],
                heads_recv.at[h, origin],
                tp_peer(target),
            )

        def attend(pair, begin, rows):
            reach_rows = rows + WIN
            keys = kv_ref[pair, 0, begin : begin + reach_rows]
            seen_values = kv_ref[pair, 1, begin : begin + reach_rows]
            queries = query_ref[begin : begin + rows, pair * share : (pair + 1) * share]
            head_of = iota((rows, share), 1) // EH
            stacked = jnp.concatenate(
                [jnp.where(head_of == h, queries, jnp.zeros_like(queries)) for h in range(share // EH)],
                axis=0,
            )
            near_bias = near_ref[begin : begin + rows, 0:reach_rows]
            scores = across_lanes(stacked, keys)
            raised, sums = [], []
            for h in range(share // EH):
                here = scores[h * rows : (h + 1) * rows] + near_bias
                here = jnp.exp(here - jnp.max(here, axis=1, keepdims=True))
                sums.append(jnp.sum(here, axis=1, keepdims=True))
                raised.append(here.astype(jnp.bfloat16))
            seen = product(jnp.concatenate(raised, axis=0), seen_values)
            attended = jnp.zeros((rows, share), jnp.float32)
            for h in range(share // EH):
                attended = jnp.where(
                    head_of == h, seen[h * rows : (h + 1) * rows] / sums[h], attended
                )
            att_ref[t, pair, begin : begin + rows] = attended.astype(jnp.bfloat16)

        for h in range(2):
            if h:
                halo_arrives(1)
                beside(1).wait_recv()
            for begin, rows in row_spans:
                attend(h, begin, rows)
                if begin != rows_half:
                    piece_id = 2 * h + (begin > 0)
                    to_near(lambda target, sem: share_heads(t, piece_id, target, sem))

        swaps = [launch(remote(w_own_hbm, w_other, w_sems.at[0], w_sems.at[1], partner))]
        sources = (first_from, second_from, third_from)
        beyond = (outer, outer, first_from)

        def hand_over(which, h):
            return share_heads(sources[which], h, beyond[which], 2 + which)

        def gain_heads(which, h):
            hand_over(which, h).wait_recv()

            @pl.when(inner)
            def _():
                hand_over(which, h).start()

        def blended(h):
            attended = jnp.concatenate([att_ref[tower(-k), h] for k in range(count)], axis=1)
            return product(attended, proj_ref[h].reshape(count * share, width))
        for h in range(4):
            gain_heads(0, h)

            @pl.when(inner)
            def _():
                gain_heads(2, h)
                if h > 1:
                    gain_heads(1, h - 2)
        @pl.when(inner)
        def _():
            for h in (2, 3):
                gain_heads(1, h)
        for k, copy in zip(far_first[::-1], spread[::-1]):
            copy.wait_recv()
            launch(shared(k))
        quarters = [
            launch(
                remote(
                    o_hbm.at[pl.ds(pl.multiple_of(flip(k) * HD, HD), HD)],
                    out_quarter.at[p],
                    oq_s.at[k - 1],
                    oq_r.at[k - 1],
                    plane(flip(k)),
                )
            )
            for k in far_first
        ]
        @pl.when(jnp.logical_not(inner))
        def _():
            for h in (0, 1):
                gain_heads(1, h)
                gain_heads(2, h)

        loads[3].wait()
        loads[4].wait()
        @pl.when(jnp.logical_not(inner))
        def _():
            for h in (2, 3):
                gain_heads(1, h)
                gain_heads(2, h)
        blend_ref[...] = states_ref[...].astype(jnp.float32) + blended(c)
        for k in range(count):
            shared(k).wait_recv()
        full_ref[...] = (blend_ref[...] + blended(1 - c)).astype(jnp.bfloat16)
        enc_out = pltpu.make_async_copy(full_ref.at[pl.ds(0, byte_rows)], enc_ref, enc_sem.at[0])
        enc_out.start()

        totals = product(member, full_ref[...])
        pooled_ref[...] = (totals / lengths).astype(jnp.bfloat16)
        loads[5].wait()
        loads[6].wait()

        half_lanes = columns // 2

        def window(r, i):
            if r == 0:
                return pl.ds(pl.multiple_of(i * group, group), group)
            return pl.ds(i * half_lanes, half_lanes)

        def slot_of(r, i):
            return i if r == 0 else panel_count + i

        def away(k, r, i):
            return remote(
                panels.at[r, :, window(r, i)],
                rows_ref.at[r, p, :, window(r, i)],
                panel_send.at[k, slot_of(r, i)],
                panel_recv.at[p, slot_of(r, i)],
                {"seq": 2 * t + c, "tp": outward[k]},
            )

        def stay(r, i):
            return pltpu.make_async_copy(
                panels.at[r, :, window(r, i)],
                rows_ref.at[r, p, :, window(r, i)],
                stay_sems.at[slot_of(r, i)],
            )

        def ship(r, i):
            for k in range(1, count):
                away(k, r, i).start()

            @pl.when(p != t)
            def _():
                away(0, r, i).start()

            @pl.when(p == t)
            def _():
                stay(r, i).start()

        widths = (panel_count, 2)

        def heads(i, carry):
            cols = pl.ds(pl.multiple_of(i * group, group), group)
            rows = full_ref[...]
            lifted = product(pooled_ref[...], lift_ref[:, cols])
            keys = product(rows, cross_ref[0, :, cols]).astype(jnp.bfloat16)
            seen_values = product(rows, cross_ref[1, :, cols]).astype(jnp.bfloat16)
            queries = lifted.astype(jnp.bfloat16)
            crossed = []
            for j in range(2):
                lanes = slice(j * HD, (j + 1) * HD)
                scores = across_lanes(queries[:, lanes], keys[:, lanes])
                scores = scores * (1.0 / math.sqrt(HD)) + bias
                raised = jnp.exp(scores - jnp.max(scores, axis=1, keepdims=True))
                crossed.append(
                    product(raised.astype(jnp.bfloat16), seen_values[:, lanes])
                    / jnp.sum(raised, axis=1, keepdims=True)
                )
            patch = lifted + jnp.concatenate(crossed, axis=1)
            panel = jnp.where(in_use, patch, 0.0).astype(jnp.bfloat16)
            patch_ref[:, cols] = panel
            for r in range(2):
                panels[r, :, cols] = panel[r * part_rows : (r + 1) * part_rows]
            ship(0, i)
            return carry
        lax.fori_loop(0, panel_count, heads, 0)
        for i in range(widths[1]):
            ship(1, i)
        for copy in quarters:
            copy.wait_recv()
        loads[8].wait()
        mine_out = pltpu.make_async_copy(
            out_quarter.at[t], out_rows.at[c, t], own_sems.at[0]
        )
        mine_out.start()
        ups = [
            remote(
                out_quarter.at[tower(k)],
                out_rows.at[c, t],
                oz_s.at[k - 1],
                oz_r.at[k - 1],
                tp_peer(tower(k)),
            )
            for k in range(1, count)
        ]

        @pl.when(inner)
        def _():
            for copy in ups:
                copy.start()

        @pl.when(t == 0)
        def _():
            ups[0].start()

        @pl.when(t == count - 1)
        def _():
            ups[2].start()

        arriving, flats = ([], []), []
        eye = iota((half_total, half_total), 0) == iota((half_total, half_total), 1)
        loads[11].wait()
        chip_gain = lgain_ref[pl.ds(pl.multiple_of(p * columns, columns), columns)]
        chip_gain = chip_gain.astype(jnp.float32).reshape(1, columns)
        for r in range(2):
            for q in range(count):

                @pl.when((p != q) | (p != t))
                def _():
                    for i in range(widths[r]):
                        remote(
                            panels.at[r, :, window(r, i)],
                            rows_ref.at[r, q, :, window(r, i)],
                            panel_send.at[0, slot_of(r, i)],
                            panel_recv.at[q, slot_of(r, i)],
                            plane(p),
                        ).wait_recv()

            @pl.when(p == t)
            def _():
                for i in range(widths[r]):
                    stay(r, i).wait()

            if r:

                @pl.when(t == 0)
                def _():
                    ups[2].start()
                    ups[1].start()

                @pl.when(t == count - 1)
                def _():
                    ups[0].start()
                    ups[1].start()
            values = rows_ref[r].reshape(half_total, columns).astype(jnp.float32)
            squares = jnp.sum(values * values, axis=1, keepdims=True)
            flat = jnp.sum(jnp.where(eye, squares, 0.0), axis=0, keepdims=True)
            flats.append(flat)
            sq_send[r] = jnp.broadcast_to(flat, (8, half_total))
            geared[...] = (values * chip_gain).astype(jnp.bfloat16)
            for k in far_first:
                arriving[r].append(
                    launch(
                        remote(
                            sq_send.at[r],
                            sq_land.at[r, k - 1],
                            sq_s.at[r, k - 1],
                            sq_r.at[r, k - 1],
                            plane(flip(k)),
                        )
                    )
                )
            if r == 0:
                loads[7].wait()
                swaps[0].wait_recv()
            mine = geared[:, pl.ds(pl.multiple_of(c * half, half), half)]
            theirs = geared[:, pl.ds(pl.multiple_of((1 - c) * half, half), half)]
            for k in far_first + (0,):
                target = flip(k)
                lanes = pl.ds(pl.multiple_of(target * HD, HD), HD)
                for i in range(3):
                    part = product(mine, w_own[i, :, lanes]) + product(theirs, w_other[i, :, lanes])
                    if k:
                        qkv_send[r, k - 1, i] = part.astype(jnp.bfloat16)
                    else:
                        own_part[r, i] = part
                if k:
                    arriving[r].append(
                        launch(
                            remote(
                                qkv_send.at[r, k - 1],
                                qkv_land.at[r, k - 1],
                                qkv_s.at[r, k - 1],
                                qkv_r.at[r, k - 1],
                                plane(target),
                            )
                        )
                    )

        sent.extend(ups)

        def turned(vectors, rows):
            return (
                vectors * cos_ref[rows] + pltpu.roll(vectors, HD // 2, 1) * sin_ref[rows]
            ).astype(jnp.bfloat16)

        swaps_kv, queries = [], []
        for r in range(2):
            for copy in arriving[r]:
                copy.wait_recv()
            flat = flats[r] + jnp.sum(sq_land[r, :, 0:1, :], axis=0)
            square_sum = jnp.sum(jnp.where(eye, flat, 0.0), axis=1, keepdims=True)
            scale = lax.rsqrt(square_sum / full_width + epsilon)
            total = []
            for i in range(3):
                band = own_part[r, i]
                for k in range(count - 1):
                    band = band + qkv_land[r, k, i].astype(jnp.float32)
                total.append(band * scale)
            rows = slice(r * half_total, (r + 1) * half_total)
            kv_own[r, 0] = turned(total[1], rows)
            kv_own[r, 1] = total[2].astype(jnp.bfloat16)
            swaps_kv.append(
                launch(remote(kv_own.at[r], kv_other.at[r], kv_s.at[r], kv_r.at[r], partner))
            )
            queries.append(turned(total[0], rows))
        queries = jnp.concatenate(queries, axis=0)

        def both(ref, i):
            return jnp.concatenate([ref[0, i], ref[1, i]], axis=0)
        def scored(keys, key_position):
            scores = across_lanes(queries, keys) * (1.0 / math.sqrt(HD))
            return jnp.where(key_position <= position, scores, -1e30)

        scores_a = scored(both(kv_own, 0), key_positions[0])
        for copy in swaps_kv:
            copy.wait_recv()
        scores_b = scored(both(kv_other, 0), key_positions[1])
        largest = jnp.maximum(
            jnp.max(scores_a, axis=1, keepdims=True), jnp.max(scores_b, axis=1, keepdims=True)
        )
        raised_a = jnp.exp(scores_a - largest)
        raised_b = jnp.exp(scores_b - largest)
        weight_sum = jnp.sum(raised_a, axis=1, keepdims=True) + jnp.sum(
            raised_b, axis=1, keepdims=True
        )
        weighted = product(raised_a.astype(jnp.bfloat16), both(kv_own, 1)) + product(
            raised_b.astype(jnp.bfloat16), both(kv_other, 1)
        )
        tall[t] = (weighted / weight_sum).astype(jnp.bfloat16).reshape(2, half_total, HD)
        for k in far_first + (0,):
            take = pl.ds(pl.multiple_of(flip(k) * part_rows, part_rows), part_rows)
            for d in range(1, count):
                launch(
                    remote(
                        tall.at[t, :, take],
                        tall.at[t, :, take],
                        tz_s.at[k, d - 1],
                        tz_r.at[k, t],
                        tp_peer(outward[d]),
                    )
                )
        def beside_rows(k):
            return remote(
                out_rows.at[c, tower(-k)],
                out_rows.at[c, tower(-k)],
                oc_s.at[k],
                oc_r.at[k],
                partner,
            )

        mine_out.wait()
        launch(beside_rows(0))
        for k in (1, 3, 2):
            ups[k - 1].wait_recv()
            launch(beside_rows(k))
        for k in range(count):
            beside_rows(k).wait_recv()
        hops, parts_own = [], []
        summed = patch_ref[...].astype(jnp.float32)
        for k in far_first + (0,):
            for d in range(1, count):
                take = pl.ds(pl.multiple_of(flip(k) * part_rows, part_rows), part_rows)
                remote(
                    tall.at[tower(-d), :, take],
                    tall.at[tower(-d), :, take],
                    tz_s.at[k, d - 1],
                    tz_r.at[k, tower(-d)],
                    tp_peer(tower(-d)),
                ).wait_recv()
            take = pl.ds(pl.multiple_of(flip(k) * part_rows, part_rows), part_rows)
            attended = jnp.concatenate(
                [tall[q, :, take].reshape(slots, HD) for q in range(count)], axis=1
            )
            for core in range(2):
                lanes = slice(core * half, (core + 1) * half)
                part = product(attended, out_rows[core].reshape(count * HD, half))
                if k:
                    parts[k - 1, :, lanes] = part.astype(jnp.bfloat16)
                else:
                    parts_own.append(part)
            if k:
                hops.append(
                    launch(
                        remote(
                            parts.at[k - 1],
                            land.at[k - 1],
                            a_s.at[k - 1],
                            a_r.at[k - 1],
                            plane(flip(k)),
                        )
                    )
                )
        summed = summed + jnp.concatenate(parts_own, axis=1)
        for copy in hops:
            copy.wait_recv()
        for k in range(count - 1):
            summed = summed + land[k].astype(jnp.float32)
        out_ref[...] = jnp.where(in_use, summed, 0.0).astype(jnp.bfloat16)
        enc_out.wait()
        for copy in sent:
            copy.wait_send()
        for i in range(2):
            beside(i).wait_send()
        for h in range(4):
            sent_near(
                lambda target, sem: share_heads(t, h, target, sem), lambda which: hand_over(which, h)
            )

        for r in range(2):
            for i in range(widths[r]):
                for k in range(1, count):
                    away(k, r, i).wait_send()

                @pl.when(p != t)
                def _():
                    away(0, r, i).wait_send()
    hbm = pl.BlockSpec(memory_space=pl.ANY)
    vmem = pl.BlockSpec(memory_space=pltpu.VMEM)
    dma = pltpu.SemaphoreType.DMA

    def buffer(*shape, dtype=jnp.bfloat16):
        return pltpu.VMEM(shape, dtype)

    return pl.pallas_call(
        kernel,
        out_shape=[like((byte_rows, width)), like((slots, columns))],
        in_specs=[hbm] * 11,
        out_specs=[vmem, vmem],
        scratch_shapes=[
            buffer(width),
            buffer(1, slots, dtype=jnp.int32),
            buffer(full_width),
            buffer(total_rows, width),
            buffer(*enc_qkv.shape),
            buffer(total_rows, enc_cols),
            buffer(2, 2, WIN + total_rows, share),
            buffer(size, 8, 128, dtype=jnp.int32),
            buffer(2, count, share, width),
            buffer(count, 2, total_rows, share),
            buffer(total_rows, rows_half + WIN, dtype=jnp.float32),
            buffer(total_rows, width, dtype=jnp.float32),
            buffer(*table.shape, dtype=jnp.float32),
            buffer(row_total, HD, dtype=jnp.float32),
            buffer(row_total, HD, dtype=jnp.float32),
            buffer(*lift.shape),
            buffer(*cross_kv.shape),
            buffer(slots, width),
            buffer(total_rows, width),
            buffer(2, part_rows, columns),
            buffer(2, count, part_rows, columns),
            buffer(slots, columns),
            buffer(*lat_qkv.shape),
            buffer(*lat_qkv.shape),
            buffer(half_total, columns),
            buffer(2, 3, half_total, HD, dtype=jnp.float32),
            buffer(2, near, 3, half_total, HD),
            buffer(2, near, 3, half_total, HD),
            buffer(2, 8, half_total, dtype=jnp.float32),
            buffer(2, near, 8, half_total, dtype=jnp.float32),
            buffer(2, 2, half_total, HD),
            buffer(2, 2, half_total, HD),
            buffer(count, HD, half),
            buffer(2, count, HD, half),
            buffer(count, 2, half_total, HD),
            buffer(near, slots, columns),
            buffer(near, slots, columns),
            dma((12,)),
            dma((size - 1,)),
            dma((size - 1,)),
            dma((2, 2)),
            dma((2, 2)),
            dma((3,)),
            dma((3,)),
            dma((near,)),
            dma((near,)),
            dma((near,)),
            dma((near,)),
            dma((count,)),
            dma((count,)),
            dma((2,)),
            dma((4, 5)),
            dma((4, count)),
            dma((count, panel_count + 2)),
            dma((count, panel_count + 2)),
            dma((panel_count + 2,)),
            dma((2, near)),
            dma((2, near)),
            dma((2, near)),
            dma((2, near)),
            dma((2,)),
            dma((2,)),
            dma((near,)),
            dma((near,)),
            dma((near,)),
            dma((near,)),
            dma((count,)),
            dma((count,)),
            dma((1,)),
            dma((count, near)),
            dma((count, count)),
            dma((near,)),
            dma((near,)),
            dma((1,)),
        ],
        compiler_params=pltpu.CompilerParams(
            collective_id=call_id, has_side_effects=True, vmem_limit_bytes=52428800
        ),
    )(
        states, gain, enc_qkv, proj, starts, lift, cross_kv, latent_gain, lat_qkv, lat_proj, table,
    )


def settle(*arrays):
    total = len(arrays)

    def kernel(*refs):
        ins, outs, sems = refs[:total], refs[total : 2 * total], refs[2 * total]
        puts = [pltpu.make_async_copy(ins[i], outs[i], sems.at[i]) for i in range(total)]
        for put in puts:
            put.start()
        for put in puts:
            put.wait()

    return pl.pallas_call(
        kernel,
        out_shape=[like(value.shape, value.dtype) for value in arrays],
        in_specs=[pl.BlockSpec(memory_space=pl.ANY)] * total,
        out_specs=[pl.BlockSpec(memory_space=pltpu.HBM)] * total,
        scratch_shapes=[pltpu.SemaphoreType.DMA((total,))],
        compiler_params=pltpu.CompilerParams(vmem_limit_bytes=2**20),
    )(*arrays)


def fused_shards(
    byte_states,
    enc_gain,
    enc_qkv,
    enc_proj_out,
    starts,
    counts,
    lift,
    cross_kv,
    latent_gain,
    lat_qkv,
    lat_proj_out,
):
    table = jnp.asarray(turn_table(lax.axis_size("seq") * starts.shape[1]))
    operands = [
        pltpu.with_memory_space_constraint(value, pltpu.HBM)
        for value in (
            byte_states,
            enc_gain,
            enc_qkv,
            enc_proj_out,
            starts,
            lift,
            cross_kv,
            latent_gain,
            lat_qkv,
            lat_proj_out,
            table,
        )
    ]
    encoded, latent = whole_layer(*operands, 1)
    return settle(encoded, latent)


def fits_pairs(mesh, byte_states, enc_qkv, starts, lat_qkv):
    size, tp_size = mesh.shape["seq"], mesh.shape["tp"]
    byte_rows = byte_states.shape[0] // size
    return (
        size == 2 * tp_size
        and tp_size == 4
        and WIN % byte_rows == 0
        and WIN == 2 * byte_rows
        and byte_rows % (32 * tp_size) == 0
        and lat_qkv.shape[2] // tp_size == HD * tp_size
        and lat_qkv.shape[1] % (128 * size) == 0
        and starts.shape[1] * tp_size % 128 == 0
        and starts.shape[1] * tp_size <= 1024
        and starts.shape[1] % 16 == 0
        and enc_qkv.shape[2] % (128 * tp_size) == 0
    )


def solution(mesh):
    specs = dict(
        mesh=mesh,
        in_specs=(
            P("seq", None),
            P(),
            P(None, None, "tp"),
            P("tp", None),
            P("seq", None),
            P("seq"),
            P(None, "tp"),
            P(None, None, "tp"),
            P(),
            P(None, "seq", "tp"),
            P("tp", "seq"),
        ),
        out_specs=(P("seq", None), P("seq", "tp")),
        check_vma=False,
    )

    def run(*arrays):
        paired = fits_pairs(mesh, arrays[0], arrays[2], arrays[4], arrays[9])
        return jax.shard_map(fused_shards if paired else gathered_shards, **specs)(*arrays)

    return run
```

```python
import math

import jax
import numpy as np
import jax.numpy as jnp
from jax import lax
from jax.experimental import pallas as pl
from jax.experimental.pallas import tpu as pltpu
from jax.sharding import PartitionSpec as P

EH = 64
HD = 128
WIN = 512
SPILL = 8


epsilon = 1e-05
rope_base = 500000.0
far_position = 1 << 30


def from_behind(value, axis, steps):
    count = lax.axis_size(axis)
    leading, last = (max(0, -steps), min(count, count - steps))
    return lax.ppermute(value, axis, [(source, source + steps) for source in range(leading, last)])


def prefix(value, axis, join, neutral):
    count, mine = (lax.axis_size(axis), lax.axis_index(axis))
    pieces = lax.all_gather(value, axis)
    subtotal = jnp.full_like(value, 0) + jnp.asarray(neutral, value.dtype)

    def hop(position, subtotal):
        longer = join(subtotal, pieces[position])
        return jnp.where(position < mine, longer, subtotal)

    return lax.fori_loop(0, count - 1, hop, subtotal)


def shortened(value):

    def short(part):
        return part.astype(jnp.bfloat16) if part.dtype == jnp.float32 else part

    return jax.tree.map(short, value)


def rms_scale(values, gain_row):
    mean_square = jnp.mean(values * values, axis=-1, keepdims=True)
    return values * lax.rsqrt(mean_square + epsilon) * gain_row


def masked_softmax(scores, allowed):
    scores = jnp.where(allowed, scores, -1e30)
    largest = jnp.max(scores, axis=-1, keepdims=True)
    raised = jnp.where(allowed, jnp.exp(scores - largest), 0.0)
    return raised / jnp.sum(raised, axis=-1, keepdims=True)


def rotate(values, position):
    halfway = values.shape[-1] // 2
    frequency = jnp.power(
        rope_base, -2.0 * jnp.arange(halfway, dtype=jnp.float32) / values.shape[-1]
    )
    angles = position.astype(jnp.float32)[:, None] * frequency[None, :]
    cosine = jnp.cos(angles)[:, None, :]
    sine_rows = jnp.sin(angles)[:, None, :]
    lower_half = values[..., :halfway]
    upper_half = values[..., halfway:]
    return jnp.concatenate(
        [
            lower_half * cosine - upper_half * sine_rows,
            upper_half * cosine + lower_half * sine_rows,
        ],
        axis=-1,
    )


def patch_block(extended, first_byte, end_byte, in_use, anchor, lift, cross_kv):
    columns = anchor + jnp.arange(extended.shape[0], dtype=jnp.int32)
    inside = (
        (columns[None, :] >= first_byte[:, None])
        & (columns[None, :] < end_byte[:, None])
        & in_use[:, None]
    )
    member = inside.astype(jnp.bfloat16)
    totals = jnp.dot(member, extended, preferred_element_type=jnp.float32)
    lengths = jnp.maximum(jnp.sum(inside.astype(jnp.float32), axis=1), 1.0)
    pooled = (totals / lengths[:, None]).astype(jnp.bfloat16)
    lifted = jnp.dot(pooled, lift, preferred_element_type=jnp.float32)
    key_rows = jnp.dot(extended, cross_kv[0], preferred_element_type=jnp.float32).astype(
        jnp.bfloat16
    )
    value_rows = jnp.dot(extended, cross_kv[1], preferred_element_type=jnp.float32).astype(
        jnp.bfloat16
    )
    slot_total = first_byte.shape[0]
    head_count = lifted.shape[1] // HD
    queries = lifted.astype(jnp.bfloat16).reshape(slot_total, head_count, HD)
    scores = jnp.einsum(
        "phd,khd->hpk",
        queries,
        key_rows.reshape(-1, head_count, HD),
        preferred_element_type=jnp.float32,
    ) * (1.0 / math.sqrt(HD))
    allowed = inside | (~in_use)[:, None] & (columns[None, :] == anchor)
    weights = masked_softmax(scores, allowed[None]).astype(jnp.bfloat16)
    crossed = jnp.einsum(
        "hpk,khd->phd",
        weights,
        value_rows.reshape(-1, head_count, HD),
        preferred_element_type=jnp.float32,
    )
    crossed = crossed.reshape(slot_total, head_count * HD)
    return jnp.where(in_use[:, None], lifted + crossed, 0.0).astype(jnp.bfloat16)


def add_counts(earlier, later):
    return earlier + later


def gathered_shards(
    byte_states,
    enc_gain,
    enc_qkv,
    enc_proj_out,
    starts,
    counts,
    lift,
    cross_kv,
    latent_gain,
    lat_qkv,
    lat_proj_out,
):
    byte_rows = byte_states.shape[0]
    anchor = lax.axis_index("seq") * byte_rows
    states = byte_states.astype(jnp.float32)
    normed = rms_scale(states, enc_gain.astype(jnp.float32)).astype(jnp.bfloat16)
    projected = jnp.einsum(
        "bd,idc->ibc", normed, enc_qkv, preferred_element_type=jnp.float32
    ).astype(jnp.bfloat16)
    reach_blocks = max(WIN // byte_rows, 1)
    tail_rows = min(WIN, byte_rows)
    key_parts = []
    value_parts = []
    for distance in range(reach_blocks, 0, -1):
        moved_keys, moved_values = from_behind(
            (projected[1, byte_rows - tail_rows :], projected[2, byte_rows - tail_rows :]),
            "seq",
            distance,
        )
        key_parts.append(moved_keys)
        value_parts.append(moved_values)
    key_rows = jnp.concatenate(key_parts + [projected[1]], axis=0)
    value_rows = jnp.concatenate(value_parts + [projected[2]], axis=0)
    head_count = projected.shape[2] // EH
    scores = jnp.einsum(
        "qhd,khd->hqk",
        projected[0].reshape(byte_rows, head_count, EH),
        key_rows.reshape(-1, head_count, EH),
        preferred_element_type=jnp.float32,
    ) * (1.0 / math.sqrt(EH))
    query_pos = anchor + jnp.arange(byte_rows, dtype=jnp.int32)
    key_pos = anchor - WIN + jnp.arange(WIN + byte_rows, dtype=jnp.int32)
    allowed = (
        (key_pos[None, :] <= query_pos[:, None])
        & (key_pos[None, :] > query_pos[:, None] - WIN)
        & (key_pos[None, :] >= 0)
    )
    weights = masked_softmax(scores, allowed[None]).astype(jnp.bfloat16)
    attended = jnp.einsum(
        "hqk,khd->qhd",
        weights,
        value_rows.reshape(-1, head_count, EH),
        preferred_element_type=jnp.float32,
    )
    attended = attended.reshape(byte_rows, head_count * EH).astype(jnp.bfloat16)
    blended = lax.psum(jnp.dot(attended, enc_proj_out, preferred_element_type=jnp.float32), "tp")
    encoded = (states + blended).astype(jnp.bfloat16)
    patch_count = counts[0]
    local_starts = starts[0]
    first_local = (local_starts[0:1] - anchor).astype(jnp.bfloat16)
    next_rows, next_first = from_behind((encoded[:SPILL], first_local), "seq", -1)
    next_first = next_first.astype(jnp.int32)[0]
    extended = jnp.concatenate([encoded, next_rows], axis=0)
    slot_ids = jnp.arange(local_starts.shape[0], dtype=jnp.int32)
    in_use = slot_ids < patch_count
    following = jnp.concatenate([local_starts[1:], jnp.zeros((1,), jnp.int32)])
    patch_end = jnp.where(slot_ids + 1 < patch_count, following, anchor + byte_rows + next_first)
    patches = patch_block(extended, local_starts, patch_end, in_use, anchor, lift, cross_kv)
    offset = prefix(counts, "seq", add_counts, jnp.zeros((1,), jnp.int32))[0]
    position = offset + slot_ids
    slot_total = patches.shape[0]
    full_rows = lax.all_gather(patches, "tp", axis=1, tiled=True)
    normed_rows = rms_scale(full_rows.astype(jnp.float32), latent_gain.astype(jnp.float32)).astype(
        jnp.bfloat16
    )
    inner_width = lat_qkv.shape[2]
    projected = jnp.einsum(
        "pd,idc->ipc",
        normed_rows,
        lax.all_gather(lat_qkv, "seq", axis=1, tiled=True),
        preferred_element_type=jnp.float32,
    )
    heads_here = inner_width // HD
    queries = rotate(projected[0].reshape(slot_total, heads_here, HD), position).astype(
        jnp.bfloat16
    )
    latent_keys = (
        rotate(projected[1].reshape(slot_total, heads_here, HD), position)
        .astype(jnp.bfloat16)
        .reshape(slot_total, inner_width)
    )
    latent_values = projected[2].astype(jnp.bfloat16)
    latent_pos = jnp.where(in_use, position, far_position)
    largest = jnp.full((heads_here, slot_total), -1e30, jnp.float32)
    piece_keys = lax.all_gather(latent_keys, "seq", axis=0, tiled=True)
    piece_values = lax.all_gather(latent_values, "seq", axis=0, tiled=True)
    piece_pos = lax.all_gather(shortened(latent_pos), "seq", axis=0, tiled=True)
    rows_here = piece_keys.shape[0]
    piece_scores = jnp.einsum(
        "qhd,khd->hqk",
        queries,
        piece_keys.reshape(rows_here, heads_here, HD),
        preferred_element_type=jnp.float32,
    ) * (1.0 / math.sqrt(HD))
    permitted = (piece_pos[None, :] <= position[:, None])[None]
    piece_scores = jnp.where(permitted, piece_scores, -1e30)
    renewed = jnp.maximum(largest, jnp.max(piece_scores, axis=-1))
    raised = jnp.where(permitted, jnp.exp(piece_scores - renewed[..., None]), 0.0)
    weight_sum = jnp.sum(raised, axis=-1)
    weighted = jnp.einsum(
        "hqk,khd->hqd",
        raised.astype(jnp.bfloat16),
        piece_values.reshape(rows_here, heads_here, HD),
        preferred_element_type=jnp.float32,
    )
    largest, weight_sum, weighted = (renewed, weight_sum, weighted)
    latent_heads = (
        (weighted / weight_sum[..., None])
        .transpose(1, 0, 2)
        .reshape(slot_total, inner_width)
        .astype(jnp.bfloat16)
    )
    partials = jnp.dot(
        latent_heads,
        lax.all_gather(lat_proj_out, "seq", axis=1, tiled=True),
        preferred_element_type=jnp.float32,
    )
    reduced = lax.psum_scatter(partials, "tp", scatter_dimension=1, tiled=True)
    latent = jnp.where(in_use[:, None], patches.astype(jnp.float32) + reduced, 0.0).astype(
        jnp.bfloat16
    )
    return (encoded, latent)


MESH = pl.DeviceIdType.MESH
EDGE = 16


def seq_peer(index):
    return {"seq": index}


def tp_peer(index):
    return {"tp": index}


def like(shape, dtype=jnp.bfloat16):
    return jax.ShapeDtypeStruct(shape, dtype)


def iota(shape, axis):
    return lax.broadcasted_iota(jnp.int32, shape, axis)


def across_lanes(left, right):
    return lax.dot_general(
        left, right, (((1,), (1,)), ((), ())), preferred_element_type=jnp.float32
    )


def product(left, right):
    return jnp.dot(left, right, preferred_element_type=jnp.float32)


def remote(source, target, send_sem, recv_sem, device):
    return pltpu.make_async_remote_copy(
        src_ref=source,
        dst_ref=target,
        send_sem=send_sem,
        recv_sem=recv_sem,
        device_id=device,
        device_id_type=MESH,
    )


def turn_table(rows):
    frequency = rope_base ** (-2.0 * np.arange(HD // 2, dtype=np.float64) / HD)
    frequency = frequency.astype(np.float32)
    angles = np.arange(rows, dtype=np.float32)[:, None] * frequency[None, :]
    angles = angles.astype(np.float64)
    return np.concatenate([np.cos(angles), np.sin(angles)], axis=1).astype(np.float32)


def whole_layer(
    states, gain, enc_qkv, proj, starts, lift, cross_kv, latent_gain, lat_qkv, lat_proj, table,
    call_id,
):
    count, size = lax.axis_size("tp"), lax.axis_size("seq")
    near = count - 1
    byte_rows, width = states.shape
    total_rows = byte_rows + EDGE
    enc_cols = enc_qkv.shape[2]
    enc_heads = enc_cols // EH
    slots = starts.shape[1]
    columns = lift.shape[1]
    group = 2 * HD
    panel_count = columns // group
    row_total = count * slots
    half = lat_qkv.shape[1]
    full_width = columns * count
    rows_half = byte_rows // 2
    row_spans = ((0, rows_half), (rows_half, rows_half), (byte_rows, EDGE))
    halves_of = ((0, rows_half), (rows_half, total_rows - rows_half))
    part_rows = slots // 2
    half_total = row_total // 2
    share = enc_cols // 2
    piece = share // count

    def kernel(
        states_hbm, gain_hbm, qkv_hbm, proj_hbm, starts_hbm, lift_hbm, cross_hbm,
        lgain_hbm, w_own_hbm, o_hbm, table_hbm,
        enc_ref, out_ref,
        gain_ref, starts_ref, lgain_ref, states_ref, qkv_ref, query_ref, kv_ref, infos, proj_ref, att_ref, near_ref, blend_ref, table_ref, cos_ref, sin_ref,
        lift_ref, cross_ref, pooled_ref, full_ref, panels, rows_ref, patch_ref,
        w_own, w_other, geared, own_part, qkv_send, qkv_land, sq_send, sq_land,
        kv_own, kv_other, out_quarter, out_rows, tall, parts, land,
        load_sems, info_s, info_r, halo_s, halo_r, edge_s, edge_r, pz_s, pz_r, pp_s, pp_r, pc_s, pc_r,
        w_sems, heads_send, heads_recv,
        panel_send, panel_recv, stay_sems,
        qkv_s, qkv_r, sq_s, sq_r, kv_s, kv_r,
        oq_s, oq_r, oz_s, oz_r, oc_s, oc_r, own_sems, tz_s, tz_r, a_s, a_r, enc_sem,
    ):
        s, t = lax.axis_index("seq"), lax.axis_index("tp")
        p, c = s // 2, lax.rem(s, 2)
        partner = seq_peer(s + 1 - 2 * c)

        def plane(index):
            return {"seq": 2 * index + c}

        def ring(k):
            return lax.rem(s + k + size, size)

        def tower(k):
            return lax.rem(t + k + count, count)

        def flip(k):
            if k == 0:
                return p
            if k == 1:
                return p + 1 - 2 * lax.rem(p, 2)
            if k == 2:
                return lax.rem(p + 2, 4)
            return 3 - p

        far_first = (3, 2, 1)
        low = t < 2
        inner = (t == 1) | (t == 2)
        first_from = jnp.where(low, t + 1, t - 1)
        second_from = jnp.where(low, t + 2, t - 2)
        third_from = jnp.where(lax.rem(t, 2) == 0, count - 1, 0)
        outer = jnp.where(low, 0, count - 1)
        outward = (t, third_from, second_from, first_from)

        def to_near(copy_to):
            copy_to(first_from, 0).start()

            @pl.when(inner)
            def _():
                copy_to(outer, 1).start()

        def sent_near(copy_to, over):
            copy_to(first_from, 0).wait_send()

            @pl.when(inner)
            def _():
                copy_to(outer, 1).wait_send()
                for i in range(3):
                    over(i).wait_send()

        barrier = pltpu.get_barrier_semaphore()
        for k in range(1, size):
            pl.semaphore_signal(barrier, inc=1, device_id=seq_peer(ring(k)), device_id_type=MESH)
        for k in range(1, count):
            pl.semaphore_signal(barrier, inc=1, device_id=tp_peer(tower(k)), device_id_type=MESH)

        @pl.when(p != t)
        def _():
            for k in far_first:
                away_peer = {"seq": 2 * flip(k) + c, "tp": p}
                pl.semaphore_signal(barrier, inc=1, device_id=away_peer, device_id_type=MESH)

        own_rows = pl.ds(pl.multiple_of(p * HD, HD), HD)
        load_plan = (
            (states_hbm, states_ref.at[pl.ds(0, byte_rows)]),
            (qkv_hbm, qkv_ref),
            (table_hbm, table_ref),
            (proj_hbm.at[pl.ds(0, share)], proj_ref.at[0, 0]),
            (proj_hbm.at[pl.ds(share, share)], proj_ref.at[1, 0]),
            (lift_hbm, lift_ref),
            (cross_hbm, cross_ref),
            (w_own_hbm, w_own),
            (o_hbm.at[own_rows], out_quarter.at[p]),
            (gain_hbm, gain_ref),
            (starts_hbm, starts_ref),
            (lgain_hbm, lgain_ref),
        )
        loads = [
            pltpu.make_async_copy(source, target, load_sems.at[i])
            for i, (source, target) in enumerate(load_plan)
        ]
        for i in (0, 9, 1, 10, 2, 3, 4, 5, 6, 7, 8, 11):
            loads[i].start()
        sent = []

        def launch(copy):
            copy.start()
            sent.append(copy)
            return copy
        loads[0].wait()
        loads[9].wait()
        values = states_ref[0:byte_rows].astype(jnp.float32)
        chip_row = gain_ref[...].astype(jnp.float32).reshape(1, width)
        normed = rms_scale(values, chip_row).astype(jnp.bfloat16)
        own = pl.ds(WIN, byte_rows)
        loads[1].wait()
        for i in range(2):
            fresh = product(normed, qkv_ref[i + 1]).astype(jnp.bfloat16)
            for h in range(2):
                kv_ref[h, i, own] = fresh[:, h * share : (h + 1) * share]
        query_ref[0:byte_rows] = (
            product(normed, qkv_ref[0]) * (1.0 / math.sqrt(EH))
        ).astype(jnp.bfloat16)
        loads[10].wait()
        listed = jnp.where(starts_ref[...] < size * byte_rows, 1, 0)
        my_count = jnp.sum(listed, axis=1, keepdims=True)
        info_lane = iota((8, 128), 1)
        infos[s] = jnp.where(
            info_lane == 0, my_count, jnp.where(info_lane == 1, starts_ref[0:1, 0:1], 0)
        )
        greetings = size - 1 + count - 1

        @pl.when(p == t)
        def _():
            pl.semaphore_wait(barrier, greetings)

        @pl.when(p != t)
        def _():
            pl.semaphore_wait(barrier, greetings + count - 1)

        mine_at = pl.multiple_of(p * piece, piece)
        lifts = [
            launch(
                remote(
                    proj_hbm.at[pl.ds(pl.multiple_of(c * share + p * piece, piece), piece)],
                    proj_ref.at[c, k, pl.ds(mine_at, piece)],
                    pz_s.at[k - 1],
                    pz_r.at[k - 1],
                    tp_peer(tower(k)),
                )
            )
            for k in range(1, count)
        ]
        notes = [
            launch(
                remote(infos.at[s], infos.at[s], info_s.at[k - 1], info_r.at[k - 1], seq_peer(ring(k)))
            )
            for k in range(1, size)
        ]
        behind = seq_peer(ring(-1))
        edges = [
            launch(remote(source, target, edge_s.at[i], edge_r.at[i], behind))
            for i, (source, target) in enumerate(
                (
                    (
                        kv_ref.at[:, :, pl.ds(WIN, EDGE)],
                        kv_ref.at[:, :, pl.ds(WIN + byte_rows, EDGE)],
                    ),
                    (query_ref.at[pl.ds(0, EDGE)], query_ref.at[pl.ds(byte_rows, EDGE)]),
                    (states_ref.at[pl.ds(0, EDGE)], states_ref.at[pl.ds(byte_rows, EDGE)]),
                )
            )
        ]
        halos = [
            launch(
                remote(
                    kv_ref.at[h, :, own],
                    kv_ref.at[h, :, pl.ds(0, byte_rows)],
                    halo_s.at[0, h],
                    halo_r.at[0, h],
                    seq_peer(ring(2)),
                )
            )
            for h in range(2)
        ]
        def beside(i):
            first = pl.multiple_of(jnp.where(c == 0, WIN, 0), byte_rows)
            return remote(
                kv_ref.at[i, :, pl.ds(first, byte_rows)],
                kv_ref.at[i, :, pl.ds(byte_rows, byte_rows)],
                halo_s.at[1, i],
                halo_r.at[1, i],
                partner,
            )

        @pl.when(c == 0)
        def _():
            for i in range(2):
                beside(i).start()
        for copy in notes:
            copy.wait_recv()
        counted = [infos[m][0:1, 0:1] for m in range(size)]
        offsets = [jnp.zeros((1, 1), jnp.int32)]
        for m in range(size - 1):
            offsets.append(offsets[m] + counted[m])
        next_first = jnp.where(
            s + 1 < size, infos[jnp.minimum(s + 1, size - 1)][0:1, 1:2], size * byte_rows
        )
        square = (slots, slots)
        start_row = jnp.broadcast_to(starts_ref[...], square)
        apart = iota(square, 1) - iota(square, 0)
        first_byte = jnp.sum(jnp.where(apart == 0, start_row, 0), axis=1, keepdims=True)
        following = jnp.sum(jnp.where(apart == 1, start_row, 0), axis=1, keepdims=True)
        slot_at = iota((slots, 1), 0)
        in_use = slot_at < my_count
        patch_end = jnp.where(slot_at + 1 < my_count, following, next_first)
        anchor = s * byte_rows
        lower = jnp.where(in_use, first_byte - anchor, 0)
        upper = jnp.where(in_use, patch_end - anchor, 1)
        where_at = iota((slots, total_rows), 1)
        allowed = (where_at >= lower) & (where_at < upper)
        member = jnp.where(allowed & in_use, 1.0, 0.0)
        lengths = jnp.maximum(jnp.sum(member, axis=1, keepdims=True), 1.0)
        member = member.astype(jnp.bfloat16)
        bias = jnp.where(allowed, 0.0, -1e30)
        for begin, rows in row_spans:
            reach_rows = rows + WIN
            behind_by = iota((rows, reach_rows), 0) - iota((rows, reach_rows), 1) + WIN
            known = iota((rows, reach_rows), 1) >= WIN - begin - s * byte_rows
            near_by = (behind_by >= 0) & (behind_by < WIN) & known
            near_ref[begin : begin + rows, 0:reach_rows] = jnp.where(near_by, 0.0, -1e30)
        chosen = [
            (
                jnp.where(c == 0, offsets[2 * i], offsets[2 * i + 1]),
                jnp.where(c == 0, counted[2 * i], counted[2 * i + 1]),
                jnp.where(c == 0, offsets[2 * i + 1], offsets[2 * i]),
                jnp.where(c == 0, counted[2 * i + 1], counted[2 * i]),
            )
            for i in range(count)
        ]

        def laid(shape, axis, which):
            at = iota(shape, axis)
            band = at // half_total
            within = at - band * half_total
            block = within // part_rows
            result = jnp.broadcast_to(chosen[0][which], shape)
            for i in range(1, count):
                result = jnp.where(block == i, chosen[i][which], result)
            return band * part_rows + within - block * part_rows, result

        row_slot, row_offset = laid((row_total, 1), 0, 0)
        position = row_offset + row_slot
        key_positions = []
        for which in (0, 2):
            key_slot, key_offset = laid((1, row_total), 1, which)
            _, key_count = laid((1, row_total), 1, which + 1)
            key_positions.append(
                jnp.where(key_slot < key_count, key_offset + key_slot, far_position)
            )
        loads[2].wait()
        table_rows = table_ref.shape[0]
        picked = jnp.where(iota((row_total, table_rows), 1) == position, 1.0, 0.0)
        turns = lax.dot_general(
            picked,
            table_ref[...],
            (((1,), (0,)), ((), ())),
            precision=lax.Precision.HIGHEST,
            preferred_element_type=jnp.float32,
        )
        swapped = pltpu.roll(turns, HD // 2, 1)
        low_lanes = iota((row_total, HD), 1) < HD // 2
        cos_ref[...] = jnp.where(low_lanes, turns, swapped)
        sin_ref[...] = jnp.where(low_lanes, -swapped, turns)
        def halo_arrives(h):
            halos[h].wait_recv()

            @pl.when(c == 1)
            def _():
                beside(h).start()

        halo_arrives(0)
        for copy in lifts:
            copy.wait_recv()
        spread = [
            launch(
                remote(
                    proj_ref.at[c, pl.ds(1, near), pl.ds(mine_at, piece)],
                    proj_ref.at[c, pl.ds(1, near), pl.ds(mine_at, piece)],
                    pp_s.at[k - 1],
                    pp_r.at[k - 1],
                    plane(flip(k)),
                )
            )
            for k in far_first
        ]
        def shared(k):
            rows = pl.ds(pl.multiple_of(flip(k) * piece, piece), piece)
            return remote(
                proj_ref.at[c, pl.ds(1, near), rows],
                proj_ref.at[c, pl.ds(1, near), rows],
                pc_s.at[k],
                pc_r.at[k],
                partner,
            )

        launch(shared(0))
        for copy in edges:
            copy.wait_recv()

        beside(0).wait_recv()
        def share_heads(origin, h, target, sem):
            return remote(
                att_ref.at[origin, h // 2, pl.ds(*halves_of[h % 2])],
                att_ref.at[origin, h // 2, pl.ds(*halves_of[h % 2])],
                heads_send.at[h, sem],
                heads_recv.at[h, origin],
                tp_peer(target),
            )

        def attend(pair, begin, rows):
            reach_rows = rows + WIN
            keys = kv_ref[pair, 0, begin : begin + reach_rows]
            seen_values = kv_ref[pair, 1, begin : begin + reach_rows]
            queries = query_ref[begin : begin + rows, pair * share : (pair + 1) * share]
            head_of = iota((rows, share), 1) // EH
            stacked = jnp.concatenate(
                [jnp.where(head_of == h, queries, jnp.zeros_like(queries)) for h in range(share // EH)],
                axis=0,
            )
            near_bias = near_ref[begin : begin + rows, 0:reach_rows]
            scores = across_lanes(stacked, keys)
            raised, sums = [], []
            for h in range(share // EH):
                here = scores[h * rows : (h + 1) * rows] + near_bias
                here = jnp.exp(here - jnp.max(here, axis=1, keepdims=True))
                sums.append(jnp.sum(here, axis=1, keepdims=True))
                raised.append(here.astype(jnp.bfloat16))
            seen = product(jnp.concatenate(raised, axis=0), seen_values)
            attended = jnp.zeros((rows, share), jnp.float32)
            for h in range(share // EH):
                attended = jnp.where(
                    head_of == h, seen[h * rows : (h + 1) * rows] / sums[h], attended
                )
            att_ref[t, pair, begin : begin + rows] = attended.astype(jnp.bfloat16)

        for h in range(2):
            if h:
                halo_arrives(1)
                beside(1).wait_recv()
            for begin, rows in row_spans:
                attend(h, begin, rows)
                if begin != rows_half:
                    piece_id = 2 * h + (begin > 0)
                    to_near(lambda target, sem: share_heads(t, piece_id, target, sem))

        swaps = [launch(remote(w_own_hbm, w_other, w_sems.at[0], w_sems.at[1], partner))]
        sources = (first_from, second_from, third_from)
        beyond = (outer, outer, first_from)

        def hand_over(which, h):
            return share_heads(sources[which], h, beyond[which], 2 + which)

        def gain_heads(which, h):
            hand_over(which, h).wait_recv()

            @pl.when(inner)
            def _():
                hand_over(which, h).start()

        def blended(h):
            attended = jnp.concatenate([att_ref[tower(-k), h] for k in range(count)], axis=1)
            return product(attended, proj_ref[h].reshape(count * share, width))
        for h in range(4):
            gain_heads(0, h)

            @pl.when(inner)
            def _():
                gain_heads(2, h)
                if h > 1:
                    gain_heads(1, h - 2)
        @pl.when(inner)
        def _():
            for h in (2, 3):
                gain_heads(1, h)
        for k, copy in zip(far_first[::-1], spread[::-1]):
            copy.wait_recv()
            launch(shared(k))
        quarters = [
            launch(
                remote(
                    o_hbm.at[pl.ds(pl.multiple_of(flip(k) * HD, HD), HD)],
                    out_quarter.at[p],
                    oq_s.at[k - 1],
                    oq_r.at[k - 1],
                    plane(flip(k)),
                )
            )
            for k in far_first
        ]
        @pl.when(jnp.logical_not(inner))
        def _():
            for h in (0, 1):
                gain_heads(1, h)
                gain_heads(2, h)

        loads[3].wait()
        loads[4].wait()
        @pl.when(jnp.logical_not(inner))
        def _():
            for h in (2, 3):
                gain_heads(1, h)
                gain_heads(2, h)
        blend_ref[...] = states_ref[...].astype(jnp.float32) + blended(c)
        for k in range(count):
            shared(k).wait_recv()
        full_ref[...] = (blend_ref[...] + blended(1 - c)).astype(jnp.bfloat16)
        enc_out = pltpu.make_async_copy(full_ref.at[pl.ds(0, byte_rows)], enc_ref, enc_sem.at[0])
        enc_out.start()

        totals = product(member, full_ref[...])
        pooled_ref[...] = (totals / lengths).astype(jnp.bfloat16)
        loads[5].wait()
        loads[6].wait()

        half_lanes = columns // 2

        def window(r, i):
            if r == 0:
                return pl.ds(i * group, group)
            return pl.ds(i * half_lanes, half_lanes)

        def slot_of(r, i):
            return i if r == 0 else panel_count + i

        def away(k, r, i):
            return remote(
                panels.at[r, :, window(r, i)],
                rows_ref.at[r, p, :, window(r, i)],
                panel_send.at[k, slot_of(r, i)],
                panel_recv.at[p, slot_of(r, i)],
                {"seq": 2 * t + c, "tp": outward[k]},
            )

        def stay(r, i):
            return pltpu.make_async_copy(
                panels.at[r, :, window(r, i)],
                rows_ref.at[r, p, :, window(r, i)],
                stay_sems.at[slot_of(r, i)],
            )

        def ship(r, i):
            for k in range(1, count):
                away(k, r, i).start()

            @pl.when(p != t)
            def _():
                away(0, r, i).start()

            @pl.when(p == t)
            def _():
                stay(r, i).start()

        widths = (panel_count, 2)

        def heads(i, carry):
            cols = pl.ds(i * group, group)
            rows = full_ref[...]
            lifted = product(pooled_ref[...], lift_ref[:, cols])
            keys = product(rows, cross_ref[0, :, cols]).astype(jnp.bfloat16)
            seen_values = product(rows, cross_ref[1, :, cols]).astype(jnp.bfloat16)
            queries = lifted.astype(jnp.bfloat16)
            crossed = []
            for j in range(2):
                lanes = slice(j * HD, (j + 1) * HD)
                scores = across_lanes(queries[:, lanes], keys[:, lanes])
                scores = scores * (1.0 / math.sqrt(HD)) + bias
                raised = jnp.exp(scores - jnp.max(scores, axis=1, keepdims=True))
                crossed.append(
                    product(raised.astype(jnp.bfloat16), seen_values[:, lanes])
                    / jnp.sum(raised, axis=1, keepdims=True)
                )
            patch = lifted + jnp.concatenate(crossed, axis=1)
            panel = jnp.where(in_use, patch, 0.0).astype(jnp.bfloat16)
            patch_ref[:, cols] = panel
            for r in range(2):
                panels[r, :, cols] = panel[r * part_rows : (r + 1) * part_rows]
            ship(0, i)
            return carry
        for i in range(panel_count):
            heads(i, 0)
        for i in range(widths[1]):
            ship(1, i)
        for copy in quarters:
            copy.wait_recv()
        loads[8].wait()
        mine_out = pltpu.make_async_copy(
            out_quarter.at[t], out_rows.at[c, t], own_sems.at[0]
        )
        mine_out.start()
        ups = [
            remote(
                out_quarter.at[tower(k)],
                out_rows.at[c, t],
                oz_s.at[k - 1],
                oz_r.at[k - 1],
                tp_peer(tower(k)),
            )
            for k in range(1, count)
        ]

        @pl.when(inner)
        def _():
            for copy in ups:
                copy.start()

        @pl.when(t == 0)
        def _():
            ups[0].start()

        @pl.when(t == count - 1)
        def _():
            ups[2].start()

        arriving, flats = ([], []), []
        eye = iota((half_total, half_total), 0) == iota((half_total, half_total), 1)
        loads[11].wait()
        chip_gain = lgain_ref[pl.ds(pl.multiple_of(p * columns, columns), columns)]
        chip_gain = chip_gain.astype(jnp.float32).reshape(1, columns)
        for r in range(2):
            for q in range(count):

                @pl.when((p != q) | (p != t))
                def _():
                    for i in range(widths[r]):
                        remote(
                            panels.at[r, :, window(r, i)],
                            rows_ref.at[r, q, :, window(r, i)],
                            panel_send.at[0, slot_of(r, i)],
                            panel_recv.at[q, slot_of(r, i)],
                            plane(p),
                        ).wait_recv()

            @pl.when(p == t)
            def _():
                for i in range(widths[r]):
                    stay(r, i).wait()

            if r:

                @pl.when(t == 0)
                def _():
                    ups[2].start()
                    ups[1].start()

                @pl.when(t == count - 1)
                def _():
                    ups[0].start()
                    ups[1].start()
            values = rows_ref[r].reshape(half_total, columns).astype(jnp.float32)
            squares = jnp.sum(values * values, axis=1, keepdims=True)
            flat = jnp.sum(jnp.where(eye, squares, 0.0), axis=0, keepdims=True)
            flats.append(flat)
            sq_send[r] = jnp.broadcast_to(flat, (8, half_total))
            geared[...] = (values * chip_gain).astype(jnp.bfloat16)
            for k in far_first:
                arriving[r].append(
                    launch(
                        remote(
                            sq_send.at[r],
                            sq_land.at[r, k - 1],
                            sq_s.at[r, k - 1],
                            sq_r.at[r, k - 1],
                            plane(flip(k)),
                        )
                    )
                )
            if r == 0:
                loads[7].wait()
                swaps[0].wait_recv()
            mine = geared[:, pl.ds(pl.multiple_of(c * half, half), half)]
            theirs = geared[:, pl.ds(pl.multiple_of((1 - c) * half, half), half)]
            for k in far_first + (0,):
                target = flip(k)
                lanes = pl.ds(pl.multiple_of(target * HD, HD), HD)
                for i in range(3):
                    part = product(mine, w_own[i, :, lanes]) + product(theirs, w_other[i, :, lanes])
                    if k:
                        qkv_send[r, k - 1, i] = part.astype(jnp.bfloat16)
                    else:
                        own_part[r, i] = part
                if k:
                    arriving[r].append(
                        launch(
                            remote(
                                qkv_send.at[r, k - 1],
                                qkv_land.at[r, k - 1],
                                qkv_s.at[r, k - 1],
                                qkv_r.at[r, k - 1],
                                plane(target),
                            )
                        )
                    )

        sent.extend(ups)

        def turned(vectors, rows):
            return (
                vectors * cos_ref[rows] + pltpu.roll(vectors, HD // 2, 1) * sin_ref[rows]
            ).astype(jnp.bfloat16)

        swaps_kv, queries = [], []
        for r in range(2):
            for copy in arriving[r]:
                copy.wait_recv()
            flat = flats[r] + jnp.sum(sq_land[r, :, 0:1, :], axis=0)
            square_sum = jnp.sum(jnp.where(eye, flat, 0.0), axis=1, keepdims=True)
            scale = lax.rsqrt(square_sum / full_width + epsilon)
            total = []
            for i in range(3):
                band = own_part[r, i]
                for k in range(count - 1):
                    band = band + qkv_land[r, k, i].astype(jnp.float32)
                total.append(band * scale)
            rows = slice(r * half_total, (r + 1) * half_total)
            kv_own[r, 0] = turned(total[1], rows)
            kv_own[r, 1] = total[2].astype(jnp.bfloat16)
            swaps_kv.append(
                launch(remote(kv_own.at[r], kv_other.at[r], kv_s.at[r], kv_r.at[r], partner))
            )
            queries.append(turned(total[0], rows))
        queries = jnp.concatenate(queries, axis=0)

        def both(ref, i):
            return jnp.concatenate([ref[0, i], ref[1, i]], axis=0)
        def scored(keys, key_position):
            scores = across_lanes(queries, keys) * (1.0 / math.sqrt(HD))
            return jnp.where(key_position <= position, scores, -1e30)

        scores_a = scored(both(kv_own, 0), key_positions[0])
        for copy in swaps_kv:
            copy.wait_recv()
        scores_b = scored(both(kv_other, 0), key_positions[1])
        largest = jnp.maximum(
            jnp.max(scores_a, axis=1, keepdims=True), jnp.max(scores_b, axis=1, keepdims=True)
        )
        raised_a = jnp.exp(scores_a - largest)
        raised_b = jnp.exp(scores_b - largest)
        weight_sum = jnp.sum(raised_a, axis=1, keepdims=True) + jnp.sum(
            raised_b, axis=1, keepdims=True
        )
        weighted = product(raised_a.astype(jnp.bfloat16), both(kv_own, 1)) + product(
            raised_b.astype(jnp.bfloat16), both(kv_other, 1)
        )
        tall[t] = (weighted / weight_sum).astype(jnp.bfloat16).reshape(2, half_total, HD)
        for k in far_first + (0,):
            take = pl.ds(pl.multiple_of(flip(k) * part_rows, part_rows), part_rows)
            for d in range(1, count):
                launch(
                    remote(
                        tall.at[t, :, take],
                        tall.at[t, :, take],
                        tz_s.at[k, d - 1],
                        tz_r.at[k, t],
                        tp_peer(outward[d]),
                    )
                )
        def beside_rows(k):
            return remote(
                out_rows.at[c, tower(-k)],
                out_rows.at[c, tower(-k)],
                oc_s.at[k],
                oc_r.at[k],
                partner,
            )

        mine_out.wait()
        launch(beside_rows(0))
        for k in (1, 3, 2):
            ups[k - 1].wait_recv()
            launch(beside_rows(k))
        for k in range(count):
            beside_rows(k).wait_recv()
        hops, parts_own = [], []
        summed = patch_ref[...].astype(jnp.float32)
        for k in far_first + (0,):
            for d in range(1, count):
                take = pl.ds(pl.multiple_of(flip(k) * part_rows, part_rows), part_rows)
                remote(
                    tall.at[tower(-d), :, take],
                    tall.at[tower(-d), :, take],
                    tz_s.at[k, d - 1],
                    tz_r.at[k, tower(-d)],
                    tp_peer(tower(-d)),
                ).wait_recv()
            take = pl.ds(pl.multiple_of(flip(k) * part_rows, part_rows), part_rows)
            attended = jnp.concatenate(
                [tall[q, :, take].reshape(slots, HD) for q in range(count)], axis=1
            )
            for core in range(2):
                lanes = slice(core * half, (core + 1) * half)
                part = product(attended, out_rows[core].reshape(count * HD, half))
                if k:
                    parts[k - 1, :, lanes] = part.astype(jnp.bfloat16)
                else:
                    parts_own.append(part)
            if k:
                hops.append(
                    launch(
                        remote(
                            parts.at[k - 1],
                            land.at[k - 1],
                            a_s.at[k - 1],
                            a_r.at[k - 1],
                            plane(flip(k)),
                        )
                    )
                )
        summed = summed + jnp.concatenate(parts_own, axis=1)
        for copy in hops:
            copy.wait_recv()
        for k in range(count - 1):
            summed = summed + land[k].astype(jnp.float32)
        out_ref[...] = jnp.where(in_use, summed, 0.0).astype(jnp.bfloat16)
        enc_out.wait()
        for copy in sent:
            copy.wait_send()
        for i in range(2):
            beside(i).wait_send()
        for h in range(4):
            sent_near(
                lambda target, sem: share_heads(t, h, target, sem), lambda which: hand_over(which, h)
            )

        for r in range(2):
            for i in range(widths[r]):
                for k in range(1, count):
                    away(k, r, i).wait_send()

                @pl.when(p != t)
                def _():
                    away(0, r, i).wait_send()
    hbm = pl.BlockSpec(memory_space=pl.ANY)
    vmem = pl.BlockSpec(memory_space=pltpu.VMEM)
    dma = pltpu.SemaphoreType.DMA

    def buffer(*shape, dtype=jnp.bfloat16):
        return pltpu.VMEM(shape, dtype)

    return pl.pallas_call(
        kernel,
        out_shape=[like((byte_rows, width)), like((slots, columns))],
        in_specs=[hbm] * 11,
        out_specs=[vmem, vmem],
        scratch_shapes=[
            buffer(width),
            buffer(1, slots, dtype=jnp.int32),
            buffer(full_width),
            buffer(total_rows, width),
            buffer(*enc_qkv.shape),
            buffer(total_rows, enc_cols),
            buffer(2, 2, WIN + total_rows, share),
            buffer(size, 8, 128, dtype=jnp.int32),
            buffer(2, count, share, width),
            buffer(count, 2, total_rows, share),
            buffer(total_rows, rows_half + WIN, dtype=jnp.float32),
            buffer(total_rows, width, dtype=jnp.float32),
            buffer(*table.shape, dtype=jnp.float32),
            buffer(row_total, HD, dtype=jnp.float32),
            buffer(row_total, HD, dtype=jnp.float32),
            buffer(*lift.shape),
            buffer(*cross_kv.shape),
            buffer(slots, width),
            buffer(total_rows, width),
            buffer(2, part_rows, columns),
            buffer(2, count, part_rows, columns),
            buffer(slots, columns),
            buffer(*lat_qkv.shape),
            buffer(*lat_qkv.shape),
            buffer(half_total, columns),
            buffer(2, 3, half_total, HD, dtype=jnp.float32),
            buffer(2, near, 3, half_total, HD),
            buffer(2, near, 3, half_total, HD),
            buffer(2, 8, half_total, dtype=jnp.float32),
            buffer(2, near, 8, half_total, dtype=jnp.float32),
            buffer(2, 2, half_total, HD),
            buffer(2, 2, half_total, HD),
            buffer(count, HD, half),
            buffer(2, count, HD, half),
            buffer(count, 2, half_total, HD),
            buffer(near, slots, columns),
            buffer(near, slots, columns),
            dma((12,)),
            dma((size - 1,)),
            dma((size - 1,)),
            dma((2, 2)),
            dma((2, 2)),
            dma((3,)),
            dma((3,)),
            dma((near,)),
            dma((near,)),
            dma((near,)),
            dma((near,)),
            dma((count,)),
            dma((count,)),
            dma((2,)),
            dma((4, 5)),
            dma((4, count)),
            dma((count, panel_count + 2)),
            dma((count, panel_count + 2)),
            dma((panel_count + 2,)),
            dma((2, near)),
            dma((2, near)),
            dma((2, near)),
            dma((2, near)),
            dma((2,)),
            dma((2,)),
            dma((near,)),
            dma((near,)),
            dma((near,)),
            dma((near,)),
            dma((count,)),
            dma((count,)),
            dma((1,)),
            dma((count, near)),
            dma((count, count)),
            dma((near,)),
            dma((near,)),
            dma((1,)),
        ],
        compiler_params=pltpu.CompilerParams(
            collective_id=call_id, has_side_effects=True, vmem_limit_bytes=52428800
        ),
    )(
        states, gain, enc_qkv, proj, starts, lift, cross_kv, latent_gain, lat_qkv, lat_proj, table,
    )


def settle(*arrays):
    total = len(arrays)

    def kernel(*refs):
        ins, outs, sems = refs[:total], refs[total : 2 * total], refs[2 * total]
        puts = [pltpu.make_async_copy(ins[i], outs[i], sems.at[i]) for i in range(total)]
        for put in puts:
            put.start()
        for put in puts:
            put.wait()

    return pl.pallas_call(
        kernel,
        out_shape=[like(value.shape, value.dtype) for value in arrays],
        in_specs=[pl.BlockSpec(memory_space=pl.ANY)] * total,
        out_specs=[pl.BlockSpec(memory_space=pltpu.HBM)] * total,
        scratch_shapes=[pltpu.SemaphoreType.DMA((total,))],
        compiler_params=pltpu.CompilerParams(vmem_limit_bytes=2**20),
    )(*arrays)


def fused_shards(
    byte_states,
    enc_gain,
    enc_qkv,
    enc_proj_out,
    starts,
    counts,
    lift,
    cross_kv,
    latent_gain,
    lat_qkv,
    lat_proj_out,
):
    table = jnp.asarray(turn_table(lax.axis_size("seq") * starts.shape[1]))
    operands = [
        pltpu.with_memory_space_constraint(value, pltpu.HBM)
        for value in (
            byte_states,
            enc_gain,
            enc_qkv,
            enc_proj_out,
            starts,
            lift,
            cross_kv,
            latent_gain,
            lat_qkv,
            lat_proj_out,
            table,
        )
    ]
    encoded, latent = whole_layer(*operands, 1)
    return settle(encoded, latent)


def fits_pairs(mesh, byte_states, enc_qkv, starts, lat_qkv):
    size, tp_size = mesh.shape["seq"], mesh.shape["tp"]
    byte_rows = byte_states.shape[0] // size
    return (
        size == 2 * tp_size
        and tp_size == 4
        and WIN % byte_rows == 0
        and WIN == 2 * byte_rows
        and byte_rows % (32 * tp_size) == 0
        and lat_qkv.shape[2] // tp_size == HD * tp_size
        and lat_qkv.shape[1] % (128 * size) == 0
        and starts.shape[1] * tp_size % 128 == 0
        and starts.shape[1] * tp_size <= 1024
        and starts.shape[1] % 16 == 0
        and enc_qkv.shape[2] % (128 * tp_size) == 0
    )


def solution(mesh):
    specs = dict(
        mesh=mesh,
        in_specs=(
            P("seq", None),
            P(),
            P(None, None, "tp"),
            P("tp", None),
            P("seq", None),
            P("seq"),
            P(None, "tp"),
            P(None, None, "tp"),
            P(),
            P(None, "seq", "tp"),
            P("tp", "seq"),
        ),
        out_specs=(P("seq", None), P("seq", "tp")),
        check_vma=False,
    )

    def run(*arrays):
        paired = fits_pairs(mesh, arrays[0], arrays[2], arrays[4], arrays[9])
        return jax.shard_map(fused_shards if paired else gathered_shards, **specs)(*arrays)

    return run
```
